32 devices in a mesh: dp: 4 (over x, core), fsdp: 8 (over z, y).
Axes of the slice: x: 2, y: 2, z: 4, core: 2. Of those that a mesh axis runs over, the one named last changes fastest.
Arguments:
- tokens: bfloat16 [4096, 2048], P(('dp', 'fsdp')), may hold values from -6 to 6
- cotangent: bfloat16 [4096, 2048], P(('dp', 'fsdp')), may hold values from -6 to 6
- routes: int32 [4096, 8], P(('dp', 'fsdp')), may hold values from 0 to 15, all different within a row; in each aligned block of 128 rows (0 to 127, 128 to 255, ...) at most 80 rows name the same one
- w_query: bfloat16 [2048, 2048], P(('dp', 'fsdp')), may hold values from -0.125 to 0.125
- w_key: bfloat16 [2048, 2048], P(('dp', 'fsdp')), may hold values from -0.125 to 0.125
- w_value: bfloat16 [2048, 2048], P(('dp', 'fsdp')), may hold values from -0.125 to 0.125
- w_output: bfloat16 [2048, 2048], P(('dp', 'fsdp')), may hold values from -0.5 to 0.5
- w_router: bfloat16 [2048, 16], P(('dp', 'fsdp')), may hold values from -0.0625 to 0.0625
- gain_attn: bfloat16 [2048], P(('dp', 'fsdp')), may hold values from 0.5 to 1.5
- gain_query: bfloat16 [2048], P(('dp', 'fsdp')), may hold values from 0.5 to 1.5
- gain_key: bfloat16 [2048], P(('dp', 'fsdp')), may hold values from 0.5 to 1.5
- gain_ffn: bfloat16 [2048], P(('dp', 'fsdp')), may hold values from 0.5 to 1.5
- expert_gate: bfloat16 [16, 2048, 1024], P('fsdp', None, 'dp'), may hold values from -0.125 to 0.125
- expert_up: bfloat16 [16, 2048, 1024], P('fsdp', None, 'dp'), may hold values from -0.125 to 0.125
- expert_down: bfloat16 [16, 2048, 1024], P('fsdp', None, 'dp'), may hold values from -0.75 to 0.75
Outputs:
- layer_out: bfloat16 [4096, 2048], P(('dp', 'fsdp'))
- grad_tokens: float32 [4096, 2048], P(('dp', 'fsdp'))
- grad_w_query: float32 [2048, 2048], P(('dp', 'fsdp'))
- grad_w_key: float32 [2048, 2048], P(('dp', 'fsdp'))
- grad_w_value: float32 [2048, 2048], P(('dp', 'fsdp'))
- grad_w_output: float32 [2048, 2048], P(('dp', 'fsdp'))
- grad_w_router: float32 [2048, 16], P(('dp', 'fsdp'))
- grad_gain_attn: float32 [2048], P(('dp', 'fsdp'))
- grad_gain_query: float32 [2048], P(('dp', 'fsdp'))
- grad_gain_key: float32 [2048], P(('dp', 'fsdp'))
- grad_gain_ffn: float32 [2048], P(('dp', 'fsdp'))
- grad_expert_gate: float32 [16, 2048, 1024], P('fsdp', None, 'dp')
- grad_expert_up: float32 [16, 2048, 1024], P('fsdp', None, 'dp')
- grad_expert_down: float32 [16, 2048, 1024], P('fsdp', None, 'dp')
The draws below stay inside these ranges and needn't reach their ends.
Inputs may be any that keep to these rules, and one draw needn't show every extreme that they name: Within the rows of one device no expert is named by more than 80 routes, and in every draw some expert is named by exactly 80 routes of some device; a token's 8 experts differ.
All inputs are finite; a program needn't handle non-finite values.
Results may differ from the reference program's by a relative error of at most 0.024.
Values may be sent and summed in bfloat16 or wider, within the bound.
No kernel may reach another device: no remote copies, remote signals or barrier semaphores. Data moves between devices by JAX's collectives and lax.ppermute only.
A program may use at most 512 MiB of HBM per device.

```python
import math
import jax
import jax.numpy as jnp
import numpy as np
from jax import lax

D = 2048
HEADS = 16
HD = 128
H = 1024
TOPK = 8
TOK_DEV = 128
EXPERTS = 16
SEQ_LEN = 1024
TOKENS = 4096
CAP = 80
N_DP = 4
N_FSDP = 8


def steps_of(own_key, dims, pieces, smallest, high):
    loudness, own = 1.0, jax.random.fold_in(own_key, 6)
    for position, blocks in pieces:
        draws = jnp.exp(jax.random.uniform(jax.random.fold_in(own, position), (blocks,), jnp.float32, smallest / len(pieces), high / len(pieces)))
        loudness = loudness * jnp.repeat(draws, dims[position] // blocks).reshape([-1 if axis == position else 1 for axis in range(len(dims))])
    return loudness


def deal_out(rng, own, number, rows, count, top, reach, skew):
    ranking = jax.random.permutation(rng, count)
    packed, ordinary = portions_of(count, rows * top, reach, skew, True), portions_of(count, rows * top, reach, skew, False)
    places = jnp.arange(count)

    def named(lengths, rotation):
        used = int((lengths > 0).sum())
        fixed = max(1, used // 4)
        moved = fixed + (places - fixed + rotation * (used - fixed)) % max(1, count - fixed)
        return jnp.zeros((count,), jnp.int32).at[ranking[jnp.where(places < fixed, places, moved)]].set(jnp.asarray(lengths, jnp.int32))

    lengths = jnp.where(number % 4 == 0, named(packed, number // 4), named(ordinary, number - number // 4 - 1))
    mixed = jax.random.permutation(jax.random.fold_in(own, 3), count)
    source_of, taker = mixed[0:count // 2 * 2:2], mixed[1:count // 2 * 2:2]
    slack = jnp.minimum(lengths[source_of] - 1, reach - lengths[taker]) // 2
    slack = jnp.where((source_of == ranking[0]) | (taker == ranking[0]) | (lengths[taker] == 0), 0, jnp.maximum(slack, 0))
    moved = jax.random.randint(jax.random.fold_in(own, 4), (count // 2,), 0, 1 << 20) % (slack + 1)
    lengths = lengths.at[source_of].add(-moved).at[taker].add(moved)
    labels = jnp.searchsorted(jnp.cumsum(lengths), jnp.arange(rows * top), side="right").astype(jnp.int32)
    grid = labels.reshape(top, rows).T
    grid = grid[jax.random.permutation(jax.random.fold_in(own, 1), rows)]
    rotation = jax.random.randint(jax.random.fold_in(own, 2), (rows, 1), 0, top)
    return jnp.take_along_axis(grid, (jnp.arange(top)[None, :] + rotation) % top, axis=1)


def portions_of(number_of, total, limit, slope, full):
    portions = [(1 << 20) // math.isqrt(standing ** slope) + 1 for standing in range(1, number_of + 1)]
    largest = limit if full else min(limit, max(-(-total // number_of), total * portions[0] // sum(portions)))
    least = 1 if total - largest >= number_of - 1 else 0
    counts, surplus = [largest] + [least] * (number_of - 1), total - largest - least * (number_of - 1)
    while surplus > 0:
        candidates = [i for i in range(1, number_of) if counts[i] < largest] or [i for i in range(1, number_of) if counts[i] < limit]
        whole, budget = sum([portions[i] for i in candidates]), surplus
        for i in candidates:
            extra = min(limit - counts[i], max(1, budget * portions[i] // whole), surplus)
            counts[i] = counts[i] + extra
            surplus = surplus - extra
    return np.array(counts)


def scatter_about(key, extent, width, most, split=(), kind=jnp.bfloat16):
    values = jax.random.normal(key, extent, jnp.float32) * width
    if len(split) > 0:
        values = steps_of(key, extent, split, -0.22, 0.18) * values
    return jnp.clip(values, min=-most, max=most).astype(kind)


def setup_inputs(seed: int = 0) -> dict:
    keys = jax.random.split(jax.random.key(seed), 16)
    tokens = scatter_about(keys[0], (TOKENS, D), 1.0, 6.0, ((0, 32),))
    cotangent = scatter_about(keys[1], (TOKENS, D), 1.0, 6.0, ((0, 32),))
    routes_keys = jax.random.split(jax.random.fold_in(keys[2], 1), TOKENS // TOK_DEV)
    routes_turns = jax.random.permutation(jax.random.fold_in(keys[2], 3), TOKENS // TOK_DEV)
    routes = jax.vmap(lambda own, number: deal_out(jax.random.fold_in(keys[2], 2), own, number, TOK_DEV, EXPERTS, TOPK, CAP, 0))(routes_keys, routes_turns).reshape((TOKENS, TOPK))
    w_query = scatter_about(keys[3], (D, D), D ** -0.5, 0.125, ((0, 32),))
    w_key = scatter_about(keys[4], (D, D), D ** -0.5, 0.125, ((0, 32),))
    w_value = scatter_about(keys[5], (D, D), D ** -0.5, 0.125, ((0, 32),))
    w_output = scatter_about(keys[6], (D, D), (D // 16) ** -0.5, 0.5, ((0, 32),))
    w_router = scatter_about(keys[7], (D, EXPERTS), (0.5 * D ** -0.5), 0.0625, ((0, 32),))
    gain_attn = jnp.clip(1.0 + 0.1 * jax.random.normal(keys[8], (D,), jnp.float32), 0.5, 1.5).astype(jnp.bfloat16)
    gain_query = jnp.clip(1.0 + 0.1 * jax.random.normal(keys[9], (D,), jnp.float32), 0.5, 1.5).astype(jnp.bfloat16)
    gain_key = jnp.clip(1.0 + 0.1 * jax.random.normal(keys[10], (D,), jnp.float32), 0.5, 1.5).astype(jnp.bfloat16)
    gain_ffn = jnp.clip(1.0 + 0.1 * jax.random.normal(keys[11], (D,), jnp.float32), 0.5, 1.5).astype(jnp.bfloat16)
    expert_gate = scatter_about(keys[12], (EXPERTS, D, H), D ** -0.5, 0.125, ((0, 8), (2, 4)))
    expert_up = scatter_about(keys[13], (EXPERTS, D, H), D ** -0.5, 0.125, ((0, 8), (2, 4)))
    expert_down = scatter_about(keys[14], (EXPERTS, D, H), (H // 16) ** -0.5, 0.75, ((0, 8), (2, 4)))
    return dict(tokens=tokens, cotangent=cotangent, routes=routes, w_query=w_query, w_key=w_key, w_value=w_value, w_output=w_output, w_router=w_router, gain_attn=gain_attn, gain_query=gain_query, gain_key=gain_key, gain_ffn=gain_ffn, expert_gate=expert_gate, expert_up=expert_up, expert_down=expert_down)


@jax.custom_vjp
def low(v):
    return lax.optimization_barrier(v.astype(jnp.bfloat16)).astype(jnp.float32)

@jax.custom_vjp
def low_back(v):
    return v

def low_keep(v):
    return (low(v), None)

def low_pass(kept, grad):
    return (grad,)

def back_keep(v):
    return (v, None)

def back_low(kept, grad):
    return (low(grad),)
low.defvjp(low_keep, low_pass)
low_back.defvjp(back_keep, back_low)
epsilon = 1e-05
rope_base = 10000.0
far_low = -1e+30
highest = lax.Precision.HIGHEST

def rms_norm(values, scaling):
    factor = lax.rsqrt(lax.optimization_barrier(jnp.mean(values * values, axis=-1, keepdims=True)) + epsilon)
    return values * factor * scaling

def rotary(values, positions):
    half_dim = values.shape[-1] // 2
    inv_freq = rope_base ** (-(jnp.arange(half_dim, dtype=jnp.float32) * 2.0) / values.shape[-1])
    angles = positions.astype(jnp.float32)[:, None] * inv_freq[None, :]
    cosine = jnp.cos(angles)[:, None, :]
    sine_vals = jnp.sin(angles)[:, None, :]
    first_half = values[..., :half_dim]
    second = values[..., half_dim:]
    return jnp.concatenate([first_half * cosine - second * sine_vals, second * cosine + first_half * sine_vals], axis=-1)

def matmul(left, right):
    return jnp.dot(left, right, precision=highest, preferred_element_type=jnp.float32)

def attend_block(query_block, begin_at, key_seq, value_seq):
    score_scale = query_block.shape[-1] ** (-0.5)
    scores = low_back(jnp.einsum('qhd,khd->hqk', query_block, key_seq, precision=highest) * score_scale)
    query_pos = begin_at + jnp.arange(query_block.shape[0], dtype=jnp.int32)
    key_pos = jnp.arange(key_seq.shape[0], dtype=jnp.int32)
    allowed = (key_pos[None, :] <= query_pos[:, None])[None]
    prob_vals = jax.nn.softmax(jnp.where(allowed, scores, far_low), axis=-1)
    return jnp.einsum('hqk,khd->qhd', low(prob_vals), value_seq, precision=highest)

def layer_sequence(seq_tokens, seq_routes, params):
    w_query, w_key, w_value, w_output, w_router, gain_attn, gain_query, gain_key, gain_ffn, expert_gate, expert_up, expert_down = params
    positions = jnp.arange(SEQ_LEN, dtype=jnp.int32)
    normed_in = low(rms_norm(seq_tokens, gain_attn))
    query_raw = low_back(matmul(normed_in, w_query))
    key_raw = low_back(matmul(normed_in, w_key))
    value_raw = low_back(matmul(normed_in, w_value))
    query_rot = low(rotary(rms_norm(query_raw, gain_query).reshape(SEQ_LEN, HEADS, HD), positions))
    key_rot = low(rotary(rms_norm(key_raw, gain_key).reshape(SEQ_LEN, HEADS, HD), positions))
    value_low = low(value_raw).reshape(SEQ_LEN, HEADS, HD)
    block_rows = math.gcd(SEQ_LEN, 512)
    query_blocks = query_rot.reshape(SEQ_LEN // block_rows, block_rows, HEADS, HD)
    starts = jnp.arange(SEQ_LEN // block_rows, dtype=jnp.int32) * block_rows
    attend = jax.checkpoint(attend_block)
    attn_out = lax.map(lambda seq_pair: attend(seq_pair[0], seq_pair[1], key_rot, value_low), (query_blocks, starts))
    attn_out = low(low_back(attn_out.reshape(SEQ_LEN, D)))
    resid_mid = seq_tokens + low_back(matmul(attn_out, w_output))
    normed_mid = low(rms_norm(resid_mid, gain_ffn))
    logits = low_back(matmul(normed_mid, w_router))
    prob_vals = jax.nn.softmax(logits, axis=-1)
    chosen = jnp.take_along_axis(prob_vals, seq_routes, axis=1)
    gate_vals = chosen / lax.optimization_barrier(jnp.sum(chosen, axis=-1, keepdims=True))
    route_blocks = seq_routes.reshape(N_FSDP, TOK_DEV * TOPK)
    pick_table = (route_blocks[:, :, None] == jnp.arange(EXPERTS, dtype=jnp.int32)[None, None, :]).astype(jnp.int32)
    slot_index = lax.optimization_barrier(jnp.sum(pick_table * (jnp.cumsum(pick_table, axis=1) - 1), axis=2))
    block_ids = jnp.arange(N_FSDP, dtype=jnp.int32)[:, None]
    target = ((route_blocks * N_FSDP + block_ids) * CAP + slot_index).reshape(SEQ_LEN * TOPK)
    spread = low_back(jnp.repeat(normed_mid, TOPK, axis=0))
    buffer = jnp.zeros((EXPERTS * N_FSDP * CAP, D), jnp.float32).at[target].set(spread)
    buffer = buffer.reshape(EXPERTS, N_FSDP * CAP, D)
    gate_hid = low_back(jnp.einsum('erd,edh->erh', buffer, expert_gate, precision=highest))
    up_hid = low_back(jnp.einsum('erd,edh->erh', buffer, expert_up, precision=highest))
    act_vals = low(jax.nn.silu(gate_hid) * up_hid)
    expert_out = low(low_back(jnp.einsum('erh,edh->erd', act_vals, expert_down, precision=highest)))
    picked = expert_out.reshape(EXPERTS * N_FSDP * CAP, D)[target].reshape(SEQ_LEN, TOPK, D)
    return resid_mid + lax.optimization_barrier(jnp.sum(gate_vals[:, :, None] * picked, axis=1))

def reference(tokens, cotangent, routes, w_query, w_key, w_value, w_output, w_router, gain_attn, gain_query, gain_key, gain_ffn, expert_gate, expert_up, expert_down):
    params = tuple((weight.astype(jnp.float32) for weight in (w_query, w_key, w_value, w_output, w_router, gain_attn, gain_query, gain_key, gain_ffn, expert_gate, expert_up, expert_down)))
    seq_tokens = tokens.astype(jnp.float32).reshape(N_DP, SEQ_LEN, D)
    seq_routes = routes.reshape(N_DP, SEQ_LEN, TOPK)

    def forward(inputs, weights):
        seq_step = jax.checkpoint(lambda seq_pair: layer_sequence(seq_pair[0], seq_pair[1], weights))
        return lax.map(seq_step, (inputs, seq_routes))
    result, pullback = jax.vjp(forward, seq_tokens, params)
    grad_inputs, grad_params = pullback(cotangent.astype(jnp.float32).reshape(N_DP, SEQ_LEN, D))
    return (result.reshape(TOKENS, D).astype(jnp.bfloat16), grad_inputs.reshape(TOKENS, D), grad_params[0], grad_params[1], grad_params[2], grad_params[3], grad_params[4], grad_params[5], grad_params[6], grad_params[7], grad_params[8], grad_params[9], grad_params[10], grad_params[11])
```

```python
import functools

import jax
import jax.numpy as jnp
from jax import lax
from jax.experimental import pallas as pl
from jax.experimental.pallas import tpu as pltpu
from jax.sharding import PartitionSpec as P

HEADS = 16
TOPK = 8


epsilon = 1e-05
rope_base = 10000.0
far_low = -1e30


def rms_norm(values, scaling):
    factor = lax.rsqrt(jnp.mean(values * values, axis=-1, keepdims=True) + epsilon)
    return values * factor * scaling


def rotary(values, positions):
    half_dim = values.shape[-1] // 2
    inv_freq = rope_base ** (-(jnp.arange(half_dim, dtype=jnp.float32) * 2.0) / values.shape[-1])
    angles = positions.astype(jnp.float32)[:, None] * inv_freq[None, :]
    cosine = jnp.cos(angles)[:, None, :]
    sine_vals = jnp.sin(angles)[:, None, :]
    first_half = values[..., :half_dim]
    second = values[..., half_dim:]
    return jnp.concatenate(
        [first_half * cosine - second * sine_vals, second * cosine + first_half * sine_vals],
        axis=-1,
    )


def head_prep(values, scaling, positions):
    normed = rms_norm(values, scaling)
    return rotary(normed.reshape(values.shape[0], HEADS, -1), positions)


def swiglu(gate_hid, up_hid):
    return jax.nn.silu(gate_hid) * up_hid


def gating(logits, routes, num_experts):
    prob_vals = jax.nn.softmax(logits, axis=-1)
    pick_table = (
        routes[:, :, None] == jnp.arange(num_experts, dtype=jnp.int32)[None, None, :]
    ).astype(jnp.float32)
    chosen = jnp.sum(pick_table * prob_vals[:, None, :], axis=-1)
    return chosen / jnp.sum(chosen, axis=-1, keepdims=True)


def per_device_gathered(
    tokens,
    cotangent,
    routes,
    w_query,
    w_key,
    w_value,
    w_output,
    w_router,
    gain_attn,
    gain_query,
    gain_key,
    gain_ffn,
    expert_gate,
    expert_up,
    expert_down,
):
    row_count = tokens.shape[0]
    model_width = tokens.shape[1]
    head_dim = model_width // HEADS
    score_scale = head_dim ** (-0.5)
    fsdp_size = lax.axis_size("fsdp")
    local_experts = expert_gate.shape[0]
    num_experts = local_experts * fsdp_size
    capacity = max(2, (row_count * TOPK * 5 + 4 * num_experts - 1) // (4 * num_experts))
    positions = lax.axis_index("fsdp") * row_count + jnp.arange(row_count, dtype=jnp.int32)
    first_pos = positions[0]
    last_pos = positions[row_count - 1]
    inputs = tokens.astype(jnp.float32)
    dense_full = (
        lax.all_gather(w_query, ("dp", "fsdp"), axis=0, tiled=True),
        lax.all_gather(w_key, ("dp", "fsdp"), axis=0, tiled=True),
        lax.all_gather(w_value, ("dp", "fsdp"), axis=0, tiled=True),
        lax.all_gather(w_output, ("dp", "fsdp"), axis=0, tiled=True),
        lax.all_gather(w_router, ("dp", "fsdp"), axis=0, tiled=True),
        lax.all_gather(gain_attn, ("dp", "fsdp"), axis=0, tiled=True),
        lax.all_gather(gain_query, ("dp", "fsdp"), axis=0, tiled=True),
        lax.all_gather(gain_key, ("dp", "fsdp"), axis=0, tiled=True),
        lax.all_gather(gain_ffn, ("dp", "fsdp"), axis=0, tiled=True),
    )
    expert_full = (
        lax.all_gather(expert_gate, "dp", axis=2, tiled=True),
        lax.all_gather(expert_up, "dp", axis=2, tiled=True),
        lax.all_gather(expert_down, "dp", axis=2, tiled=True),
    )
    query_full, key_full, value_full, output_full, router_full = dense_full[:5]
    gain_in_full = dense_full[5].astype(jnp.float32)
    gain_q_full = dense_full[6].astype(jnp.float32)
    gain_k_full = dense_full[7].astype(jnp.float32)
    gain_mid_full = dense_full[8].astype(jnp.float32)
    normed_low = rms_norm(inputs, gain_in_full).astype(jnp.bfloat16)
    query_raw = jnp.dot(normed_low, query_full, preferred_element_type=jnp.float32)
    key_raw = jnp.dot(normed_low, key_full, preferred_element_type=jnp.float32)
    value_raw = jnp.dot(normed_low, value_full, preferred_element_type=jnp.float32)
    query_low = head_prep(query_raw, gain_q_full, positions).astype(jnp.bfloat16)
    key_low = head_prep(key_raw, gain_k_full, positions).astype(jnp.bfloat16)
    value_low = value_raw.astype(jnp.bfloat16).reshape(row_count, HEADS, head_dim)
    start_state = (
        jnp.full((HEADS, row_count), far_low, jnp.float32),
        jnp.zeros((HEADS, row_count), jnp.float32),
        jnp.zeros((row_count, HEADS, head_dim), jnp.float32),
    )
    shard_piece = (
        lax.all_gather(key_low, "fsdp", axis=0, tiled=True),
        lax.all_gather(value_low, "fsdp", axis=0, tiled=True),
    )

    def attend_update(state):
        run_max, run_sum, run_acc = state
        key_piece, value_piece = shard_piece
        scores = (
            jnp.einsum("qhd,khd->hqk", query_low, key_piece, preferred_element_type=jnp.float32)
            * score_scale
        )
        key_pos = jnp.arange(key_piece.shape[0], dtype=jnp.int32)
        allowed = (key_pos[None, :] <= positions[:, None])[None]
        new_max = jnp.maximum(run_max, jnp.max(jnp.where(allowed, scores, far_low), axis=-1))
        exp_vals = jnp.where(allowed, jnp.exp(scores - new_max[..., None]), 0.0)
        factor = jnp.exp(run_max - new_max)
        run_sum = jnp.sum(exp_vals, axis=-1)
        run_acc = run_acc * factor.T[:, :, None] + jnp.einsum(
            "hqk,khd->qhd",
            exp_vals.astype(jnp.bfloat16),
            value_piece,
            preferred_element_type=jnp.float32,
        )
        return (new_max, run_sum, run_acc)

    run_max, run_sum, run_acc = lax.cond(
        jnp.int32(0) <= last_pos, attend_update, lambda state: state, start_state
    )
    attn_f32 = run_acc / run_sum.T[:, :, None]
    log_sum = run_max + jnp.log(run_sum)
    attn_low = attn_f32.reshape(row_count, model_width).astype(jnp.bfloat16)
    resid_mid = inputs + jnp.dot(attn_low, output_full, preferred_element_type=jnp.float32)
    mid_low = rms_norm(resid_mid, gain_mid_full).astype(jnp.bfloat16)
    logits = jnp.dot(mid_low, router_full, preferred_element_type=jnp.float32)
    gate_vals, gate_pull = jax.vjp(
        lambda logit_vals: gating(logit_vals, routes, num_experts), logits
    )
    route_flat = routes.reshape(-1)
    pick_table = (route_flat[:, None] == jnp.arange(num_experts, dtype=jnp.int32)[None, :]).astype(
        jnp.int32
    )
    slot_index = jnp.sum(pick_table * (jnp.cumsum(pick_table, axis=0) - 1), axis=1)
    target = route_flat * capacity + slot_index
    spread = jnp.repeat(mid_low, TOPK, axis=0)
    send_rows = (
        jnp.zeros((num_experts * capacity, model_width), jnp.bfloat16).at[target].set(spread)
    )
    send_rows = send_rows.reshape(fsdp_size, local_experts, capacity, model_width)
    arrived = lax.all_to_all(send_rows, "fsdp", split_axis=0, concat_axis=0, tiled=True)
    gate_w, up_w, down_w = expert_full
    gate_hid = jnp.einsum("secd,edh->sech", arrived, gate_w, preferred_element_type=jnp.float32)
    up_hid = jnp.einsum("secd,edh->sech", arrived, up_w, preferred_element_type=jnp.float32)
    act_low = swiglu(gate_hid, up_hid).astype(jnp.bfloat16)
    expert_out = jnp.einsum(
        "sech,edh->secd", act_low, down_w, preferred_element_type=jnp.float32
    ).astype(jnp.bfloat16)
    returned = lax.all_to_all(expert_out, "fsdp", split_axis=0, concat_axis=0, tiled=True).reshape(
        num_experts * capacity, model_width
    )
    picked = returned[target].reshape(row_count, TOPK, model_width).astype(jnp.float32)
    resid_out = resid_mid + jnp.sum(gate_vals[:, :, None] * picked, axis=1)
    layer_out = resid_out.astype(jnp.bfloat16)
    back_dense = (
        lax.all_gather(w_query, ("dp", "fsdp"), axis=0, tiled=True),
        lax.all_gather(w_key, ("dp", "fsdp"), axis=0, tiled=True),
        lax.all_gather(w_value, ("dp", "fsdp"), axis=0, tiled=True),
        lax.all_gather(w_output, ("dp", "fsdp"), axis=0, tiled=True),
        lax.all_gather(w_router, ("dp", "fsdp"), axis=0, tiled=True),
        lax.all_gather(gain_attn, ("dp", "fsdp"), axis=0, tiled=True),
        lax.all_gather(gain_query, ("dp", "fsdp"), axis=0, tiled=True),
        lax.all_gather(gain_key, ("dp", "fsdp"), axis=0, tiled=True),
        lax.all_gather(gain_ffn, ("dp", "fsdp"), axis=0, tiled=True),
    )
    back_experts = (
        lax.all_gather(expert_gate, "dp", axis=2, tiled=True),
        lax.all_gather(expert_up, "dp", axis=2, tiled=True),
        lax.all_gather(expert_down, "dp", axis=2, tiled=True),
    )
    query_back, key_back, value_back, output_back, router_back = back_dense[:5]
    gain_in_back = back_dense[5].astype(jnp.float32)
    gain_q_back = back_dense[6].astype(jnp.float32)
    gain_k_back = back_dense[7].astype(jnp.float32)
    gain_mid_back = back_dense[8].astype(jnp.float32)
    gate_back, up_back, down_back = back_experts
    grad_out = cotangent.astype(jnp.float32)
    grad_gates = jnp.sum(grad_out[:, None, :] * picked, axis=-1)
    grad_routed = (
        (gate_vals[:, :, None] * grad_out[:, None, :]).astype(jnp.bfloat16).reshape(-1, model_width)
    )
    send_grads = (
        jnp.zeros((num_experts * capacity, model_width), jnp.bfloat16).at[target].set(grad_routed)
    )
    send_grads = send_grads.reshape(fsdp_size, local_experts, capacity, model_width)
    grad_arrived = lax.all_to_all(send_grads, "fsdp", split_axis=0, concat_axis=0, tiled=True)
    gate_again = jnp.einsum(
        "secd,edh->sech", arrived, gate_back, preferred_element_type=jnp.float32
    )
    up_again = jnp.einsum("secd,edh->sech", arrived, up_back, preferred_element_type=jnp.float32)
    act_vals, act_pull = jax.vjp(swiglu, gate_again, up_again)
    act_again = act_vals.astype(jnp.bfloat16)
    grad_act = jnp.einsum(
        "secd,edh->sech", grad_arrived, down_back, preferred_element_type=jnp.float32
    )
    grad_down = jnp.einsum(
        "secd,sech->edh", grad_arrived, act_again, preferred_element_type=jnp.float32
    )
    grad_gate_hid, grad_up_hid = act_pull(grad_act)
    grad_gate_low = grad_gate_hid.astype(jnp.bfloat16)
    grad_up_low = grad_up_hid.astype(jnp.bfloat16)
    grad_gate_w = jnp.einsum(
        "secd,sech->edh", arrived, grad_gate_low, preferred_element_type=jnp.float32
    )
    grad_up_w = jnp.einsum(
        "secd,sech->edh", arrived, grad_up_low, preferred_element_type=jnp.float32
    )
    grad_inputs = jnp.einsum(
        "sech,edh->secd", grad_gate_low, gate_back, preferred_element_type=jnp.float32
    ) + jnp.einsum("sech,edh->secd", grad_up_low, up_back, preferred_element_type=jnp.float32)
    grad_returned = lax.all_to_all(
        grad_inputs.astype(jnp.bfloat16), "fsdp", split_axis=0, concat_axis=0, tiled=True
    )
    grad_returned = grad_returned.reshape(num_experts * capacity, model_width)
    grad_mid = jnp.sum(
        grad_returned[target].reshape(row_count, TOPK, model_width).astype(jnp.float32), axis=1
    )
    expert_grads = (
        lax.psum_scatter(
            grad_gate_w.astype(jnp.bfloat16), "dp", scatter_dimension=2, tiled=True
        ).astype(jnp.float32),
        lax.psum_scatter(
            grad_up_w.astype(jnp.bfloat16), "dp", scatter_dimension=2, tiled=True
        ).astype(jnp.float32),
        lax.psum_scatter(
            grad_down.astype(jnp.bfloat16), "dp", scatter_dimension=2, tiled=True
        ).astype(jnp.float32),
    )
    (grad_logits,) = gate_pull(grad_gates)
    grad_logits_low = grad_logits.astype(jnp.bfloat16)
    grad_router = jnp.einsum(
        "td,te->de", mid_low, grad_logits_low, preferred_element_type=jnp.float32
    )
    grad_mid = grad_mid + jnp.einsum(
        "te,de->td", grad_logits_low, router_back, preferred_element_type=jnp.float32
    )
    mid_value, mid_pull = jax.vjp(rms_norm, resid_mid, gain_mid_back)
    grad_resid_part, grad_gain_mid = mid_pull(grad_mid)
    grad_resid = grad_out + grad_resid_part
    grad_attn_out = grad_resid.astype(jnp.bfloat16)
    grad_output_w = jnp.einsum(
        "td,te->de", attn_low, grad_attn_out, preferred_element_type=jnp.float32
    )
    grad_attn = jnp.einsum(
        "te,de->td", grad_attn_out, output_back, preferred_element_type=jnp.float32
    )
    grad_attn = grad_attn.astype(jnp.bfloat16).reshape(row_count, HEADS, head_dim)
    delta_rows = jnp.sum(grad_attn.astype(jnp.float32) * attn_f32, axis=-1).T
    key_all, value_all = (
        lax.all_gather(key_low, "fsdp", axis=0, tiled=True),
        lax.all_gather(value_low, "fsdp", axis=0, tiled=True),
    )

    def probs_block(key_block, value_block, begin_at):
        scores = (
            jnp.einsum("qhd,khd->hqk", query_low, key_block, preferred_element_type=jnp.float32)
            * score_scale
        )
        key_pos = begin_at + jnp.arange(key_block.shape[0], dtype=jnp.int32)
        allowed = (key_pos[None, :] <= positions[:, None])[None]
        prob_vals = jnp.where(allowed, jnp.exp(scores - log_sum[..., None]), 0.0)
        grad_probs = jnp.einsum(
            "qhd,khd->hqk", grad_attn, value_block, preferred_element_type=jnp.float32
        )
        grad_scores = (prob_vals * (grad_probs - delta_rows[..., None])).astype(jnp.bfloat16)
        return (prob_vals, grad_scores)

    block_rows = 8 * row_count
    block_needed = last_pos // block_rows + 1
    zero_query = jnp.zeros((row_count, HEADS, head_dim), jnp.float32)

    def query_step(block_index, accum):
        begin_at = block_index * block_rows
        key_block = lax.dynamic_slice_in_dim(key_all, begin_at, block_rows, 0)
        value_block = lax.dynamic_slice_in_dim(value_all, begin_at, block_rows, 0)
        prob_vals, grad_scores = probs_block(key_block, value_block, begin_at)
        return accum + jnp.einsum(
            "hqk,khd->qhd", grad_scores, key_block, preferred_element_type=jnp.float32
        )

    grad_query_rot = lax.fori_loop(0, block_needed, query_step, zero_query) * score_scale
    stats_all = (
        lax.all_gather(log_sum.T, "fsdp", axis=0, tiled=True),
        lax.all_gather(delta_rows.T, "fsdp", axis=0, tiled=True),
    )
    query_piece = lax.all_gather(query_low, "fsdp", axis=0, tiled=True)
    grad_piece = lax.all_gather(grad_attn, "fsdp", axis=0, tiled=True)
    span = query_piece.shape[0]

    def add_update(state):
        lse_piece = stats_all[0].T
        delta_piece = stats_all[1].T
        scores = (
            jnp.einsum("qhd,khd->hqk", query_piece, key_low, preferred_element_type=jnp.float32)
            * score_scale
        )
        query_pos = jnp.arange(span, dtype=jnp.int32)
        allowed = (positions[None, :] <= query_pos[:, None])[None]
        prob_vals = jnp.where(allowed, jnp.exp(scores - lse_piece[..., None]), 0.0)
        grad_probs = jnp.einsum(
            "qhd,khd->hqk", grad_piece, value_low, preferred_element_type=jnp.float32
        )
        grad_scores = (prob_vals * (grad_probs - delta_piece[..., None])).astype(jnp.bfloat16)
        grad_value_acc = jnp.einsum(
            "hqk,qhd->khd",
            prob_vals.astype(jnp.bfloat16),
            grad_piece,
            preferred_element_type=jnp.float32,
        )
        grad_key_acc = jnp.einsum(
            "hqk,qhd->khd", grad_scores, query_piece, preferred_element_type=jnp.float32
        )
        return (grad_key_acc, grad_value_acc)

    grad_key_sum, grad_value_sum = lax.cond(
        jnp.int32(0) + span > first_pos, add_update, lambda state: state, (zero_query, zero_query)
    )
    grad_key_rot = grad_key_sum * score_scale
    grad_value_low = grad_value_sum.reshape(row_count, model_width).astype(jnp.bfloat16)
    query_value, query_pull = jax.vjp(
        lambda raw_vals, scaling: head_prep(raw_vals, scaling, positions), query_raw, gain_q_back
    )
    grad_query_raw, grad_gain_query = query_pull(grad_query_rot)
    key_value, key_pull = jax.vjp(
        lambda raw_vals, scaling: head_prep(raw_vals, scaling, positions), key_raw, gain_k_back
    )
    grad_key_raw, grad_gain_key = key_pull(grad_key_rot)
    grad_query_low = grad_query_raw.astype(jnp.bfloat16)
    grad_key_low = grad_key_raw.astype(jnp.bfloat16)
    grad_wq = jnp.einsum(
        "td,te->de", normed_low, grad_query_low, preferred_element_type=jnp.float32
    )
    grad_wk = jnp.einsum("td,te->de", normed_low, grad_key_low, preferred_element_type=jnp.float32)
    grad_wv = jnp.einsum(
        "td,te->de", normed_low, grad_value_low, preferred_element_type=jnp.float32
    )
    grad_normed = (
        jnp.einsum("te,de->td", grad_query_low, query_back, preferred_element_type=jnp.float32)
        + jnp.einsum("te,de->td", grad_key_low, key_back, preferred_element_type=jnp.float32)
        + jnp.einsum("te,de->td", grad_value_low, value_back, preferred_element_type=jnp.float32)
    )
    in_value, input_pull = jax.vjp(rms_norm, inputs, gain_in_back)
    grad_input_part, grad_gain_in = input_pull(grad_normed)
    grad_tokens = grad_resid + grad_input_part
    dense_grads = (
        lax.psum_scatter(grad_wq, ("dp", "fsdp"), scatter_dimension=0, tiled=True),
        lax.psum_scatter(grad_wk, ("dp", "fsdp"), scatter_dimension=0, tiled=True),
        lax.psum_scatter(grad_wv, ("dp", "fsdp"), scatter_dimension=0, tiled=True),
        lax.psum_scatter(grad_output_w, ("dp", "fsdp"), scatter_dimension=0, tiled=True),
        lax.psum_scatter(grad_router, ("dp", "fsdp"), scatter_dimension=0, tiled=True),
        lax.psum_scatter(grad_gain_in, ("dp", "fsdp"), scatter_dimension=0, tiled=True),
        lax.psum_scatter(grad_gain_query, ("dp", "fsdp"), scatter_dimension=0, tiled=True),
        lax.psum_scatter(grad_gain_key, ("dp", "fsdp"), scatter_dimension=0, tiled=True),
        lax.psum_scatter(grad_gain_mid, ("dp", "fsdp"), scatter_dimension=0, tiled=True),
    )
    return (
        layer_out,
        grad_tokens,
        dense_grads[0],
        dense_grads[1],
        dense_grads[2],
        dense_grads[3],
        dense_grads[4],
        dense_grads[5],
        dense_grads[6],
        dense_grads[7],
        dense_grads[8],
        expert_grads[0],
        expert_grads[1],
        expert_grads[2],
    )


def small_bits(size):
    return max(size - 1, 0).bit_length()


def exchange_pairs(size, bit):
    return [(i, i ^ bit) for i in range(size)]


class Ring:
    def __init__(self, size):
        self.size = size
        self.half = size // 2
        self.order = list(range(0, size, 2)) + list(range(size - 1, 0, -2))
        place = [self.order.index(i) for i in range(size)]
        mine = lax.axis_index("fsdp")
        rank = jnp.asarray(place, jnp.int32)[mine]
        self.slot_device = jnp.asarray(self.order, jnp.int32)[
            (rank + jnp.arange(size, dtype=jnp.int32)) % size
        ]
        self.device_slot = (jnp.asarray(place, jnp.int32) - rank) % size
        self.up = [(self.order[i], self.order[(i + 1) % size]) for i in range(size)]
        self.down = [(self.order[i], self.order[i - 1]) for i in range(size)]

    def forward(self, values):
        return lax.ppermute(values, "fsdp", self.up)

    def backward(self, values):
        return lax.ppermute(values, "fsdp", self.down)

    def sum_rows(self, values):
        blocks = values.reshape(values.shape[0], self.size, -1)
        blocks = pair_sum(blocks[:, self.device_slot], "fsdp", self.size)
        return blocks[:, self.slot_device].reshape(values.shape)

    def gather(self, block):
        blocks = [None] * self.size
        blocks[0] = block
        from_low, from_high = block, block
        for step in range(1, self.half):
            from_low = self.forward(from_low)
            from_high = self.backward(from_high)
            blocks[-step] = from_low
            blocks[step] = from_high
        middle = block.shape[0] // 2
        blocks[self.half] = jnp.concatenate(
            [self.forward(from_low[:middle]), self.backward(from_high[middle:])], axis=0
        )
        return blocks

    def reduce(self, blocks):
        middle = blocks[0].shape[0] // 2
        half = self.half
        rising = self.forward(blocks[half][:middle])
        falling = self.backward(blocks[half][middle:])
        for step in range(half - 1, 0, -1):
            upper, lower = blocks[step], blocks[-step]
            if step == half - 1:
                upper = jnp.concatenate([upper[:middle] + rising, upper[middle:]], axis=0)
                lower = jnp.concatenate([lower[:middle], lower[middle:] + falling], axis=0)
            else:
                upper = upper + rising
                lower = lower + falling
            rising = self.forward(upper)
            falling = self.backward(lower)
        return (
            blocks[0].astype(jnp.float32)
            + rising.astype(jnp.float32)
            + falling.astype(jnp.float32)
        )


def pair_sum(values, axis, size):
    bit = 1
    while bit < size:
        values = values + lax.ppermute(values, axis, exchange_pairs(size, bit))
        bit *= 2
    return values


def pair_gather(values, axis, size):
    mine = lax.axis_index(axis)
    values = values[None]
    bit = 1
    while bit < size:
        other = lax.ppermute(values, axis, exchange_pairs(size, bit))
        upper = (mine & bit) != 0
        values = jnp.where(
            upper,
            jnp.concatenate([other, values], axis=0),
            jnp.concatenate([values, other], axis=0),
        )
        bit *= 2
    return values


def pair_scatter(values, axis, size):
    mine = lax.axis_index(axis)
    bit = size // 2
    while bit >= 1:
        span = values.shape[0] // 2
        upper = (mine & bit) != 0
        low_half, high_half = values[:span], values[span:]
        kept = jnp.where(upper, high_half, low_half)
        sent = jnp.where(upper, low_half, high_half)
        values = kept + lax.ppermute(sent, axis, exchange_pairs(size, bit))
        bit //= 2
    return values


def share_relative(block, size):
    blocks = [block]
    bit = size // 2
    while bit >= 1:
        blocks = blocks + [
            lax.ppermute(piece, "dp", exchange_pairs(size, bit)) for piece in blocks
        ]
        bit //= 2
    order = [0]
    bit = size // 2
    while bit >= 1:
        order = order + [i ^ bit for i in order]
        bit //= 2
    placed = [None] * size
    for piece, index in zip(blocks, order):
        placed[index] = piece
    return placed


def combine_relative(blocks, size):
    bit = 1
    held = dict(enumerate(blocks))
    while bit < size:
        kept = {}
        for index in held:
            if index & bit == 0:
                other = lax.ppermute(
                    held[index | bit].astype(jnp.bfloat16), "dp", exchange_pairs(size, bit)
                )
                kept[index] = held[index].astype(jnp.float32) + other.astype(jnp.float32)
        held = kept
        bit *= 2
    return held[0]


def attend_kernel(scale, chunk, pos_row, pos_col, query, key, value, out, lse):
    keys, values = key[...], value[...]
    key_pos = pos_row[...]
    for begin in range(0, query.shape[0], chunk):
        rows = pl.ds(begin, chunk)
        scores = (
            lax.dot_general(
                query[rows, :], keys, (((1,), (1,)), ((), ())), preferred_element_type=jnp.float32
            )
            * scale
        )
        scores = jnp.where(key_pos <= pos_col[rows, :], scores, far_low)
        top = jnp.max(scores, axis=-1, keepdims=True)
        weights = jnp.exp(scores - top)
        total = jnp.sum(weights, axis=-1, keepdims=True)
        mixed = jnp.dot(weights.astype(jnp.bfloat16), values, preferred_element_type=jnp.float32)
        out[rows, :] = mixed / total
        lse[rows, :] = top + jnp.log(total)


def attend(query, key, value, positions, head_dim):
    tokens, width = query.shape
    heads = width // head_dim
    whole = pl.BlockSpec((tokens, head_dim), lambda h: (0, h))
    return pl.pallas_call(
        functools.partial(attend_kernel, head_dim ** (-0.5), min(256, tokens)),
        grid=(heads,),
        in_specs=[
            pl.BlockSpec((1, tokens), lambda h: (0, 0)),
            pl.BlockSpec((tokens, 1), lambda h: (0, 0)),
            whole,
            whole,
            whole,
        ],
        out_specs=[whole, pl.BlockSpec((None, tokens, 1), lambda h: (h, 0, 0))],
        out_shape=[
            jax.ShapeDtypeStruct((tokens, width), jnp.float32),
            jax.ShapeDtypeStruct((heads, tokens, 1), jnp.float32),
        ],
        name="attend",
    )(positions[None, :], positions[:, None], query, key, value)


def attend_back_kernel(
    scale, chunk, pos_row, pos_col, query, key, value, grad, mixed, lse, d_query, d_key, d_value
):
    keys, values = key[...], value[...]
    key_pos = pos_row[...]
    rows_first = (((0,), (0,)), ((), ()))
    for begin in range(0, query.shape[0], chunk):
        rows = pl.ds(begin, chunk)
        queries, grads = query[rows, :], grad[rows, :]
        scores = (
            lax.dot_general(
                queries, keys, (((1,), (1,)), ((), ())), preferred_element_type=jnp.float32
            )
            * scale
        )
        probs = jnp.where(
            key_pos <= pos_col[rows, :], jnp.exp(scores - lse[rows, :]), 0.0
        )
        grad_probs = lax.dot_general(
            grads, values, (((1,), (1,)), ((), ())), preferred_element_type=jnp.float32
        )
        delta = jnp.sum(grads.astype(jnp.float32) * mixed[rows, :], axis=-1, keepdims=True)
        grad_scores = (probs * (grad_probs - delta)).astype(jnp.bfloat16)
        d_query[rows, :] = (
            jnp.dot(grad_scores, keys, preferred_element_type=jnp.float32) * scale
        )
        part_key = (
            lax.dot_general(grad_scores, queries, rows_first, preferred_element_type=jnp.float32)
            * scale
        )
        part_value = lax.dot_general(
            probs.astype(jnp.bfloat16), grads, rows_first, preferred_element_type=jnp.float32
        )
        if begin == 0:
            d_key[...] = part_key
            d_value[...] = part_value
        else:
            d_key[...] += part_key
            d_value[...] += part_value


def attend_back(query, key, value, grad, mixed, lse, positions, head_dim):
    tokens, width = query.shape
    heads = width // head_dim
    whole = pl.BlockSpec((tokens, head_dim), lambda h: (0, h))
    result = jax.ShapeDtypeStruct((tokens, width), jnp.float32)
    return pl.pallas_call(
        functools.partial(attend_back_kernel, head_dim ** (-0.5), min(256, tokens)),
        grid=(heads,),
        in_specs=[
            pl.BlockSpec((1, tokens), lambda h: (0, 0)),
            pl.BlockSpec((tokens, 1), lambda h: (0, 0)),
            whole,
            whole,
            whole,
            whole,
            whole,
            pl.BlockSpec((None, tokens, 1), lambda h: (h, 0, 0)),
        ],
        out_specs=[whole, whole, whole],
        out_shape=[result, result, result],
        name="attend_back",
    )(positions[None, :], positions[:, None], query, key, value, grad, mixed, lse)


def turn(values, cosine, sine, heads):
    rows, width = values.shape
    parts = values.reshape(rows, heads, 2, -1)
    first, second = parts[:, :, 0], parts[:, :, 1]
    cosine, sine = cosine[:, None, :], sine[:, None, :]
    return jnp.stack(
        [first * cosine - second * sine, second * cosine + first * sine], axis=2
    ).reshape(rows, width)


def per_device(
    tokens,
    cotangent,
    routes,
    w_query,
    w_key,
    w_value,
    w_output,
    w_router,
    gain_attn,
    gain_query,
    gain_key,
    gain_ffn,
    expert_gate,
    expert_up,
    expert_down,
):
    rows, width = tokens.shape
    size = lax.axis_size("fsdp")
    dp_size = lax.axis_size("dp")
    head_dim = width // HEADS
    own_heads = HEADS // size
    part = own_heads * head_dim
    own_rows = w_query.shape[0]
    local_experts = expert_gate.shape[0]
    num_experts = local_experts * size
    group = part // own_rows
    span = rows * size
    f_index = lax.axis_index("fsdp")
    d_index = lax.axis_index("dp")
    low, f32 = jnp.bfloat16, jnp.float32
    ring = Ring(size)
    positions = (
        ring.slot_device[:, None] * rows + jnp.arange(rows, dtype=jnp.int32)[None, :]
    ).reshape(span)
    dp_flat = ("dp", "fsdp")
    to_rows = []
    for d in range(dp_size):
        for f in range(size):
            flat = d * size + f
            to_rows.append((flat, (flat % group) * size + flat // group))
    from_rows = [(b, a) for a, b in to_rows]

    token_blocks = ring.gather(tokens)
    x_all = jnp.concatenate(token_blocks, axis=0).astype(f32)

    small = jnp.concatenate(
        [w_router, gain_attn[:, None], gain_query[:, None], gain_key[:, None], gain_ffn[:, None]],
        axis=1,
    )
    small = pair_gather(pair_gather(small, "fsdp", size), "dp", dp_size)
    small = small.reshape(width, -1)
    router = small[:, :num_experts]
    gains = small[:, num_experts:].astype(f32)
    gain_in, gain_q, gain_k, gain_mid = (gains[:, i] for i in range(4))
    gain_q = lax.dynamic_slice_in_dim(gain_q, f_index * part, part)
    gain_k = lax.dynamic_slice_in_dim(gain_k, f_index * part, part)

    packed = jnp.stack(
        [w.reshape(own_rows, size, part) for w in (w_query, w_key, w_value)], axis=2
    ).transpose(1, 0, 2, 3)
    packed = lax.all_to_all(packed, "fsdp", split_axis=0, concat_axis=0, tiled=True)
    packed = packed.reshape(size * own_rows, 3 * part)
    w_in = jnp.zeros((width, 3 * part), low)
    for index, piece in enumerate(share_relative(packed, dp_size)):
        w_in = lax.dynamic_update_slice_in_dim(
            w_in, piece, (d_index ^ index) * packed.shape[0], 0
        )
    out_rows = lax.ppermute(w_output, dp_flat, to_rows)
    w_out = jnp.zeros((part, width), low)
    for index, piece in enumerate(share_relative(out_rows, dp_size)):
        w_out = lax.dynamic_update_slice_in_dim(w_out, piece, (d_index ^ index) * own_rows, 0)

    down_w = jnp.concatenate(share_relative(expert_down, dp_size), axis=2)
    gate_w = jnp.concatenate(share_relative(expert_gate, dp_size), axis=2)
    up_w = jnp.concatenate(share_relative(expert_up, dp_size), axis=2)

    in_factor = lax.rsqrt(jnp.mean(x_all * x_all, axis=-1, keepdims=True) + epsilon)
    normed = (x_all * in_factor * gain_in).astype(low)
    raw = jnp.dot(normed, w_in, preferred_element_type=f32)
    q_raw, k_raw, v_raw = raw[:, :part], raw[:, part : 2 * part], raw[:, 2 * part :]
    squares = jnp.stack([jnp.sum(q_raw * q_raw, axis=-1), jnp.sum(k_raw * k_raw, axis=-1)])
    squares = ring.sum_rows(squares)
    factors = lax.rsqrt(squares / width + epsilon)
    q_factor, k_factor = factors[0][:, None], factors[1][:, None]
    half_dim = head_dim // 2
    inv_freq = rope_base ** (-(jnp.arange(half_dim, dtype=f32) * 2.0) / head_dim)
    angles = positions.astype(f32)[:, None] * inv_freq[None, :]
    cosine, sine = jnp.cos(angles), jnp.sin(angles)
    q_low = turn(q_raw * q_factor * gain_q, cosine, sine, own_heads).astype(low)
    k_low = turn(k_raw * k_factor * gain_k, cosine, sine, own_heads).astype(low)
    v_low = v_raw.astype(low)
    mixed, lse = attend(q_low, k_low, v_low, positions, head_dim)
    mixed_low = mixed.astype(low)
    attn_part = jnp.dot(mixed_low, w_out, preferred_element_type=f32).astype(low)
    attn_blocks = [attn_part[k * rows : (k + 1) * rows] for k in range(size)]
    resid_mid = tokens.astype(f32) + ring.reduce(attn_blocks)

    mid_factor = lax.rsqrt(jnp.mean(resid_mid * resid_mid, axis=-1, keepdims=True) + epsilon)
    mid_low = (resid_mid * mid_factor * gain_mid).astype(low)
    mid_all = jnp.concatenate(ring.gather(mid_low), axis=0)
    logits = jnp.dot(mid_low, router, preferred_element_type=f32)
    chosen_mask = jnp.any(
        routes[:, :, None] == jnp.arange(num_experts, dtype=jnp.int32)[None, None, :], axis=1
    )
    router_probs = jax.nn.softmax(logits, axis=-1)
    chosen = jnp.where(chosen_mask, router_probs, 0.0)
    chosen_sum = jnp.sum(chosen, axis=-1, keepdims=True)
    gates = chosen / chosen_sum
    gates_all = pair_gather(gates, "fsdp", size)[ring.slot_device]
    own_gates = lax.dynamic_slice_in_dim(
        gates_all.reshape(span, num_experts), f_index * local_experts, local_experts, 1
    ).T[:, :, None]
    cot_all = jnp.concatenate(ring.gather(cotangent), axis=0)
    back_act = jnp.einsum("td,edh->eth", cot_all, down_w, preferred_element_type=f32)
    gate_hid = jnp.einsum("td,edh->eth", mid_all, gate_w, preferred_element_type=f32)
    up_hid = jnp.einsum("td,edh->eth", mid_all, up_w, preferred_element_type=f32)
    sig = jax.nn.sigmoid(gate_hid)
    silu = gate_hid * sig
    act = (silu * up_hid).astype(low)
    grad_gates = jnp.sum(act.astype(f32) * back_act, axis=-1)
    grad_act = own_gates * back_act
    d_gate = (grad_act * up_hid * (sig * (1.0 + gate_hid * (1.0 - sig)))).astype(low)
    d_up = (grad_act * silu).astype(low)
    act_gated = (own_gates * act.astype(f32)).astype(low)
    grad_in = (
        jnp.einsum("eth,edh->td", d_gate, gate_w, preferred_element_type=f32)
        + jnp.einsum("eth,edh->td", d_up, up_w, preferred_element_type=f32)
    ).astype(low)
    expert_out = jnp.einsum("eth,edh->etd", act, down_w, preferred_element_type=f32).astype(low)
    moe_part = jnp.sum(own_gates * expert_out.astype(f32), axis=0).astype(low)

    by_device = grad_gates.reshape(local_experts, size, rows)[:, ring.device_slot]
    gates_back = pair_gather(by_device, "fsdp", size)
    gates_back = lax.dynamic_slice_in_dim(gates_back, f_index, 1, 2)
    gates_back = gates_back.reshape(num_experts, rows).T
    inner = jnp.sum(jnp.where(chosen_mask, gates_back * gates, 0.0), axis=-1, keepdims=True)
    grad_probs = jnp.where(chosen_mask, (gates_back - inner) / chosen_sum, 0.0)
    grad_logits = router_probs * (
        grad_probs - jnp.sum(router_probs * grad_probs, axis=-1, keepdims=True)
    )
    grad_logits_low = grad_logits.astype(low)
    grad_router = lax.dot_general(
        mid_low, grad_logits_low, (((0,), (0,)), ((), ())), preferred_element_type=f32
    )
    grad_mid = ring.reduce([grad_in[k * rows : (k + 1) * rows] for k in range(size)])
    grad_mid = grad_mid + lax.dot_general(
        grad_logits_low, router, (((1,), (1,)), ((), ())), preferred_element_type=f32
    )
    grad_out = cotangent.astype(f32)
    scaled = grad_mid * gain_mid
    grad_resid = (
        grad_out
        + mid_factor * scaled
        - resid_mid * mid_factor**3 * jnp.mean(scaled * resid_mid, axis=-1, keepdims=True)
    )
    grad_gain_mid = jnp.sum(grad_mid * resid_mid * mid_factor, axis=0)
    grad_attn_out = jnp.concatenate(ring.gather(grad_resid.astype(low)), axis=0)
    layer_out = (
        resid_mid + ring.reduce([moe_part[k * rows : (k + 1) * rows] for k in range(size)])
    ).astype(low)

    def weight_grad(left, right):
        whole = jnp.einsum("td,eth->edh", left, right, preferred_element_type=f32).astype(low)
        step = whole.shape[2] // dp_size
        return combine_relative(
            [whole[:, :, k * step : (k + 1) * step] for k in range(dp_size)], dp_size
        )

    grad_down_w = weight_grad(cot_all, act_gated)
    grad_gate_w = weight_grad(mid_all, d_gate)
    grad_up_w = weight_grad(mid_all, d_up)

    def to_rows_sum(values, step):
        pieces = [
            lax.dynamic_slice_in_dim(values, (d_index ^ k) * step, step, 0) for k in range(dp_size)
        ]
        return combine_relative(pieces, dp_size)

    grad_w_out = lax.dot_general(
        mixed_low, grad_attn_out, (((0,), (0,)), ((), ())), preferred_element_type=f32
    )
    grad_w_out = lax.ppermute(
        to_rows_sum(grad_w_out, own_rows), dp_flat, from_rows
    )
    grad_mixed = lax.dot_general(
        grad_attn_out, w_out, (((1,), (1,)), ((), ())), preferred_element_type=f32
    ).astype(low)
    d_query, d_key, d_value = attend_back(
        q_low, k_low, v_low, grad_mixed, mixed, lse, positions, head_dim
    )
    e_query = turn(d_query, cosine, -sine, own_heads)
    e_key = turn(d_key, cosine, -sine, own_heads)
    g_query, g_key = e_query * gain_q, e_key * gain_k
    dots = jnp.stack([jnp.sum(g_query * q_raw, axis=-1), jnp.sum(g_key * k_raw, axis=-1)])
    dots = ring.sum_rows(dots) / width
    grad_gain_q = jnp.sum(e_query * q_raw * q_factor, axis=0)
    grad_gain_k = jnp.sum(e_key * k_raw * k_factor, axis=0)
    grad_raw = jnp.concatenate(
        [
            q_factor * g_query - q_raw * q_factor**3 * dots[0][:, None],
            k_factor * g_key - k_raw * k_factor**3 * dots[1][:, None],
            d_value,
        ],
        axis=1,
    ).astype(low)
    grad_w_in = lax.dot_general(
        normed, grad_raw, (((0,), (0,)), ((), ())), preferred_element_type=f32
    )
    grad_normed_part = lax.dot_general(
        grad_raw, w_in, (((1,), (1,)), ((), ())), preferred_element_type=f32
    )
    grad_gain_in = jnp.sum(grad_normed_part * x_all * in_factor, axis=0)
    grad_normed_low = grad_normed_part.astype(low)
    grad_normed = ring.reduce([grad_normed_low[k * rows : (k + 1) * rows] for k in range(size)])
    own_x = tokens.astype(f32)
    own_factor = in_factor[:rows]
    scaled_in = grad_normed * gain_in
    grad_tokens = (
        grad_resid
        + own_factor * scaled_in
        - own_x * own_factor**3 * jnp.mean(scaled_in * own_x, axis=-1, keepdims=True)
    )
    grad_w_in = to_rows_sum(grad_w_in, size * own_rows).astype(low)
    grad_w_in = grad_w_in.reshape(size, own_rows, 3 * part)
    grad_w_in = lax.all_to_all(grad_w_in, "fsdp", split_axis=0, concat_axis=0, tiled=True)
    grad_w_in = grad_w_in.reshape(size, own_rows, 3, part).transpose(2, 1, 0, 3)
    grad_w_in = grad_w_in.reshape(3, own_rows, width).astype(f32)

    sums = jnp.concatenate([grad_router, grad_gain_mid[:, None], grad_gain_in[:, None]], axis=1)
    sums = pair_scatter(sums, "fsdp", size)
    sums = jnp.concatenate([sums, grad_gain_q[:, None], grad_gain_k[:, None]], axis=1)
    sums = pair_scatter(sums, "dp", dp_size)
    sums = lax.ppermute(sums, dp_flat, from_rows)
    return (
        layer_out,
        grad_tokens,
        grad_w_in[0],
        grad_w_in[1],
        grad_w_in[2],
        grad_w_out,
        sums[:, :num_experts],
        sums[:, num_experts + 1],
        sums[:, num_experts + 2],
        sums[:, num_experts + 3],
        sums[:, num_experts],
        grad_gate_w,
        grad_up_w,
        grad_down_w,
    )


def splits_evenly(mesh):
    size, dp_size = mesh.shape["fsdp"], mesh.shape["dp"]
    powers = size & (size - 1) == 0 and dp_size & (dp_size - 1) == 0
    return powers and size >= 4 and HEADS % size == 0


def solution(mesh):
    in_specs = (
        P(("dp", "fsdp"), None),
        P(("dp", "fsdp"), None),
        P(("dp", "fsdp"), None),
        P(("dp", "fsdp"), None),
        P(("dp", "fsdp"), None),
        P(("dp", "fsdp"), None),
        P(("dp", "fsdp"), None),
        P(("dp", "fsdp"), None),
        P(("dp", "fsdp")),
        P(("dp", "fsdp")),
        P(("dp", "fsdp")),
        P(("dp", "fsdp")),
        P("fsdp", None, "dp"),
        P("fsdp", None, "dp"),
        P("fsdp", None, "dp"),
    )
    out_specs = (
        P(("dp", "fsdp"), None),
        P(("dp", "fsdp"), None),
        P(("dp", "fsdp"), None),
        P(("dp", "fsdp"), None),
        P(("dp", "fsdp"), None),
        P(("dp", "fsdp"), None),
        P(("dp", "fsdp"), None),
        P(("dp", "fsdp")),
        P(("dp", "fsdp")),
        P(("dp", "fsdp")),
        P(("dp", "fsdp")),
        P("fsdp", None, "dp"),
        P("fsdp", None, "dp"),
        P("fsdp", None, "dp"),
    )
    return jax.shard_map(
        per_device if splits_evenly(mesh) else per_device_gathered,
        mesh=mesh, in_specs=in_specs, out_specs=out_specs, check_vma=False
    )
```

```python
import functools

import jax
import jax.numpy as jnp
from jax import lax
from jax.experimental import pallas as pl
from jax.experimental.pallas import tpu as pltpu
from jax.sharding import PartitionSpec as P

HEADS = 16
TOPK = 8


epsilon = 1e-05
rope_base = 10000.0
hidden_parts = 4
dp_axes = ("x", "core")
far_low = -1e30


def rms_norm(values, scaling):
    factor = lax.rsqrt(jnp.mean(values * values, axis=-1, keepdims=True) + epsilon)
    return values * factor * scaling


def rotary(values, positions):
    half_dim = values.shape[-1] // 2
    inv_freq = rope_base ** (-(jnp.arange(half_dim, dtype=jnp.float32) * 2.0) / values.shape[-1])
    angles = positions.astype(jnp.float32)[:, None] * inv_freq[None, :]
    cosine = jnp.cos(angles)[:, None, :]
    sine_vals = jnp.sin(angles)[:, None, :]
    first_half = values[..., :half_dim]
    second = values[..., half_dim:]
    return jnp.concatenate(
        [first_half * cosine - second * sine_vals, second * cosine + first_half * sine_vals],
        axis=-1,
    )


def head_prep(values, scaling, positions):
    normed = rms_norm(values, scaling)
    return rotary(normed.reshape(values.shape[0], HEADS, -1), positions)


def swiglu(gate_hid, up_hid):
    return jax.nn.silu(gate_hid) * up_hid


def gating(logits, routes, num_experts):
    prob_vals = jax.nn.softmax(logits, axis=-1)
    pick_table = (
        routes[:, :, None] == jnp.arange(num_experts, dtype=jnp.int32)[None, None, :]
    ).astype(jnp.float32)
    chosen = jnp.sum(pick_table * prob_vals[:, None, :], axis=-1)
    return chosen / jnp.sum(chosen, axis=-1, keepdims=True)


def per_device_gathered(
    tokens,
    cotangent,
    routes,
    w_query,
    w_key,
    w_value,
    w_output,
    w_router,
    gain_attn,
    gain_query,
    gain_key,
    gain_ffn,
    expert_gate,
    expert_up,
    expert_down,
):
    row_count = tokens.shape[0]
    model_width = tokens.shape[1]
    head_dim = model_width // HEADS
    score_scale = head_dim ** (-0.5)
    fsdp_size = lax.axis_size("fsdp")
    local_experts = expert_gate.shape[0]
    num_experts = local_experts * fsdp_size
    capacity = max(2, (row_count * TOPK * 5 + 4 * num_experts - 1) // (4 * num_experts))
    positions = lax.axis_index("fsdp") * row_count + jnp.arange(row_count, dtype=jnp.int32)
    first_pos = positions[0]
    last_pos = positions[row_count - 1]
    inputs = tokens.astype(jnp.float32)
    dense_full = (
        lax.all_gather(w_query, ("dp", "fsdp"), axis=0, tiled=True),
        lax.all_gather(w_key, ("dp", "fsdp"), axis=0, tiled=True),
        lax.all_gather(w_value, ("dp", "fsdp"), axis=0, tiled=True),
        lax.all_gather(w_output, ("dp", "fsdp"), axis=0, tiled=True),
        lax.all_gather(w_router, ("dp", "fsdp"), axis=0, tiled=True),
        lax.all_gather(gain_attn, ("dp", "fsdp"), axis=0, tiled=True),
        lax.all_gather(gain_query, ("dp", "fsdp"), axis=0, tiled=True),
        lax.all_gather(gain_key, ("dp", "fsdp"), axis=0, tiled=True),
        lax.all_gather(gain_ffn, ("dp", "fsdp"), axis=0, tiled=True),
    )
    expert_full = (
        lax.all_gather(expert_gate, "dp", axis=2, tiled=True),
        lax.all_gather(expert_up, "dp", axis=2, tiled=True),
        lax.all_gather(expert_down, "dp", axis=2, tiled=True),
    )
    query_full, key_full, value_full, output_full, router_full = dense_full[:5]
    gain_in_full = dense_full[5].astype(jnp.float32)
    gain_q_full = dense_full[6].astype(jnp.float32)
    gain_k_full = dense_full[7].astype(jnp.float32)
    gain_mid_full = dense_full[8].astype(jnp.float32)
    normed_low = rms_norm(inputs, gain_in_full).astype(jnp.bfloat16)
    query_raw = jnp.dot(normed_low, query_full, preferred_element_type=jnp.float32)
    key_raw = jnp.dot(normed_low, key_full, preferred_element_type=jnp.float32)
    value_raw = jnp.dot(normed_low, value_full, preferred_element_type=jnp.float32)
    query_low = head_prep(query_raw, gain_q_full, positions).astype(jnp.bfloat16)
    key_low = head_prep(key_raw, gain_k_full, positions).astype(jnp.bfloat16)
    value_low = value_raw.astype(jnp.bfloat16).reshape(row_count, HEADS, head_dim)
    start_state = (
        jnp.full((HEADS, row_count), far_low, jnp.float32),
        jnp.zeros((HEADS, row_count), jnp.float32),
        jnp.zeros((row_count, HEADS, head_dim), jnp.float32),
    )
    shard_piece = (
        lax.all_gather(key_low, "fsdp", axis=0, tiled=True),
        lax.all_gather(value_low, "fsdp", axis=0, tiled=True),
    )

    def attend_update(state):
        run_max, run_sum, run_acc = state
        key_piece, value_piece = shard_piece
        scores = (
            jnp.einsum("qhd,khd->hqk", query_low, key_piece, preferred_element_type=jnp.float32)
            * score_scale
        )
        key_pos = jnp.arange(key_piece.shape[0], dtype=jnp.int32)
        allowed = (key_pos[None, :] <= positions[:, None])[None]
        new_max = jnp.maximum(run_max, jnp.max(jnp.where(allowed, scores, far_low), axis=-1))
        exp_vals = jnp.where(allowed, jnp.exp(scores - new_max[..., None]), 0.0)
        factor = jnp.exp(run_max - new_max)
        run_sum = jnp.sum(exp_vals, axis=-1)
        run_acc = run_acc * factor.T[:, :, None] + jnp.einsum(
            "hqk,khd->qhd",
            exp_vals.astype(jnp.bfloat16),
            value_piece,
            preferred_element_type=jnp.float32,
        )
        return (new_max, run_sum, run_acc)

    run_max, run_sum, run_acc = lax.cond(
        jnp.int32(0) <= last_pos, attend_update, lambda state: state, start_state
    )
    attn_f32 = run_acc / run_sum.T[:, :, None]
    log_sum = run_max + jnp.log(run_sum)
    attn_low = attn_f32.reshape(row_count, model_width).astype(jnp.bfloat16)
    resid_mid = inputs + jnp.dot(attn_low, output_full, preferred_element_type=jnp.float32)
    mid_low = rms_norm(resid_mid, gain_mid_full).astype(jnp.bfloat16)
    logits = jnp.dot(mid_low, router_full, preferred_element_type=jnp.float32)
    gate_vals, gate_pull = jax.vjp(
        lambda logit_vals: gating(logit_vals, routes, num_experts), logits
    )
    route_flat = routes.reshape(-1)
    pick_table = (route_flat[:, None] == jnp.arange(num_experts, dtype=jnp.int32)[None, :]).astype(
        jnp.int32
    )
    slot_index = jnp.sum(pick_table * (jnp.cumsum(pick_table, axis=0) - 1), axis=1)
    target = route_flat * capacity + slot_index
    spread = jnp.repeat(mid_low, TOPK, axis=0)
    send_rows = (
        jnp.zeros((num_experts * capacity, model_width), jnp.bfloat16).at[target].set(spread)
    )
    send_rows = send_rows.reshape(fsdp_size, local_experts, capacity, model_width)
    arrived = lax.all_to_all(send_rows, "fsdp", split_axis=0, concat_axis=0, tiled=True)
    gate_w, up_w, down_w = expert_full
    gate_hid = jnp.einsum("secd,edh->sech", arrived, gate_w, preferred_element_type=jnp.float32)
    up_hid = jnp.einsum("secd,edh->sech", arrived, up_w, preferred_element_type=jnp.float32)
    act_low = swiglu(gate_hid, up_hid).astype(jnp.bfloat16)
    expert_out = jnp.einsum(
        "sech,edh->secd", act_low, down_w, preferred_element_type=jnp.float32
    ).astype(jnp.bfloat16)
    returned = lax.all_to_all(expert_out, "fsdp", split_axis=0, concat_axis=0, tiled=True).reshape(
        num_experts * capacity, model_width
    )
    picked = returned[target].reshape(row_count, TOPK, model_width).astype(jnp.float32)
    resid_out = resid_mid + jnp.sum(gate_vals[:, :, None] * picked, axis=1)
    layer_out = resid_out.astype(jnp.bfloat16)
    back_dense = (
        lax.all_gather(w_query, ("dp", "fsdp"), axis=0, tiled=True),
        lax.all_gather(w_key, ("dp", "fsdp"), axis=0, tiled=True),
        lax.all_gather(w_value, ("dp", "fsdp"), axis=0, tiled=True),
        lax.all_gather(w_output, ("dp", "fsdp"), axis=0, tiled=True),
        lax.all_gather(w_router, ("dp", "fsdp"), axis=0, tiled=True),
        lax.all_gather(gain_attn, ("dp", "fsdp"), axis=0, tiled=True),
        lax.all_gather(gain_query, ("dp", "fsdp"), axis=0, tiled=True),
        lax.all_gather(gain_key, ("dp", "fsdp"), axis=0, tiled=True),
        lax.all_gather(gain_ffn, ("dp", "fsdp"), axis=0, tiled=True),
    )
    back_experts = (
        lax.all_gather(expert_gate, "dp", axis=2, tiled=True),
        lax.all_gather(expert_up, "dp", axis=2, tiled=True),
        lax.all_gather(expert_down, "dp", axis=2, tiled=True),
    )
    query_back, key_back, value_back, output_back, router_back = back_dense[:5]
    gain_in_back = back_dense[5].astype(jnp.float32)
    gain_q_back = back_dense[6].astype(jnp.float32)
    gain_k_back = back_dense[7].astype(jnp.float32)
    gain_mid_back = back_dense[8].astype(jnp.float32)
    gate_back, up_back, down_back = back_experts
    grad_out = cotangent.astype(jnp.float32)
    grad_gates = jnp.sum(grad_out[:, None, :] * picked, axis=-1)
    grad_routed = (
        (gate_vals[:, :, None] * grad_out[:, None, :]).astype(jnp.bfloat16).reshape(-1, model_width)
    )
    send_grads = (
        jnp.zeros((num_experts * capacity, model_width), jnp.bfloat16).at[target].set(grad_routed)
    )
    send_grads = send_grads.reshape(fsdp_size, local_experts, capacity, model_width)
    grad_arrived = lax.all_to_all(send_grads, "fsdp", split_axis=0, concat_axis=0, tiled=True)
    gate_again = jnp.einsum(
        "secd,edh->sech", arrived, gate_back, preferred_element_type=jnp.float32
    )
    up_again = jnp.einsum("secd,edh->sech", arrived, up_back, preferred_element_type=jnp.float32)
    act_vals, act_pull = jax.vjp(swiglu, gate_again, up_again)
    act_again = act_vals.astype(jnp.bfloat16)
    grad_act = jnp.einsum(
        "secd,edh->sech", grad_arrived, down_back, preferred_element_type=jnp.float32
    )
    grad_down = jnp.einsum(
        "secd,sech->edh", grad_arrived, act_again, preferred_element_type=jnp.float32
    )
    grad_gate_hid, grad_up_hid = act_pull(grad_act)
    grad_gate_low = grad_gate_hid.astype(jnp.bfloat16)
    grad_up_low = grad_up_hid.astype(jnp.bfloat16)
    grad_gate_w = jnp.einsum(
        "secd,sech->edh", arrived, grad_gate_low, preferred_element_type=jnp.float32
    )
    grad_up_w = jnp.einsum(
        "secd,sech->edh", arrived, grad_up_low, preferred_element_type=jnp.float32
    )
    grad_inputs = jnp.einsum(
        "sech,edh->secd", grad_gate_low, gate_back, preferred_element_type=jnp.float32
    ) + jnp.einsum("sech,edh->secd", grad_up_low, up_back, preferred_element_type=jnp.float32)
    grad_returned = lax.all_to_all(
        grad_inputs.astype(jnp.bfloat16), "fsdp", split_axis=0, concat_axis=0, tiled=True
    )
    grad_returned = grad_returned.reshape(num_experts * capacity, model_width)
    grad_mid = jnp.sum(
        grad_returned[target].reshape(row_count, TOPK, model_width).astype(jnp.float32), axis=1
    )
    expert_grads = (
        lax.psum_scatter(
            grad_gate_w.astype(jnp.bfloat16), "dp", scatter_dimension=2, tiled=True
        ).astype(jnp.float32),
        lax.psum_scatter(
            grad_up_w.astype(jnp.bfloat16), "dp", scatter_dimension=2, tiled=True
        ).astype(jnp.float32),
        lax.psum_scatter(
            grad_down.astype(jnp.bfloat16), "dp", scatter_dimension=2, tiled=True
        ).astype(jnp.float32),
    )
    (grad_logits,) = gate_pull(grad_gates)
    grad_logits_low = grad_logits.astype(jnp.bfloat16)
    grad_router = jnp.einsum(
        "td,te->de", mid_low, grad_logits_low, preferred_element_type=jnp.float32
    )
    grad_mid = grad_mid + jnp.einsum(
        "te,de->td", grad_logits_low, router_back, preferred_element_type=jnp.float32
    )
    mid_value, mid_pull = jax.vjp(rms_norm, resid_mid, gain_mid_back)
    grad_resid_part, grad_gain_mid = mid_pull(grad_mid)
    grad_resid = grad_out + grad_resid_part
    grad_attn_out = grad_resid.astype(jnp.bfloat16)
    grad_output_w = jnp.einsum(
        "td,te->de", attn_low, grad_attn_out, preferred_element_type=jnp.float32
    )
    grad_attn = jnp.einsum(
        "te,de->td", grad_attn_out, output_back, preferred_element_type=jnp.float32
    )
    grad_attn = grad_attn.astype(jnp.bfloat16).reshape(row_count, HEADS, head_dim)
    delta_rows = jnp.sum(grad_attn.astype(jnp.float32) * attn_f32, axis=-1).T
    key_all, value_all = (
        lax.all_gather(key_low, "fsdp", axis=0, tiled=True),
        lax.all_gather(value_low, "fsdp", axis=0, tiled=True),
    )

    def probs_block(key_block, value_block, begin_at):
        scores = (
            jnp.einsum("qhd,khd->hqk", query_low, key_block, preferred_element_type=jnp.float32)
            * score_scale
        )
        key_pos = begin_at + jnp.arange(key_block.shape[0], dtype=jnp.int32)
        allowed = (key_pos[None, :] <= positions[:, None])[None]
        prob_vals = jnp.where(allowed, jnp.exp(scores - log_sum[..., None]), 0.0)
        grad_probs = jnp.einsum(
            "qhd,khd->hqk", grad_attn, value_block, preferred_element_type=jnp.float32
        )
        grad_scores = (prob_vals * (grad_probs - delta_rows[..., None])).astype(jnp.bfloat16)
        return (prob_vals, grad_scores)

    block_rows = 8 * row_count
    block_needed = last_pos // block_rows + 1
    zero_query = jnp.zeros((row_count, HEADS, head_dim), jnp.float32)

    def query_step(block_index, accum):
        begin_at = block_index * block_rows
        key_block = lax.dynamic_slice_in_dim(key_all, begin_at, block_rows, 0)
        value_block = lax.dynamic_slice_in_dim(value_all, begin_at, block_rows, 0)
        prob_vals, grad_scores = probs_block(key_block, value_block, begin_at)
        return accum + jnp.einsum(
            "hqk,khd->qhd", grad_scores, key_block, preferred_element_type=jnp.float32
        )

    grad_query_rot = lax.fori_loop(0, block_needed, query_step, zero_query) * score_scale
    stats_all = (
        lax.all_gather(log_sum.T, "fsdp", axis=0, tiled=True),
        lax.all_gather(delta_rows.T, "fsdp", axis=0, tiled=True),
    )
    query_piece = lax.all_gather(query_low, "fsdp", axis=0, tiled=True)
    grad_piece = lax.all_gather(grad_attn, "fsdp", axis=0, tiled=True)
    span = query_piece.shape[0]

    def add_update(state):
        lse_piece = stats_all[0].T
        delta_piece = stats_all[1].T
        scores = (
            jnp.einsum("qhd,khd->hqk", query_piece, key_low, preferred_element_type=jnp.float32)
            * score_scale
        )
        query_pos = jnp.arange(span, dtype=jnp.int32)
        allowed = (positions[None, :] <= query_pos[:, None])[None]
        prob_vals = jnp.where(allowed, jnp.exp(scores - lse_piece[..., None]), 0.0)
        grad_probs = jnp.einsum(
            "qhd,khd->hqk", grad_piece, value_low, preferred_element_type=jnp.float32
        )
        grad_scores = (prob_vals * (grad_probs - delta_piece[..., None])).astype(jnp.bfloat16)
        grad_value_acc = jnp.einsum(
            "hqk,qhd->khd",
            prob_vals.astype(jnp.bfloat16),
            grad_piece,
            preferred_element_type=jnp.float32,
        )
        grad_key_acc = jnp.einsum(
            "hqk,qhd->khd", grad_scores, query_piece, preferred_element_type=jnp.float32
        )
        return (grad_key_acc, grad_value_acc)

    grad_key_sum, grad_value_sum = lax.cond(
        jnp.int32(0) + span > first_pos, add_update, lambda state: state, (zero_query, zero_query)
    )
    grad_key_rot = grad_key_sum * score_scale
    grad_value_low = grad_value_sum.reshape(row_count, model_width).astype(jnp.bfloat16)
    query_value, query_pull = jax.vjp(
        lambda raw_vals, scaling: head_prep(raw_vals, scaling, positions), query_raw, gain_q_back
    )
    grad_query_raw, grad_gain_query = query_pull(grad_query_rot)
    key_value, key_pull = jax.vjp(
        lambda raw_vals, scaling: head_prep(raw_vals, scaling, positions), key_raw, gain_k_back
    )
    grad_key_raw, grad_gain_key = key_pull(grad_key_rot)
    grad_query_low = grad_query_raw.astype(jnp.bfloat16)
    grad_key_low = grad_key_raw.astype(jnp.bfloat16)
    grad_wq = jnp.einsum(
        "td,te->de", normed_low, grad_query_low, preferred_element_type=jnp.float32
    )
    grad_wk = jnp.einsum("td,te->de", normed_low, grad_key_low, preferred_element_type=jnp.float32)
    grad_wv = jnp.einsum(
        "td,te->de", normed_low, grad_value_low, preferred_element_type=jnp.float32
    )
    grad_normed = (
        jnp.einsum("te,de->td", grad_query_low, query_back, preferred_element_type=jnp.float32)
        + jnp.einsum("te,de->td", grad_key_low, key_back, preferred_element_type=jnp.float32)
        + jnp.einsum("te,de->td", grad_value_low, value_back, preferred_element_type=jnp.float32)
    )
    in_value, input_pull = jax.vjp(rms_norm, inputs, gain_in_back)
    grad_input_part, grad_gain_in = input_pull(grad_normed)
    grad_tokens = grad_resid + grad_input_part
    dense_grads = (
        lax.psum_scatter(grad_wq, ("dp", "fsdp"), scatter_dimension=0, tiled=True),
        lax.psum_scatter(grad_wk, ("dp", "fsdp"), scatter_dimension=0, tiled=True),
        lax.psum_scatter(grad_wv, ("dp", "fsdp"), scatter_dimension=0, tiled=True),
        lax.psum_scatter(grad_output_w, ("dp", "fsdp"), scatter_dimension=0, tiled=True),
        lax.psum_scatter(grad_router, ("dp", "fsdp"), scatter_dimension=0, tiled=True),
        lax.psum_scatter(grad_gain_in, ("dp", "fsdp"), scatter_dimension=0, tiled=True),
        lax.psum_scatter(grad_gain_query, ("dp", "fsdp"), scatter_dimension=0, tiled=True),
        lax.psum_scatter(grad_gain_key, ("dp", "fsdp"), scatter_dimension=0, tiled=True),
        lax.psum_scatter(grad_gain_mid, ("dp", "fsdp"), scatter_dimension=0, tiled=True),
    )
    return (
        layer_out,
        grad_tokens,
        dense_grads[0],
        dense_grads[1],
        dense_grads[2],
        dense_grads[3],
        dense_grads[4],
        dense_grads[5],
        dense_grads[6],
        dense_grads[7],
        dense_grads[8],
        expert_grads[0],
        expert_grads[1],
        expert_grads[2],
    )


def after(values, ties):
    if callable(ties):
        ties = ties(values)
    if ties is None:
        return values
    return lax.optimization_barrier((values, ties))[0]


class Ring:
    def __init__(self, size, rows):
        self.size = size
        self.half = size // 2
        self.rows = rows
        middle = rows // 2
        self.pieces = [(k, 0, rows) for k in range(self.half)]
        self.pieces += [(self.half, 0, middle), (self.half, middle, middle)]
        self.pieces += [(k, 0, rows) for k in range(self.half + 1, size)]
        self.order = list(range(0, size, 2)) + list(range(size - 1, 0, -2))
        place = [self.order.index(i) for i in range(size)]
        rank = jnp.asarray(place, jnp.int32)[lax.axis_index("fsdp")]
        self.slot_device = jnp.asarray(self.order, jnp.int32)[
            (rank + jnp.arange(size, dtype=jnp.int32)) % size
        ]
        self.device_slot = (jnp.asarray(place, jnp.int32) - rank) % size
        self.up = [(self.order[i], self.order[(i + 1) % size]) for i in range(size)]
        self.down = [(self.order[i], self.order[i - 1]) for i in range(size)]

    def forward(self, values):
        return lax.ppermute(values, "fsdp", self.up)

    def backward(self, values):
        return lax.ppermute(values, "fsdp", self.down)

    def gather(self, block, halves=True):
        return Gather(self, block, halves)

    def reduce(self, pieces):
        return Reduce(self, pieces)


class Gather:
    def __init__(self, ring, block, halves=True):
        self.ring, self.halves = ring, halves
        self.low, self.high, self.opposite = [block], [block], None

    def step(self, ties=None):
        ring, middle = self.ring, self.ring.rows // 2
        from_low, from_high = after((self.low[-1], self.high[-1]), ties)
        if len(self.low) < ring.half:
            self.low.append(ring.forward(from_low))
            self.high.append(ring.backward(from_high))
            return self.low[-1], self.high[-1]
        if self.halves:
            self.opposite = [ring.forward(from_low[:middle]), ring.backward(from_high[middle:])]
        else:
            self.opposite = [ring.forward(from_low)]
        return tuple(self.opposite)

    def stacked(self):
        return jnp.stack(self.blocks())[self.ring.device_slot]

    def blocks(self):
        return self.high + self.opposite + self.low[:0:-1]


class Reduce:
    def __init__(self, ring, pieces):
        self.ring, self.pieces, self.arrived, self.left = ring, pieces, None, ring.half

    def step(self, ties=None):
        ring, pieces, middle = self.ring, self.pieces, self.ring.rows // 2
        if self.arrived is None:
            upper, lower = pieces[ring.half], pieces[ring.half + 1]
        else:
            rising, falling = self.arrived
            upper, lower = pieces[self.left], pieces[-self.left]
            if self.left == ring.half - 1:
                upper = jnp.concatenate([upper[:middle] + rising, upper[middle:]], axis=0)
                lower = jnp.concatenate([lower[:middle], lower[middle:] + falling], axis=0)
            else:
                upper, lower = upper + rising, lower + falling
        upper, lower = after((upper, lower), ties)
        self.arrived = (ring.forward(upper), ring.backward(lower))
        self.left -= 1
        return self.arrived

    def total(self):
        rising, falling = self.arrived
        return (
            self.pieces[0].astype(jnp.float32)
            + rising.astype(jnp.float32)
            + falling.astype(jnp.float32)
        )


def exchange_pairs(size, bit):
    return [(i, i ^ bit) for i in range(size)]


def pair_sum(values, axis, size):
    bit = 1
    while bit < size:
        values = values + lax.ppermute(values, axis, exchange_pairs(size, bit))
        bit *= 2
    return values


def pair_gather(values, axis, size, ties=()):
    ties = dict(ties)
    mine = lax.axis_index(axis)
    values = values[None]
    bit = 1
    while bit < size:
        values = after(values, ties.get(bit))
        other = lax.ppermute(values, axis, exchange_pairs(size, bit))
        upper = (mine & bit) != 0
        values = jnp.where(
            upper,
            jnp.concatenate([other, values], axis=0),
            jnp.concatenate([values, other], axis=0),
        )
        bit *= 2
    return values


def pair_scatter(values, axis, size, ties=()):
    ties = dict(ties)
    mine = lax.axis_index(axis)
    bit = size // 2
    while bit >= 1:
        span = values.shape[1] // 2
        upper = (mine & bit) != 0
        low_half, high_half = values[:, :span], values[:, span:]
        kept = jnp.where(upper, high_half, low_half)
        sent = after(jnp.where(upper, low_half, high_half), ties.get(bit))
        values = kept + lax.ppermute(sent, axis, exchange_pairs(size, bit))
        bit //= 2
    return values


def share_relative(block, size, ties=(), second=()):
    block = after(block, ties)
    held = {0: block}
    bit = size // 2
    while bit >= 1:
        for index in list(held):
            sent = held[index] if index == 0 else after(held[index], second)
            held[index ^ bit] = lax.ppermute(sent, dp_axes, exchange_pairs(size, bit))
        bit //= 2
    return [held[index] for index in range(size)]


def combine_relative(blocks, ties=(None, None)):
    half = blocks.shape[0] // 2
    far = lax.ppermute(after(blocks[:half], ties[0]), dp_axes, exchange_pairs(4, 1))
    sums = blocks[half:].astype(jnp.float32) + far.astype(jnp.float32)
    other = after(sums[half // 2 :].astype(jnp.bfloat16), ties[1])
    other = lax.ppermute(other, dp_axes, exchange_pairs(4, 2))
    return sums[: half // 2] + other.astype(jnp.float32)


anywhere = pl.BlockSpec(memory_space=pl.ANY)
rows_first = (((0,), (0,)), ((), ()))
columns_last = (((1,), (1,)), ((), ()))


def dot(left, right, dims=(((1,), (0,)), ((), ()))):
    return lax.dot_general(left, right, dims, preferred_element_type=jnp.float32)


def row_sums(*columns):
    total = None
    for i, values in enumerate(columns):
        place = lax.broadcasted_iota(jnp.int32, (8, values.shape[1]), 0) == i
        sums = lax.dot_general(
            place.astype(jnp.float32),
            values,
            columns_last,
            precision=lax.Precision.HIGHEST,
            preferred_element_type=jnp.float32,
        )
        total = sums if total is None else total + sums
    return total


def as_columns(rows):
    same = lax.broadcasted_iota(jnp.int32, (8, 8), 0) == lax.broadcasted_iota(jnp.int32, (8, 8), 1)
    return lax.dot_general(
        rows,
        same.astype(jnp.float32),
        rows_first,
        precision=lax.Precision.HIGHEST,
        preferred_element_type=jnp.float32,
    )


def whole_block(shape):
    return pl.BlockSpec(shape, lambda *_: (0,) * len(shape))


def piece_copies(pieces, scalars, blocks, target, sems):
    rows = pieces[0][2]
    copies = []
    for i, (slot, first, count) in enumerate(pieces):
        begin = pl.multiple_of(scalars[slot] * rows + first, count)
        copies.append(
            pltpu.make_async_copy(blocks[i], target.at[pl.ds(begin, count), :], sems.at[i])
        )
    return copies


def piece_results(pieces, scalars, source, blocks, sems):
    rows = pieces[0][2]
    copies = []
    for i, (slot, first, count) in enumerate(pieces):
        begin = pl.multiple_of(scalars[slot] * rows + first, count)
        copies.append(
            pltpu.make_async_copy(source.at[pl.ds(begin, count), :], blocks[i], sems.at[i])
        )
    return copies


def row_copies(scalars, which, blocks, target, sems):
    own = scalars[which]
    count = blocks[0].shape[0]
    return [
        pltpu.make_async_copy(
            block, target.at[pl.ds(pl.multiple_of((own ^ i) * count, count), count), :], sems.at[i]
        )
        for i, block in enumerate(blocks)
    ]


def run_copies(copies):
    for copy in copies:
        copy.start()
    for copy in copies:
        copy.wait()


def piece_shapes(pieces, width):
    return [jax.ShapeDtypeStruct((count, width), jnp.bfloat16) for _, _, count in pieces]


def project_kernel(pieces, parts, chunk, scalars, *refs):
    n = len(pieces)
    blocks, weights, gain = refs[:n], refs[n : n + parts], refs[n + parts]
    normed, raw, factor, squares, kept, tokens, weight, sems, w_sems, k_sem = refs[n + parts + 1 :]
    step = pl.program_id(0)

    @pl.when(step == 0)
    def _():
        run_copies(
            piece_copies(pieces, scalars, blocks, tokens, sems)
            + row_copies(scalars, len(scalars) - 1, weights, weight, w_sems)
        )
        pltpu.make_async_copy(tokens, kept, k_sem).start()

    rows = pl.ds(pl.multiple_of(step * chunk, chunk), chunk)
    values = tokens[rows, :].astype(jnp.float32)
    scale = lax.rsqrt(jnp.mean(values * values, axis=-1, keepdims=True) + epsilon)
    low = (values * scale * gain[...]).astype(jnp.bfloat16)
    normed[...] = low
    factor[...] = scale
    product = dot(low, weight[...])
    raw[...] = product
    part = product.shape[1] // 3
    squares[...] = row_sums(product[:, :part] ** 2, product[:, part : 2 * part] ** 2)

    @pl.when(step == pl.num_programs(0) - 1)
    def _():
        pltpu.make_async_copy(tokens, kept, k_sem).wait()


def project(ring, scalars, blocks, weights, gain):
    width = blocks[0].shape[1]
    span = ring.rows * ring.size
    columns = weights[0].shape[1]
    chunk = min(256, span)
    n = len(ring.pieces)
    by_rows = lambda i, s: (i, 0)
    return pl.pallas_call(
        functools.partial(project_kernel, ring.pieces, len(weights), chunk),
        grid_spec=pltpu.PrefetchScalarGridSpec(
            num_scalar_prefetch=1,
            grid=(span // chunk,),
            in_specs=[anywhere] * (n + len(weights)) + [whole_block((1, width))],
            out_specs=[
                pl.BlockSpec((chunk, width), by_rows),
                pl.BlockSpec((chunk, columns), by_rows),
                pl.BlockSpec((chunk, 1), by_rows),
                pl.BlockSpec((8, chunk), lambda i, s: (0, i)),
                anywhere,
            ],
            scratch_shapes=[
                pltpu.VMEM((span, width), jnp.bfloat16),
                pltpu.VMEM((width, columns), jnp.bfloat16),
                pltpu.SemaphoreType.DMA((n,)),
                pltpu.SemaphoreType.DMA((len(weights),)),
                pltpu.SemaphoreType.DMA,
            ],
        ),
        out_shape=[
            jax.ShapeDtypeStruct((span, width), jnp.bfloat16),
            jax.ShapeDtypeStruct((span, columns), jnp.float32),
            jax.ShapeDtypeStruct((span, 1), jnp.float32),
            jax.ShapeDtypeStruct((8, span), jnp.float32),
            jax.ShapeDtypeStruct((span, width), jnp.bfloat16),
        ],
        name="project",
    )(scalars, *blocks, *weights, gain)


def turned(values, cosine, sine):
    return values * cosine + pltpu.roll(values, values.shape[-1] // 2, 1) * sine


def attend_kernel(pieces, parts, chunk, scale, scalars, *refs):
    q_raw, k_raw, v_raw, factors, gain_q, gain_k, cosine, sine = refs[:8]
    weights = refs[8 : 8 + parts]
    query, key, value, mixed, lse = refs[8 + parts : 13 + parts]
    n = len(pieces)
    results = refs[13 + parts : 13 + parts + n]
    weight, total, summed, w_sems, sems = refs[13 + parts + n :]
    head = pl.program_id(0)
    last = pl.num_programs(0) - 1
    tokens, head_dim = query.shape

    @pl.when(head == 0)
    def _():
        run_copies(row_copies(scalars, len(scalars) - 1, weights, weight, w_sems))

    columns = as_columns(factors[...])
    query[...] = turned(
        q_raw[...] * columns[:, 0:1] * gain_q[...], cosine[...], sine[...]
    ).astype(jnp.bfloat16)
    key[...] = turned(
        k_raw[...] * columns[:, 1:2] * gain_k[...], cosine[...], sine[...]
    ).astype(jnp.bfloat16)
    value[...] = v_raw[...].astype(jnp.bfloat16)
    own_rows = weight[pl.ds(pl.multiple_of(head * head_dim, head_dim), head_dim), :]
    for begin in range(0, tokens, chunk):
        rows, seen = pl.ds(begin, chunk), pl.ds(0, begin + chunk)
        scores = dot(query[rows, :], key[seen, :], columns_last) * scale
        shape = scores.shape
        allowed = lax.broadcasted_iota(jnp.int32, shape, 1) <= begin + lax.broadcasted_iota(
            jnp.int32, shape, 0
        )
        scores = jnp.where(allowed, scores, far_low)
        top = jnp.max(scores, axis=-1, keepdims=True)
        weights_now = jnp.exp(scores - top)
        sums = jnp.sum(weights_now, axis=-1, keepdims=True)
        out = dot(weights_now.astype(jnp.bfloat16), value[seen, :]) / sums
        mixed[rows, :] = out
        lse[rows, :] = top + jnp.log(sums)
        product = dot(out.astype(jnp.bfloat16), own_rows)

        @pl.when(head == 0)
        def _():
            total[rows, :] = product

        @pl.when(jnp.logical_and(head > 0, head < last))
        def _():
            total[rows, :] += product

        @pl.when(jnp.logical_and(head > 0, head == last))
        def _():
            summed[rows, :] = (total[rows, :] + product).astype(jnp.bfloat16)

        @pl.when(jnp.logical_and(head == 0, head == last))
        def _():
            summed[rows, :] = product.astype(jnp.bfloat16)

    @pl.when(head == last)
    def _():
        run_copies(piece_results(pieces, scalars, summed, results, sems))


def attend(ring, scalars, raw, factors, gain_q, gain_k, cosine, sine, weights, head_dim):
    tokens = raw.shape[0]
    part = raw.shape[1] // 3
    heads = part // head_dim
    width = weights[0].shape[1]
    n = len(ring.pieces)
    column = lambda first: pl.BlockSpec((tokens, head_dim), lambda h, s: (0, first + h))
    gain = pl.BlockSpec((1, head_dim), lambda h, s: (0, h))
    table = whole_block((tokens, head_dim))
    low = jax.ShapeDtypeStruct((tokens, part), jnp.bfloat16)
    out = pl.pallas_call(
        functools.partial(
            attend_kernel, ring.pieces, len(weights), min(256, tokens), head_dim ** (-0.5)
        ),
        grid_spec=pltpu.PrefetchScalarGridSpec(
            num_scalar_prefetch=1,
            grid=(heads,),
            in_specs=[column(0), column(heads), column(2 * heads), whole_block((8, tokens))]
            + [gain, gain, table, table]
            + [anywhere] * len(weights),
            out_specs=[column(0)] * 4
            + [pl.BlockSpec((None, tokens, 1), lambda h, s: (h, 0, 0))]
            + [anywhere] * n,
            scratch_shapes=[
                pltpu.VMEM((part, width), jnp.bfloat16),
                pltpu.VMEM((tokens, width), jnp.float32),
                pltpu.VMEM((tokens, width), jnp.bfloat16),
                pltpu.SemaphoreType.DMA((len(weights),)),
                pltpu.SemaphoreType.DMA((n,)),
            ],
        ),
        out_shape=[low, low, low, jax.ShapeDtypeStruct((tokens, part), jnp.float32)]
        + [jax.ShapeDtypeStruct((heads, tokens, 1), jnp.float32)]
        + piece_shapes(ring.pieces, width),
        name="attend",
    )(scalars, raw, raw, raw, factors, gain_q, gain_k, cosine, sine, *weights)
    return out[:5], out[5:]


def attend_back_kernel(pieces, parts, chunk, scale, head, scalars, *refs):
    query, key, value, mixed, lse, q_raw, k_raw, factors, gain_q, gain_k, cosine, sine = refs[:12]
    n = len(pieces)
    weights = refs[12 : 12 + parts]
    blocks = refs[12 + parts : 12 + parts + n]
    outs = refs[12 + parts + n :]
    turn_q, turn_k, d_value, dots, sum_q, sum_k = outs[:6]
    kept = outs[6] if head == 0 else None
    weight, grads, d_key, d_val, d_query, w_sems, sems, k_sem = outs[-8:]
    tokens, head_dim = query.shape
    run_copies(
        row_copies(scalars, len(scalars) - 1, weights, weight, w_sems)
        + piece_copies(pieces, scalars, blocks, grads, sems)
    )
    if kept is not None:
        pltpu.make_async_copy(grads, kept, k_sem).start()
    own_rows = weight[pl.ds(head * head_dim, head_dim), :]
    for begin in range(0, tokens, chunk):
        rows, seen = pl.ds(begin, chunk), pl.ds(0, begin + chunk)
        grad = dot(grads[rows, :], own_rows, columns_last).astype(jnp.bfloat16)
        queries = query[rows, :]
        scores = dot(queries, key[seen, :], columns_last) * scale
        shape = scores.shape
        allowed = lax.broadcasted_iota(jnp.int32, shape, 1) <= begin + lax.broadcasted_iota(
            jnp.int32, shape, 0
        )
        probs = jnp.where(allowed, jnp.exp(scores - lse[rows, :]), 0.0)
        delta = jnp.sum(grad.astype(jnp.float32) * mixed[rows, :], axis=-1, keepdims=True)
        grad_probs = dot(grad, value[seen, :], columns_last)
        grad_scores = (probs * (grad_probs - delta)).astype(jnp.bfloat16)
        d_query[rows, :] = dot(grad_scores, key[seen, :]) * scale
        part_key = dot(grad_scores, queries, rows_first) * scale
        part_value = dot(probs.astype(jnp.bfloat16), grad, rows_first)
        if begin > 0:
            before = pl.ds(0, begin)
            d_key[before, :] += part_key[:begin]
            d_val[before, :] += part_value[:begin]
        d_key[rows, :] = part_key[begin:]
        d_val[rows, :] = part_value[begin:]
    d_value[...] = d_val[...].astype(jnp.bfloat16)
    back_q = turned(d_query[...], cosine[...], -sine[...])
    back_k = turned(d_key[...], cosine[...], -sine[...])
    turn_q[...] = back_q
    turn_k[...] = back_k
    with_q, with_k = back_q * q_raw[...], back_k * k_raw[...]
    columns = as_columns(factors[...])
    sum_q[...] = jnp.sum(with_q * columns[:, 0:1], axis=0, keepdims=True)
    sum_k[...] = jnp.sum(with_k * columns[:, 1:2], axis=0, keepdims=True)
    dots[...] = row_sums(with_q * gain_q[...], with_k * gain_k[...])
    if kept is not None:
        pltpu.make_async_copy(grads, kept, k_sem).wait()


def attend_back(
    ring, scalars, saved, raw, factors, gain_q, gain_k, cosine, sine, weights, blocks, head_dim,
    head,
):
    query, key, value, mixed, lse = saved
    tokens, part = query.shape
    heads = part // head_dim
    width = weights[0].shape[1]
    n = len(ring.pieces)
    column = lambda first: pl.BlockSpec((tokens, head_dim), lambda i, s: (0, first + head))
    gain = pl.BlockSpec((1, head_dim), lambda i, s: (0, head))
    table = whole_block((tokens, head_dim))
    result = jax.ShapeDtypeStruct((tokens, head_dim), jnp.float32)
    sums = jax.ShapeDtypeStruct((1, head_dim), jnp.float32)
    kept = [anywhere] if head == 0 else []
    accumulate = pltpu.VMEM((tokens, head_dim), jnp.float32)
    return pl.pallas_call(
        functools.partial(
            attend_back_kernel, ring.pieces, len(weights), min(256, tokens), head_dim ** (-0.5),
            head,
        ),
        grid_spec=pltpu.PrefetchScalarGridSpec(
            num_scalar_prefetch=1,
            grid=(1,),
            in_specs=[column(0)] * 4
            + [pl.BlockSpec((None, tokens, 1), lambda i, s: (head, 0, 0))]
            + [column(0), column(heads), whole_block((8, tokens)), gain, gain, table, table]
            + [anywhere] * (len(weights) + n),
            out_specs=[table] * 3
            + [whole_block((8, tokens))]
            + [whole_block((1, head_dim))] * 2
            + kept,
            scratch_shapes=[
                pltpu.VMEM((part, width), jnp.bfloat16),
                pltpu.VMEM((tokens, width), jnp.bfloat16),
                accumulate,
                accumulate,
                accumulate,
                pltpu.SemaphoreType.DMA((len(weights),)),
                pltpu.SemaphoreType.DMA((n,)),
                pltpu.SemaphoreType.DMA,
            ],
        ),
        out_shape=[
            result,
            result,
            jax.ShapeDtypeStruct((tokens, head_dim), jnp.bfloat16),
            jax.ShapeDtypeStruct((8, tokens), jnp.float32),
            sums,
            sums,
        ]
        + [jax.ShapeDtypeStruct((tokens, width), jnp.bfloat16)] * len(kept),
        name="attend_back",
    )(
        scalars, query, key, value, mixed, lse, raw, raw, factors, gain_q, gain_k, cosine, sine,
        *weights, *blocks,
    )


def project_back_kernel(pieces, parts, chunk, heads, scalars, *refs):
    turns, refs = refs[: 3 * heads], refs[3 * heads :]
    raw, factors, dots, gain_q, gain_k, tokens, in_factor = refs[:7]
    n = len(pieces)
    weights = refs[7 : 7 + parts]
    grad_raw, sum_in = refs[7 + parts : 9 + parts]
    results = refs[9 + parts : 9 + parts + n]
    weight, summed, w_sems, sems = refs[9 + parts + n :]
    step = pl.program_id(0)
    head_dim = turns[0].shape[1]
    part = heads * head_dim

    @pl.when(step == 0)
    def _():
        run_copies(row_copies(scalars, len(scalars) - 1, weights, weight, w_sems))
        sum_in[...] = jnp.zeros_like(sum_in)

    factor_columns, dot_columns = as_columns(factors[...]), as_columns(dots[...])
    for i, gain in enumerate((gain_q, gain_k)):
        factor = factor_columns[:, i : i + 1]
        cubed = factor * factor * factor * dot_columns[:, i : i + 1]
        for head in range(heads):
            columns = pl.ds(i * part + head * head_dim, head_dim)
            turn = turns[3 * head + i][...] * gain[:, head * head_dim : (head + 1) * head_dim]
            grad_raw[:, columns] = (factor * turn - raw[:, columns] * cubed).astype(jnp.bfloat16)
    for head in range(heads):
        grad_raw[:, pl.ds(2 * part + head * head_dim, head_dim)] = turns[3 * head + 2][...]
    normed = dot(grad_raw[...], weight[...], columns_last)
    sum_in[...] += jnp.sum(
        normed * (tokens[...].astype(jnp.float32) * in_factor[...]), axis=0, keepdims=True
    )
    summed[pl.ds(pl.multiple_of(step * chunk, chunk), chunk), :] = normed.astype(jnp.bfloat16)

    @pl.when(step == pl.num_programs(0) - 1)
    def _():
        run_copies(piece_results(pieces, scalars, summed, results, sems))


def project_back(
    ring, scalars, turns, raw, factors, dots, gain_q, gain_k, tokens, in_factor, weights
):
    span, width = tokens.shape
    heads, head_dim = len(turns) // 3, turns[0].shape[1]
    part = heads * head_dim
    columns = weights[0].shape[1]
    chunk = min(256, span)
    n = len(ring.pieces)
    by_rows = lambda wide: pl.BlockSpec((chunk, wide), lambda i, s: (i, 0))
    out = pl.pallas_call(
        functools.partial(project_back_kernel, ring.pieces, len(weights), chunk, heads),
        grid_spec=pltpu.PrefetchScalarGridSpec(
            num_scalar_prefetch=1,
            grid=(span // chunk,),
            in_specs=[by_rows(head_dim)] * (3 * heads)
            + [by_rows(columns)]
            + [pl.BlockSpec((8, chunk), lambda i, s: (0, i))] * 2
            + [whole_block((1, part))] * 2
            + [by_rows(width), by_rows(1)]
            + [anywhere] * len(weights),
            out_specs=[by_rows(columns), whole_block((1, width))] + [anywhere] * n,
            scratch_shapes=[
                pltpu.VMEM((width, columns), jnp.bfloat16),
                pltpu.VMEM((span, width), jnp.bfloat16),
                pltpu.SemaphoreType.DMA((len(weights),)),
                pltpu.SemaphoreType.DMA((n,)),
            ],
        ),
        out_shape=[
            jax.ShapeDtypeStruct((span, columns), jnp.bfloat16),
            jax.ShapeDtypeStruct((1, width), jnp.float32),
        ]
        + piece_shapes(ring.pieces, width),
        name="project_back",
    )(
        scalars, *turns, raw, factors, dots, gain_q, gain_k, tokens, in_factor, *weights
    )
    return out[0], out[1], out[2:]


def expert_column(scalars, part, parts, wide):
    half = parts // 2
    relative = 2 * (part % half) + jnp.where(part < half, 1, 0)
    return pl.multiple_of((scalars[len(scalars) - 1] ^ relative) * wide, wide)


def weight_copies(groups, scalars, buffers, sems, step, parts):
    expert, part, place = step // parts, step % parts, step % 2
    wide = buffers.shape[3]
    columns = pl.ds(expert_column(scalars, part, parts, wide), wide)
    return [
        pltpu.make_async_copy(
            group.at[expert, :, columns], buffers.at[place, g], sems.at[place, g]
        )
        for g, group in enumerate(groups)
    ]


def stream(groups, scalars, buffers, sems, parts):
    step = pl.program_id(0)

    @pl.when(step == 0)
    def _():
        for copy in weight_copies(groups, scalars, buffers, sems, step, parts):
            copy.start()

    @pl.when(step + 1 < pl.num_programs(0))
    def _():
        for copy in weight_copies(groups, scalars, buffers, sems, step + 1, parts):
            copy.start()

    for copy in weight_copies(groups, scalars, buffers, sems, step, parts):
        copy.wait()
    return buffers.at[step % 2]


def expert_first_kernel(pieces, parts, chunk, scalars, *refs):
    n = len(pieces)
    blocks, down = refs[:n], refs[n]
    product, kept, rows_all, buffers, sems, w_sems, k_sem = refs[n + 1 :]
    step = pl.program_id(0)

    @pl.when(step == 0)
    def _():
        copies = piece_copies(pieces, scalars, blocks, rows_all, sems)
        for copy in copies:
            copy.start()

    weight = stream([down], scalars, buffers, w_sems, parts)

    @pl.when(step == 0)
    def _():
        for copy in piece_copies(pieces, scalars, blocks, rows_all, sems):
            copy.wait()
        pltpu.make_async_copy(rows_all, kept, k_sem).start()

    for begin in range(0, rows_all.shape[0], chunk):
        rows = pl.ds(begin, chunk)
        product[rows, :] = dot(rows_all[rows, :], weight[0])

    @pl.when(step == pl.num_programs(0) - 1)
    def _():
        pltpu.make_async_copy(rows_all, kept, k_sem).wait()


def expert_first(ring, scalars, blocks, down):
    experts, width, hidden = down.shape
    parts = hidden_parts
    step_hidden = hidden // parts
    span = ring.rows * ring.size
    n = len(ring.pieces)
    return pl.pallas_call(
        functools.partial(expert_first_kernel, ring.pieces, parts, min(256, span)),
        grid_spec=pltpu.PrefetchScalarGridSpec(
            num_scalar_prefetch=1,
            grid=(experts * parts,),
            in_specs=[anywhere] * (n + 1),
            out_specs=[
                pl.BlockSpec((None, span, step_hidden), lambda i, s: (i // parts, 0, i % parts)),
                anywhere,
            ],
            scratch_shapes=[
                pltpu.VMEM((span, width), jnp.bfloat16),
                pltpu.VMEM((2, 1, width, step_hidden), jnp.bfloat16),
                pltpu.SemaphoreType.DMA((n,)),
                pltpu.SemaphoreType.DMA((2, 1)),
                pltpu.SemaphoreType.DMA,
            ],
        ),
        out_shape=[
            jax.ShapeDtypeStruct((experts, span, parts * step_hidden), jnp.float32),
            jax.ShapeDtypeStruct((span, width), jnp.bfloat16),
        ],
        name="expert_first",
    )(scalars, *blocks, down)


def expert_hidden_kernel(pieces, parts, chunk, scalars, *refs):
    n = len(pieces)
    blocks, gate, up = refs[:n], refs[n], refs[n + 1]
    product, gates = refs[n + 2 : n + 4]
    act, gated, d_gate, d_up, grad_gates, kept = refs[n + 4 : n + 10]
    rows_all, buffers, sems, w_sems, k_sem = refs[n + 10 :]
    step = pl.program_id(0)

    @pl.when(step == 0)
    def _():
        copies = piece_copies(pieces, scalars, blocks, rows_all, sems)
        for copy in copies:
            copy.start()

    weight = stream([gate, up], scalars, buffers, w_sems, parts)

    @pl.when(step == 0)
    def _():
        for copy in piece_copies(pieces, scalars, blocks, rows_all, sems):
            copy.wait()
        pltpu.make_async_copy(rows_all, kept, k_sem).start()

    @pl.when(step % parts == 0)
    def _():
        grad_gates[...] = jnp.zeros_like(grad_gates)

    for begin in range(0, rows_all.shape[0], chunk):
        rows = pl.ds(begin, chunk)
        gate_hid = dot(rows_all[rows, :], weight[0])
        up_hid = dot(rows_all[rows, :], weight[1])
        own_gate = gates[rows, :]
        back = product[rows, :]
        sig = 1.0 / (1.0 + jnp.exp(-gate_hid))
        silu = gate_hid * sig
        act_low = (silu * up_hid).astype(jnp.bfloat16)
        act_now = act_low.astype(jnp.float32)
        act[rows, :] = act_low
        gated[rows, :] = (own_gate * act_now).astype(jnp.bfloat16)
        grad_gates[rows, :] += jnp.sum(act_now * back, axis=-1, keepdims=True)
        grad_act = own_gate * back
        d_gate[rows, :] = (grad_act * up_hid * (sig * (1.0 + gate_hid * (1.0 - sig)))).astype(
            jnp.bfloat16
        )
        d_up[rows, :] = (grad_act * silu).astype(jnp.bfloat16)

    @pl.when(step == pl.num_programs(0) - 1)
    def _():
        pltpu.make_async_copy(rows_all, kept, k_sem).wait()


def hidden_place(parts, experts):
    half = parts // 2
    return lambda i: ((i % parts) // half * experts + i // parts) * half + (i % parts) % half


def expert_hidden(ring, scalars, blocks, gate, up, product, gates):
    experts, width, hidden_units = gate.shape
    parts = hidden_parts
    step_hidden = hidden_units // parts
    span = ring.rows * ring.size
    n = len(ring.pieces)
    place = hidden_place(parts, experts)
    relative = pl.BlockSpec((None, span, step_hidden), lambda i, s: (i // parts, 0, i % parts))
    placed = pl.BlockSpec((span, step_hidden), lambda i, s: (0, place(i)))
    column = pl.BlockSpec((None, span, 1), lambda i, s: (i // parts, 0, 0))
    hidden = jax.ShapeDtypeStruct((span, experts * parts * step_hidden), jnp.bfloat16)
    return pl.pallas_call(
        functools.partial(expert_hidden_kernel, ring.pieces, parts, min(256, span)),
        grid_spec=pltpu.PrefetchScalarGridSpec(
            num_scalar_prefetch=1,
            grid=(experts * parts,),
            in_specs=[anywhere] * (n + 2) + [relative, column],
            out_specs=[placed] * 4 + [column, anywhere],
            scratch_shapes=[
                pltpu.VMEM((span, width), jnp.bfloat16),
                pltpu.VMEM((2, 2, width, step_hidden), jnp.bfloat16),
                pltpu.SemaphoreType.DMA((n,)),
                pltpu.SemaphoreType.DMA((2, 2)),
                pltpu.SemaphoreType.DMA,
            ],
        ),
        out_shape=[
            hidden,
            hidden,
            hidden,
            hidden,
            jax.ShapeDtypeStruct((experts, span, 1), jnp.float32),
            jax.ShapeDtypeStruct((span, width), jnp.bfloat16),
        ],
        name="expert_hidden",
    )(scalars, *blocks, gate, up, product, gates)


def pack_weights(scalars, weights, packed, parts):
    experts, _, hidden = weights.shape
    wide = hidden // parts
    place = hidden_place(parts, experts)
    for expert in range(experts):
        for part in range(parts):
            column = place(expert * parts + part) * wide
            relative = 2 * (part % (parts // 2)) + (1 if part < parts // 2 else 0)
            source = pl.multiple_of((scalars[len(scalars) - 1] ^ relative) * wide, wide)
            packed[:, column : column + wide] = weights[expert, :, pl.ds(source, wide)]


def store_pieces(pieces, scalars, source, results):
    rows = pieces[0][2]
    for (slot, first, count), result in zip(pieces, results):
        begin = pl.multiple_of(scalars[slot] * rows + first, count)
        result[...] = source[pl.ds(begin, count), :]


def expert_inputs_kernel(pieces, parts, scalars, *refs):
    d_gate, d_up = refs[:2]
    gate, up = refs[2:4]
    n = len(pieces)
    results = refs[4 : 4 + n]
    packed, summed = refs[4 + n :]
    pack_weights(scalars, gate, packed.at[0], parts)
    pack_weights(scalars, up, packed.at[1], parts)
    total = dot(d_gate[...], packed[0], columns_last) + dot(d_up[...], packed[1], columns_last)
    summed[...] = total.astype(jnp.bfloat16)
    store_pieces(pieces, scalars, summed, results)


def expert_inputs(ring, scalars, d_gate, d_up, gate, up):
    experts, width, hidden_units = gate.shape
    parts = hidden_parts
    span, hidden = d_gate.shape
    wide = min(256, width)
    whole = pl.BlockSpec((span, hidden), lambda i, s: (0, 0), pipeline_mode=pl.Buffered(1))
    weight = pl.BlockSpec((experts, wide, hidden_units), lambda i, s: (0, i, 0))
    return pl.pallas_call(
        functools.partial(expert_inputs_kernel, ring.pieces, parts),
        grid_spec=pltpu.PrefetchScalarGridSpec(
            num_scalar_prefetch=1,
            grid=(width // wide,),
            in_specs=[whole] * 2 + [weight] * 2,
            out_specs=[
                pl.BlockSpec((count, wide), lambda i, s: (0, i)) for _, _, count in ring.pieces
            ],
            scratch_shapes=[
                pltpu.VMEM((2, wide, hidden), jnp.bfloat16),
                pltpu.VMEM((span, wide), jnp.bfloat16),
            ],
        ),
        out_shape=piece_shapes(ring.pieces, width),
        name="expert_inputs",
    )(scalars, d_gate, d_up, gate, up)


def expert_outputs_kernel(pieces, parts, scalars, *refs):
    act, gates = refs[:2]
    down = refs[2]
    n = len(pieces)
    results = refs[3 : 3 + n]
    packed, summed = refs[3 + n :]
    experts, _, hidden_units = down.shape
    pack_weights(scalars, down, packed, parts)
    half = hidden_units // 2
    total = None
    for expert in range(experts):
        first = pl.ds(expert * half, half)
        second = pl.ds((experts + expert) * half, half)
        out = dot(act[:, first], packed[:, first], columns_last)
        out = out + dot(act[:, second], packed[:, second], columns_last)
        out = gates[expert] * out.astype(jnp.bfloat16).astype(jnp.float32)
        total = out if total is None else total + out
    summed[...] = total.astype(jnp.bfloat16)
    store_pieces(pieces, scalars, summed, results)


def expert_outputs(ring, scalars, act, gates, down):
    experts, width, hidden_units = down.shape
    parts = hidden_parts
    span, hidden = act.shape
    wide = min(256, width)
    whole = pl.BlockSpec((span, hidden), lambda i, s: (0, 0), pipeline_mode=pl.Buffered(1))
    return pl.pallas_call(
        functools.partial(expert_outputs_kernel, ring.pieces, parts),
        grid_spec=pltpu.PrefetchScalarGridSpec(
            num_scalar_prefetch=1,
            grid=(width // wide,),
            in_specs=[whole, whole_block((experts, span, 1))]
            + [pl.BlockSpec((experts, wide, hidden_units), lambda i, s: (0, i, 0))],
            out_specs=[
                pl.BlockSpec((count, wide), lambda i, s: (0, i)) for _, _, count in ring.pieces
            ],
            scratch_shapes=[
                pltpu.VMEM((wide, hidden), jnp.bfloat16),
                pltpu.VMEM((span, wide), jnp.bfloat16),
            ],
        ),
        out_shape=piece_shapes(ring.pieces, width),
        name="expert_outputs",
    )(scalars, act, gates, down)


def weight_far_kernel(left, right, result):
    result[...] = dot(left[...], right[...], rows_first).astype(jnp.bfloat16)


def weight_far(left, right):
    span, width = left.shape
    split = right.shape[1] // 2
    wide = min(256, width)
    return pl.pallas_call(
        weight_far_kernel,
        grid=(width // wide,),
        in_specs=[
            pl.BlockSpec((span, wide), lambda i: (0, i)),
            pl.BlockSpec((span, split), lambda i: (0, 0), pipeline_mode=pl.Buffered(1)),
        ],
        out_specs=pl.BlockSpec((wide, split), lambda i: (i, 0)),
        out_shape=jax.ShapeDtypeStruct((width, split), jnp.bfloat16),
        name="weight_far",
    )(left, right)


def weight_near_kernel(scalars, left, right, arrived, result):
    total = dot(left[...], right[...], rows_first) + arrived[...].astype(jnp.float32)
    experts, step_hidden = result.shape[0] // 2, result.shape[2]
    own = scalars[len(scalars) - 1] // 2
    for expert in range(experts):
        for other in range(2):
            column = (2 * expert + other) * step_hidden
            result[(own ^ other) * experts + expert] = total[
                :, column : column + step_hidden
            ].astype(jnp.bfloat16)


def weight_near(scalars, left, right, arrived, experts):
    span, width = left.shape
    split = right.shape[1] // 2
    step_hidden = split // (2 * experts)
    wide = min(256, width)
    return pl.pallas_call(
        weight_near_kernel,
        grid_spec=pltpu.PrefetchScalarGridSpec(
            num_scalar_prefetch=1,
            grid=(width // wide,),
            in_specs=[
                pl.BlockSpec((span, wide), lambda i, s: (0, i)),
                pl.BlockSpec((span, split), lambda i, s: (0, 1), pipeline_mode=pl.Buffered(1)),
                pl.BlockSpec((wide, split), lambda i, s: (i, 0)),
            ],
            out_specs=pl.BlockSpec((2 * experts, wide, step_hidden), lambda i, s: (0, i, 0)),
        ),
        out_shape=jax.ShapeDtypeStruct((2 * experts, width, step_hidden), jnp.bfloat16),
        name="weight_near",
    )(scalars, left, right, arrived)


def weight_rows_kernel(scalars, left, right, result):
    result[...] = dot(left[...], right[...], rows_first).astype(jnp.bfloat16)


def weight_rows(scalars, left, right, parts):
    span, width = left.shape
    columns = right.shape[1]
    count = width // parts
    own = scalars.shape[0] - 1
    relative = lambda i: 2 * (i % 2) + jnp.where(i < 2, 1, 0)
    return pl.pallas_call(
        weight_rows_kernel,
        grid_spec=pltpu.PrefetchScalarGridSpec(
            num_scalar_prefetch=1,
            grid=(parts,),
            in_specs=[
                pl.BlockSpec((span, count), lambda i, s: (0, s[own] ^ relative(i))),
                whole_block((span, columns)),
            ],
            out_specs=pl.BlockSpec((None, count, columns), lambda i, s: (i, 0, 0)),
        ),
        out_shape=jax.ShapeDtypeStruct((parts, count, columns), jnp.bfloat16),
        name="weight_rows",
    )(scalars, left, right)


def per_device(
    tokens,
    cotangent,
    routes,
    w_query,
    w_key,
    w_value,
    w_output,
    w_router,
    gain_attn,
    gain_query,
    gain_key,
    gain_ffn,
    expert_gate,
    expert_up,
    expert_down,
):
    rows, width = tokens.shape
    size = lax.axis_size("fsdp")
    dp_size = lax.axis_size("x") * lax.axis_size("core")
    head_dim = width // HEADS
    own_heads = HEADS // size
    part = own_heads * head_dim
    own_rows = w_query.shape[0]
    local_experts = expert_gate.shape[0]
    num_experts = local_experts * size
    group = part // own_rows
    span = rows * size
    f_index = lax.axis_index("fsdp")
    d_index = lax.axis_index(dp_axes)
    low, f32 = jnp.bfloat16, jnp.float32
    ring = Ring(size, rows)
    half = ring.half
    scalars = jnp.concatenate([ring.slot_device, d_index[None].astype(jnp.int32)])
    dp_flat = (*dp_axes, "fsdp")
    to_rows = []
    for flat in range(dp_size * size):
        to_rows.append((flat, (flat % group) * size + flat // group))
    from_rows = [(b, a) for a, b in to_rows]

    packed = jnp.concatenate(
        [w.reshape(own_rows, size, part) for w in (w_query, w_key, w_value)], axis=2
    ).transpose(1, 0, 2)
    packed = lax.all_to_all(packed, "fsdp", split_axis=0, concat_axis=0, tiled=True)
    packed = packed.reshape(size * own_rows, 3 * part)

    small = jnp.concatenate(
        [w_router.T, gain_attn[None], gain_query[None], gain_key[None], gain_ffn[None]], axis=0
    )
    small = pair_gather(small, dp_axes, dp_size)

    token_ring, small_ring = ring.gather(tokens), ring.gather(small, False)
    token_steps, small_steps = [token_ring.step()], [small_ring.step()]
    out_rows = lax.ppermute(after(w_output, token_steps[0]), dp_flat, to_rows)
    for k in range(1, half):
        ties = {1: packed, half - 1: (token_steps[-1], out_rows)}.get(k, token_steps[-1])
        small_steps.append(small_ring.step(ties))
        token_steps.append(token_ring.step((ties, small_steps[k - 1])))
    token_blocks = token_ring.blocks()
    w_in = share_relative(packed, dp_size, None, token_steps[2])
    small = small_ring.stacked().transpose(2, 1, 0, 3).reshape(-1, width)
    router = small[:num_experts]
    gains = small[num_experts:].astype(f32)
    gain_in, gain_q, gain_k, gain_mid = (gains[i][None, :] for i in range(4))
    gain_q = lax.dynamic_slice_in_dim(gain_q, f_index * part, part, 1)
    gain_k = lax.dynamic_slice_in_dim(gain_k, f_index * part, part, 1)
    half_dim = head_dim // 2
    inv_freq = rope_base ** (-(jnp.arange(half_dim, dtype=f32) * 2.0) / head_dim)
    angles = jnp.arange(span, dtype=jnp.int32).astype(f32)[:, None] * inv_freq[None, :]
    cosine, sine = jnp.cos(angles), jnp.sin(angles)
    cosine = jnp.concatenate([cosine, cosine], axis=1)
    sine = jnp.concatenate([-sine, sine], axis=1)
    w_out = share_relative(out_rows, dp_size, token_steps[2], token_steps[3])

    down_w = lax.all_gather(expert_down, dp_axes, axis=2, tiled=True)
    gate_w = lax.all_gather(expert_gate, dp_axes, axis=2, tiled=True)
    up_w = lax.all_gather(expert_up, dp_axes, axis=2, tiled=True)

    cot_ring = ring.gather(cotangent)
    cot_step = cot_ring.step(token_steps[3])
    normed, raw, in_factor, squares, x_all = project(
        ring, scalars, token_blocks, w_in, gain_in
    )
    squares = pair_sum(after(squares, (cot_step, w_out)), "fsdp", size)
    cot_step = cot_ring.step(squares)
    factors = lax.rsqrt(squares / width + epsilon)
    saved, attn_pieces = attend(
        ring, scalars, raw, factors, gain_q, gain_k, cosine, sine, w_out, head_dim
    )
    attn_ring = ring.reduce(after(attn_pieces, cot_step))
    attn_ring.step()
    cot_step = cot_ring.step(attn_pieces[0])
    attn_step = attn_ring.step(cot_step)
    cot_step = cot_ring.step(attn_step)
    attn_ring.step(cot_step)
    attn_ring.step()
    resid_mid = tokens.astype(f32) + attn_ring.total()

    mid_factor = lax.rsqrt(jnp.mean(resid_mid * resid_mid, axis=-1, keepdims=True) + epsilon)
    mid_low = (resid_mid * mid_factor * gain_mid).astype(low)
    mid_ring = ring.gather(mid_low)
    mid_steps = [mid_ring.step()]
    logits = dot(mid_low, router, columns_last)
    chosen_mask = jnp.any(
        routes[:, :, None] == jnp.arange(num_experts, dtype=jnp.int32)[None, None, :], axis=1
    )
    router_probs = jax.nn.softmax(logits, axis=-1)
    chosen = jnp.where(chosen_mask, router_probs, 0.0)
    chosen_sum = jnp.sum(chosen, axis=-1, keepdims=True)
    gates = chosen / chosen_sum
    gate_ring = ring.gather(gates.T, False)
    gate_steps = [gate_ring.step(mid_steps[0])]
    mid_steps.append(mid_ring.step())
    back_act, cot_all = expert_first(
        ring, after(scalars, mid_steps[0]), cot_ring.blocks(), down_w
    )
    gate_steps.append(gate_ring.step((mid_steps[1], back_act)))
    mid_steps.append(mid_ring.step((back_act, gate_steps[0])))
    gate_steps.append(gate_ring.step(mid_steps[2]))
    mid_steps.append(mid_ring.step(gate_steps[1]))
    gate_steps.append(gate_ring.step(mid_steps[2]))
    mid_blocks = mid_ring.blocks()
    gates_all = gate_ring.stacked()
    own_gates = lax.dynamic_slice_in_dim(gates_all, f_index * local_experts, local_experts, 1)
    own_gates = own_gates.transpose(1, 0, 2).reshape(local_experts, span)[:, :, None]
    act, act_gated, d_gate, d_up, grad_gates, mid_all = expert_hidden(
        ring, scalars, mid_blocks, gate_w, up_w, back_act, own_gates
    )
    grad_in = expert_inputs(ring, scalars, d_gate, d_up, gate_w, up_w)

    def far_part(left, right, ties):
        return weight_far(after(left, ties), right)

    def near_part(left, right, far, ties):
        far = lax.ppermute(after(far, ties), dp_axes, exchange_pairs(dp_size, 1))
        return weight_near(scalars, after(left, ties), right, far, local_experts)

    def finish(near):
        return lax.psum_scatter(near, "x", scatter_dimension=0, tiled=True).astype(f32)

    by_device = grad_gates.reshape(local_experts, size, rows)
    grad_ring, route_ring = ring.reduce(grad_in), ring.gather(by_device, False)
    route_steps = [route_ring.step(grad_in)]
    grad_steps = [grad_ring.step()]
    gate_far = far_part(mid_all, d_gate, grad_in)
    route_steps.append(route_ring.step(grad_steps[0]))
    grad_steps.append(grad_ring.step((gate_far, route_steps[0])))
    up_far = far_part(mid_all, d_up, grad_steps[0])
    route_steps.append(route_ring.step(grad_steps[1]))
    grad_steps.append(grad_ring.step((up_far, route_steps[1])))
    gate_near = near_part(mid_all, d_gate, gate_far, grad_steps[1])
    route_steps.append(route_ring.step(grad_steps[2]))
    grad_steps.append(grad_ring.step((gate_near, route_steps[2])))
    up_near = near_part(mid_all, d_up, up_far, grad_steps[2])
    grad_mid = after(grad_ring.total(), up_near)

    gates_back = route_ring.stacked()
    gates_back = lax.dynamic_slice_in_dim(gates_back, f_index, 1, 2)
    gates_back = gates_back.reshape(num_experts, rows).T
    inner = jnp.sum(jnp.where(chosen_mask, gates_back * gates, 0.0), axis=-1, keepdims=True)
    grad_probs = jnp.where(chosen_mask, (gates_back - inner) / chosen_sum, 0.0)
    grad_logits = router_probs * (
        grad_probs - jnp.sum(router_probs * grad_probs, axis=-1, keepdims=True)
    )
    grad_logits_low = grad_logits.astype(low)
    grad_router = dot(grad_logits_low, mid_low, rows_first)
    grad_mid = grad_mid + dot(grad_logits_low, router)
    grad_out = cotangent.astype(f32)
    scaled = grad_mid * gain_mid
    grad_resid = (
        grad_out
        + mid_factor * scaled
        - resid_mid * mid_factor**3 * jnp.mean(scaled * resid_mid, axis=-1, keepdims=True)
    )
    grad_gain_mid = jnp.sum(grad_mid * resid_mid * mid_factor, axis=0)
    grad_low = grad_resid.astype(low)

    back_ring = ring.gather(grad_low)
    back_steps = [back_ring.step()]
    down_far = far_part(cot_all, act_gated, grad_low)
    back_steps.append(back_ring.step(down_far))
    moe_pieces = expert_outputs(ring, after(scalars, back_steps[0]), act, own_gates, down_w)
    back_steps.append(back_ring.step(moe_pieces[0]))
    down_near = near_part(cot_all, act_gated, down_far, back_steps[1])
    back_steps.append(back_ring.step(down_near))
    grad_blocks = back_ring.blocks()

    def head_back(head, ties):
        return attend_back(
            ring, after(scalars, ties), saved, raw, factors, gain_q, gain_k, cosine, sine, w_out,
            grad_blocks, head_dim, head,
        )

    moe_ring = ring.reduce(after(moe_pieces, back_steps[3]))
    moe_step = moe_ring.step()
    backs = [head_back(0, back_steps[3])]
    for head in range(1, own_heads):
        if moe_ring.left > 2:
            moe_step = moe_ring.step(backs[-1])
        backs.append(head_back(head, backs[-1][0]))
    grad_attn_out = backs[0][6]
    dots = after(sum(back[3] for back in backs), moe_step)
    grad_gain_q = jnp.concatenate([back[4] for back in backs], axis=1)
    grad_gain_k = jnp.concatenate([back[5] for back in backs], axis=1)
    grad_w_out = dot(saved[3].astype(low), after(grad_attn_out, dots), rows_first)
    dots = pair_sum(dots, "fsdp", size) / width
    grad_w_out = jnp.concatenate(
        [
            lax.dynamic_slice_in_dim(grad_w_out, (d_index ^ k) * own_rows, own_rows, 0)[None]
            for k in (1, 3, 0, 2)
        ],
        axis=0,
    ).astype(low)
    while moe_ring.left > 1:
        moe_step = moe_ring.step(dots)
    grad_raw, grad_gain_in, normed_pieces = project_back(
        ring, scalars, [value for back in backs for value in back[:3]], raw, factors,
        after(dots, grad_w_out), gain_q, gain_k, x_all, in_factor, w_in,
    )
    grad_w_out = combine_relative(grad_w_out)[0].astype(low)
    grad_w_out = lax.ppermute(grad_w_out, dp_flat, from_rows).astype(f32)
    normed_pieces = after(normed_pieces, moe_step)
    moe_step = moe_ring.step(normed_pieces)
    layer_out = (resid_mid + moe_ring.total()).astype(low)

    in_ring = ring.reduce(normed_pieces)
    in_steps = [in_ring.step()]
    grad_w_in = weight_rows(scalars, after(normed, normed_pieces), grad_raw, dp_size)
    grad_gains = lax.dynamic_update_slice(
        jnp.zeros((2, width), f32),
        jnp.concatenate([grad_gain_q, grad_gain_k], axis=0),
        (0, f_index * part),
    )
    sums = jnp.concatenate([grad_router, grad_gain_mid[None], grad_gain_in, grad_gains], axis=0)
    sums = pair_scatter(after(sums, normed_pieces), dp_axes, dp_size)
    in_steps.append(in_ring.step((grad_w_in, moe_step)))
    grad_w_in = combine_relative(grad_w_in, (in_steps[0], in_steps[0]))[0].astype(low)
    sums = pair_scatter(sums, "fsdp", size, {4: in_steps[0], 2: in_steps[1]})
    in_steps.append(in_ring.step())
    in_steps.append(in_ring.step(grad_w_in))
    grad_normed = in_ring.total()
    grad_gate_w, grad_up_w, grad_down_w = (
        finish(near) for near in (gate_near, up_near, down_near)
    )
    grad_w_in = grad_w_in.reshape(size, own_rows, 3 * part)
    grad_w_in = lax.all_to_all(grad_w_in, "fsdp", split_axis=0, concat_axis=0, tiled=True)
    grad_w_in = [
        grad_w_in[:, :, i * part : (i + 1) * part].transpose(1, 0, 2).reshape(own_rows, width)
        for i in range(3)
    ]
    grad_w_in = [values.astype(f32) for values in grad_w_in]
    own_x = tokens.astype(f32)
    own_factor = lax.rsqrt(jnp.mean(own_x * own_x, axis=-1, keepdims=True) + epsilon)
    scaled_in = grad_normed * gain_in
    grad_tokens = (
        grad_resid
        + own_factor * scaled_in
        - own_x * own_factor**3 * jnp.mean(scaled_in * own_x, axis=-1, keepdims=True)
    )
    return (
        layer_out,
        grad_tokens,
        grad_w_in[0],
        grad_w_in[1],
        grad_w_in[2],
        grad_w_out,
        sums[:num_experts].T,
        sums[num_experts + 1],
        sums[num_experts + 2],
        sums[num_experts + 3],
        sums[num_experts],
        grad_gate_w,
        grad_up_w,
        grad_down_w,
    )


def splits_evenly(mesh):
    size, dp_size = mesh.shape["fsdp"], mesh.shape["dp"]
    powers = size & (size - 1) == 0 and dp_size & (dp_size - 1) == 0
    return powers and dp_size == 4 and size == 8 and HEADS % size == 0


def solution(mesh):
    split = splits_evenly(mesh)
    dp = "dp"
    if split:
        devices = mesh.devices.reshape(2, 2, mesh.shape["fsdp"])
        mesh, dp = jax.sharding.Mesh(devices, (*dp_axes, "fsdp")), dp_axes
    flat = (*dp_axes, "fsdp") if split else ("dp", "fsdp")
    in_specs = (
        P(flat, None),
        P(flat, None),
        P(flat, None),
        P(flat, None),
        P(flat, None),
        P(flat, None),
        P(flat, None),
        P(flat, None),
        P(flat),
        P(flat),
        P(flat),
        P(flat),
        P("fsdp", None, dp),
        P("fsdp", None, dp),
        P("fsdp", None, dp),
    )
    out_specs = (
        P(flat, None),
        P(flat, None),
        P(flat, None),
        P(flat, None),
        P(flat, None),
        P(flat, None),
        P(flat, None),
        P(flat),
        P(flat),
        P(flat),
        P(flat),
        P("fsdp", None, dp),
        P("fsdp", None, dp),
        P("fsdp", None, dp),
    )
    return jax.shard_map(
        per_device if split else per_device_gathered,
        mesh=mesh,
        in_specs=in_specs,
        out_specs=out_specs,
        check_vma=False,
    )
```

```python
import functools

import jax
import jax.numpy as jnp
from jax import lax
from jax.experimental import pallas as pl
from jax.experimental.pallas import tpu as pltpu
from jax.sharding import PartitionSpec as P

HEADS = 16
TOPK = 8


epsilon = 1e-05
rope_base = 10000.0
hidden_parts = 4
rest_column = 128
gate_columns = 64
sum_columns = 128
dp_axes = ("x", "core")
far_low = -1e30


def rms_norm(values, scaling):
    factor = lax.rsqrt(jnp.mean(values * values, axis=-1, keepdims=True) + epsilon)
    return values * factor * scaling


def rotary(values, positions):
    half_dim = values.shape[-1] // 2
    inv_freq = rope_base ** (-(jnp.arange(half_dim, dtype=jnp.float32) * 2.0) / values.shape[-1])
    angles = positions.astype(jnp.float32)[:, None] * inv_freq[None, :]
    cosine = jnp.cos(angles)[:, None, :]
    sine_vals = jnp.sin(angles)[:, None, :]
    first_half = values[..., :half_dim]
    second = values[..., half_dim:]
    return jnp.concatenate(
        [first_half * cosine - second * sine_vals, second * cosine + first_half * sine_vals],
        axis=-1,
    )


def head_prep(values, scaling, positions):
    normed = rms_norm(values, scaling)
    return rotary(normed.reshape(values.shape[0], HEADS, -1), positions)


def swiglu(gate_hid, up_hid):
    return jax.nn.silu(gate_hid) * up_hid


def gating(logits, routes, num_experts):
    prob_vals = jax.nn.softmax(logits, axis=-1)
    pick_table = (
        routes[:, :, None] == jnp.arange(num_experts, dtype=jnp.int32)[None, None, :]
    ).astype(jnp.float32)
    chosen = jnp.sum(pick_table * prob_vals[:, None, :], axis=-1)
    return chosen / jnp.sum(chosen, axis=-1, keepdims=True)


def per_device_gathered(
    tokens,
    cotangent,
    routes,
    w_query,
    w_key,
    w_value,
    w_output,
    w_router,
    gain_attn,
    gain_query,
    gain_key,
    gain_ffn,
    expert_gate,
    expert_up,
    expert_down,
):
    row_count = tokens.shape[0]
    model_width = tokens.shape[1]
    head_dim = model_width // HEADS
    score_scale = head_dim ** (-0.5)
    fsdp_size = lax.axis_size("fsdp")
    local_experts = expert_gate.shape[0]
    num_experts = local_experts * fsdp_size
    capacity = max(2, (row_count * TOPK * 5 + 4 * num_experts - 1) // (4 * num_experts))
    positions = lax.axis_index("fsdp") * row_count + jnp.arange(row_count, dtype=jnp.int32)
    first_pos = positions[0]
    last_pos = positions[row_count - 1]
    inputs = tokens.astype(jnp.float32)
    dense_full = (
        lax.all_gather(w_query, ("dp", "fsdp"), axis=0, tiled=True),
        lax.all_gather(w_key, ("dp", "fsdp"), axis=0, tiled=True),
        lax.all_gather(w_value, ("dp", "fsdp"), axis=0, tiled=True),
        lax.all_gather(w_output, ("dp", "fsdp"), axis=0, tiled=True),
        lax.all_gather(w_router, ("dp", "fsdp"), axis=0, tiled=True),
        lax.all_gather(gain_attn, ("dp", "fsdp"), axis=0, tiled=True),
        lax.all_gather(gain_query, ("dp", "fsdp"), axis=0, tiled=True),
        lax.all_gather(gain_key, ("dp", "fsdp"), axis=0, tiled=True),
        lax.all_gather(gain_ffn, ("dp", "fsdp"), axis=0, tiled=True),
    )
    expert_full = (
        lax.all_gather(expert_gate, "dp", axis=2, tiled=True),
        lax.all_gather(expert_up, "dp", axis=2, tiled=True),
        lax.all_gather(expert_down, "dp", axis=2, tiled=True),
    )
    query_full, key_full, value_full, output_full, router_full = dense_full[:5]
    gain_in_full = dense_full[5].astype(jnp.float32)
    gain_q_full = dense_full[6].astype(jnp.float32)
    gain_k_full = dense_full[7].astype(jnp.float32)
    gain_mid_full = dense_full[8].astype(jnp.float32)
    normed_low = rms_norm(inputs, gain_in_full).astype(jnp.bfloat16)
    query_raw = jnp.dot(normed_low, query_full, preferred_element_type=jnp.float32)
    key_raw = jnp.dot(normed_low, key_full, preferred_element_type=jnp.float32)
    value_raw = jnp.dot(normed_low, value_full, preferred_element_type=jnp.float32)
    query_low = head_prep(query_raw, gain_q_full, positions).astype(jnp.bfloat16)
    key_low = head_prep(key_raw, gain_k_full, positions).astype(jnp.bfloat16)
    value_low = value_raw.astype(jnp.bfloat16).reshape(row_count, HEADS, head_dim)
    start_state = (
        jnp.full((HEADS, row_count), far_low, jnp.float32),
        jnp.zeros((HEADS, row_count), jnp.float32),
        jnp.zeros((row_count, HEADS, head_dim), jnp.float32),
    )
    shard_piece = (
        lax.all_gather(key_low, "fsdp", axis=0, tiled=True),
        lax.all_gather(value_low, "fsdp", axis=0, tiled=True),
    )

    def attend_update(state):
        run_max, run_sum, run_acc = state
        key_piece, value_piece = shard_piece
        scores = (
            jnp.einsum("qhd,khd->hqk", query_low, key_piece, preferred_element_type=jnp.float32)
            * score_scale
        )
        key_pos = jnp.arange(key_piece.shape[0], dtype=jnp.int32)
        allowed = (key_pos[None, :] <= positions[:, None])[None]
        new_max = jnp.maximum(run_max, jnp.max(jnp.where(allowed, scores, far_low), axis=-1))
        exp_vals = jnp.where(allowed, jnp.exp(scores - new_max[..., None]), 0.0)
        factor = jnp.exp(run_max - new_max)
        run_sum = jnp.sum(exp_vals, axis=-1)
        run_acc = run_acc * factor.T[:, :, None] + jnp.einsum(
            "hqk,khd->qhd",
            exp_vals.astype(jnp.bfloat16),
            value_piece,
            preferred_element_type=jnp.float32,
        )
        return (new_max, run_sum, run_acc)

    run_max, run_sum, run_acc = lax.cond(
        jnp.int32(0) <= last_pos, attend_update, lambda state: state, start_state
    )
    attn_f32 = run_acc / run_sum.T[:, :, None]
    log_sum = run_max + jnp.log(run_sum)
    attn_low = attn_f32.reshape(row_count, model_width).astype(jnp.bfloat16)
    resid_mid = inputs + jnp.dot(attn_low, output_full, preferred_element_type=jnp.float32)
    mid_low = rms_norm(resid_mid, gain_mid_full).astype(jnp.bfloat16)
    logits = jnp.dot(mid_low, router_full, preferred_element_type=jnp.float32)
    gate_vals, gate_pull = jax.vjp(
        lambda logit_vals: gating(logit_vals, routes, num_experts), logits
    )
    route_flat = routes.reshape(-1)
    pick_table = (route_flat[:, None] == jnp.arange(num_experts, dtype=jnp.int32)[None, :]).astype(
        jnp.int32
    )
    slot_index = jnp.sum(pick_table * (jnp.cumsum(pick_table, axis=0) - 1), axis=1)
    target = route_flat * capacity + slot_index
    spread = jnp.repeat(mid_low, TOPK, axis=0)
    send_rows = (
        jnp.zeros((num_experts * capacity, model_width), jnp.bfloat16).at[target].set(spread)
    )
    send_rows = send_rows.reshape(fsdp_size, local_experts, capacity, model_width)
    arrived = lax.all_to_all(send_rows, "fsdp", split_axis=0, concat_axis=0, tiled=True)
    gate_w, up_w, down_w = expert_full
    gate_hid = jnp.einsum("secd,edh->sech", arrived, gate_w, preferred_element_type=jnp.float32)
    up_hid = jnp.einsum("secd,edh->sech", arrived, up_w, preferred_element_type=jnp.float32)
    act_low = swiglu(gate_hid, up_hid).astype(jnp.bfloat16)
    expert_out = jnp.einsum(
        "sech,edh->secd", act_low, down_w, preferred_element_type=jnp.float32
    ).astype(jnp.bfloat16)
    returned = lax.all_to_all(expert_out, "fsdp", split_axis=0, concat_axis=0, tiled=True).reshape(
        num_experts * capacity, model_width
    )
    picked = returned[target].reshape(row_count, TOPK, model_width).astype(jnp.float32)
    resid_out = resid_mid + jnp.sum(gate_vals[:, :, None] * picked, axis=1)
    layer_out = resid_out.astype(jnp.bfloat16)
    back_dense = (
        lax.all_gather(w_query, ("dp", "fsdp"), axis=0, tiled=True),
        lax.all_gather(w_key, ("dp", "fsdp"), axis=0, tiled=True),
        lax.all_gather(w_value, ("dp", "fsdp"), axis=0, tiled=True),
        lax.all_gather(w_output, ("dp", "fsdp"), axis=0, tiled=True),
        lax.all_gather(w_router, ("dp", "fsdp"), axis=0, tiled=True),
        lax.all_gather(gain_attn, ("dp", "fsdp"), axis=0, tiled=True),
        lax.all_gather(gain_query, ("dp", "fsdp"), axis=0, tiled=True),
        lax.all_gather(gain_key, ("dp", "fsdp"), axis=0, tiled=True),
        lax.all_gather(gain_ffn, ("dp", "fsdp"), axis=0, tiled=True),
    )
    back_experts = (
        lax.all_gather(expert_gate, "dp", axis=2, tiled=True),
        lax.all_gather(expert_up, "dp", axis=2, tiled=True),
        lax.all_gather(expert_down, "dp", axis=2, tiled=True),
    )
    query_back, key_back, value_back, output_back, router_back = back_dense[:5]
    gain_in_back = back_dense[5].astype(jnp.float32)
    gain_q_back = back_dense[6].astype(jnp.float32)
    gain_k_back = back_dense[7].astype(jnp.float32)
    gain_mid_back = back_dense[8].astype(jnp.float32)
    gate_back, up_back, down_back = back_experts
    grad_out = cotangent.astype(jnp.float32)
    grad_gates = jnp.sum(grad_out[:, None, :] * picked, axis=-1)
    grad_routed = (
        (gate_vals[:, :, None] * grad_out[:, None, :]).astype(jnp.bfloat16).reshape(-1, model_width)
    )
    send_grads = (
        jnp.zeros((num_experts * capacity, model_width), jnp.bfloat16).at[target].set(grad_routed)
    )
    send_grads = send_grads.reshape(fsdp_size, local_experts, capacity, model_width)
    grad_arrived = lax.all_to_all(send_grads, "fsdp", split_axis=0, concat_axis=0, tiled=True)
    gate_again = jnp.einsum(
        "secd,edh->sech", arrived, gate_back, preferred_element_type=jnp.float32
    )
    up_again = jnp.einsum("secd,edh->sech", arrived, up_back, preferred_element_type=jnp.float32)
    act_vals, act_pull = jax.vjp(swiglu, gate_again, up_again)
    act_again = act_vals.astype(jnp.bfloat16)
    grad_act = jnp.einsum(
        "secd,edh->sech", grad_arrived, down_back, preferred_element_type=jnp.float32
    )
    grad_down = jnp.einsum(
        "secd,sech->edh", grad_arrived, act_again, preferred_element_type=jnp.float32
    )
    grad_gate_hid, grad_up_hid = act_pull(grad_act)
    grad_gate_low = grad_gate_hid.astype(jnp.bfloat16)
    grad_up_low = grad_up_hid.astype(jnp.bfloat16)
    grad_gate_w = jnp.einsum(
        "secd,sech->edh", arrived, grad_gate_low, preferred_element_type=jnp.float32
    )
    grad_up_w = jnp.einsum(
        "secd,sech->edh", arrived, grad_up_low, preferred_element_type=jnp.float32
    )
    grad_inputs = jnp.einsum(
        "sech,edh->secd", grad_gate_low, gate_back, preferred_element_type=jnp.float32
    ) + jnp.einsum("sech,edh->secd", grad_up_low, up_back, preferred_element_type=jnp.float32)
    grad_returned = lax.all_to_all(
        grad_inputs.astype(jnp.bfloat16), "fsdp", split_axis=0, concat_axis=0, tiled=True
    )
    grad_returned = grad_returned.reshape(num_experts * capacity, model_width)
    grad_mid = jnp.sum(
        grad_returned[target].reshape(row_count, TOPK, model_width).astype(jnp.float32), axis=1
    )
    expert_grads = (
        lax.psum_scatter(
            grad_gate_w.astype(jnp.bfloat16), "dp", scatter_dimension=2, tiled=True
        ).astype(jnp.float32),
        lax.psum_scatter(
            grad_up_w.astype(jnp.bfloat16), "dp", scatter_dimension=2, tiled=True
        ).astype(jnp.float32),
        lax.psum_scatter(
            grad_down.astype(jnp.bfloat16), "dp", scatter_dimension=2, tiled=True
        ).astype(jnp.float32),
    )
    (grad_logits,) = gate_pull(grad_gates)
    grad_logits_low = grad_logits.astype(jnp.bfloat16)
    grad_router = jnp.einsum(
        "td,te->de", mid_low, grad_logits_low, preferred_element_type=jnp.float32
    )
    grad_mid = grad_mid + jnp.einsum(
        "te,de->td", grad_logits_low, router_back, preferred_element_type=jnp.float32
    )
    mid_value, mid_pull = jax.vjp(rms_norm, resid_mid, gain_mid_back)
    grad_resid_part, grad_gain_mid = mid_pull(grad_mid)
    grad_resid = grad_out + grad_resid_part
    grad_attn_out = grad_resid.astype(jnp.bfloat16)
    grad_output_w = jnp.einsum(
        "td,te->de", attn_low, grad_attn_out, preferred_element_type=jnp.float32
    )
    grad_attn = jnp.einsum(
        "te,de->td", grad_attn_out, output_back, preferred_element_type=jnp.float32
    )
    grad_attn = grad_attn.astype(jnp.bfloat16).reshape(row_count, HEADS, head_dim)
    delta_rows = jnp.sum(grad_attn.astype(jnp.float32) * attn_f32, axis=-1).T
    key_all, value_all = (
        lax.all_gather(key_low, "fsdp", axis=0, tiled=True),
        lax.all_gather(value_low, "fsdp", axis=0, tiled=True),
    )

    def probs_block(key_block, value_block, begin_at):
        scores = (
            jnp.einsum("qhd,khd->hqk", query_low, key_block, preferred_element_type=jnp.float32)
            * score_scale
        )
        key_pos = begin_at + jnp.arange(key_block.shape[0], dtype=jnp.int32)
        allowed = (key_pos[None, :] <= positions[:, None])[None]
        prob_vals = jnp.where(allowed, jnp.exp(scores - log_sum[..., None]), 0.0)
        grad_probs = jnp.einsum(
            "qhd,khd->hqk", grad_attn, value_block, preferred_element_type=jnp.float32
        )
        grad_scores = (prob_vals * (grad_probs - delta_rows[..., None])).astype(jnp.bfloat16)
        return (prob_vals, grad_scores)

    block_rows = 8 * row_count
    block_needed = last_pos // block_rows + 1
    zero_query = jnp.zeros((row_count, HEADS, head_dim), jnp.float32)

    def query_step(block_index, accum):
        begin_at = block_index * block_rows
        key_block = lax.dynamic_slice_in_dim(key_all, begin_at, block_rows, 0)
        value_block = lax.dynamic_slice_in_dim(value_all, begin_at, block_rows, 0)
        prob_vals, grad_scores = probs_block(key_block, value_block, begin_at)
        return accum + jnp.einsum(
            "hqk,khd->qhd", grad_scores, key_block, preferred_element_type=jnp.float32
        )

    grad_query_rot = lax.fori_loop(0, block_needed, query_step, zero_query) * score_scale
    stats_all = (
        lax.all_gather(log_sum.T, "fsdp", axis=0, tiled=True),
        lax.all_gather(delta_rows.T, "fsdp", axis=0, tiled=True),
    )
    query_piece = lax.all_gather(query_low, "fsdp", axis=0, tiled=True)
    grad_piece = lax.all_gather(grad_attn, "fsdp", axis=0, tiled=True)
    span = query_piece.shape[0]

    def add_update(state):
        lse_piece = stats_all[0].T
        delta_piece = stats_all[1].T
        scores = (
            jnp.einsum("qhd,khd->hqk", query_piece, key_low, preferred_element_type=jnp.float32)
            * score_scale
        )
        query_pos = jnp.arange(span, dtype=jnp.int32)
        allowed = (positions[None, :] <= query_pos[:, None])[None]
        prob_vals = jnp.where(allowed, jnp.exp(scores - lse_piece[..., None]), 0.0)
        grad_probs = jnp.einsum(
            "qhd,khd->hqk", grad_piece, value_low, preferred_element_type=jnp.float32
        )
        grad_scores = (prob_vals * (grad_probs - delta_piece[..., None])).astype(jnp.bfloat16)
        grad_value_acc = jnp.einsum(
            "hqk,qhd->khd",
            prob_vals.astype(jnp.bfloat16),
            grad_piece,
            preferred_element_type=jnp.float32,
        )
        grad_key_acc = jnp.einsum(
            "hqk,qhd->khd", grad_scores, query_piece, preferred_element_type=jnp.float32
        )
        return (grad_key_acc, grad_value_acc)

    grad_key_sum, grad_value_sum = lax.cond(
        jnp.int32(0) + span > first_pos, add_update, lambda state: state, (zero_query, zero_query)
    )
    grad_key_rot = grad_key_sum * score_scale
    grad_value_low = grad_value_sum.reshape(row_count, model_width).astype(jnp.bfloat16)
    query_value, query_pull = jax.vjp(
        lambda raw_vals, scaling: head_prep(raw_vals, scaling, positions), query_raw, gain_q_back
    )
    grad_query_raw, grad_gain_query = query_pull(grad_query_rot)
    key_value, key_pull = jax.vjp(
        lambda raw_vals, scaling: head_prep(raw_vals, scaling, positions), key_raw, gain_k_back
    )
    grad_key_raw, grad_gain_key = key_pull(grad_key_rot)
    grad_query_low = grad_query_raw.astype(jnp.bfloat16)
    grad_key_low = grad_key_raw.astype(jnp.bfloat16)
    grad_wq = jnp.einsum(
        "td,te->de", normed_low, grad_query_low, preferred_element_type=jnp.float32
    )
    grad_wk = jnp.einsum("td,te->de", normed_low, grad_key_low, preferred_element_type=jnp.float32)
    grad_wv = jnp.einsum(
        "td,te->de", normed_low, grad_value_low, preferred_element_type=jnp.float32
    )
    grad_normed = (
        jnp.einsum("te,de->td", grad_query_low, query_back, preferred_element_type=jnp.float32)
        + jnp.einsum("te,de->td", grad_key_low, key_back, preferred_element_type=jnp.float32)
        + jnp.einsum("te,de->td", grad_value_low, value_back, preferred_element_type=jnp.float32)
    )
    in_value, input_pull = jax.vjp(rms_norm, inputs, gain_in_back)
    grad_input_part, grad_gain_in = input_pull(grad_normed)
    grad_tokens = grad_resid + grad_input_part
    dense_grads = (
        lax.psum_scatter(grad_wq, ("dp", "fsdp"), scatter_dimension=0, tiled=True),
        lax.psum_scatter(grad_wk, ("dp", "fsdp"), scatter_dimension=0, tiled=True),
        lax.psum_scatter(grad_wv, ("dp", "fsdp"), scatter_dimension=0, tiled=True),
        lax.psum_scatter(grad_output_w, ("dp", "fsdp"), scatter_dimension=0, tiled=True),
        lax.psum_scatter(grad_router, ("dp", "fsdp"), scatter_dimension=0, tiled=True),
        lax.psum_scatter(grad_gain_in, ("dp", "fsdp"), scatter_dimension=0, tiled=True),
        lax.psum_scatter(grad_gain_query, ("dp", "fsdp"), scatter_dimension=0, tiled=True),
        lax.psum_scatter(grad_gain_key, ("dp", "fsdp"), scatter_dimension=0, tiled=True),
        lax.psum_scatter(grad_gain_mid, ("dp", "fsdp"), scatter_dimension=0, tiled=True),
    )
    return (
        layer_out,
        grad_tokens,
        dense_grads[0],
        dense_grads[1],
        dense_grads[2],
        dense_grads[3],
        dense_grads[4],
        dense_grads[5],
        dense_grads[6],
        dense_grads[7],
        dense_grads[8],
        expert_grads[0],
        expert_grads[1],
        expert_grads[2],
    )


def after(values, ties):
    if callable(ties):
        ties = ties(values)
    if ties is None:
        return values
    return lax.optimization_barrier((values, ties))[0]


class Ring:
    def __init__(self, size, rows):
        self.size = size
        self.half = size // 2
        self.rows = rows
        middle = rows // 2
        self.pieces = [(k, 0, rows) for k in range(self.half)]
        self.pieces += [(self.half, 0, middle), (self.half, middle, middle)]
        self.pieces += [(k, 0, rows) for k in range(self.half + 1, size)]
        self.order = list(range(0, size, 2)) + list(range(size - 1, 0, -2))
        place = [self.order.index(i) for i in range(size)]
        rank = jnp.asarray(place, jnp.int32)[lax.axis_index("fsdp")]
        self.slot_device = jnp.asarray(self.order, jnp.int32)[
            (rank + jnp.arange(size, dtype=jnp.int32)) % size
        ]
        self.device_slot = (jnp.asarray(place, jnp.int32) - rank) % size
        self.up = [(self.order[i], self.order[(i + 1) % size]) for i in range(size)]
        self.down = [(self.order[i], self.order[i - 1]) for i in range(size)]

    def forward(self, values):
        return lax.ppermute(values, "fsdp", self.up)

    def backward(self, values):
        return lax.ppermute(values, "fsdp", self.down)

    def gather(self, block, halves=True):
        return Gather(self, block, halves)

    def reduce(self, pieces):
        return Reduce(self, pieces)


def add_pair_kernel(upper, rising, lower, falling, first, second):
    count, arrived = upper.shape[0], rising.shape[0]
    first[:arrived, :] = upper[:arrived, :] + rising[...]
    second[count - arrived :, :] = lower[count - arrived :, :] + falling[...]
    if arrived < count:
        first[arrived:, :] = upper[arrived:, :]
        second[: count - arrived, :] = lower[: count - arrived, :]


def add_pair(upper, rising, lower, falling):
    shape = jax.ShapeDtypeStruct(upper.shape, upper.dtype)
    return pl.pallas_call(add_pair_kernel, out_shape=[shape, shape], name="add_pair")(
        upper, rising, lower, falling
    )


class Gather:
    def __init__(self, ring, block, halves=True):
        self.ring, self.halves = ring, halves
        self.low, self.high, self.opposite = [block], [block], None

    def step(self, ties=None):
        ring, middle = self.ring, self.ring.rows // 2
        from_low, from_high = after((self.low[-1], self.high[-1]), ties)
        if len(self.low) < ring.half:
            self.low.append(ring.forward(from_low))
            self.high.append(ring.backward(from_high))
            return self.low[-1], self.high[-1]
        if self.halves:
            self.opposite = [ring.forward(from_low[:middle]), ring.backward(from_high[middle:])]
        else:
            self.opposite = [ring.forward(from_low)]
        return tuple(self.opposite)

    def stacked(self):
        return jnp.stack(self.blocks())[self.ring.device_slot]

    def blocks(self):
        return self.high + self.opposite + self.low[:0:-1]


class Reduce:
    def __init__(self, ring, pieces):
        self.ring, self.pieces, self.arrived, self.left = ring, pieces, None, ring.half

    def step(self, ties=None, early=None):
        ring, pieces = self.ring, self.pieces
        if self.arrived is None:
            upper, lower = pieces[ring.half], pieces[ring.half + 1]
        else:
            rising, falling = after(self.arrived, early)
            upper, lower = pieces[self.left], pieces[-self.left]
            upper, lower = add_pair(upper, rising, lower, falling)
        upper, lower = after((upper, lower), ties)
        self.arrived = (ring.forward(upper), ring.backward(lower))
        self.left -= 1
        return self.arrived

    def last(self):
        return self.pieces[0], *self.arrived

    def total(self, early=None):
        rising, falling = after(self.arrived, early)
        return (
            self.pieces[0].astype(jnp.float32)
            + rising.astype(jnp.float32)
            + falling.astype(jnp.float32)
        )


def exchange_pairs(size, bit):
    return [(i, i ^ bit) for i in range(size)]


def pair_sum(values, axis, size):
    bit = 1
    while bit < size:
        values = values + lax.ppermute(values, axis, exchange_pairs(size, bit))
        bit *= 2
    return values


def pair_gather(values, axis, size, ties=()):
    ties = dict(ties)
    mine = lax.axis_index(axis)
    values = values[None]
    bit = 1
    while bit < size:
        values = after(values, ties.get(bit))
        other = lax.ppermute(values, axis, exchange_pairs(size, bit))
        upper = (mine & bit) != 0
        values = jnp.where(
            upper,
            jnp.concatenate([other, values], axis=0),
            jnp.concatenate([values, other], axis=0),
        )
        bit *= 2
    return values


def share_relative(block, size, ties=(), second=()):
    block = after(block, ties)
    held = {0: block}
    bit = size // 2
    while bit >= 1:
        for index in list(held):
            sent = held[index] if index == 0 else after(held[index], second)
            held[index ^ bit] = lax.ppermute(sent, dp_axes, exchange_pairs(size, bit))
        bit //= 2
    return [held[index] for index in range(size)]


def combine_relative(far, near, ties=(None, None)):
    far = lax.ppermute(after(far, ties[0]), dp_axes, exchange_pairs(4, 1))
    other = near[1] + far[1].astype(jnp.float32)
    other = after(other.astype(jnp.bfloat16), ties[1])
    other = lax.ppermute(other, dp_axes, exchange_pairs(4, 2))
    return near[0] + far[0].astype(jnp.float32) + other.astype(jnp.float32)


anywhere = pl.BlockSpec(memory_space=pl.ANY)
rows_first = (((0,), (0,)), ((), ()))
columns_last = (((1,), (1,)), ((), ()))


def dot(left, right, dims=(((1,), (0,)), ((), ()))):
    return lax.dot_general(left, right, dims, preferred_element_type=jnp.float32)


def row_sums(*columns):
    total = None
    for i, values in enumerate(columns):
        place = lax.broadcasted_iota(jnp.int32, (8, values.shape[1]), 0) == i
        sums = lax.dot_general(
            place.astype(jnp.float32),
            values,
            columns_last,
            precision=lax.Precision.HIGHEST,
            preferred_element_type=jnp.float32,
        )
        total = sums if total is None else total + sums
    return total


def as_columns(rows):
    return rows_as_columns(rows, 8)


def rows_as_columns(rows, columns):
    shape = (rows.shape[0], columns)
    same = lax.broadcasted_iota(jnp.int32, shape, 0) == lax.broadcasted_iota(jnp.int32, shape, 1)
    return lax.dot_general(
        rows,
        same.astype(jnp.float32),
        rows_first,
        precision=lax.Precision.HIGHEST,
        preferred_element_type=jnp.float32,
    )


def whole_block(shape):
    return pl.BlockSpec(shape, lambda *_: (0,) * len(shape))


def piece_copies(pieces, scalars, blocks, target, sems, first_column=0):
    rows = pieces[0][2]
    columns = pl.ds(first_column, target.shape[1])
    copies = []
    for i, (slot, first, count) in enumerate(pieces):
        begin = pl.multiple_of(scalars[slot] * rows + first, count)
        copies.append(
            pltpu.make_async_copy(
                blocks[i].at[:, columns], target.at[pl.ds(begin, count), :], sems.at[i]
            )
        )
    return copies


def piece_results(pieces, scalars, source, blocks, sems):
    rows = pieces[0][2]
    copies = []
    for i, (slot, first, count) in enumerate(pieces):
        begin = pl.multiple_of(scalars[slot] * rows + first, count)
        copies.append(
            pltpu.make_async_copy(source.at[pl.ds(begin, count), :], blocks[i], sems.at[i])
        )
    return copies


def row_copies(scalars, which, blocks, target, sems):
    own = scalars[which]
    count = blocks[0].shape[0]
    return [
        pltpu.make_async_copy(
            block, target.at[pl.ds(pl.multiple_of((own ^ i) * count, count), count), :], sems.at[i]
        )
        for i, block in enumerate(blocks)
    ]


def run_copies(copies):
    for copy in copies:
        copy.start()
    for copy in copies:
        copy.wait()


def piece_shapes(pieces, width):
    return [jax.ShapeDtypeStruct((count, width), jnp.bfloat16) for _, _, count in pieces]


def project_kernel(pieces, parts, chunk, scalars, *refs):
    n = len(pieces)
    blocks, weights, gain = refs[:n], refs[n : n + parts], refs[n + parts]
    normed, raw, factor, squares, kept, tokens, weight, sems, w_sems, k_sem = refs[n + parts + 1 :]
    step = pl.program_id(0)

    @pl.when(step == 0)
    def _():
        run_copies(
            piece_copies(pieces, scalars, blocks, tokens, sems)
            + row_copies(scalars, len(scalars) - 1, weights, weight, w_sems)
        )
        pltpu.make_async_copy(tokens, kept, k_sem).start()

    rows = pl.ds(pl.multiple_of(step * chunk, chunk), chunk)
    values = tokens[rows, :].astype(jnp.float32)
    scale = lax.rsqrt(jnp.mean(values * values, axis=-1, keepdims=True) + epsilon)
    low = (values * scale * gain[...]).astype(jnp.bfloat16)
    normed[...] = low
    factor[...] = scale
    product = dot(low, weight[...])
    raw[...] = product
    part = product.shape[1] // 3
    squares[...] = row_sums(product[:, :part] ** 2, product[:, part : 2 * part] ** 2)

    @pl.when(step == pl.num_programs(0) - 1)
    def _():
        pltpu.make_async_copy(tokens, kept, k_sem).wait()


def project(ring, scalars, blocks, weights, gain):
    width = blocks[0].shape[1]
    span = ring.rows * ring.size
    columns = weights[0].shape[1]
    chunk = min(256, span)
    n = len(ring.pieces)
    by_rows = lambda i, s: (i, 0)
    return pl.pallas_call(
        functools.partial(project_kernel, ring.pieces, len(weights), chunk),
        grid_spec=pltpu.PrefetchScalarGridSpec(
            num_scalar_prefetch=1,
            grid=(span // chunk,),
            in_specs=[anywhere] * (n + len(weights)) + [whole_block((1, width))],
            out_specs=[
                pl.BlockSpec((chunk, width), by_rows),
                pl.BlockSpec((chunk, columns), by_rows),
                pl.BlockSpec((chunk, 1), by_rows),
                pl.BlockSpec((8, chunk), lambda i, s: (0, i)),
                anywhere,
            ],
            scratch_shapes=[
                pltpu.VMEM((span, width), jnp.bfloat16),
                pltpu.VMEM((width, columns), jnp.bfloat16),
                pltpu.SemaphoreType.DMA((n,)),
                pltpu.SemaphoreType.DMA((len(weights),)),
                pltpu.SemaphoreType.DMA,
            ],
        ),
        out_shape=[
            jax.ShapeDtypeStruct((span, width), jnp.bfloat16),
            jax.ShapeDtypeStruct((span, columns), jnp.float32),
            jax.ShapeDtypeStruct((span, 1), jnp.float32),
            jax.ShapeDtypeStruct((8, span), jnp.float32),
            jax.ShapeDtypeStruct((span, width), jnp.bfloat16),
        ],
        name="project",
    )(scalars, *blocks, *weights, gain)


def turned(values, cosine, sine):
    return values * cosine + pltpu.roll(values, values.shape[-1] // 2, 1) * sine


def attend_kernel(pieces, parts, chunk, scale, scalars, *refs):
    q_raw, k_raw, v_raw, factors, gain_q, gain_k, cosine, sine = refs[:8]
    weights = refs[8 : 8 + parts]
    query, key, value, mixed, lse = refs[8 + parts : 13 + parts]
    n = len(pieces)
    results = refs[13 + parts : 13 + parts + n]
    weight, total, summed, w_sems, sems = refs[13 + parts + n :]
    head = pl.program_id(0)
    last = pl.num_programs(0) - 1
    tokens, head_dim = query.shape

    @pl.when(head == 0)
    def _():
        run_copies(row_copies(scalars, len(scalars) - 1, weights, weight, w_sems))

    columns = as_columns(factors[...])
    query[...] = turned(
        q_raw[...] * columns[:, 0:1] * gain_q[...], cosine[...], sine[...]
    ).astype(jnp.bfloat16)
    key[...] = turned(
        k_raw[...] * columns[:, 1:2] * gain_k[...], cosine[...], sine[...]
    ).astype(jnp.bfloat16)
    value[...] = v_raw[...].astype(jnp.bfloat16)
    own_rows = weight[pl.ds(pl.multiple_of(head * head_dim, head_dim), head_dim), :]
    for begin in range(0, tokens, chunk):
        rows, seen = pl.ds(begin, chunk), pl.ds(0, begin + chunk)
        scores = dot(query[rows, :], key[seen, :], columns_last) * scale
        shape = scores.shape
        allowed = lax.broadcasted_iota(jnp.int32, shape, 1) <= begin + lax.broadcasted_iota(
            jnp.int32, shape, 0
        )
        scores = jnp.where(allowed, scores, far_low)
        top = jnp.max(scores, axis=-1, keepdims=True)
        weights_now = jnp.exp(scores - top)
        sums = jnp.sum(weights_now, axis=-1, keepdims=True)
        out = dot(weights_now.astype(jnp.bfloat16), value[seen, :]) / sums
        mixed[rows, :] = out
        lse[rows, :] = top + jnp.log(sums)
        product = dot(out.astype(jnp.bfloat16), own_rows)

        @pl.when(head == 0)
        def _():
            total[rows, :] = product

        @pl.when(jnp.logical_and(head > 0, head < last))
        def _():
            total[rows, :] += product

        @pl.when(jnp.logical_and(head > 0, head == last))
        def _():
            summed[rows, :] = (total[rows, :] + product).astype(jnp.bfloat16)

        @pl.when(jnp.logical_and(head == 0, head == last))
        def _():
            summed[rows, :] = product.astype(jnp.bfloat16)

    @pl.when(head == last)
    def _():
        run_copies(piece_results(pieces, scalars, summed, results, sems))


def attend(ring, scalars, raw, factors, gain_q, gain_k, cosine, sine, weights, head_dim):
    tokens = raw.shape[0]
    part = raw.shape[1] // 3
    heads = part // head_dim
    width = weights[0].shape[1]
    n = len(ring.pieces)
    column = lambda first: pl.BlockSpec((tokens, head_dim), lambda h, s: (0, first + h))
    gain = pl.BlockSpec((1, head_dim), lambda h, s: (0, h))
    table = whole_block((tokens, head_dim))
    low = jax.ShapeDtypeStruct((tokens, part), jnp.bfloat16)
    out = pl.pallas_call(
        functools.partial(
            attend_kernel, ring.pieces, len(weights), min(256, tokens), head_dim ** (-0.5)
        ),
        grid_spec=pltpu.PrefetchScalarGridSpec(
            num_scalar_prefetch=1,
            grid=(heads,),
            in_specs=[column(0), column(heads), column(2 * heads), whole_block((8, tokens))]
            + [gain, gain, table, table]
            + [anywhere] * len(weights),
            out_specs=[column(0)] * 4
            + [pl.BlockSpec((None, tokens, 1), lambda h, s: (h, 0, 0))]
            + [anywhere] * n,
            scratch_shapes=[
                pltpu.VMEM((part, width), jnp.bfloat16),
                pltpu.VMEM((tokens, width), jnp.float32),
                pltpu.VMEM((tokens, width), jnp.bfloat16),
                pltpu.SemaphoreType.DMA((len(weights),)),
                pltpu.SemaphoreType.DMA((n,)),
            ],
        ),
        out_shape=[low, low, low, jax.ShapeDtypeStruct((tokens, part), jnp.float32)]
        + [jax.ShapeDtypeStruct((heads, tokens, 1), jnp.float32)]
        + piece_shapes(ring.pieces, width),
        name="attend",
    )(scalars, raw, raw, raw, factors, gain_q, gain_k, cosine, sine, *weights)
    return out[:5], out[5:]


def attend_back_kernel(pieces, parts, chunk, scale, head, scalars, *refs):
    query, key, value, mixed, lse, q_raw, k_raw, factors, gain_q, gain_k, cosine, sine = refs[:12]
    n = len(pieces)
    weights = refs[12 : 12 + parts]
    blocks = refs[12 + parts : 12 + parts + n]
    outs = refs[12 + parts + n :]
    turn_q, turn_k, d_value, dots, sum_q, sum_k = outs[:6]
    kept = outs[6] if head == 0 else None
    weight, grads, d_key, d_val, d_query, w_sems, sems, k_sem = outs[-8:]
    tokens, head_dim = query.shape
    run_copies(
        row_copies(scalars, len(scalars) - 1, weights, weight, w_sems)
        + piece_copies(pieces, scalars, blocks, grads, sems)
    )
    if kept is not None:
        pltpu.make_async_copy(grads, kept, k_sem).start()
    own_rows = weight[pl.ds(head * head_dim, head_dim), :]
    for begin in range(0, tokens, chunk):
        rows, seen = pl.ds(begin, chunk), pl.ds(0, begin + chunk)
        grad = dot(grads[rows, :], own_rows, columns_last).astype(jnp.bfloat16)
        queries = query[rows, :]
        scores = dot(queries, key[seen, :], columns_last) * scale
        shape = scores.shape
        allowed = lax.broadcasted_iota(jnp.int32, shape, 1) <= begin + lax.broadcasted_iota(
            jnp.int32, shape, 0
        )
        probs = jnp.where(allowed, jnp.exp(scores - lse[rows, :]), 0.0)
        delta = jnp.sum(grad.astype(jnp.float32) * mixed[rows, :], axis=-1, keepdims=True)
        grad_probs = dot(grad, value[seen, :], columns_last)
        grad_scores = (probs * (grad_probs - delta)).astype(jnp.bfloat16)
        d_query[rows, :] = dot(grad_scores, key[seen, :]) * scale
        part_key = dot(grad_scores, queries, rows_first) * scale
        part_value = dot(probs.astype(jnp.bfloat16), grad, rows_first)
        if begin > 0:
            before = pl.ds(0, begin)
            d_key[before, :] += part_key[:begin]
            d_val[before, :] += part_value[:begin]
        d_key[rows, :] = part_key[begin:]
        d_val[rows, :] = part_value[begin:]
    d_value[...] = d_val[...].astype(jnp.bfloat16)
    back_q = turned(d_query[...], cosine[...], -sine[...])
    back_k = turned(d_key[...], cosine[...], -sine[...])
    turn_q[...] = back_q
    turn_k[...] = back_k
    with_q, with_k = back_q * q_raw[...], back_k * k_raw[...]
    columns = as_columns(factors[...])
    sum_q[...] = jnp.sum(with_q * columns[:, 0:1], axis=0, keepdims=True)
    sum_k[...] = jnp.sum(with_k * columns[:, 1:2], axis=0, keepdims=True)
    dots[...] = row_sums(with_q * gain_q[...], with_k * gain_k[...])
    if kept is not None:
        pltpu.make_async_copy(grads, kept, k_sem).wait()


def attend_back(
    ring, scalars, saved, raw, factors, gain_q, gain_k, cosine, sine, weights, blocks, head_dim,
    head,
):
    query, key, value, mixed, lse = saved
    tokens, part = query.shape
    heads = part // head_dim
    width = weights[0].shape[1]
    n = len(ring.pieces)
    column = lambda first: pl.BlockSpec((tokens, head_dim), lambda i, s: (0, first + head))
    gain = pl.BlockSpec((1, head_dim), lambda i, s: (0, head))
    table = whole_block((tokens, head_dim))
    result = jax.ShapeDtypeStruct((tokens, head_dim), jnp.float32)
    sums = jax.ShapeDtypeStruct((1, head_dim), jnp.float32)
    kept = [anywhere] if head == 0 else []
    accumulate = pltpu.VMEM((tokens, head_dim), jnp.float32)
    return pl.pallas_call(
        functools.partial(
            attend_back_kernel, ring.pieces, len(weights), min(256, tokens), head_dim ** (-0.5),
            head,
        ),
        grid_spec=pltpu.PrefetchScalarGridSpec(
            num_scalar_prefetch=1,
            grid=(1,),
            in_specs=[column(0)] * 4
            + [pl.BlockSpec((None, tokens, 1), lambda i, s: (head, 0, 0))]
            + [column(0), column(heads), whole_block((8, tokens)), gain, gain, table, table]
            + [anywhere] * (len(weights) + n),
            out_specs=[table] * 3
            + [whole_block((8, tokens))]
            + [whole_block((1, head_dim))] * 2
            + kept,
            scratch_shapes=[
                pltpu.VMEM((part, width), jnp.bfloat16),
                pltpu.VMEM((tokens, width), jnp.bfloat16),
                accumulate,
                accumulate,
                accumulate,
                pltpu.SemaphoreType.DMA((len(weights),)),
                pltpu.SemaphoreType.DMA((n,)),
                pltpu.SemaphoreType.DMA,
            ],
        ),
        out_shape=[
            result,
            result,
            jax.ShapeDtypeStruct((tokens, head_dim), jnp.bfloat16),
            jax.ShapeDtypeStruct((8, tokens), jnp.float32),
            sums,
            sums,
        ]
        + [jax.ShapeDtypeStruct((tokens, width), jnp.bfloat16)] * len(kept),
        name="attend_back",
    )(
        scalars, query, key, value, mixed, lse, raw, raw, factors, gain_q, gain_k, cosine, sine,
        *weights, *blocks,
    )


def project_back_kernel(pieces, parts, chunk, heads, scalars, *refs):
    turns, refs = refs[: 3 * heads], refs[3 * heads :]
    raw, factors, dots, gain_q, gain_k, tokens, in_factor = refs[:7]
    n = len(pieces)
    weights = refs[7 : 7 + parts]
    grad_raw, sum_in = refs[7 + parts : 9 + parts]
    results = refs[9 + parts : 9 + parts + n]
    weight, summed, w_sems, sems = refs[9 + parts + n :]
    step = pl.program_id(0)
    head_dim = turns[0].shape[1]
    part = heads * head_dim

    @pl.when(step == 0)
    def _():
        run_copies(row_copies(scalars, len(scalars) - 1, weights, weight, w_sems))
        sum_in[...] = jnp.zeros_like(sum_in)

    factor_columns, dot_columns = as_columns(factors[...]), as_columns(dots[...])
    for i, gain in enumerate((gain_q, gain_k)):
        factor = factor_columns[:, i : i + 1]
        cubed = factor * factor * factor * dot_columns[:, i : i + 1]
        for head in range(heads):
            columns = pl.ds(i * part + head * head_dim, head_dim)
            turn = turns[3 * head + i][...] * gain[:, head * head_dim : (head + 1) * head_dim]
            grad_raw[:, columns] = (factor * turn - raw[:, columns] * cubed).astype(jnp.bfloat16)
    for head in range(heads):
        grad_raw[:, pl.ds(2 * part + head * head_dim, head_dim)] = turns[3 * head + 2][...]
    normed = dot(grad_raw[...], weight[...], columns_last)
    sum_in[...] += jnp.sum(
        normed * (tokens[...].astype(jnp.float32) * in_factor[...]), axis=0, keepdims=True
    )
    summed[pl.ds(pl.multiple_of(step * chunk, chunk), chunk), :] = normed.astype(jnp.bfloat16)

    @pl.when(step == pl.num_programs(0) - 1)
    def _():
        run_copies(piece_results(pieces, scalars, summed, results, sems))


def project_back(
    ring, scalars, turns, raw, factors, dots, gain_q, gain_k, tokens, in_factor, weights
):
    span, width = tokens.shape
    heads, head_dim = len(turns) // 3, turns[0].shape[1]
    part = heads * head_dim
    columns = weights[0].shape[1]
    chunk = min(256, span)
    n = len(ring.pieces)
    by_rows = lambda wide: pl.BlockSpec((chunk, wide), lambda i, s: (i, 0))
    out = pl.pallas_call(
        functools.partial(project_back_kernel, ring.pieces, len(weights), chunk, heads),
        grid_spec=pltpu.PrefetchScalarGridSpec(
            num_scalar_prefetch=1,
            grid=(span // chunk,),
            in_specs=[by_rows(head_dim)] * (3 * heads)
            + [by_rows(columns)]
            + [pl.BlockSpec((8, chunk), lambda i, s: (0, i))] * 2
            + [whole_block((1, part))] * 2
            + [by_rows(width), by_rows(1)]
            + [anywhere] * len(weights),
            out_specs=[by_rows(columns), whole_block((1, width))] + [anywhere] * n,
            scratch_shapes=[
                pltpu.VMEM((width, columns), jnp.bfloat16),
                pltpu.VMEM((span, width), jnp.bfloat16),
                pltpu.SemaphoreType.DMA((len(weights),)),
                pltpu.SemaphoreType.DMA((n,)),
            ],
        ),
        out_shape=[
            jax.ShapeDtypeStruct((span, columns), jnp.bfloat16),
            jax.ShapeDtypeStruct((1, width), jnp.float32),
        ]
        + piece_shapes(ring.pieces, width),
        name="project_back",
    )(
        scalars, *turns, raw, factors, dots, gain_q, gain_k, tokens, in_factor, *weights
    )
    return out[0], out[1], out[2:]


def expert_column(scalars, part, parts, wide):
    half = parts // 2
    relative = 2 * (part % half) + jnp.where(part < half, 1, 0)
    return pl.multiple_of((scalars[len(scalars) - 1] ^ relative) * wide, wide)


def weight_copies(groups, scalars, buffers, sems, step, parts):
    expert, part, place = step // parts, step % parts, step % 2
    wide = buffers.shape[3]
    columns = pl.ds(expert_column(scalars, part, parts, wide), wide)
    return [
        pltpu.make_async_copy(
            group.at[expert, :, columns], buffers.at[place, g], sems.at[place, g]
        )
        for g, group in enumerate(groups)
    ]


def stream(groups, scalars, buffers, sems, parts):
    step = pl.program_id(0)

    @pl.when(step == 0)
    def _():
        for copy in weight_copies(groups, scalars, buffers, sems, step, parts):
            copy.start()

    @pl.when(step + 1 < pl.num_programs(0))
    def _():
        for copy in weight_copies(groups, scalars, buffers, sems, step + 1, parts):
            copy.start()

    for copy in weight_copies(groups, scalars, buffers, sems, step, parts):
        copy.wait()
    return buffers.at[step % 2]


def middle_kernel(experts, tokens, first, rising, falling, gain, router, routes, *refs):
    resid, factor, block, gates, probs, mask, total = refs
    width = tokens.shape[1]
    values = tokens[...].astype(jnp.float32) + (
        first[...].astype(jnp.float32)
        + rising[...].astype(jnp.float32)
        + falling[...].astype(jnp.float32)
    )
    resid[...] = values
    scale = lax.rsqrt(jnp.mean(values * values, axis=-1, keepdims=True) + epsilon)
    factor[...] = scale
    low = (values * scale * gain[...]).astype(jnp.bfloat16)
    block[:, :width] = low
    logits = dot(low, router[...], columns_last)
    column = lax.broadcasted_iota(jnp.int32, logits.shape, 1)
    real = column < experts
    top = jnp.max(jnp.where(real, logits, far_low), axis=-1, keepdims=True)
    weights = jnp.where(real, jnp.exp(logits - top), 0.0)
    prob_vals = weights / jnp.sum(weights, axis=-1, keepdims=True)
    chosen_mask = jnp.zeros(logits.shape, jnp.float32)
    for j in range(routes.shape[1]):
        chosen_mask = jnp.where(column == routes[:, j : j + 1], 1.0, chosen_mask)
    chosen = chosen_mask * prob_vals
    chosen_sum = jnp.sum(chosen, axis=-1, keepdims=True)
    gate_vals = chosen / chosen_sum
    gates[...], probs[...], mask[...], total[...] = gate_vals, prob_vals, chosen_mask, chosen_sum
    high = gate_vals.astype(jnp.bfloat16).astype(jnp.float32)
    rest = pltpu.roll(gate_vals - high, gate_columns, 1)
    block[:, width:] = (high + rest).astype(jnp.bfloat16)


def middle(tokens, sums, gain, router, routes, experts):
    rows, width = tokens.shape
    lanes = 2 * gate_columns
    table = jax.ShapeDtypeStruct((rows, lanes), jnp.float32)
    column = jax.ShapeDtypeStruct((rows, 1), jnp.float32)
    return pl.pallas_call(
        functools.partial(middle_kernel, experts),
        out_shape=[
            jax.ShapeDtypeStruct((rows, width), jnp.float32),
            column,
            jax.ShapeDtypeStruct((rows, width + lanes), jnp.bfloat16),
            table,
            table,
            table,
            column,
        ],
        name="middle",
    )(tokens, *sums, gain, router, routes)


def middle_back_kernel(first, rising, falling, cotangent, resid, factor, block, *refs):
    gates, probs, mask, total, gain, router = refs[:6]
    grad_resid, grad_low, sum_gain, grad_router = refs[6:]
    width = resid.shape[1]
    summed = (
        first[...].astype(jnp.float32)
        + rising[...].astype(jnp.float32)
        + falling[...].astype(jnp.float32)
    )
    lanes = 2 * gate_columns
    gates_back = summed[:, width : width + lanes]
    gates_back = gates_back + summed[:, width + rest_column : width + rest_column + lanes]
    inner = jnp.sum(gates_back * gates[...], axis=-1, keepdims=True)
    grad_probs = mask[...] * ((gates_back - inner) / total[...])
    grad_logits = probs[...] * (
        grad_probs - jnp.sum(probs[...] * grad_probs, axis=-1, keepdims=True)
    )
    logits_low = grad_logits.astype(jnp.bfloat16)
    grad_router[...] = dot(logits_low, block[:, :width], rows_first)
    grad_mid = summed[:, :width] + dot(logits_low, router[...])
    scale, values = factor[...], resid[...]
    scaled = grad_mid * gain[...]
    sum_gain[...] = jnp.sum(grad_mid * values * scale, axis=0, keepdims=True)
    mean = jnp.mean(scaled * values, axis=-1, keepdims=True)
    result = (
        cotangent[...].astype(jnp.float32)
        + scale * scaled
        - values * (scale * scale * scale * mean)
    )
    grad_resid[...] = result
    grad_low[...] = result.astype(jnp.bfloat16)


def middle_back(sums, cotangent, resid, factor, block, gates, probs, mask, total, gain, router):
    rows, width = resid.shape
    return pl.pallas_call(
        middle_back_kernel,
        out_shape=[
            jax.ShapeDtypeStruct((rows, width), jnp.float32),
            jax.ShapeDtypeStruct((rows, width), jnp.bfloat16),
            jax.ShapeDtypeStruct((1, width), jnp.float32),
            jax.ShapeDtypeStruct((2 * gate_columns, width), jnp.float32),
        ],
        name="middle_back",
    )(*sums, cotangent, resid, factor, block, gates, probs, mask, total, gain, router)


def expert_first_kernel(pieces, parts, chunk, scalars, *refs):
    n = len(pieces)
    blocks, down = refs[:n], refs[n]
    product, kept, rows_all, buffers, sems, w_sems, k_sem = refs[n + 1 :]
    step = pl.program_id(0)

    @pl.when(step == 0)
    def _():
        copies = piece_copies(pieces, scalars, blocks, rows_all, sems)
        for copy in copies:
            copy.start()

    weight = stream([down], scalars, buffers, w_sems, parts)

    @pl.when(step == 0)
    def _():
        for copy in piece_copies(pieces, scalars, blocks, rows_all, sems):
            copy.wait()
        pltpu.make_async_copy(rows_all, kept, k_sem).start()

    for begin in range(0, rows_all.shape[0], chunk):
        rows = pl.ds(begin, chunk)
        product[rows, :] = dot(rows_all[rows, :], weight[0])

    @pl.when(step == pl.num_programs(0) - 1)
    def _():
        pltpu.make_async_copy(rows_all, kept, k_sem).wait()


def expert_first(ring, scalars, blocks, down):
    experts, width, hidden = down.shape
    parts = hidden_parts
    step_hidden = hidden // parts
    span = ring.rows * ring.size
    n = len(ring.pieces)
    return pl.pallas_call(
        functools.partial(expert_first_kernel, ring.pieces, parts, min(256, span)),
        grid_spec=pltpu.PrefetchScalarGridSpec(
            num_scalar_prefetch=1,
            grid=(experts * parts,),
            in_specs=[anywhere] * (n + 1),
            out_specs=[
                pl.BlockSpec((None, span, step_hidden), lambda i, s: (i // parts, 0, i % parts)),
                anywhere,
            ],
            scratch_shapes=[
                pltpu.VMEM((span, width), jnp.bfloat16),
                pltpu.VMEM((2, 1, width, step_hidden), jnp.bfloat16),
                pltpu.SemaphoreType.DMA((n,)),
                pltpu.SemaphoreType.DMA((2, 1)),
                pltpu.SemaphoreType.DMA,
            ],
        ),
        out_shape=[
            jax.ShapeDtypeStruct((experts, span, parts * step_hidden), jnp.float32),
            jax.ShapeDtypeStruct((span, width), jnp.bfloat16),
        ],
        name="expert_first",
    )(scalars, *blocks, down)


def expert_hidden_kernel(pieces, parts, chunk, scalars, *refs):
    n = len(pieces)
    blocks, gate, up = refs[:n], refs[n], refs[n + 1]
    product = refs[n + 2]
    act, gated, d_gate, d_up, grad_gates, gates, kept = refs[n + 3 : n + 10]
    rows_all, gates_all, buffers, sems, g_sems, w_sems, k_sem = refs[n + 10 :]
    step = pl.program_id(0)
    experts = gates.shape[0]
    g_copies = piece_copies(pieces, scalars, blocks, gates_all, g_sems, rows_all.shape[1])

    @pl.when(step == 0)
    def _():
        for copy in piece_copies(pieces, scalars, blocks, rows_all, sems) + g_copies:
            copy.start()

    weight = stream([gate, up], scalars, buffers, w_sems, parts)

    @pl.when(step == 0)
    def _():
        for copy in piece_copies(pieces, scalars, blocks, rows_all, sems) + g_copies:
            copy.wait()
        pltpu.make_async_copy(rows_all, kept, k_sem).start()
        values = gates_all[...].astype(jnp.float32)
        column = lax.broadcasted_iota(jnp.int32, values.shape, 1) % gate_columns
        for expert in range(experts):
            own = scalars[0] * experts + expert
            gates[expert] = jnp.sum(
                jnp.where(column == own, values, 0.0), axis=-1, keepdims=True
            )

    @pl.when(step % parts == 0)
    def _():
        grad_gates[...] = jnp.zeros_like(grad_gates)

    for begin in range(0, rows_all.shape[0], chunk):
        rows = pl.ds(begin, chunk)
        gate_hid = dot(rows_all[rows, :], weight[0])
        up_hid = dot(rows_all[rows, :], weight[1])
        own_gate = gates[step // parts, rows, :]
        back = product[rows, :]
        sig = 1.0 / (1.0 + jnp.exp(-gate_hid))
        silu = gate_hid * sig
        act_low = (silu * up_hid).astype(jnp.bfloat16)
        act_now = act_low.astype(jnp.float32)
        act[rows, :] = act_low
        gated[rows, :] = (own_gate * act_now).astype(jnp.bfloat16)
        grad_gates[rows, :] += jnp.sum(act_now * back, axis=-1, keepdims=True)
        grad_act = own_gate * back
        d_gate[rows, :] = (grad_act * up_hid * (sig * (1.0 + gate_hid * (1.0 - sig)))).astype(
            jnp.bfloat16
        )
        d_up[rows, :] = (grad_act * silu).astype(jnp.bfloat16)

    @pl.when(step == pl.num_programs(0) - 1)
    def _():
        pltpu.make_async_copy(rows_all, kept, k_sem).wait()


def hidden_place(parts, experts):
    half = parts // 2
    return lambda i: ((i % parts) // half * experts + i // parts) * half + (i % parts) % half


def expert_hidden(ring, scalars, blocks, gate, up, product):
    experts, width, hidden_units = gate.shape
    parts = hidden_parts
    step_hidden = hidden_units // parts
    span = ring.rows * ring.size
    n = len(ring.pieces)
    place = hidden_place(parts, experts)
    relative = pl.BlockSpec((None, span, step_hidden), lambda i, s: (i // parts, 0, i % parts))
    placed = pl.BlockSpec((span, step_hidden), lambda i, s: (0, place(i)))
    column = pl.BlockSpec((None, span, 1), lambda i, s: (i // parts, 0, 0))
    hidden = jax.ShapeDtypeStruct((span, experts * parts * step_hidden), jnp.bfloat16)
    return pl.pallas_call(
        functools.partial(expert_hidden_kernel, ring.pieces, parts, min(256, span)),
        grid_spec=pltpu.PrefetchScalarGridSpec(
            num_scalar_prefetch=1,
            grid=(experts * parts,),
            in_specs=[anywhere] * (n + 2) + [relative],
            out_specs=[placed] * 4 + [column, whole_block((experts, span, 1)), anywhere],
            scratch_shapes=[
                pltpu.VMEM((span, width), jnp.bfloat16),
                pltpu.VMEM((span, 2 * gate_columns), jnp.bfloat16),
                pltpu.VMEM((2, 2, width, step_hidden), jnp.bfloat16),
                pltpu.SemaphoreType.DMA((n,)),
                pltpu.SemaphoreType.DMA((n,)),
                pltpu.SemaphoreType.DMA((2, 2)),
                pltpu.SemaphoreType.DMA,
            ],
        ),
        out_shape=[
            hidden,
            hidden,
            hidden,
            hidden,
            jax.ShapeDtypeStruct((experts, span, 1), jnp.float32),
            jax.ShapeDtypeStruct((experts, span, 1), jnp.float32),
            jax.ShapeDtypeStruct((span, width), jnp.bfloat16),
        ],
        name="expert_hidden",
    )(scalars, *blocks, gate, up, product)


def pack_weights(scalars, weights, packed, parts):
    experts, _, hidden = weights.shape
    wide = hidden // parts
    place = hidden_place(parts, experts)
    for expert in range(experts):
        for part in range(parts):
            column = place(expert * parts + part) * wide
            relative = 2 * (part % (parts // 2)) + (1 if part < parts // 2 else 0)
            source = pl.multiple_of((scalars[len(scalars) - 1] ^ relative) * wide, wide)
            packed[:, column : column + wide] = weights[expert, :, pl.ds(source, wide)]


def store_pieces(pieces, scalars, source, results):
    rows = pieces[0][2]
    for (slot, first, count), result in zip(pieces, results):
        begin = pl.multiple_of(scalars[slot] * rows + first, count)
        result[...] = source[pl.ds(begin, count), :]


def expert_inputs_kernel(pieces, parts, scalars, *refs):
    d_gate, d_up, gate, up, grad_gates = refs[:5]
    n = len(pieces)
    results = refs[5 : 5 + n]
    packed, summed = refs[5 + n :]
    step = pl.program_id(0)
    last = pl.num_programs(0) - 1

    @pl.when(step < last)
    def _():
        pack_weights(scalars, gate, packed.at[0], parts)
        pack_weights(scalars, up, packed.at[1], parts)
        total = dot(d_gate[...], packed[0], columns_last) + dot(d_up[...], packed[1], columns_last)
        summed[...] = total.astype(jnp.bfloat16)

    @pl.when(step == last)
    def _():
        experts = grad_gates.shape[0]
        column = lax.broadcasted_iota(jnp.int32, summed.shape, 1)
        placed = jnp.zeros(summed.shape, jnp.float32)
        for expert in range(experts):
            value = grad_gates[expert]
            high = value.astype(jnp.bfloat16).astype(jnp.float32)
            own = scalars[0] * experts + expert
            placed = jnp.where(column == own, high, placed)
            placed = jnp.where(column == own + rest_column, value - high, placed)
        summed[...] = placed.astype(jnp.bfloat16)

    store_pieces(pieces, scalars, summed, results)


def expert_inputs(ring, scalars, d_gate, d_up, gate, up, grad_gates):
    experts, width, hidden_units = gate.shape
    parts = hidden_parts
    span, hidden = d_gate.shape
    wide = min(256, width)
    steps = width // wide
    whole = pl.BlockSpec((span, hidden), lambda i, s: (0, 0), pipeline_mode=pl.Buffered(1))
    weight = pl.BlockSpec(
        (experts, wide, hidden_units), lambda i, s: (0, jnp.minimum(i, steps - 1), 0)
    )
    return pl.pallas_call(
        functools.partial(expert_inputs_kernel, ring.pieces, parts),
        grid_spec=pltpu.PrefetchScalarGridSpec(
            num_scalar_prefetch=1,
            grid=(steps + 1,),
            in_specs=[whole] * 2 + [weight] * 2 + [whole_block((experts, span, 1))],
            out_specs=[
                pl.BlockSpec((count, wide), lambda i, s: (0, i)) for _, _, count in ring.pieces
            ],
            scratch_shapes=[
                pltpu.VMEM((2, wide, hidden), jnp.bfloat16),
                pltpu.VMEM((span, wide), jnp.bfloat16),
            ],
        ),
        out_shape=piece_shapes(ring.pieces, width + wide),
        name="expert_inputs",
    )(scalars, d_gate, d_up, gate, up, grad_gates)


def expert_outputs_kernel(pieces, parts, scalars, *refs):
    act, gates = refs[:2]
    down = refs[2]
    n = len(pieces)
    results = refs[3 : 3 + n]
    packed, summed = refs[3 + n :]
    experts, _, hidden_units = down.shape
    pack_weights(scalars, down, packed, parts)
    half = hidden_units // 2
    total = None
    for expert in range(experts):
        first = pl.ds(expert * half, half)
        second = pl.ds((experts + expert) * half, half)
        out = dot(act[:, first], packed[:, first], columns_last)
        out = out + dot(act[:, second], packed[:, second], columns_last)
        out = gates[expert] * out.astype(jnp.bfloat16).astype(jnp.float32)
        total = out if total is None else total + out
    summed[...] = total.astype(jnp.bfloat16)
    store_pieces(pieces, scalars, summed, results)


def expert_outputs(ring, scalars, act, gates, down):
    experts, width, hidden_units = down.shape
    parts = hidden_parts
    span, hidden = act.shape
    wide = min(256, width)
    whole = pl.BlockSpec((span, hidden), lambda i, s: (0, 0), pipeline_mode=pl.Buffered(1))
    return pl.pallas_call(
        functools.partial(expert_outputs_kernel, ring.pieces, parts),
        grid_spec=pltpu.PrefetchScalarGridSpec(
            num_scalar_prefetch=1,
            grid=(width // wide,),
            in_specs=[whole, whole_block((experts, span, 1))]
            + [pl.BlockSpec((experts, wide, hidden_units), lambda i, s: (0, i, 0))],
            out_specs=[
                pl.BlockSpec((count, wide), lambda i, s: (0, i)) for _, _, count in ring.pieces
            ],
            scratch_shapes=[
                pltpu.VMEM((wide, hidden), jnp.bfloat16),
                pltpu.VMEM((span, wide), jnp.bfloat16),
            ],
        ),
        out_shape=piece_shapes(ring.pieces, width),
        name="expert_outputs",
    )(scalars, act, gates, down)


def weight_far_kernel(left, right, result):
    result[...] = dot(left[...], right[...], rows_first).astype(jnp.bfloat16)


def weight_far(left, right):
    span, width = left.shape
    split = right.shape[1] // 2
    wide = min(256, width)
    return pl.pallas_call(
        weight_far_kernel,
        grid=(width // wide,),
        in_specs=[
            pl.BlockSpec((span, wide), lambda i: (0, i)),
            pl.BlockSpec((span, split), lambda i: (0, 0), pipeline_mode=pl.Buffered(1)),
        ],
        out_specs=pl.BlockSpec((wide, split), lambda i: (i, 0)),
        out_shape=jax.ShapeDtypeStruct((width, split), jnp.bfloat16),
        name="weight_far",
    )(left, right)


def weight_near_kernel(scalars, left, right, arrived, result):
    total = dot(left[...], right[...], rows_first) + arrived[...].astype(jnp.float32)
    experts, step_hidden = result.shape[0] // 2, result.shape[2]
    own = scalars[len(scalars) - 1] // 2
    for expert in range(experts):
        for other in range(2):
            column = (2 * expert + other) * step_hidden
            result[(own ^ other) * experts + expert] = total[
                :, column : column + step_hidden
            ].astype(jnp.bfloat16)


def weight_near(scalars, left, right, arrived, experts):
    span, width = left.shape
    split = right.shape[1] // 2
    step_hidden = split // (2 * experts)
    wide = min(256, width)
    return pl.pallas_call(
        weight_near_kernel,
        grid_spec=pltpu.PrefetchScalarGridSpec(
            num_scalar_prefetch=1,
            grid=(width // wide,),
            in_specs=[
                pl.BlockSpec((span, wide), lambda i, s: (0, i)),
                pl.BlockSpec((span, split), lambda i, s: (0, 1), pipeline_mode=pl.Buffered(1)),
                pl.BlockSpec((wide, split), lambda i, s: (i, 0)),
            ],
            out_specs=pl.BlockSpec((2 * experts, wide, step_hidden), lambda i, s: (0, i, 0)),
        ),
        out_shape=jax.ShapeDtypeStruct((2 * experts, width, step_hidden), jnp.bfloat16),
        name="weight_near",
    )(scalars, left, right, arrived)


def weight_rows_kernel(scalars, left, right, sums, far, near):
    columns = right.shape[1]
    value = dot(left[...], right[...], rows_first)
    beside = rows_as_columns(sums[...], far.shape[1] - columns)
    half = pl.num_programs(0) // 2

    @pl.when(pl.program_id(0) < half)
    def _():
        far[:, :columns] = value.astype(jnp.bfloat16)
        far[:, columns:] = beside.astype(jnp.bfloat16)

    @pl.when(pl.program_id(0) >= half)
    def _():
        near[:, :columns] = value
        near[:, columns:] = beside


def weight_rows(scalars, left, right, sums, parts):
    span, width = left.shape
    columns = right.shape[1]
    count = width // parts
    half = parts // 2
    own = scalars.shape[0] - 1
    relative = lambda i: 2 * (i % half) + jnp.where(i < half, 1, 0)
    wide = columns + sum_columns
    return pl.pallas_call(
        weight_rows_kernel,
        grid_spec=pltpu.PrefetchScalarGridSpec(
            num_scalar_prefetch=1,
            grid=(parts,),
            in_specs=[
                pl.BlockSpec((span, count), lambda i, s: (0, s[own] ^ relative(i))),
                whole_block((span, columns)),
                pl.BlockSpec((sums.shape[0], count), lambda i, s: (0, s[own] ^ relative(i))),
            ],
            out_specs=[
                pl.BlockSpec((None, count, wide), lambda i, s: (jnp.minimum(i, half - 1), 0, 0)),
                pl.BlockSpec((None, count, wide), lambda i, s: (jnp.maximum(i - half, 0), 0, 0)),
            ],
        ),
        out_shape=[
            jax.ShapeDtypeStruct((half, count, wide), jnp.bfloat16),
            jax.ShapeDtypeStruct((half, count, wide), jnp.float32),
        ],
        name="weight_rows",
    )(scalars, left, right, sums)


def per_device(
    tokens,
    cotangent,
    routes,
    w_query,
    w_key,
    w_value,
    w_output,
    w_router,
    gain_attn,
    gain_query,
    gain_key,
    gain_ffn,
    expert_gate,
    expert_up,
    expert_down,
):
    rows, width = tokens.shape
    size = lax.axis_size("fsdp")
    dp_size = lax.axis_size("x") * lax.axis_size("core")
    head_dim = width // HEADS
    own_heads = HEADS // size
    part = own_heads * head_dim
    own_rows = w_query.shape[0]
    local_experts = expert_gate.shape[0]
    num_experts = local_experts * size
    group = part // own_rows
    span = rows * size
    f_index = lax.axis_index("fsdp")
    d_index = lax.axis_index(dp_axes)
    low, f32 = jnp.bfloat16, jnp.float32
    ring = Ring(size, rows)
    half = ring.half
    scalars = jnp.concatenate([ring.slot_device, d_index[None].astype(jnp.int32)])
    dp_flat = (*dp_axes, "fsdp")
    to_rows = []
    for flat in range(dp_size * size):
        to_rows.append((flat, (flat % group) * size + flat // group))
    from_rows = [(b, a) for a, b in to_rows]

    packed = jnp.concatenate(
        [w.reshape(own_rows, size, part) for w in (w_query, w_key, w_value)], axis=2
    ).transpose(1, 0, 2)
    packed = lax.all_to_all(packed, "fsdp", split_axis=0, concat_axis=0, tiled=True)
    packed = packed.reshape(size * own_rows, 3 * part)

    small = jnp.concatenate(
        [w_router.T, gain_attn[None], gain_query[None], gain_key[None], gain_ffn[None]], axis=0
    )
    small = pair_gather(small, dp_axes, dp_size)

    token_ring, small_ring = ring.gather(tokens), ring.gather(small, False)
    token_steps, small_steps = [token_ring.step()], [small_ring.step()]
    out_rows = lax.ppermute(after(w_output, token_steps[0]), dp_flat, to_rows)
    for k in range(1, half):
        ties = {1: packed, half - 1: (token_steps[-1], out_rows)}.get(k, token_steps[-1])
        small_steps.append(small_ring.step(ties))
        token_steps.append(token_ring.step(ties))
    token_blocks = token_ring.blocks()
    w_in = share_relative(packed, dp_size, None, token_steps[2])
    small = small_ring.stacked().transpose(2, 1, 0, 3).reshape(-1, width)
    router = jnp.pad(small[:num_experts], ((0, 2 * gate_columns - num_experts), (0, 0)))
    gains = small[num_experts:].astype(f32)
    gain_in, gain_q, gain_k, gain_mid = (gains[i][None, :] for i in range(4))
    gain_q = lax.dynamic_slice_in_dim(gain_q, f_index * part, part, 1)
    gain_k = lax.dynamic_slice_in_dim(gain_k, f_index * part, part, 1)
    half_dim = head_dim // 2
    inv_freq = rope_base ** (-(jnp.arange(half_dim, dtype=f32) * 2.0) / head_dim)
    angles = jnp.arange(span, dtype=jnp.int32).astype(f32)[:, None] * inv_freq[None, :]
    cosine, sine = jnp.cos(angles), jnp.sin(angles)
    cosine = jnp.concatenate([cosine, cosine], axis=1)
    sine = jnp.concatenate([-sine, sine], axis=1)
    w_out = share_relative(out_rows, dp_size, token_steps[2], token_steps[3])

    down_w = lax.all_gather(expert_down, dp_axes, axis=2, tiled=True)
    gate_w = lax.all_gather(expert_gate, dp_axes, axis=2, tiled=True)
    up_w = lax.all_gather(expert_up, dp_axes, axis=2, tiled=True)

    cot_ring = ring.gather(cotangent)
    cot_step = cot_ring.step(token_steps[3])
    normed, raw, in_factor, squares, x_all = project(
        ring, scalars, token_blocks, w_in, gain_in
    )
    squares = pair_sum(after(squares, (cot_step, w_out)), "fsdp", size)
    cot_step = cot_ring.step(squares)
    factors = lax.rsqrt(squares / width + epsilon)
    saved, attn_pieces = attend(
        ring, scalars, raw, factors, gain_q, gain_k, cosine, sine, w_out, head_dim
    )
    attn_ring = ring.reduce(after(attn_pieces, cot_step))
    attn_step = attn_ring.step()
    cot_step = cot_ring.step(attn_step)
    attn_ring.step()
    last_cot = cot_ring.step()
    attn_ring.step(cot_step)
    attn_ring.step(last_cot)
    resid_mid, mid_factor, mid_block, *routing = middle(
        tokens, attn_ring.last(), gain_mid, router, routes, num_experts
    )

    mid_ring = ring.gather(mid_block)
    mid_steps = [mid_ring.step()]
    mid_steps.append(mid_ring.step())
    back_act, cot_all = expert_first(
        ring, after(scalars, mid_steps[0]), cot_ring.blocks(), down_w
    )
    mid_ring.step(back_act)
    mid_ring.step()
    act, act_gated, d_gate, d_up, grad_gates, own_gates, mid_all = expert_hidden(
        ring, scalars, mid_ring.blocks(), gate_w, up_w, back_act
    )
    grad_in = expert_inputs(ring, scalars, d_gate, d_up, gate_w, up_w, grad_gates)

    def far_part(left, right, ties):
        return weight_far(after(left, ties), right)

    def cross(far, ties):
        return lax.ppermute(after(far, ties), dp_axes, exchange_pairs(dp_size, 1))

    def near_part(left, right, far, ties):
        return weight_near(scalars, after(left, ties), right, far, local_experts)

    def finish(near, ties):
        near = after(near, ties)
        return lax.psum_scatter(near, "x", scatter_dimension=0, tiled=True).astype(f32)

    grad_ring = ring.reduce(grad_in)
    grad_steps = [grad_ring.step()]
    gate_far = far_part(mid_all, d_gate, grad_in)
    grad_steps.append(grad_ring.step(gate_far))
    gate_cross = cross(gate_far, grad_steps[0])
    up_far = far_part(mid_all, d_up, grad_steps[0])
    grad_steps.append(grad_ring.step(up_far))
    up_cross = cross(up_far, grad_steps[1])
    down_far = far_part(cot_all, act_gated, grad_steps[1])
    grad_steps.append(grad_ring.step((down_far, gate_cross)))
    down_cross = cross(down_far, grad_steps[2])
    gate_near = near_part(mid_all, d_gate, gate_cross, grad_steps[2])
    grad_resid, grad_low, grad_gain_mid, grad_router = middle_back(
        after(grad_ring.last(), (gate_near, up_cross)), cotangent, resid_mid, mid_factor,
        mid_block, *routing, gain_mid, router,
    )

    back_ring = ring.gather(grad_low)
    back_steps = [back_ring.step()]
    up_near = near_part(mid_all, d_up, up_cross, grad_low)
    back_steps.append(back_ring.step((up_near, down_cross)))
    down_near = near_part(cot_all, act_gated, down_cross, back_steps[0])
    back_steps.append(back_ring.step(down_near))
    moe_pieces = expert_outputs(ring, after(scalars, back_steps[1]), act, own_gates, down_w)
    back_steps.append(back_ring.step(moe_pieces[0]))
    grad_blocks = back_ring.blocks()

    def head_back(head, ties):
        return attend_back(
            ring, after(scalars, ties), saved, raw, factors, gain_q, gain_k, cosine, sine, w_out,
            grad_blocks, head_dim, head,
        )

    moe_ring = ring.reduce(moe_pieces)
    moe_step = moe_ring.step()
    backs = [head_back(0, (back_steps[3], moe_step))]
    moe_step = moe_ring.step()
    for head in range(1, own_heads):
        backs.append(head_back(head, moe_step))
        if moe_ring.left > 1:
            moe_step = moe_ring.step(early=backs[head - 1][0])
    grad_attn_out = backs[0][6]
    dots = after(sum(back[3] for back in backs), moe_step)
    grad_gain_q = jnp.concatenate([back[4] for back in backs], axis=1)
    grad_gain_k = jnp.concatenate([back[5] for back in backs], axis=1)
    grad_w_out = dot(saved[3].astype(low), after(grad_attn_out, dots), rows_first)
    dots = pair_sum(dots, "fsdp", size) / width
    out_blocks = [
        lax.dynamic_slice_in_dim(grad_w_out, (d_index ^ k) * own_rows, own_rows, 0)
        for k in range(dp_size)
    ]
    out_far = jnp.stack([out_blocks[1], out_blocks[3]]).astype(low)
    while moe_ring.left > 0:
        moe_step = moe_ring.step(dots, backs[-1][0])
    layer_out = (resid_mid + moe_ring.total()).astype(low)
    grad_raw, grad_gain_in, normed_pieces = project_back(
        ring, scalars, [value for back in backs for value in back[:3]], raw, factors,
        after(dots, out_far), gain_q, gain_k, x_all, in_factor, w_in,
    )
    grad_w_out = combine_relative(out_far, [out_blocks[0], out_blocks[2]]).astype(low)
    normed_pieces = after(normed_pieces, (moe_step, grad_w_out))

    in_ring = ring.reduce(normed_pieces)
    in_steps = [in_ring.step()]
    grad_gains = lax.dynamic_update_slice(
        jnp.zeros((2, width), f32),
        jnp.concatenate([grad_gain_q, grad_gain_k], axis=0),
        (0, f_index * part),
    )
    sums = [grad_router[:num_experts], grad_gain_mid, grad_gain_in, grad_gains]
    sums.append(jnp.zeros((-(num_experts + 4) % 8, width), f32))
    grad_w_in = weight_rows(
        scalars, after(normed, normed_pieces), grad_raw, jnp.concatenate(sums, axis=0), dp_size
    )
    grad_gate_w = finish(gate_near, grad_low)
    grad_up_w = finish(up_near, back_steps[3])
    grad_down_w = finish(down_near, back_steps[3])
    in_steps.append(in_ring.step(early=grad_w_in))
    grad_w_in = combine_relative(*grad_w_in, (in_steps[0], in_steps[0])).astype(low)
    in_steps.append(in_ring.step(early=grad_gate_w))
    in_steps.append(in_ring.step(early=(grad_w_in, grad_up_w, grad_down_w)))
    grad_normed = in_ring.total()
    grad_w_in = after(grad_w_in, in_steps[2]).reshape(size, own_rows, -1)
    grad_w_in = lax.all_to_all(grad_w_in, "fsdp", split_axis=0, concat_axis=0, tiled=True)
    sums = jnp.sum(grad_w_in[:, :, 3 * part :].astype(f32), axis=0)
    grad_w_in = [
        grad_w_in[:, :, i * part : (i + 1) * part].transpose(1, 0, 2).reshape(own_rows, width)
        for i in range(3)
    ]
    grad_w_in = [values.astype(f32) for values in grad_w_in]
    grad_w_out = lax.ppermute(after(grad_w_out, in_steps[2]), dp_flat, from_rows).astype(f32)
    own_x = tokens.astype(f32)
    own_factor = lax.rsqrt(jnp.mean(own_x * own_x, axis=-1, keepdims=True) + epsilon)
    scaled_in = grad_normed * gain_in
    grad_tokens = (
        grad_resid
        + own_factor * scaled_in
        - own_x * own_factor**3 * jnp.mean(scaled_in * own_x, axis=-1, keepdims=True)
    )
    return (
        layer_out,
        grad_tokens,
        grad_w_in[0],
        grad_w_in[1],
        grad_w_in[2],
        grad_w_out,
        sums[:, :num_experts],
        sums[:, num_experts + 1],
        sums[:, num_experts + 2],
        sums[:, num_experts + 3],
        sums[:, num_experts],
        grad_gate_w,
        grad_up_w,
        grad_down_w,
    )


def splits_evenly(mesh):
    size, dp_size = mesh.shape["fsdp"], mesh.shape["dp"]
    powers = size & (size - 1) == 0 and dp_size & (dp_size - 1) == 0
    return powers and dp_size == 4 and size == 8 and HEADS % size == 0


def solution(mesh):
    split = splits_evenly(mesh)
    dp = "dp"
    if split:
        devices = mesh.devices.reshape(2, 2, mesh.shape["fsdp"])
        mesh, dp = jax.sharding.Mesh(devices, (*dp_axes, "fsdp")), dp_axes
    flat = (*dp_axes, "fsdp") if split else ("dp", "fsdp")
    in_specs = (
        P(flat, None),
        P(flat, None),
        P(flat, None),
        P(flat, None),
        P(flat, None),
        P(flat, None),
        P(flat, None),
        P(flat, None),
        P(flat),
        P(flat),
        P(flat),
        P(flat),
        P("fsdp", None, dp),
        P("fsdp", None, dp),
        P("fsdp", None, dp),
    )
    out_specs = (
        P(flat, None),
        P(flat, None),
        P(flat, None),
        P(flat, None),
        P(flat, None),
        P(flat, None),
        P(flat, None),
        P(flat),
        P(flat),
        P(flat),
        P(flat),
        P("fsdp", None, dp),
        P("fsdp", None, dp),
        P("fsdp", None, dp),
    )
    return jax.shard_map(
        per_device if split else per_device_gathered,
        mesh=mesh,
        in_specs=in_specs,
        out_specs=out_specs,
        check_vma=False,
    )
```

```python
import functools

import jax
import jax.numpy as jnp
from jax import lax
from jax.experimental import pallas as pl
from jax.experimental.pallas import tpu as pltpu
from jax.sharding import PartitionSpec as P

HEADS = 16
TOPK = 8


epsilon = 1e-05
rope_base = 10000.0
hidden_parts = 4
rest_column = 128
gate_columns = 64
sum_columns = 128
dp_axes = ("x", "core")
far_low = -1e30


def rms_norm(values, scaling):
    factor = lax.rsqrt(jnp.mean(values * values, axis=-1, keepdims=True) + epsilon)
    return values * factor * scaling


def rotary(values, positions):
    half_dim = values.shape[-1] // 2
    inv_freq = rope_base ** (-(jnp.arange(half_dim, dtype=jnp.float32) * 2.0) / values.shape[-1])
    angles = positions.astype(jnp.float32)[:, None] * inv_freq[None, :]
    cosine = jnp.cos(angles)[:, None, :]
    sine_vals = jnp.sin(angles)[:, None, :]
    first_half = values[..., :half_dim]
    second = values[..., half_dim:]
    return jnp.concatenate(
        [first_half * cosine - second * sine_vals, second * cosine + first_half * sine_vals],
        axis=-1,
    )


def head_prep(values, scaling, positions):
    normed = rms_norm(values, scaling)
    return rotary(normed.reshape(values.shape[0], HEADS, -1), positions)


def swiglu(gate_hid, up_hid):
    return jax.nn.silu(gate_hid) * up_hid


def gating(logits, routes, num_experts):
    prob_vals = jax.nn.softmax(logits, axis=-1)
    pick_table = (
        routes[:, :, None] == jnp.arange(num_experts, dtype=jnp.int32)[None, None, :]
    ).astype(jnp.float32)
    chosen = jnp.sum(pick_table * prob_vals[:, None, :], axis=-1)
    return chosen / jnp.sum(chosen, axis=-1, keepdims=True)


def per_device_gathered(
    tokens,
    cotangent,
    routes,
    w_query,
    w_key,
    w_value,
    w_output,
    w_router,
    gain_attn,
    gain_query,
    gain_key,
    gain_ffn,
    expert_gate,
    expert_up,
    expert_down,
):
    row_count = tokens.shape[0]
    model_width = tokens.shape[1]
    head_dim = model_width // HEADS
    score_scale = head_dim ** (-0.5)
    fsdp_size = lax.axis_size("fsdp")
    local_experts = expert_gate.shape[0]
    num_experts = local_experts * fsdp_size
    capacity = max(2, (row_count * TOPK * 5 + 4 * num_experts - 1) // (4 * num_experts))
    positions = lax.axis_index("fsdp") * row_count + jnp.arange(row_count, dtype=jnp.int32)
    first_pos = positions[0]
    last_pos = positions[row_count - 1]
    inputs = tokens.astype(jnp.float32)
    dense_full = (
        lax.all_gather(w_query, ("dp", "fsdp"), axis=0, tiled=True),
        lax.all_gather(w_key, ("dp", "fsdp"), axis=0, tiled=True),
        lax.all_gather(w_value, ("dp", "fsdp"), axis=0, tiled=True),
        lax.all_gather(w_output, ("dp", "fsdp"), axis=0, tiled=True),
        lax.all_gather(w_router, ("dp", "fsdp"), axis=0, tiled=True),
        lax.all_gather(gain_attn, ("dp", "fsdp"), axis=0, tiled=True),
        lax.all_gather(gain_query, ("dp", "fsdp"), axis=0, tiled=True),
        lax.all_gather(gain_key, ("dp", "fsdp"), axis=0, tiled=True),
        lax.all_gather(gain_ffn, ("dp", "fsdp"), axis=0, tiled=True),
    )
    expert_full = (
        lax.all_gather(expert_gate, "dp", axis=2, tiled=True),
        lax.all_gather(expert_up, "dp", axis=2, tiled=True),
        lax.all_gather(expert_down, "dp", axis=2, tiled=True),
    )
    query_full, key_full, value_full, output_full, router_full = dense_full[:5]
    gain_in_full = dense_full[5].astype(jnp.float32)
    gain_q_full = dense_full[6].astype(jnp.float32)
    gain_k_full = dense_full[7].astype(jnp.float32)
    gain_mid_full = dense_full[8].astype(jnp.float32)
    normed_low = rms_norm(inputs, gain_in_full).astype(jnp.bfloat16)
    query_raw = jnp.dot(normed_low, query_full, preferred_element_type=jnp.float32)
    key_raw = jnp.dot(normed_low, key_full, preferred_element_type=jnp.float32)
    value_raw = jnp.dot(normed_low, value_full, preferred_element_type=jnp.float32)
    query_low = head_prep(query_raw, gain_q_full, positions).astype(jnp.bfloat16)
    key_low = head_prep(key_raw, gain_k_full, positions).astype(jnp.bfloat16)
    value_low = value_raw.astype(jnp.bfloat16).reshape(row_count, HEADS, head_dim)
    start_state = (
        jnp.full((HEADS, row_count), far_low, jnp.float32),
        jnp.zeros((HEADS, row_count), jnp.float32),
        jnp.zeros((row_count, HEADS, head_dim), jnp.float32),
    )
    shard_piece = (
        lax.all_gather(key_low, "fsdp", axis=0, tiled=True),
        lax.all_gather(value_low, "fsdp", axis=0, tiled=True),
    )

    def attend_update(state):
        run_max, run_sum, run_acc = state
        key_piece, value_piece = shard_piece
        scores = (
            jnp.einsum("qhd,khd->hqk", query_low, key_piece, preferred_element_type=jnp.float32)
            * score_scale
        )
        key_pos = jnp.arange(key_piece.shape[0], dtype=jnp.int32)
        allowed = (key_pos[None, :] <= positions[:, None])[None]
        new_max = jnp.maximum(run_max, jnp.max(jnp.where(allowed, scores, far_low), axis=-1))
        exp_vals = jnp.where(allowed, jnp.exp(scores - new_max[..., None]), 0.0)
        factor = jnp.exp(run_max - new_max)
        run_sum = jnp.sum(exp_vals, axis=-1)
        run_acc = run_acc * factor.T[:, :, None] + jnp.einsum(
            "hqk,khd->qhd",
            exp_vals.astype(jnp.bfloat16),
            value_piece,
            preferred_element_type=jnp.float32,
        )
        return (new_max, run_sum, run_acc)

    run_max, run_sum, run_acc = lax.cond(
        jnp.int32(0) <= last_pos, attend_update, lambda state: state, start_state
    )
    attn_f32 = run_acc / run_sum.T[:, :, None]
    log_sum = run_max + jnp.log(run_sum)
    attn_low = attn_f32.reshape(row_count, model_width).astype(jnp.bfloat16)
    resid_mid = inputs + jnp.dot(attn_low, output_full, preferred_element_type=jnp.float32)
    mid_low = rms_norm(resid_mid, gain_mid_full).astype(jnp.bfloat16)
    logits = jnp.dot(mid_low, router_full, preferred_element_type=jnp.float32)
    gate_vals, gate_pull = jax.vjp(
        lambda logit_vals: gating(logit_vals, routes, num_experts), logits
    )
    route_flat = routes.reshape(-1)
    pick_table = (route_flat[:, None] == jnp.arange(num_experts, dtype=jnp.int32)[None, :]).astype(
        jnp.int32
    )
    slot_index = jnp.sum(pick_table * (jnp.cumsum(pick_table, axis=0) - 1), axis=1)
    target = route_flat * capacity + slot_index
    spread = jnp.repeat(mid_low, TOPK, axis=0)
    send_rows = (
        jnp.zeros((num_experts * capacity, model_width), jnp.bfloat16).at[target].set(spread)
    )
    send_rows = send_rows.reshape(fsdp_size, local_experts, capacity, model_width)
    arrived = lax.all_to_all(send_rows, "fsdp", split_axis=0, concat_axis=0, tiled=True)
    gate_w, up_w, down_w = expert_full
    gate_hid = jnp.einsum("secd,edh->sech", arrived, gate_w, preferred_element_type=jnp.float32)
    up_hid = jnp.einsum("secd,edh->sech", arrived, up_w, preferred_element_type=jnp.float32)
    act_low = swiglu(gate_hid, up_hid).astype(jnp.bfloat16)
    expert_out = jnp.einsum(
        "sech,edh->secd", act_low, down_w, preferred_element_type=jnp.float32
    ).astype(jnp.bfloat16)
    returned = lax.all_to_all(expert_out, "fsdp", split_axis=0, concat_axis=0, tiled=True).reshape(
        num_experts * capacity, model_width
    )
    picked = returned[target].reshape(row_count, TOPK, model_width).astype(jnp.float32)
    resid_out = resid_mid + jnp.sum(gate_vals[:, :, None] * picked, axis=1)
    layer_out = resid_out.astype(jnp.bfloat16)
    back_dense = (
        lax.all_gather(w_query, ("dp", "fsdp"), axis=0, tiled=True),
        lax.all_gather(w_key, ("dp", "fsdp"), axis=0, tiled=True),
        lax.all_gather(w_value, ("dp", "fsdp"), axis=0, tiled=True),
        lax.all_gather(w_output, ("dp", "fsdp"), axis=0, tiled=True),
        lax.all_gather(w_router, ("dp", "fsdp"), axis=0, tiled=True),
        lax.all_gather(gain_attn, ("dp", "fsdp"), axis=0, tiled=True),
        lax.all_gather(gain_query, ("dp", "fsdp"), axis=0, tiled=True),
        lax.all_gather(gain_key, ("dp", "fsdp"), axis=0, tiled=True),
        lax.all_gather(gain_ffn, ("dp", "fsdp"), axis=0, tiled=True),
    )
    back_experts = (
        lax.all_gather(expert_gate, "dp", axis=2, tiled=True),
        lax.all_gather(expert_up, "dp", axis=2, tiled=True),
        lax.all_gather(expert_down, "dp", axis=2, tiled=True),
    )
    query_back, key_back, value_back, output_back, router_back = back_dense[:5]
    gain_in_back = back_dense[5].astype(jnp.float32)
    gain_q_back = back_dense[6].astype(jnp.float32)
    gain_k_back = back_dense[7].astype(jnp.float32)
    gain_mid_back = back_dense[8].astype(jnp.float32)
    gate_back, up_back, down_back = back_experts
    grad_out = cotangent.astype(jnp.float32)
    grad_gates = jnp.sum(grad_out[:, None, :] * picked, axis=-1)
    grad_routed = (
        (gate_vals[:, :, None] * grad_out[:, None, :]).astype(jnp.bfloat16).reshape(-1, model_width)
    )
    send_grads = (
        jnp.zeros((num_experts * capacity, model_width), jnp.bfloat16).at[target].set(grad_routed)
    )
    send_grads = send_grads.reshape(fsdp_size, local_experts, capacity, model_width)
    grad_arrived = lax.all_to_all(send_grads, "fsdp", split_axis=0, concat_axis=0, tiled=True)
    gate_again = jnp.einsum(
        "secd,edh->sech", arrived, gate_back, preferred_element_type=jnp.float32
    )
    up_again = jnp.einsum("secd,edh->sech", arrived, up_back, preferred_element_type=jnp.float32)
    act_vals, act_pull = jax.vjp(swiglu, gate_again, up_again)
    act_again = act_vals.astype(jnp.bfloat16)
    grad_act = jnp.einsum(
        "secd,edh->sech", grad_arrived, down_back, preferred_element_type=jnp.float32
    )
    grad_down = jnp.einsum(
        "secd,sech->edh", grad_arrived, act_again, preferred_element_type=jnp.float32
    )
    grad_gate_hid, grad_up_hid = act_pull(grad_act)
    grad_gate_low = grad_gate_hid.astype(jnp.bfloat16)
    grad_up_low = grad_up_hid.astype(jnp.bfloat16)
    grad_gate_w = jnp.einsum(
        "secd,sech->edh", arrived, grad_gate_low, preferred_element_type=jnp.float32
    )
    grad_up_w = jnp.einsum(
        "secd,sech->edh", arrived, grad_up_low, preferred_element_type=jnp.float32
    )
    grad_inputs = jnp.einsum(
        "sech,edh->secd", grad_gate_low, gate_back, preferred_element_type=jnp.float32
    ) + jnp.einsum("sech,edh->secd", grad_up_low, up_back, preferred_element_type=jnp.float32)
    grad_returned = lax.all_to_all(
        grad_inputs.astype(jnp.bfloat16), "fsdp", split_axis=0, concat_axis=0, tiled=True
    )
    grad_returned = grad_returned.reshape(num_experts * capacity, model_width)
    grad_mid = jnp.sum(
        grad_returned[target].reshape(row_count, TOPK, model_width).astype(jnp.float32), axis=1
    )
    expert_grads = (
        lax.psum_scatter(
            grad_gate_w.astype(jnp.bfloat16), "dp", scatter_dimension=2, tiled=True
        ).astype(jnp.float32),
        lax.psum_scatter(
            grad_up_w.astype(jnp.bfloat16), "dp", scatter_dimension=2, tiled=True
        ).astype(jnp.float32),
        lax.psum_scatter(
            grad_down.astype(jnp.bfloat16), "dp", scatter_dimension=2, tiled=True
        ).astype(jnp.float32),
    )
    (grad_logits,) = gate_pull(grad_gates)
    grad_logits_low = grad_logits.astype(jnp.bfloat16)
    grad_router = jnp.einsum(
        "td,te->de", mid_low, grad_logits_low, preferred_element_type=jnp.float32
    )
    grad_mid = grad_mid + jnp.einsum(
        "te,de->td", grad_logits_low, router_back, preferred_element_type=jnp.float32
    )
    mid_value, mid_pull = jax.vjp(rms_norm, resid_mid, gain_mid_back)
    grad_resid_part, grad_gain_mid = mid_pull(grad_mid)
    grad_resid = grad_out + grad_resid_part
    grad_attn_out = grad_resid.astype(jnp.bfloat16)
    grad_output_w = jnp.einsum(
        "td,te->de", attn_low, grad_attn_out, preferred_element_type=jnp.float32
    )
    grad_attn = jnp.einsum(
        "te,de->td", grad_attn_out, output_back, preferred_element_type=jnp.float32
    )
    grad_attn = grad_attn.astype(jnp.bfloat16).reshape(row_count, HEADS, head_dim)
    delta_rows = jnp.sum(grad_attn.astype(jnp.float32) * attn_f32, axis=-1).T
    key_all, value_all = (
        lax.all_gather(key_low, "fsdp", axis=0, tiled=True),
        lax.all_gather(value_low, "fsdp", axis=0, tiled=True),
    )

    def probs_block(key_block, value_block, begin_at):
        scores = (
            jnp.einsum("qhd,khd->hqk", query_low, key_block, preferred_element_type=jnp.float32)
            * score_scale
        )
        key_pos = begin_at + jnp.arange(key_block.shape[0], dtype=jnp.int32)
        allowed = (key_pos[None, :] <= positions[:, None])[None]
        prob_vals = jnp.where(allowed, jnp.exp(scores - log_sum[..., None]), 0.0)
        grad_probs = jnp.einsum(
            "qhd,khd->hqk", grad_attn, value_block, preferred_element_type=jnp.float32
        )
        grad_scores = (prob_vals * (grad_probs - delta_rows[..., None])).astype(jnp.bfloat16)
        return (prob_vals, grad_scores)

    block_rows = 8 * row_count
    block_needed = last_pos // block_rows + 1
    zero_query = jnp.zeros((row_count, HEADS, head_dim), jnp.float32)

    def query_step(block_index, accum):
        begin_at = block_index * block_rows
        key_block = lax.dynamic_slice_in_dim(key_all, begin_at, block_rows, 0)
        value_block = lax.dynamic_slice_in_dim(value_all, begin_at, block_rows, 0)
        prob_vals, grad_scores = probs_block(key_block, value_block, begin_at)
        return accum + jnp.einsum(
            "hqk,khd->qhd", grad_scores, key_block, preferred_element_type=jnp.float32
        )

    grad_query_rot = lax.fori_loop(0, block_needed, query_step, zero_query) * score_scale
    stats_all = (
        lax.all_gather(log_sum.T, "fsdp", axis=0, tiled=True),
        lax.all_gather(delta_rows.T, "fsdp", axis=0, tiled=True),
    )
    query_piece = lax.all_gather(query_low, "fsdp", axis=0, tiled=True)
    grad_piece = lax.all_gather(grad_attn, "fsdp", axis=0, tiled=True)
    span = query_piece.shape[0]

    def add_update(state):
        lse_piece = stats_all[0].T
        delta_piece = stats_all[1].T
        scores = (
            jnp.einsum("qhd,khd->hqk", query_piece, key_low, preferred_element_type=jnp.float32)
            * score_scale
        )
        query_pos = jnp.arange(span, dtype=jnp.int32)
        allowed = (positions[None, :] <= query_pos[:, None])[None]
        prob_vals = jnp.where(allowed, jnp.exp(scores - lse_piece[..., None]), 0.0)
        grad_probs = jnp.einsum(
            "qhd,khd->hqk", grad_piece, value_low, preferred_element_type=jnp.float32
        )
        grad_scores = (prob_vals * (grad_probs - delta_piece[..., None])).astype(jnp.bfloat16)
        grad_value_acc = jnp.einsum(
            "hqk,qhd->khd",
            prob_vals.astype(jnp.bfloat16),
            grad_piece,
            preferred_element_type=jnp.float32,
        )
        grad_key_acc = jnp.einsum(
            "hqk,qhd->khd", grad_scores, query_piece, preferred_element_type=jnp.float32
        )
        return (grad_key_acc, grad_value_acc)

    grad_key_sum, grad_value_sum = lax.cond(
        jnp.int32(0) + span > first_pos, add_update, lambda state: state, (zero_query, zero_query)
    )
    grad_key_rot = grad_key_sum * score_scale
    grad_value_low = grad_value_sum.reshape(row_count, model_width).astype(jnp.bfloat16)
    query_value, query_pull = jax.vjp(
        lambda raw_vals, scaling: head_prep(raw_vals, scaling, positions), query_raw, gain_q_back
    )
    grad_query_raw, grad_gain_query = query_pull(grad_query_rot)
    key_value, key_pull = jax.vjp(
        lambda raw_vals, scaling: head_prep(raw_vals, scaling, positions), key_raw, gain_k_back
    )
    grad_key_raw, grad_gain_key = key_pull(grad_key_rot)
    grad_query_low = grad_query_raw.astype(jnp.bfloat16)
    grad_key_low = grad_key_raw.astype(jnp.bfloat16)
    grad_wq = jnp.einsum(
        "td,te->de", normed_low, grad_query_low, preferred_element_type=jnp.float32
    )
    grad_wk = jnp.einsum("td,te->de", normed_low, grad_key_low, preferred_element_type=jnp.float32)
    grad_wv = jnp.einsum(
        "td,te->de", normed_low, grad_value_low, preferred_element_type=jnp.float32
    )
    grad_normed = (
        jnp.einsum("te,de->td", grad_query_low, query_back, preferred_element_type=jnp.float32)
        + jnp.einsum("te,de->td", grad_key_low, key_back, preferred_element_type=jnp.float32)
        + jnp.einsum("te,de->td", grad_value_low, value_back, preferred_element_type=jnp.float32)
    )
    in_value, input_pull = jax.vjp(rms_norm, inputs, gain_in_back)
    grad_input_part, grad_gain_in = input_pull(grad_normed)
    grad_tokens = grad_resid + grad_input_part
    dense_grads = (
        lax.psum_scatter(grad_wq, ("dp", "fsdp"), scatter_dimension=0, tiled=True),
        lax.psum_scatter(grad_wk, ("dp", "fsdp"), scatter_dimension=0, tiled=True),
        lax.psum_scatter(grad_wv, ("dp", "fsdp"), scatter_dimension=0, tiled=True),
        lax.psum_scatter(grad_output_w, ("dp", "fsdp"), scatter_dimension=0, tiled=True),
        lax.psum_scatter(grad_router, ("dp", "fsdp"), scatter_dimension=0, tiled=True),
        lax.psum_scatter(grad_gain_in, ("dp", "fsdp"), scatter_dimension=0, tiled=True),
        lax.psum_scatter(grad_gain_query, ("dp", "fsdp"), scatter_dimension=0, tiled=True),
        lax.psum_scatter(grad_gain_key, ("dp", "fsdp"), scatter_dimension=0, tiled=True),
        lax.psum_scatter(grad_gain_mid, ("dp", "fsdp"), scatter_dimension=0, tiled=True),
    )
    return (
        layer_out,
        grad_tokens,
        dense_grads[0],
        dense_grads[1],
        dense_grads[2],
        dense_grads[3],
        dense_grads[4],
        dense_grads[5],
        dense_grads[6],
        dense_grads[7],
        dense_grads[8],
        expert_grads[0],
        expert_grads[1],
        expert_grads[2],
    )


def after(values, ties):
    if callable(ties):
        ties = ties(values)
    if ties is None:
        return values
    return lax.optimization_barrier((values, ties))[0]


class Ring:
    def __init__(self, size, rows):
        self.size = size
        self.half = size // 2
        self.rows = rows
        middle = rows // 2
        self.pieces = [(k, 0, rows) for k in range(self.half)]
        self.pieces += [(self.half, 0, middle), (self.half, middle, middle)]
        self.pieces += [(k, 0, rows) for k in range(self.half + 1, size)]
        self.order = list(range(0, size, 2)) + list(range(size - 1, 0, -2))
        place = [self.order.index(i) for i in range(size)]
        rank = jnp.asarray(place, jnp.int32)[lax.axis_index("fsdp")]
        self.slot_device = jnp.asarray(self.order, jnp.int32)[
            (rank + jnp.arange(size, dtype=jnp.int32)) % size
        ]
        self.device_slot = (jnp.asarray(place, jnp.int32) - rank) % size
        self.up = [(self.order[i], self.order[(i + 1) % size]) for i in range(size)]
        self.down = [(self.order[i], self.order[i - 1]) for i in range(size)]

    def forward(self, values):
        return lax.ppermute(values, "fsdp", self.up)

    def backward(self, values):
        return lax.ppermute(values, "fsdp", self.down)

    def gather(self, block, halves=True):
        return Gather(self, block, halves)

    def reduce(self, pieces):
        return Reduce(self, pieces)


def add_pair_kernel(upper, rising, lower, falling, first, second):
    count, arrived = upper.shape[0], rising.shape[0]
    first[:arrived, :] = upper[:arrived, :] + rising[...]
    second[count - arrived :, :] = lower[count - arrived :, :] + falling[...]
    if arrived < count:
        first[arrived:, :] = upper[arrived:, :]
        second[: count - arrived, :] = lower[: count - arrived, :]


def add_pair(upper, rising, lower, falling):
    shape = jax.ShapeDtypeStruct(upper.shape, upper.dtype)
    return pl.pallas_call(add_pair_kernel, out_shape=[shape, shape], name="add_pair")(
        upper, rising, lower, falling
    )


class Gather:
    def __init__(self, ring, block, halves=True):
        self.ring, self.halves = ring, halves
        self.low, self.high, self.opposite = [block], [block], None

    def step(self, ties=None):
        ring, middle = self.ring, self.ring.rows // 2
        from_low, from_high = after((self.low[-1], self.high[-1]), ties)
        if len(self.low) < ring.half:
            self.low.append(ring.forward(from_low))
            self.high.append(ring.backward(from_high))
            return self.low[-1], self.high[-1]
        if self.halves:
            self.opposite = [ring.forward(from_low[:middle]), ring.backward(from_high[middle:])]
        else:
            self.opposite = [ring.forward(from_low)]
        return tuple(self.opposite)

    def stacked(self):
        return jnp.stack(self.blocks())[self.ring.device_slot]

    def blocks(self):
        return self.high + self.opposite + self.low[:0:-1]


class Reduce:
    def __init__(self, ring, pieces):
        self.ring, self.pieces, self.arrived, self.left = ring, pieces, None, ring.half

    def step(self, ties=None, early=None):
        ring, pieces = self.ring, self.pieces
        if self.arrived is None:
            upper, lower = pieces[ring.half], pieces[ring.half + 1]
        else:
            rising, falling = after(self.arrived, early)
            upper, lower = pieces[self.left], pieces[-self.left]
            upper, lower = add_pair(upper, rising, lower, falling)
        upper, lower = after((upper, lower), ties)
        self.sent = (upper, lower)
        self.arrived = (ring.forward(upper), ring.backward(lower))
        self.left -= 1
        return self.arrived

    def last(self):
        return self.pieces[0], *self.arrived

    def total(self, early=None):
        rising, falling = after(self.arrived, early)
        return (
            self.pieces[0].astype(jnp.float32)
            + rising.astype(jnp.float32)
            + falling.astype(jnp.float32)
        )


def exchange_pairs(size, bit):
    return [(i, i ^ bit) for i in range(size)]


def pair_sum(values, axis, size):
    bit = 1
    while bit < size:
        values = values + lax.ppermute(values, axis, exchange_pairs(size, bit))
        bit *= 2
    return values


def pair_gather(values, axis, size, ties=()):
    ties = dict(ties)
    mine = lax.axis_index(axis)
    values = values[None]
    bit = 1
    while bit < size:
        values = after(values, ties.get(bit))
        other = lax.ppermute(values, axis, exchange_pairs(size, bit))
        upper = (mine & bit) != 0
        values = jnp.where(
            upper,
            jnp.concatenate([other, values], axis=0),
            jnp.concatenate([values, other], axis=0),
        )
        bit *= 2
    return values


def share_relative(block, size, ties=(), second=()):
    block = after(block, ties)
    held = {0: block}
    bit = size // 2
    while bit >= 1:
        for index in list(held):
            sent = held[index] if index == 0 else after(held[index], second)
            held[index ^ bit] = lax.ppermute(sent, dp_axes, exchange_pairs(size, bit))
        bit //= 2
    return [held[index] for index in range(size)]


def combine_relative(far, near, ties=(None, None)):
    far = lax.ppermute(after(far, ties[0]), dp_axes, exchange_pairs(4, 1))
    other = near[1] + far[1].astype(jnp.float32)
    other = after(other.astype(jnp.bfloat16), ties[1])
    other = lax.ppermute(other, dp_axes, exchange_pairs(4, 2))
    return near[0] + far[0].astype(jnp.float32) + other.astype(jnp.float32)


anywhere = pl.BlockSpec(memory_space=pl.ANY)
rows_first = (((0,), (0,)), ((), ()))
columns_last = (((1,), (1,)), ((), ()))


def dot(left, right, dims=(((1,), (0,)), ((), ()))):
    return lax.dot_general(left, right, dims, preferred_element_type=jnp.float32)


def row_sums(*columns):
    total = None
    for i, values in enumerate(columns):
        place = lax.broadcasted_iota(jnp.int32, (8, values.shape[1]), 0) == i
        sums = lax.dot_general(
            place.astype(jnp.float32),
            values,
            columns_last,
            precision=lax.Precision.HIGHEST,
            preferred_element_type=jnp.float32,
        )
        total = sums if total is None else total + sums
    return total


def as_columns(rows):
    return rows_as_columns(rows, 8)


def rows_as_columns(rows, columns):
    shape = (rows.shape[0], columns)
    same = lax.broadcasted_iota(jnp.int32, shape, 0) == lax.broadcasted_iota(jnp.int32, shape, 1)
    return lax.dot_general(
        rows,
        same.astype(jnp.float32),
        rows_first,
        precision=lax.Precision.HIGHEST,
        preferred_element_type=jnp.float32,
    )


def whole_block(shape):
    return pl.BlockSpec(shape, lambda *_: (0,) * len(shape))


def piece_copies(pieces, scalars, blocks, target, sems, first_column=0):
    rows = pieces[0][2]
    columns = pl.ds(first_column, target.shape[1])
    copies = []
    for i, (slot, first, count) in enumerate(pieces):
        begin = pl.multiple_of(scalars[slot] * rows + first, count)
        copies.append(
            pltpu.make_async_copy(
                blocks[i].at[:, columns], target.at[pl.ds(begin, count), :], sems.at[i]
            )
        )
    return copies


def piece_results(pieces, scalars, source, blocks, sems):
    rows = pieces[0][2]
    copies = []
    for i, (slot, first, count) in enumerate(pieces):
        begin = pl.multiple_of(scalars[slot] * rows + first, count)
        copies.append(
            pltpu.make_async_copy(source.at[pl.ds(begin, count), :], blocks[i], sems.at[i])
        )
    return copies


def row_copies(scalars, which, blocks, target, sems):
    own = scalars[which]
    count = blocks[0].shape[0]
    return [
        pltpu.make_async_copy(
            block, target.at[pl.ds(pl.multiple_of((own ^ i) * count, count), count), :], sems.at[i]
        )
        for i, block in enumerate(blocks)
    ]


def run_copies(copies):
    for copy in copies:
        copy.start()
    for copy in copies:
        copy.wait()


def piece_shapes(pieces, width):
    return [jax.ShapeDtypeStruct((count, width), jnp.bfloat16) for _, _, count in pieces]


def project_kernel(pieces, parts, chunk, scalars, *refs):
    n = len(pieces)
    blocks, weights, gain = refs[:n], refs[n : n + parts], refs[n + parts]
    normed, raw, factor, squares, kept, tokens, weight, sems, w_sems, k_sem = refs[n + parts + 1 :]
    step = pl.program_id(0)

    @pl.when(step == 0)
    def _():
        run_copies(
            piece_copies(pieces, scalars, blocks, tokens, sems)
            + row_copies(scalars, len(scalars) - 1, weights, weight, w_sems)
        )
        pltpu.make_async_copy(tokens, kept, k_sem).start()

    rows = pl.ds(pl.multiple_of(step * chunk, chunk), chunk)
    values = tokens[rows, :].astype(jnp.float32)
    scale = lax.rsqrt(jnp.mean(values * values, axis=-1, keepdims=True) + epsilon)
    low = (values * scale * gain[...]).astype(jnp.bfloat16)
    normed[...] = low
    factor[...] = scale
    product = dot(low, weight[...])
    raw[...] = product
    part = product.shape[1] // 3
    squares[...] = row_sums(product[:, :part] ** 2, product[:, part : 2 * part] ** 2)

    @pl.when(step == pl.num_programs(0) - 1)
    def _():
        pltpu.make_async_copy(tokens, kept, k_sem).wait()


def project(ring, scalars, blocks, weights, gain):
    width = blocks[0].shape[1]
    span = ring.rows * ring.size
    columns = weights[0].shape[1]
    chunk = min(256, span)
    n = len(ring.pieces)
    by_rows = lambda i, s: (i, 0)
    return pl.pallas_call(
        functools.partial(project_kernel, ring.pieces, len(weights), chunk),
        grid_spec=pltpu.PrefetchScalarGridSpec(
            num_scalar_prefetch=1,
            grid=(span // chunk,),
            in_specs=[anywhere] * (n + len(weights)) + [whole_block((1, width))],
            out_specs=[
                pl.BlockSpec((chunk, width), by_rows),
                pl.BlockSpec((chunk, columns), by_rows),
                pl.BlockSpec((chunk, 1), by_rows),
                pl.BlockSpec((8, chunk), lambda i, s: (0, i)),
                anywhere,
            ],
            scratch_shapes=[
                pltpu.VMEM((span, width), jnp.bfloat16),
                pltpu.VMEM((width, columns), jnp.bfloat16),
                pltpu.SemaphoreType.DMA((n,)),
                pltpu.SemaphoreType.DMA((len(weights),)),
                pltpu.SemaphoreType.DMA,
            ],
        ),
        out_shape=[
            jax.ShapeDtypeStruct((span, width), jnp.bfloat16),
            jax.ShapeDtypeStruct((span, columns), jnp.float32),
            jax.ShapeDtypeStruct((span, 1), jnp.float32),
            jax.ShapeDtypeStruct((8, span), jnp.float32),
            jax.ShapeDtypeStruct((span, width), jnp.bfloat16),
        ],
        name="project",
    )(scalars, *blocks, *weights, gain)


def turned(values, cosine, sine):
    return values * cosine + pltpu.roll(values, values.shape[-1] // 2, 1) * sine


def attend_kernel(pieces, parts, chunk, scale, scalars, *refs):
    q_raw, k_raw, v_raw, factors, gain_q, gain_k, cosine, sine = refs[:8]
    weights = refs[8 : 8 + parts]
    query, key, value, mixed, lse = refs[8 + parts : 13 + parts]
    n = len(pieces)
    results = refs[13 + parts : 13 + parts + n]
    weight, total, summed, w_sems, sems = refs[13 + parts + n :]
    head = pl.program_id(0)
    last = pl.num_programs(0) - 1
    tokens, head_dim = query.shape

    @pl.when(head == 0)
    def _():
        run_copies(row_copies(scalars, len(scalars) - 1, weights, weight, w_sems))

    columns = as_columns(factors[...])
    query[...] = turned(
        q_raw[...] * columns[:, 0:1] * gain_q[...], cosine[...], sine[...]
    ).astype(jnp.bfloat16)
    key[...] = turned(
        k_raw[...] * columns[:, 1:2] * gain_k[...], cosine[...], sine[...]
    ).astype(jnp.bfloat16)
    value[...] = v_raw[...].astype(jnp.bfloat16)
    own_rows = weight[pl.ds(pl.multiple_of(head * head_dim, head_dim), head_dim), :]
    for begin in range(0, tokens, chunk):
        rows, seen = pl.ds(begin, chunk), pl.ds(0, begin + chunk)
        scores = dot(query[rows, :], key[seen, :], columns_last) * scale
        shape = scores.shape
        allowed = lax.broadcasted_iota(jnp.int32, shape, 1) <= begin + lax.broadcasted_iota(
            jnp.int32, shape, 0
        )
        scores = jnp.where(allowed, scores, far_low)
        top = jnp.max(scores, axis=-1, keepdims=True)
        weights_now = jnp.exp(scores - top)
        sums = jnp.sum(weights_now, axis=-1, keepdims=True)
        out = dot(weights_now.astype(jnp.bfloat16), value[seen, :]) / sums
        mixed[rows, :] = out
        lse[rows, :] = top + jnp.log(sums)
        product = dot(out.astype(jnp.bfloat16), own_rows)

        @pl.when(head == 0)
        def _():
            total[rows, :] = product

        @pl.when(jnp.logical_and(head > 0, head < last))
        def _():
            total[rows, :] += product

        @pl.when(jnp.logical_and(head > 0, head == last))
        def _():
            summed[rows, :] = (total[rows, :] + product).astype(jnp.bfloat16)

        @pl.when(jnp.logical_and(head == 0, head == last))
        def _():
            summed[rows, :] = product.astype(jnp.bfloat16)

    @pl.when(head == last)
    def _():
        run_copies(piece_results(pieces, scalars, summed, results, sems))


def attend(ring, scalars, raw, factors, gain_q, gain_k, cosine, sine, weights, head_dim):
    tokens = raw.shape[0]
    part = raw.shape[1] // 3
    heads = part // head_dim
    width = weights[0].shape[1]
    n = len(ring.pieces)
    column = lambda first: pl.BlockSpec((tokens, head_dim), lambda h, s: (0, first + h))
    gain = pl.BlockSpec((1, head_dim), lambda h, s: (0, h))
    table = whole_block((tokens, head_dim))
    low = jax.ShapeDtypeStruct((tokens, part), jnp.bfloat16)
    out = pl.pallas_call(
        functools.partial(
            attend_kernel, ring.pieces, len(weights), min(256, tokens), head_dim ** (-0.5)
        ),
        grid_spec=pltpu.PrefetchScalarGridSpec(
            num_scalar_prefetch=1,
            grid=(heads,),
            in_specs=[column(0), column(heads), column(2 * heads), whole_block((8, tokens))]
            + [gain, gain, table, table]
            + [anywhere] * len(weights),
            out_specs=[column(0)] * 4
            + [pl.BlockSpec((None, tokens, 1), lambda h, s: (h, 0, 0))]
            + [anywhere] * n,
            scratch_shapes=[
                pltpu.VMEM((part, width), jnp.bfloat16),
                pltpu.VMEM((tokens, width), jnp.float32),
                pltpu.VMEM((tokens, width), jnp.bfloat16),
                pltpu.SemaphoreType.DMA((len(weights),)),
                pltpu.SemaphoreType.DMA((n,)),
            ],
        ),
        out_shape=[low, low, low, jax.ShapeDtypeStruct((tokens, part), jnp.float32)]
        + [jax.ShapeDtypeStruct((heads, tokens, 1), jnp.float32)]
        + piece_shapes(ring.pieces, width),
        name="attend",
    )(scalars, raw, raw, raw, factors, gain_q, gain_k, cosine, sine, *weights)
    return out[:5], out[5:]


def attend_back_kernel(pieces, parts, chunk, scale, head, scalars, *refs):
    query, key, value, mixed, lse, q_raw, k_raw, factors, gain_q, gain_k, cosine, sine = refs[:12]
    n = len(pieces)
    weights = refs[12 : 12 + parts]
    blocks = refs[12 + parts : 12 + parts + n]
    outs = refs[12 + parts + n :]
    turn_q, turn_k, d_value, dots, sum_q, sum_k = outs[:6]
    kept = outs[6] if head == 0 else None
    weight, grads, d_key, d_val, d_query, w_sems, sems, k_sem = outs[-8:]
    tokens, head_dim = query.shape
    run_copies(
        row_copies(scalars, len(scalars) - 1, weights, weight, w_sems)
        + piece_copies(pieces, scalars, blocks, grads, sems)
    )
    if kept is not None:
        pltpu.make_async_copy(grads, kept, k_sem).start()
    own_rows = weight[pl.ds(head * head_dim, head_dim), :]
    for begin in range(0, tokens, chunk):
        rows, seen = pl.ds(begin, chunk), pl.ds(0, begin + chunk)
        grad = dot(grads[rows, :], own_rows, columns_last).astype(jnp.bfloat16)
        queries = query[rows, :]
        scores = dot(queries, key[seen, :], columns_last) * scale
        shape = scores.shape
        allowed = lax.broadcasted_iota(jnp.int32, shape, 1) <= begin + lax.broadcasted_iota(
            jnp.int32, shape, 0
        )
        probs = jnp.where(allowed, jnp.exp(scores - lse[rows, :]), 0.0)
        delta = jnp.sum(grad.astype(jnp.float32) * mixed[rows, :], axis=-1, keepdims=True)
        grad_probs = dot(grad, value[seen, :], columns_last)
        grad_scores = (probs * (grad_probs - delta)).astype(jnp.bfloat16)
        d_query[rows, :] = dot(grad_scores, key[seen, :]) * scale
        part_key = dot(grad_scores, queries, rows_first) * scale
        part_value = dot(probs.astype(jnp.bfloat16), grad, rows_first)
        if begin > 0:
            before = pl.ds(0, begin)
            d_key[before, :] += part_key[:begin]
            d_val[before, :] += part_value[:begin]
        d_key[rows, :] = part_key[begin:]
        d_val[rows, :] = part_value[begin:]
    d_value[...] = d_val[...].astype(jnp.bfloat16)
    back_q = turned(d_query[...], cosine[...], -sine[...])
    back_k = turned(d_key[...], cosine[...], -sine[...])
    turn_q[...] = back_q
    turn_k[...] = back_k
    with_q, with_k = back_q * q_raw[...], back_k * k_raw[...]
    columns = as_columns(factors[...])
    sum_q[...] = jnp.sum(with_q * columns[:, 0:1], axis=0, keepdims=True)
    sum_k[...] = jnp.sum(with_k * columns[:, 1:2], axis=0, keepdims=True)
    dots[...] = row_sums(with_q * gain_q[...], with_k * gain_k[...])
    if kept is not None:
        pltpu.make_async_copy(grads, kept, k_sem).wait()


def attend_back(
    ring, scalars, saved, raw, factors, gain_q, gain_k, cosine, sine, weights, blocks, head_dim,
    head,
):
    query, key, value, mixed, lse = saved
    tokens, part = query.shape
    heads = part // head_dim
    width = weights[0].shape[1]
    n = len(ring.pieces)
    column = lambda first: pl.BlockSpec((tokens, head_dim), lambda i, s: (0, first + head))
    gain = pl.BlockSpec((1, head_dim), lambda i, s: (0, head))
    table = whole_block((tokens, head_dim))
    result = jax.ShapeDtypeStruct((tokens, head_dim), jnp.float32)
    sums = jax.ShapeDtypeStruct((1, head_dim), jnp.float32)
    kept = [anywhere] if head == 0 else []
    accumulate = pltpu.VMEM((tokens, head_dim), jnp.float32)
    return pl.pallas_call(
        functools.partial(
            attend_back_kernel, ring.pieces, len(weights), min(256, tokens), head_dim ** (-0.5),
            head,
        ),
        grid_spec=pltpu.PrefetchScalarGridSpec(
            num_scalar_prefetch=1,
            grid=(1,),
            in_specs=[column(0)] * 4
            + [pl.BlockSpec((None, tokens, 1), lambda i, s: (head, 0, 0))]
            + [column(0), column(heads), whole_block((8, tokens)), gain, gain, table, table]
            + [anywhere] * (len(weights) + n),
            out_specs=[table] * 3
            + [whole_block((8, tokens))]
            + [whole_block((1, head_dim))] * 2
            + kept,
            scratch_shapes=[
                pltpu.VMEM((part, width), jnp.bfloat16),
                pltpu.VMEM((tokens, width), jnp.bfloat16),
                accumulate,
                accumulate,
                accumulate,
                pltpu.SemaphoreType.DMA((len(weights),)),
                pltpu.SemaphoreType.DMA((n,)),
                pltpu.SemaphoreType.DMA,
            ],
        ),
        out_shape=[
            result,
            result,
            jax.ShapeDtypeStruct((tokens, head_dim), jnp.bfloat16),
            jax.ShapeDtypeStruct((8, tokens), jnp.float32),
            sums,
            sums,
        ]
        + [jax.ShapeDtypeStruct((tokens, width), jnp.bfloat16)] * len(kept),
        name="attend_back",
    )(
        scalars, query, key, value, mixed, lse, raw, raw, factors, gain_q, gain_k, cosine, sine,
        *weights, *blocks,
    )


def project_back_kernel(pieces, parts, chunk, heads, scalars, *refs):
    turns, refs = refs[: 3 * heads], refs[3 * heads :]
    raw, factors, dots, gain_q, gain_k, tokens, in_factor = refs[:7]
    n = len(pieces)
    weights = refs[7 : 7 + parts]
    grad_raw, sum_in = refs[7 + parts : 9 + parts]
    results = refs[9 + parts : 9 + parts + n]
    weight, summed, w_sems, sems = refs[9 + parts + n :]
    step = pl.program_id(0)
    head_dim = turns[0].shape[1]
    part = heads * head_dim

    @pl.when(step == 0)
    def _():
        run_copies(row_copies(scalars, len(scalars) - 1, weights, weight, w_sems))
        sum_in[...] = jnp.zeros_like(sum_in)

    factor_columns, dot_columns = as_columns(factors[...]), as_columns(dots[...])
    for i, gain in enumerate((gain_q, gain_k)):
        factor = factor_columns[:, i : i + 1]
        cubed = factor * factor * factor * dot_columns[:, i : i + 1]
        for head in range(heads):
            columns = pl.ds(i * part + head * head_dim, head_dim)
            turn = turns[3 * head + i][...] * gain[:, head * head_dim : (head + 1) * head_dim]
            grad_raw[:, columns] = (factor * turn - raw[:, columns] * cubed).astype(jnp.bfloat16)
    for head in range(heads):
        grad_raw[:, pl.ds(2 * part + head * head_dim, head_dim)] = turns[3 * head + 2][...]
    normed = dot(grad_raw[...], weight[...], columns_last)
    sum_in[...] += jnp.sum(
        normed * (tokens[...].astype(jnp.float32) * in_factor[...]), axis=0, keepdims=True
    )
    summed[pl.ds(pl.multiple_of(step * chunk, chunk), chunk), :] = normed.astype(jnp.bfloat16)

    @pl.when(step == pl.num_programs(0) - 1)
    def _():
        run_copies(piece_results(pieces, scalars, summed, results, sems))


def project_back(
    ring, scalars, turns, raw, factors, dots, gain_q, gain_k, tokens, in_factor, weights
):
    span, width = tokens.shape
    heads, head_dim = len(turns) // 3, turns[0].shape[1]
    part = heads * head_dim
    columns = weights[0].shape[1]
    chunk = min(256, span)
    n = len(ring.pieces)
    by_rows = lambda wide: pl.BlockSpec((chunk, wide), lambda i, s: (i, 0))
    out = pl.pallas_call(
        functools.partial(project_back_kernel, ring.pieces, len(weights), chunk, heads),
        grid_spec=pltpu.PrefetchScalarGridSpec(
            num_scalar_prefetch=1,
            grid=(span // chunk,),
            in_specs=[by_rows(head_dim)] * (3 * heads)
            + [by_rows(columns)]
            + [pl.BlockSpec((8, chunk), lambda i, s: (0, i))] * 2
            + [whole_block((1, part))] * 2
            + [by_rows(width), by_rows(1)]
            + [anywhere] * len(weights),
            out_specs=[by_rows(columns), whole_block((1, width))] + [anywhere] * n,
            scratch_shapes=[
                pltpu.VMEM((width, columns), jnp.bfloat16),
                pltpu.VMEM((span, width), jnp.bfloat16),
                pltpu.SemaphoreType.DMA((len(weights),)),
                pltpu.SemaphoreType.DMA((n,)),
            ],
        ),
        out_shape=[
            jax.ShapeDtypeStruct((span, columns), jnp.bfloat16),
            jax.ShapeDtypeStruct((1, width), jnp.float32),
        ]
        + piece_shapes(ring.pieces, width),
        name="project_back",
    )(
        scalars, *turns, raw, factors, dots, gain_q, gain_k, tokens, in_factor, *weights
    )
    return out[0], out[1], out[2:]


def expert_column(scalars, part, parts, wide):
    half = parts // 2
    relative = 2 * (part % half) + jnp.where(part < half, 1, 0)
    return pl.multiple_of((scalars[len(scalars) - 1] ^ relative) * wide, wide)


def weight_copies(groups, scalars, buffers, sems, step, parts):
    expert, part, place = step // parts, step % parts, step % 2
    wide = buffers.shape[2] // len(groups)
    columns = pl.ds(expert_column(scalars, part, parts, wide), wide)
    return [
        pltpu.make_async_copy(
            group.at[expert, :, columns],
            buffers.at[place, :, pl.ds(g * wide, wide)],
            sems.at[place, g],
        )
        for g, group in enumerate(groups)
    ]


def stream(groups, scalars, buffers, sems, parts):
    step = pl.program_id(0)

    @pl.when(step == 0)
    def _():
        for copy in weight_copies(groups, scalars, buffers, sems, step, parts):
            copy.start()

    @pl.when(step + 1 < pl.num_programs(0))
    def _():
        for copy in weight_copies(groups, scalars, buffers, sems, step + 1, parts):
            copy.start()

    for copy in weight_copies(groups, scalars, buffers, sems, step, parts):
        copy.wait()
    return buffers.at[step % 2]


def middle_kernel(experts, tokens, first, rising, falling, gain, router, routes, *refs):
    resid, factor, block, gates, probs, mask, total = refs
    width = tokens.shape[1]
    values = tokens[...].astype(jnp.float32) + (
        first[...].astype(jnp.float32)
        + rising[...].astype(jnp.float32)
        + falling[...].astype(jnp.float32)
    )
    resid[...] = values
    scale = lax.rsqrt(jnp.mean(values * values, axis=-1, keepdims=True) + epsilon)
    factor[...] = scale
    low = (values * scale * gain[...]).astype(jnp.bfloat16)
    block[:, :width] = low
    logits = dot(low, router[...], columns_last)
    column = lax.broadcasted_iota(jnp.int32, logits.shape, 1)
    real = column < experts
    top = jnp.max(jnp.where(real, logits, far_low), axis=-1, keepdims=True)
    weights = jnp.where(real, jnp.exp(logits - top), 0.0)
    prob_vals = weights / jnp.sum(weights, axis=-1, keepdims=True)
    chosen_mask = jnp.zeros(logits.shape, jnp.float32)
    for j in range(routes.shape[1]):
        chosen_mask = jnp.where(column == routes[:, j : j + 1], 1.0, chosen_mask)
    chosen = chosen_mask * prob_vals
    chosen_sum = jnp.sum(chosen, axis=-1, keepdims=True)
    gate_vals = chosen / chosen_sum
    gates[...], probs[...], mask[...], total[...] = gate_vals, prob_vals, chosen_mask, chosen_sum
    high = gate_vals.astype(jnp.bfloat16).astype(jnp.float32)
    rest = pltpu.roll(gate_vals - high, gate_columns, 1)
    block[:, width:] = (high + rest).astype(jnp.bfloat16)


def middle(tokens, sums, gain, router, routes, experts):
    rows, width = tokens.shape
    lanes = 2 * gate_columns
    table = jax.ShapeDtypeStruct((rows, lanes), jnp.float32)
    column = jax.ShapeDtypeStruct((rows, 1), jnp.float32)
    return pl.pallas_call(
        functools.partial(middle_kernel, experts),
        out_shape=[
            jax.ShapeDtypeStruct((rows, width), jnp.float32),
            column,
            jax.ShapeDtypeStruct((rows, width + lanes), jnp.bfloat16),
            table,
            table,
            table,
            column,
        ],
        name="middle",
    )(tokens, *sums, gain, router, routes)


def middle_back_kernel(first, rising, falling, cotangent, resid, factor, block, *refs):
    gates, probs, mask, total, gain, router = refs[:6]
    grad_resid, grad_low, sum_gain, grad_router = refs[6:]
    width = resid.shape[1]
    summed = (
        first[...].astype(jnp.float32)
        + rising[...].astype(jnp.float32)
        + falling[...].astype(jnp.float32)
    )
    lanes = 2 * gate_columns
    gates_back = summed[:, width : width + lanes]
    gates_back = gates_back + summed[:, width + rest_column : width + rest_column + lanes]
    inner = jnp.sum(gates_back * gates[...], axis=-1, keepdims=True)
    grad_probs = mask[...] * ((gates_back - inner) / total[...])
    grad_logits = probs[...] * (
        grad_probs - jnp.sum(probs[...] * grad_probs, axis=-1, keepdims=True)
    )
    logits_low = grad_logits.astype(jnp.bfloat16)
    grad_router[...] = dot(logits_low, block[:, :width], rows_first)
    grad_mid = summed[:, :width] + dot(logits_low, router[...])
    scale, values = factor[...], resid[...]
    scaled = grad_mid * gain[...]
    sum_gain[...] = jnp.sum(grad_mid * values * scale, axis=0, keepdims=True)
    mean = jnp.mean(scaled * values, axis=-1, keepdims=True)
    result = (
        cotangent[...].astype(jnp.float32)
        + scale * scaled
        - values * (scale * scale * scale * mean)
    )
    grad_resid[...] = result
    grad_low[...] = result.astype(jnp.bfloat16)


def middle_back(sums, cotangent, resid, factor, block, gates, probs, mask, total, gain, router):
    rows, width = resid.shape
    return pl.pallas_call(
        middle_back_kernel,
        out_shape=[
            jax.ShapeDtypeStruct((rows, width), jnp.float32),
            jax.ShapeDtypeStruct((rows, width), jnp.bfloat16),
            jax.ShapeDtypeStruct((1, width), jnp.float32),
            jax.ShapeDtypeStruct((2 * gate_columns, width), jnp.float32),
        ],
        name="middle_back",
    )(*sums, cotangent, resid, factor, block, gates, probs, mask, total, gain, router)


def turn_columns(rows_all, result):
    wide = result.shape[0]
    columns = pl.ds(pl.multiple_of(pl.program_id(0) * wide, wide), wide)
    result[...] = rows_all[:, columns].T


def expert_first_kernel(pieces, parts, chunk, scalars, *refs):
    n = len(pieces)
    blocks, down = refs[:n], refs[n]
    product, turned_rows, rows_all, buffers, sems, w_sems = refs[n + 1 :]
    step = pl.program_id(0)

    @pl.when(step == 0)
    def _():
        copies = piece_copies(pieces, scalars, blocks, rows_all, sems)
        for copy in copies:
            copy.start()

    weight = stream([down], scalars, buffers, w_sems, parts)

    @pl.when(step == 0)
    def _():
        for copy in piece_copies(pieces, scalars, blocks, rows_all, sems):
            copy.wait()

    for begin in range(0, rows_all.shape[0], chunk):
        rows = pl.ds(begin, chunk)
        product[rows, :] = dot(rows_all[rows, :], weight[...])
    turn_columns(rows_all, turned_rows)


def expert_first(ring, scalars, blocks, down):
    experts, width, hidden = down.shape
    parts = hidden_parts
    step_hidden = hidden // parts
    span = ring.rows * ring.size
    n = len(ring.pieces)
    return pl.pallas_call(
        functools.partial(expert_first_kernel, ring.pieces, parts, min(256, span)),
        grid_spec=pltpu.PrefetchScalarGridSpec(
            num_scalar_prefetch=1,
            grid=(experts * parts,),
            in_specs=[anywhere] * (n + 1),
            out_specs=[
                pl.BlockSpec((None, span, step_hidden), lambda i, s: (i // parts, 0, i % parts)),
                pl.BlockSpec((width // (experts * parts), span), lambda i, s: (i, 0)),
            ],
            scratch_shapes=[
                pltpu.VMEM((span, width), jnp.bfloat16),
                pltpu.VMEM((2, width, step_hidden), jnp.bfloat16),
                pltpu.SemaphoreType.DMA((n,)),
                pltpu.SemaphoreType.DMA((2, 1)),
            ],
        ),
        out_shape=[
            jax.ShapeDtypeStruct((experts, span, parts * step_hidden), jnp.float32),
            jax.ShapeDtypeStruct((width, span), jnp.bfloat16),
        ],
        name="expert_first",
    )(scalars, *blocks, down)


def expert_hidden_kernel(pieces, parts, chunk, scalars, *refs):
    n = len(pieces)
    blocks, gate, up = refs[:n], refs[n], refs[n + 1]
    product = refs[n + 2]
    act, gated, d_gate, d_up, grad_gates, gates, turned_rows = refs[n + 3 : n + 10]
    rows_all, gates_all, buffers, sems, g_sems, w_sems = refs[n + 10 :]
    step = pl.program_id(0)
    experts = gates.shape[0]
    g_copies = piece_copies(pieces, scalars, blocks, gates_all, g_sems, rows_all.shape[1])

    @pl.when(step == 0)
    def _():
        for copy in piece_copies(pieces, scalars, blocks, rows_all, sems) + g_copies:
            copy.start()

    weight = stream([gate, up], scalars, buffers, w_sems, parts)

    @pl.when(step == 0)
    def _():
        for copy in piece_copies(pieces, scalars, blocks, rows_all, sems) + g_copies:
            copy.wait()
        values = gates_all[...].astype(jnp.float32)
        column = lax.broadcasted_iota(jnp.int32, values.shape, 1) % gate_columns
        for expert in range(experts):
            own = scalars[0] * experts + expert
            gates[expert] = jnp.sum(
                jnp.where(column == own, values, 0.0), axis=-1, keepdims=True
            )

    @pl.when(step % parts == 0)
    def _():
        grad_gates[...] = jnp.zeros_like(grad_gates)

    for begin in range(0, rows_all.shape[0], chunk):
        rows = pl.ds(begin, chunk)
        both = dot(rows_all[rows, :], weight[...])
        gate_hid, up_hid = both[:, : act.shape[1]], both[:, act.shape[1] :]
        own_gate = gates[step // parts, rows, :]
        back = product[rows, :]
        sig = 0.5 + 0.5 * jnp.tanh(0.5 * gate_hid)
        silu = gate_hid * sig
        act_low = (silu * up_hid).astype(jnp.bfloat16)
        act_now = act_low.astype(jnp.float32)
        act[rows, :] = act_low
        gated[rows, :] = (own_gate * act_now).astype(jnp.bfloat16)
        grad_gates[rows, :] += jnp.sum(act_now * back, axis=-1, keepdims=True)
        grad_act = own_gate * back
        d_gate[rows, :] = (grad_act * up_hid * (sig * (1.0 + gate_hid * (1.0 - sig)))).astype(
            jnp.bfloat16
        )
        d_up[rows, :] = (grad_act * silu).astype(jnp.bfloat16)

    turn_columns(rows_all, turned_rows)


def hidden_place(parts, experts):
    half = parts // 2
    return lambda i: ((i % parts) // half * experts + i // parts) * half + (i % parts) % half


def expert_hidden(ring, scalars, blocks, gate, up, product):
    experts, width, hidden_units = gate.shape
    parts = hidden_parts
    step_hidden = hidden_units // parts
    span = ring.rows * ring.size
    n = len(ring.pieces)
    place = hidden_place(parts, experts)
    relative = pl.BlockSpec((None, span, step_hidden), lambda i, s: (i // parts, 0, i % parts))
    placed = pl.BlockSpec((span, step_hidden), lambda i, s: (0, place(i)))
    column = pl.BlockSpec((None, span, 1), lambda i, s: (i // parts, 0, 0))
    hidden = jax.ShapeDtypeStruct((span, experts * parts * step_hidden), jnp.bfloat16)
    return pl.pallas_call(
        functools.partial(expert_hidden_kernel, ring.pieces, parts, min(256, span)),
        grid_spec=pltpu.PrefetchScalarGridSpec(
            num_scalar_prefetch=1,
            grid=(experts * parts,),
            in_specs=[anywhere] * (n + 2) + [relative],
            out_specs=[placed] * 4
            + [column, whole_block((experts, span, 1))]
            + [pl.BlockSpec((width // (experts * parts), span), lambda i, s: (i, 0))],
            scratch_shapes=[
                pltpu.VMEM((span, width), jnp.bfloat16),
                pltpu.VMEM((span, 2 * gate_columns), jnp.bfloat16),
                pltpu.VMEM((2, width, 2 * step_hidden), jnp.bfloat16),
                pltpu.SemaphoreType.DMA((n,)),
                pltpu.SemaphoreType.DMA((n,)),
                pltpu.SemaphoreType.DMA((2, 2)),
            ],
        ),
        out_shape=[
            hidden,
            hidden,
            hidden,
            hidden,
            jax.ShapeDtypeStruct((experts, span, 1), jnp.float32),
            jax.ShapeDtypeStruct((experts, span, 1), jnp.float32),
            jax.ShapeDtypeStruct((width, span), jnp.bfloat16),
        ],
        name="expert_hidden",
    )(scalars, *blocks, gate, up, product)


def pack_weights(scalars, weights, packed, parts):
    experts, _, hidden = weights.shape
    wide = hidden // parts
    place = hidden_place(parts, experts)
    for expert in range(experts):
        for part in range(parts):
            column = place(expert * parts + part) * wide
            relative = 2 * (part % (parts // 2)) + (1 if part < parts // 2 else 0)
            source = pl.multiple_of((scalars[len(scalars) - 1] ^ relative) * wide, wide)
            packed[:, column : column + wide] = weights[expert, :, pl.ds(source, wide)]


def store_pieces(pieces, scalars, source, results):
    rows = pieces[0][2]
    for (slot, first, count), result in zip(pieces, results):
        begin = pl.multiple_of(scalars[slot] * rows + first, count)
        result[...] = source[pl.ds(begin, count), :]


def expert_inputs_kernel(pieces, parts, scalars, *refs):
    d_gate, d_up, gate, up, grad_gates = refs[:5]
    n = len(pieces)
    results = refs[5 : 5 + n]
    packed, summed = refs[5 + n :]
    step = pl.program_id(0)
    last = pl.num_programs(0) - 1

    @pl.when(step < last)
    def _():
        pack_weights(scalars, gate, packed.at[0], parts)
        pack_weights(scalars, up, packed.at[1], parts)
        total = dot(d_gate[...], packed[0], columns_last) + dot(d_up[...], packed[1], columns_last)
        summed[...] = total.astype(jnp.bfloat16)

    @pl.when(step == last)
    def _():
        experts = grad_gates.shape[0]
        column = lax.broadcasted_iota(jnp.int32, summed.shape, 1)
        placed = jnp.zeros(summed.shape, jnp.float32)
        for expert in range(experts):
            value = grad_gates[expert]
            high = value.astype(jnp.bfloat16).astype(jnp.float32)
            own = scalars[0] * experts + expert
            placed = jnp.where(column == own, high, placed)
            placed = jnp.where(column == own + rest_column, value - high, placed)
        summed[...] = placed.astype(jnp.bfloat16)

    store_pieces(pieces, scalars, summed, results)


def expert_inputs(ring, scalars, d_gate, d_up, gate, up, grad_gates):
    experts, width, hidden_units = gate.shape
    parts = hidden_parts
    span, hidden = d_gate.shape
    wide = min(256, width)
    steps = width // wide
    whole = pl.BlockSpec((span, hidden), lambda i, s: (0, 0), pipeline_mode=pl.Buffered(1))
    weight = pl.BlockSpec(
        (experts, wide, hidden_units), lambda i, s: (0, jnp.minimum(i, steps - 1), 0)
    )
    return pl.pallas_call(
        functools.partial(expert_inputs_kernel, ring.pieces, parts),
        grid_spec=pltpu.PrefetchScalarGridSpec(
            num_scalar_prefetch=1,
            grid=(steps + 1,),
            in_specs=[whole] * 2 + [weight] * 2 + [whole_block((experts, span, 1))],
            out_specs=[
                pl.BlockSpec((count, wide), lambda i, s: (0, i)) for _, _, count in ring.pieces
            ],
            scratch_shapes=[
                pltpu.VMEM((2, wide, hidden), jnp.bfloat16),
                pltpu.VMEM((span, wide), jnp.bfloat16),
            ],
        ),
        out_shape=piece_shapes(ring.pieces, width + wide),
        name="expert_inputs",
    )(scalars, d_gate, d_up, gate, up, grad_gates)


def expert_outputs_kernel(pieces, parts, scalars, *refs):
    act, gates = refs[:2]
    down = refs[2]
    n = len(pieces)
    results = refs[3 : 3 + n]
    packed, summed = refs[3 + n :]
    experts, _, hidden_units = down.shape
    pack_weights(scalars, down, packed, parts)
    half = hidden_units // 2
    total = None
    for expert in range(experts):
        first = pl.ds(expert * half, half)
        second = pl.ds((experts + expert) * half, half)
        out = dot(act[:, first], packed[:, first], columns_last)
        out = out + dot(act[:, second], packed[:, second], columns_last)
        out = gates[expert] * out.astype(jnp.bfloat16).astype(jnp.float32)
        total = out if total is None else total + out
    summed[...] = total.astype(jnp.bfloat16)
    store_pieces(pieces, scalars, summed, results)


def expert_outputs(ring, scalars, act, gates, down):
    experts, width, hidden_units = down.shape
    parts = hidden_parts
    span, hidden = act.shape
    wide = min(256, width)
    whole = pl.BlockSpec((span, hidden), lambda i, s: (0, 0), pipeline_mode=pl.Buffered(1))
    return pl.pallas_call(
        functools.partial(expert_outputs_kernel, ring.pieces, parts),
        grid_spec=pltpu.PrefetchScalarGridSpec(
            num_scalar_prefetch=1,
            grid=(width // wide,),
            in_specs=[whole, whole_block((experts, span, 1))]
            + [pl.BlockSpec((experts, wide, hidden_units), lambda i, s: (0, i, 0))],
            out_specs=[
                pl.BlockSpec((count, wide), lambda i, s: (0, i)) for _, _, count in ring.pieces
            ],
            scratch_shapes=[
                pltpu.VMEM((wide, hidden), jnp.bfloat16),
                pltpu.VMEM((span, wide), jnp.bfloat16),
            ],
        ),
        out_shape=piece_shapes(ring.pieces, width),
        name="expert_outputs",
    )(scalars, act, gates, down)


def weight_far_kernel(left, right, result):
    result[...] = dot(left[...], right[...]).astype(jnp.bfloat16)


def weight_far(left, right):
    width, span = left.shape
    split = right.shape[1] // 2
    wide = min(512, width)
    return pl.pallas_call(
        weight_far_kernel,
        grid=(width // wide,),
        in_specs=[
            pl.BlockSpec((wide, span), lambda i: (i, 0)),
            pl.BlockSpec((span, split), lambda i: (0, 0), pipeline_mode=pl.Buffered(1)),
        ],
        out_specs=pl.BlockSpec((wide, split), lambda i: (i, 0)),
        out_shape=jax.ShapeDtypeStruct((width, split), jnp.bfloat16),
        name="weight_far",
    )(left, right)


def weight_near_kernel(scalars, left, right, arrived, result):
    total = dot(left[...], right[...]) + arrived[...].astype(jnp.float32)
    experts, step_hidden = result.shape[0] // 2, result.shape[2]
    own = scalars[len(scalars) - 1] // 2
    for expert in range(experts):
        for other in range(2):
            column = (2 * expert + other) * step_hidden
            result[(own ^ other) * experts + expert] = total[
                :, column : column + step_hidden
            ].astype(jnp.bfloat16)


def weight_near(scalars, left, right, arrived, experts):
    width, span = left.shape
    split = right.shape[1] // 2
    step_hidden = split // (2 * experts)
    wide = min(512, width)
    return pl.pallas_call(
        weight_near_kernel,
        grid_spec=pltpu.PrefetchScalarGridSpec(
            num_scalar_prefetch=1,
            grid=(width // wide,),
            in_specs=[
                pl.BlockSpec((wide, span), lambda i, s: (i, 0)),
                pl.BlockSpec((span, split), lambda i, s: (0, 1), pipeline_mode=pl.Buffered(1)),
                pl.BlockSpec((wide, split), lambda i, s: (i, 0)),
            ],
            out_specs=pl.BlockSpec((2 * experts, wide, step_hidden), lambda i, s: (0, i, 0)),
        ),
        out_shape=jax.ShapeDtypeStruct((2 * experts, width, step_hidden), jnp.bfloat16),
        name="weight_near",
    )(scalars, left, right, arrived)


def weight_rows_kernel(scalars, left, right, sums, far, near):
    columns = right.shape[1]
    value = dot(left[...], right[...], rows_first)
    beside = rows_as_columns(sums[...], far.shape[1] - columns)
    half = pl.num_programs(0) // 2

    @pl.when(pl.program_id(0) < half)
    def _():
        far[:, :columns] = value.astype(jnp.bfloat16)
        far[:, columns:] = beside.astype(jnp.bfloat16)

    @pl.when(pl.program_id(0) >= half)
    def _():
        near[:, :columns] = value
        near[:, columns:] = beside


def weight_rows(scalars, left, right, sums, parts):
    span, width = left.shape
    columns = right.shape[1]
    count = width // parts
    half = parts // 2
    own = scalars.shape[0] - 1
    relative = lambda i: 2 * (i % half) + jnp.where(i < half, 1, 0)
    wide = columns + sum_columns
    return pl.pallas_call(
        weight_rows_kernel,
        grid_spec=pltpu.PrefetchScalarGridSpec(
            num_scalar_prefetch=1,
            grid=(parts,),
            in_specs=[
                pl.BlockSpec((span, count), lambda i, s: (0, s[own] ^ relative(i))),
                whole_block((span, columns)),
                pl.BlockSpec((sums.shape[0], count), lambda i, s: (0, s[own] ^ relative(i))),
            ],
            out_specs=[
                pl.BlockSpec((None, count, wide), lambda i, s: (jnp.minimum(i, half - 1), 0, 0)),
                pl.BlockSpec((None, count, wide), lambda i, s: (jnp.maximum(i - half, 0), 0, 0)),
            ],
        ),
        out_shape=[
            jax.ShapeDtypeStruct((half, count, wide), jnp.bfloat16),
            jax.ShapeDtypeStruct((half, count, wide), jnp.float32),
        ],
        name="weight_rows",
    )(scalars, left, right, sums)


def per_device(
    tokens,
    cotangent,
    routes,
    w_query,
    w_key,
    w_value,
    w_output,
    w_router,
    gain_attn,
    gain_query,
    gain_key,
    gain_ffn,
    expert_gate,
    expert_up,
    expert_down,
):
    rows, width = tokens.shape
    size = lax.axis_size("fsdp")
    dp_size = lax.axis_size("x") * lax.axis_size("core")
    head_dim = width // HEADS
    own_heads = HEADS // size
    part = own_heads * head_dim
    own_rows = w_query.shape[0]
    local_experts = expert_gate.shape[0]
    num_experts = local_experts * size
    group = part // own_rows
    span = rows * size
    f_index = lax.axis_index("fsdp")
    d_index = lax.axis_index(dp_axes)
    low, f32 = jnp.bfloat16, jnp.float32
    ring = Ring(size, rows)
    half = ring.half
    scalars = jnp.concatenate([ring.slot_device, d_index[None].astype(jnp.int32)])
    dp_flat = (*dp_axes, "fsdp")
    to_rows = []
    for flat in range(dp_size * size):
        to_rows.append((flat, (flat % group) * size + flat // group))
    from_rows = [(b, a) for a, b in to_rows]

    packed = jnp.concatenate(
        [w.reshape(own_rows, size, part) for w in (w_query, w_key, w_value)], axis=2
    ).transpose(1, 0, 2)
    packed = lax.all_to_all(packed, "fsdp", split_axis=0, concat_axis=0, tiled=True)
    packed = packed.reshape(size * own_rows, 3 * part)

    small = jnp.concatenate(
        [w_router.T, gain_attn[None], gain_query[None], gain_key[None], gain_ffn[None]], axis=0
    )
    small = pair_gather(small, dp_axes, dp_size)

    token_ring, small_ring = ring.gather(tokens), ring.gather(small, False)
    token_steps = [token_ring.step()]
    for k in range(half):
        small_ring.step(token_steps[0] if k > 1 else None)
    small = small_ring.stacked().transpose(2, 1, 0, 3).reshape(-1, width)
    router = jnp.pad(small[:num_experts], ((0, 2 * gate_columns - num_experts), (0, 0)))
    gains = small[num_experts:].astype(f32)
    gain_in, gain_q, gain_k, gain_mid = (gains[i][None, :] for i in range(4))
    gain_q = lax.dynamic_slice_in_dim(gain_q, f_index * part, part, 1)
    gain_k = lax.dynamic_slice_in_dim(gain_k, f_index * part, part, 1)
    half_dim = head_dim // 2
    inv_freq = rope_base ** (-(jnp.arange(half_dim, dtype=f32) * 2.0) / head_dim)
    angles = jnp.arange(span, dtype=jnp.int32).astype(f32)[:, None] * inv_freq[None, :]
    cosine, sine = jnp.cos(angles), jnp.sin(angles)
    cosine = jnp.concatenate([cosine, cosine], axis=1)
    sine = jnp.concatenate([-sine, sine], axis=1)
    out_rows = lax.ppermute(after(w_output, token_steps[0]), dp_flat, to_rows)
    token_steps.append(token_ring.step(packed))
    token_steps.append(token_ring.step())
    token_steps.append(
        token_ring.step((out_rows, router, gain_in, gain_q, gain_k, gain_mid, cosine, sine))
    )
    token_blocks = token_ring.blocks()
    w_in = share_relative(packed, dp_size, None, token_steps[2])
    w_out = share_relative(out_rows, dp_size, token_steps[2], token_steps[3])

    down_w = lax.all_gather(expert_down, dp_axes, axis=2, tiled=True)
    gate_w = lax.all_gather(expert_gate, dp_axes, axis=2, tiled=True)
    up_w = lax.all_gather(expert_up, dp_axes, axis=2, tiled=True)

    cot_ring = ring.gather(cotangent)
    cot_step = cot_ring.step(token_steps[3])
    normed, raw, in_factor, squares, x_all = project(
        ring, scalars, token_blocks, w_in, gain_in
    )
    squares = pair_sum(after(squares, (cot_step, w_out)), "fsdp", size)
    cot_step = cot_ring.step(squares)
    factors = lax.rsqrt(squares / width + epsilon)
    saved, attn_pieces = attend(
        ring, scalars, raw, factors, gain_q, gain_k, cosine, sine, w_out, head_dim
    )
    attn_ring = ring.reduce(after(attn_pieces, cot_step))
    attn_step = attn_ring.step()
    cot_step = cot_ring.step(attn_step)
    attn_ring.step()
    last_cot = cot_ring.step()
    attn_ring.step(cot_step)
    attn_ring.step(last_cot)
    resid_mid, mid_factor, mid_block, *routing = middle(
        tokens, attn_ring.last(), gain_mid, router, routes, num_experts
    )

    mid_ring = ring.gather(mid_block)
    mid_steps = [mid_ring.step()]
    mid_steps.append(mid_ring.step())
    back_act, cot_all = expert_first(
        ring, after(scalars, mid_steps[0]), cot_ring.blocks(), down_w
    )
    mid_ring.step(back_act)
    mid_ring.step()
    act, act_gated, d_gate, d_up, grad_gates, own_gates, mid_all = expert_hidden(
        ring, scalars, mid_ring.blocks(), gate_w, up_w, back_act
    )
    grad_in = expert_inputs(ring, scalars, d_gate, d_up, gate_w, up_w, grad_gates)

    def far_part(left, right, ties):
        return weight_far(after(left, ties), right)

    def cross(far, ties):
        return lax.ppermute(after(far, ties), dp_axes, exchange_pairs(dp_size, 1))

    def near_part(left, right, far, ties):
        return weight_near(scalars, after(left, ties), right, far, local_experts)

    def finish(near, ties):
        near = after(near, ties)
        return lax.psum_scatter(near, "x", scatter_dimension=0, tiled=True).astype(f32)

    grad_ring = ring.reduce(grad_in)
    grad_steps = [grad_ring.step()]
    gate_far = far_part(mid_all, d_gate, grad_in)
    grad_steps.append(grad_ring.step(gate_far))
    gate_cross = cross(gate_far, grad_steps[0])
    up_far = far_part(mid_all, d_up, grad_steps[0])
    grad_steps.append(grad_ring.step((up_far, gate_cross)))
    up_cross = cross(up_far, grad_steps[1])
    gate_near = near_part(mid_all, d_gate, gate_cross, grad_steps[1])
    grad_steps.append(grad_ring.step((gate_near, up_cross)))
    up_near = near_part(mid_all, d_up, up_cross, grad_steps[2])
    grad_resid, grad_low, grad_gain_mid, grad_router = middle_back(
        after(grad_ring.last(), up_near), cotangent, resid_mid, mid_factor,
        mid_block, *routing, gain_mid, router,
    )

    back_ring = ring.gather(grad_low)
    back_steps = [back_ring.step()]
    down_far = far_part(cot_all, act_gated, grad_low)
    back_steps.append(back_ring.step(down_far))
    down_cross = cross(down_far, back_steps[0])
    moe_pieces = expert_outputs(ring, after(scalars, back_steps[0]), act, own_gates, down_w)
    back_steps.append(back_ring.step((moe_pieces[0], down_cross)))
    down_near = near_part(cot_all, act_gated, down_cross, back_steps[1])
    back_steps.append(back_ring.step(down_near))
    grad_blocks = back_ring.blocks()

    def head_back(head, ties):
        return attend_back(
            ring, after(scalars, ties), saved, raw, factors, gain_q, gain_k, cosine, sine, w_out,
            grad_blocks, head_dim, head,
        )

    moe_ring = ring.reduce(moe_pieces)
    moe_step = moe_ring.step(back_steps[3])
    backs = [head_back(0, (back_steps[3], moe_step))]
    moe_step = moe_ring.step()
    for head in range(1, own_heads):
        backs.append(head_back(head, moe_step))
        if moe_ring.left > 1:
            moe_step = moe_ring.step(early=backs[head - 1][0])
    grad_attn_out = backs[0][6]
    dots = after(sum(back[3] for back in backs), moe_step)
    grad_gain_q = jnp.concatenate([back[4] for back in backs], axis=1)
    grad_gain_k = jnp.concatenate([back[5] for back in backs], axis=1)
    grad_w_out = dot(saved[3].astype(low), after(grad_attn_out, dots), rows_first)
    dots = pair_sum(dots, "fsdp", size) / width
    out_blocks = [
        lax.dynamic_slice_in_dim(grad_w_out, (d_index ^ k) * own_rows, own_rows, 0)
        for k in range(dp_size)
    ]
    out_far = jnp.stack([out_blocks[1], out_blocks[3]]).astype(low)
    while moe_ring.left > 0:
        moe_step = moe_ring.step(dots, backs[-1][0])
    layer_out = (resid_mid + moe_ring.total()).astype(low)
    grad_raw, grad_gain_in, normed_pieces = project_back(
        ring, scalars, [value for back in backs for value in back[:3]], raw, factors,
        after(dots, out_far), gain_q, gain_k, x_all, in_factor, w_in,
    )
    grad_w_out = combine_relative(out_far, [out_blocks[0], out_blocks[2]]).astype(low)
    normed_pieces = after(normed_pieces, (moe_step, grad_w_out))

    in_ring = ring.reduce(normed_pieces)
    in_steps = [in_ring.step()]
    grad_gains = lax.dynamic_update_slice(
        jnp.zeros((2, width), f32),
        jnp.concatenate([grad_gain_q, grad_gain_k], axis=0),
        (0, f_index * part),
    )
    sums = [grad_router[:num_experts], grad_gain_mid, grad_gain_in, grad_gains]
    sums.append(jnp.zeros((-(num_experts + 4) % 8, width), f32))
    grad_w_in = weight_rows(
        scalars, after(normed, normed_pieces), grad_raw, jnp.concatenate(sums, axis=0), dp_size
    )
    grad_gate_w = finish(gate_near, grad_ring.sent)
    grad_up_w = finish(up_near, grad_low)
    grad_down_w = finish(down_near, back_steps[3])
    in_steps.append(in_ring.step(early=grad_w_in))
    grad_w_in = combine_relative(*grad_w_in, (in_steps[0], in_steps[0])).astype(low)
    in_steps.append(in_ring.step(early=(grad_gate_w, grad_up_w)))
    in_steps.append(in_ring.step(early=grad_w_in))
    grad_normed = in_ring.total(grad_down_w)
    grad_w_in = after(grad_w_in, in_steps[2]).reshape(size, own_rows, -1)
    grad_w_in = lax.all_to_all(grad_w_in, "fsdp", split_axis=0, concat_axis=0, tiled=True)
    sums = jnp.sum(grad_w_in[:, :, 3 * part :].astype(f32), axis=0)
    grad_w_in = [
        grad_w_in[:, :, i * part : (i + 1) * part].transpose(1, 0, 2).reshape(own_rows, width)
        for i in range(3)
    ]
    grad_w_in = [values.astype(f32) for values in grad_w_in]
    grad_w_out = lax.ppermute(after(grad_w_out, in_steps[2]), dp_flat, from_rows).astype(f32)
    own_x = tokens.astype(f32)
    own_factor = lax.rsqrt(jnp.mean(own_x * own_x, axis=-1, keepdims=True) + epsilon)
    scaled_in = grad_normed * gain_in
    grad_tokens = (
        grad_resid
        + own_factor * scaled_in
        - own_x * own_factor**3 * jnp.mean(scaled_in * own_x, axis=-1, keepdims=True)
    )
    return (
        layer_out,
        grad_tokens,
        grad_w_in[0],
        grad_w_in[1],
        grad_w_in[2],
        grad_w_out,
        sums[:, :num_experts],
        sums[:, num_experts + 1],
        sums[:, num_experts + 2],
        sums[:, num_experts + 3],
        sums[:, num_experts],
        grad_gate_w,
        grad_up_w,
        grad_down_w,
    )


def splits_evenly(mesh):
    size, dp_size = mesh.shape["fsdp"], mesh.shape["dp"]
    powers = size & (size - 1) == 0 and dp_size & (dp_size - 1) == 0
    return powers and dp_size == 4 and size == 8 and HEADS % size == 0


def solution(mesh):
    split = splits_evenly(mesh)
    dp = "dp"
    if split:
        devices = mesh.devices.reshape(2, 2, mesh.shape["fsdp"])
        mesh, dp = jax.sharding.Mesh(devices, (*dp_axes, "fsdp")), dp_axes
    flat = (*dp_axes, "fsdp") if split else ("dp", "fsdp")
    in_specs = (
        P(flat, None),
        P(flat, None),
        P(flat, None),
        P(flat, None),
        P(flat, None),
        P(flat, None),
        P(flat, None),
        P(flat, None),
        P(flat),
        P(flat),
        P(flat),
        P(flat),
        P("fsdp", None, dp),
        P("fsdp", None, dp),
        P("fsdp", None, dp),
    )
    out_specs = (
        P(flat, None),
        P(flat, None),
        P(flat, None),
        P(flat, None),
        P(flat, None),
        P(flat, None),
        P(flat, None),
        P(flat),
        P(flat),
        P(flat),
        P(flat),
        P("fsdp", None, dp),
        P("fsdp", None, dp),
        P("fsdp", None, dp),
    )
    return jax.shard_map(
        per_device if split else per_device_gathered,
        mesh=mesh,
        in_specs=in_specs,
        out_specs=out_specs,
        check_vma=False,
    )
```

```python
import functools

import jax
import jax.numpy as jnp
from jax import lax
from jax.experimental import pallas as pl
from jax.experimental.pallas import tpu as pltpu
from jax.sharding import PartitionSpec as P

HEADS = 16
TOPK = 8


epsilon = 1e-05
rope_base = 10000.0
hidden_parts = 4
rest_column = 128
gate_columns = 64
sum_columns = 128
dp_axes = ("x", "core")
far_low = -1e30


def rms_norm(values, scaling):
    factor = lax.rsqrt(jnp.mean(values * values, axis=-1, keepdims=True) + epsilon)
    return values * factor * scaling


def rotary(values, positions):
    half_dim = values.shape[-1] // 2
    inv_freq = rope_base ** (-(jnp.arange(half_dim, dtype=jnp.float32) * 2.0) / values.shape[-1])
    angles = positions.astype(jnp.float32)[:, None] * inv_freq[None, :]
    cosine = jnp.cos(angles)[:, None, :]
    sine_vals = jnp.sin(angles)[:, None, :]
    first_half = values[..., :half_dim]
    second = values[..., half_dim:]
    return jnp.concatenate(
        [first_half * cosine - second * sine_vals, second * cosine + first_half * sine_vals],
        axis=-1,
    )


def head_prep(values, scaling, positions):
    normed = rms_norm(values, scaling)
    return rotary(normed.reshape(values.shape[0], HEADS, -1), positions)


def swiglu(gate_hid, up_hid):
    return jax.nn.silu(gate_hid) * up_hid


def gating(logits, routes, num_experts):
    prob_vals = jax.nn.softmax(logits, axis=-1)
    pick_table = (
        routes[:, :, None] == jnp.arange(num_experts, dtype=jnp.int32)[None, None, :]
    ).astype(jnp.float32)
    chosen = jnp.sum(pick_table * prob_vals[:, None, :], axis=-1)
    return chosen / jnp.sum(chosen, axis=-1, keepdims=True)


def per_device_gathered(
    tokens,
    cotangent,
    routes,
    w_query,
    w_key,
    w_value,
    w_output,
    w_router,
    gain_attn,
    gain_query,
    gain_key,
    gain_ffn,
    expert_gate,
    expert_up,
    expert_down,
):
    row_count = tokens.shape[0]
    model_width = tokens.shape[1]
    head_dim = model_width // HEADS
    score_scale = head_dim ** (-0.5)
    fsdp_size = lax.axis_size("fsdp")
    local_experts = expert_gate.shape[0]
    num_experts = local_experts * fsdp_size
    capacity = max(2, (row_count * TOPK * 5 + 4 * num_experts - 1) // (4 * num_experts))
    positions = lax.axis_index("fsdp") * row_count + jnp.arange(row_count, dtype=jnp.int32)
    first_pos = positions[0]
    last_pos = positions[row_count - 1]
    inputs = tokens.astype(jnp.float32)
    dense_full = (
        lax.all_gather(w_query, ("dp", "fsdp"), axis=0, tiled=True),
        lax.all_gather(w_key, ("dp", "fsdp"), axis=0, tiled=True),
        lax.all_gather(w_value, ("dp", "fsdp"), axis=0, tiled=True),
        lax.all_gather(w_output, ("dp", "fsdp"), axis=0, tiled=True),
        lax.all_gather(w_router, ("dp", "fsdp"), axis=0, tiled=True),
        lax.all_gather(gain_attn, ("dp", "fsdp"), axis=0, tiled=True),
        lax.all_gather(gain_query, ("dp", "fsdp"), axis=0, tiled=True),
        lax.all_gather(gain_key, ("dp", "fsdp"), axis=0, tiled=True),
        lax.all_gather(gain_ffn, ("dp", "fsdp"), axis=0, tiled=True),
    )
    expert_full = (
        lax.all_gather(expert_gate, "dp", axis=2, tiled=True),
        lax.all_gather(expert_up, "dp", axis=2, tiled=True),
        lax.all_gather(expert_down, "dp", axis=2, tiled=True),
    )
    query_full, key_full, value_full, output_full, router_full = dense_full[:5]
    gain_in_full = dense_full[5].astype(jnp.float32)
    gain_q_full = dense_full[6].astype(jnp.float32)
    gain_k_full = dense_full[7].astype(jnp.float32)
    gain_mid_full = dense_full[8].astype(jnp.float32)
    normed_low = rms_norm(inputs, gain_in_full).astype(jnp.bfloat16)
    query_raw = jnp.dot(normed_low, query_full, preferred_element_type=jnp.float32)
    key_raw = jnp.dot(normed_low, key_full, preferred_element_type=jnp.float32)
    value_raw = jnp.dot(normed_low, value_full, preferred_element_type=jnp.float32)
    query_low = head_prep(query_raw, gain_q_full, positions).astype(jnp.bfloat16)
    key_low = head_prep(key_raw, gain_k_full, positions).astype(jnp.bfloat16)
    value_low = value_raw.astype(jnp.bfloat16).reshape(row_count, HEADS, head_dim)
    start_state = (
        jnp.full((HEADS, row_count), far_low, jnp.float32),
        jnp.zeros((HEADS, row_count), jnp.float32),
        jnp.zeros((row_count, HEADS, head_dim), jnp.float32),
    )
    shard_piece = (
        lax.all_gather(key_low, "fsdp", axis=0, tiled=True),
        lax.all_gather(value_low, "fsdp", axis=0, tiled=True),
    )

    def attend_update(state):
        run_max, run_sum, run_acc = state
        key_piece, value_piece = shard_piece
        scores = (
            jnp.einsum("qhd,khd->hqk", query_low, key_piece, preferred_element_type=jnp.float32)
            * score_scale
        )
        key_pos = jnp.arange(key_piece.shape[0], dtype=jnp.int32)
        allowed = (key_pos[None, :] <= positions[:, None])[None]
        new_max = jnp.maximum(run_max, jnp.max(jnp.where(allowed, scores, far_low), axis=-1))
        exp_vals = jnp.where(allowed, jnp.exp(scores - new_max[..., None]), 0.0)
        factor = jnp.exp(run_max - new_max)
        run_sum = jnp.sum(exp_vals, axis=-1)
        run_acc = run_acc * factor.T[:, :, None] + jnp.einsum(
            "hqk,khd->qhd",
            exp_vals.astype(jnp.bfloat16),
            value_piece,
            preferred_element_type=jnp.float32,
        )
        return (new_max, run_sum, run_acc)

    run_max, run_sum, run_acc = lax.cond(
        jnp.int32(0) <= last_pos, attend_update, lambda state: state, start_state
    )
    attn_f32 = run_acc / run_sum.T[:, :, None]
    log_sum = run_max + jnp.log(run_sum)
    attn_low = attn_f32.reshape(row_count, model_width).astype(jnp.bfloat16)
    resid_mid = inputs + jnp.dot(attn_low, output_full, preferred_element_type=jnp.float32)
    mid_low = rms_norm(resid_mid, gain_mid_full).astype(jnp.bfloat16)
    logits = jnp.dot(mid_low, router_full, preferred_element_type=jnp.float32)
    gate_vals, gate_pull = jax.vjp(
        lambda logit_vals: gating(logit_vals, routes, num_experts), logits
    )
    route_flat = routes.reshape(-1)
    pick_table = (route_flat[:, None] == jnp.arange(num_experts, dtype=jnp.int32)[None, :]).astype(
        jnp.int32
    )
    slot_index = jnp.sum(pick_table * (jnp.cumsum(pick_table, axis=0) - 1), axis=1)
    target = route_flat * capacity + slot_index
    spread = jnp.repeat(mid_low, TOPK, axis=0)
    send_rows = (
        jnp.zeros((num_experts * capacity, model_width), jnp.bfloat16).at[target].set(spread)
    )
    send_rows = send_rows.reshape(fsdp_size, local_experts, capacity, model_width)
    arrived = lax.all_to_all(send_rows, "fsdp", split_axis=0, concat_axis=0, tiled=True)
    gate_w, up_w, down_w = expert_full
    gate_hid = jnp.einsum("secd,edh->sech", arrived, gate_w, preferred_element_type=jnp.float32)
    up_hid = jnp.einsum("secd,edh->sech", arrived, up_w, preferred_element_type=jnp.float32)
    act_low = swiglu(gate_hid, up_hid).astype(jnp.bfloat16)
    expert_out = jnp.einsum(
        "sech,edh->secd", act_low, down_w, preferred_element_type=jnp.float32
    ).astype(jnp.bfloat16)
    returned = lax.all_to_all(expert_out, "fsdp", split_axis=0, concat_axis=0, tiled=True).reshape(
        num_experts * capacity, model_width
    )
    picked = returned[target].reshape(row_count, TOPK, model_width).astype(jnp.float32)
    resid_out = resid_mid + jnp.sum(gate_vals[:, :, None] * picked, axis=1)
    layer_out = resid_out.astype(jnp.bfloat16)
    back_dense = (
        lax.all_gather(w_query, ("dp", "fsdp"), axis=0, tiled=True),
        lax.all_gather(w_key, ("dp", "fsdp"), axis=0, tiled=True),
        lax.all_gather(w_value, ("dp", "fsdp"), axis=0, tiled=True),
        lax.all_gather(w_output, ("dp", "fsdp"), axis=0, tiled=True),
        lax.all_gather(w_router, ("dp", "fsdp"), axis=0, tiled=True),
        lax.all_gather(gain_attn, ("dp", "fsdp"), axis=0, tiled=True),
        lax.all_gather(gain_query, ("dp", "fsdp"), axis=0, tiled=True),
        lax.all_gather(gain_key, ("dp", "fsdp"), axis=0, tiled=True),
        lax.all_gather(gain_ffn, ("dp", "fsdp"), axis=0, tiled=True),
    )
    back_experts = (
        lax.all_gather(expert_gate, "dp", axis=2, tiled=True),
        lax.all_gather(expert_up, "dp", axis=2, tiled=True),
        lax.all_gather(expert_down, "dp", axis=2, tiled=True),
    )
    query_back, key_back, value_back, output_back, router_back = back_dense[:5]
    gain_in_back = back_dense[5].astype(jnp.float32)
    gain_q_back = back_dense[6].astype(jnp.float32)
    gain_k_back = back_dense[7].astype(jnp.float32)
    gain_mid_back = back_dense[8].astype(jnp.float32)
    gate_back, up_back, down_back = back_experts
    grad_out = cotangent.astype(jnp.float32)
    grad_gates = jnp.sum(grad_out[:, None, :] * picked, axis=-1)
    grad_routed = (
        (gate_vals[:, :, None] * grad_out[:, None, :]).astype(jnp.bfloat16).reshape(-1, model_width)
    )
    send_grads = (
        jnp.zeros((num_experts * capacity, model_width), jnp.bfloat16).at[target].set(grad_routed)
    )
    send_grads = send_grads.reshape(fsdp_size, local_experts, capacity, model_width)
    grad_arrived = lax.all_to_all(send_grads, "fsdp", split_axis=0, concat_axis=0, tiled=True)
    gate_again = jnp.einsum(
        "secd,edh->sech", arrived, gate_back, preferred_element_type=jnp.float32
    )
    up_again = jnp.einsum("secd,edh->sech", arrived, up_back, preferred_element_type=jnp.float32)
    act_vals, act_pull = jax.vjp(swiglu, gate_again, up_again)
    act_again = act_vals.astype(jnp.bfloat16)
    grad_act = jnp.einsum(
        "secd,edh->sech", grad_arrived, down_back, preferred_element_type=jnp.float32
    )
    grad_down = jnp.einsum(
        "secd,sech->edh", grad_arrived, act_again, preferred_element_type=jnp.float32
    )
    grad_gate_hid, grad_up_hid = act_pull(grad_act)
    grad_gate_low = grad_gate_hid.astype(jnp.bfloat16)
    grad_up_low = grad_up_hid.astype(jnp.bfloat16)
    grad_gate_w = jnp.einsum(
        "secd,sech->edh", arrived, grad_gate_low, preferred_element_type=jnp.float32
    )
    grad_up_w = jnp.einsum(
        "secd,sech->edh", arrived, grad_up_low, preferred_element_type=jnp.float32
    )
    grad_inputs = jnp.einsum(
        "sech,edh->secd", grad_gate_low, gate_back, preferred_element_type=jnp.float32
    ) + jnp.einsum("sech,edh->secd", grad_up_low, up_back, preferred_element_type=jnp.float32)
    grad_returned = lax.all_to_all(
        grad_inputs.astype(jnp.bfloat16), "fsdp", split_axis=0, concat_axis=0, tiled=True
    )
    grad_returned = grad_returned.reshape(num_experts * capacity, model_width)
    grad_mid = jnp.sum(
        grad_returned[target].reshape(row_count, TOPK, model_width).astype(jnp.float32), axis=1
    )
    expert_grads = (
        lax.psum_scatter(
            grad_gate_w.astype(jnp.bfloat16), "dp", scatter_dimension=2, tiled=True
        ).astype(jnp.float32),
        lax.psum_scatter(
            grad_up_w.astype(jnp.bfloat16), "dp", scatter_dimension=2, tiled=True
        ).astype(jnp.float32),
        lax.psum_scatter(
            grad_down.astype(jnp.bfloat16), "dp", scatter_dimension=2, tiled=True
        ).astype(jnp.float32),
    )
    (grad_logits,) = gate_pull(grad_gates)
    grad_logits_low = grad_logits.astype(jnp.bfloat16)
    grad_router = jnp.einsum(
        "td,te->de", mid_low, grad_logits_low, preferred_element_type=jnp.float32
    )
    grad_mid = grad_mid + jnp.einsum(
        "te,de->td", grad_logits_low, router_back, preferred_element_type=jnp.float32
    )
    mid_value, mid_pull = jax.vjp(rms_norm, resid_mid, gain_mid_back)
    grad_resid_part, grad_gain_mid = mid_pull(grad_mid)
    grad_resid = grad_out + grad_resid_part
    grad_attn_out = grad_resid.astype(jnp.bfloat16)
    grad_output_w = jnp.einsum(
        "td,te->de", attn_low, grad_attn_out, preferred_element_type=jnp.float32
    )
    grad_attn = jnp.einsum(
        "te,de->td", grad_attn_out, output_back, preferred_element_type=jnp.float32
    )
    grad_attn = grad_attn.astype(jnp.bfloat16).reshape(row_count, HEADS, head_dim)
    delta_rows = jnp.sum(grad_attn.astype(jnp.float32) * attn_f32, axis=-1).T
    key_all, value_all = (
        lax.all_gather(key_low, "fsdp", axis=0, tiled=True),
        lax.all_gather(value_low, "fsdp", axis=0, tiled=True),
    )

    def probs_block(key_block, value_block, begin_at):
        scores = (
            jnp.einsum("qhd,khd->hqk", query_low, key_block, preferred_element_type=jnp.float32)
            * score_scale
        )
        key_pos = begin_at + jnp.arange(key_block.shape[0], dtype=jnp.int32)
        allowed = (key_pos[None, :] <= positions[:, None])[None]
        prob_vals = jnp.where(allowed, jnp.exp(scores - log_sum[..., None]), 0.0)
        grad_probs = jnp.einsum(
            "qhd,khd->hqk", grad_attn, value_block, preferred_element_type=jnp.float32
        )
        grad_scores = (prob_vals * (grad_probs - delta_rows[..., None])).astype(jnp.bfloat16)
        return (prob_vals, grad_scores)

    block_rows = 8 * row_count
    block_needed = last_pos // block_rows + 1
    zero_query = jnp.zeros((row_count, HEADS, head_dim), jnp.float32)

    def query_step(block_index, accum):
        begin_at = block_index * block_rows
        key_block = lax.dynamic_slice_in_dim(key_all, begin_at, block_rows, 0)
        value_block = lax.dynamic_slice_in_dim(value_all, begin_at, block_rows, 0)
        prob_vals, grad_scores = probs_block(key_block, value_block, begin_at)
        return accum + jnp.einsum(
            "hqk,khd->qhd", grad_scores, key_block, preferred_element_type=jnp.float32
        )

    grad_query_rot = lax.fori_loop(0, block_needed, query_step, zero_query) * score_scale
    stats_all = (
        lax.all_gather(log_sum.T, "fsdp", axis=0, tiled=True),
        lax.all_gather(delta_rows.T, "fsdp", axis=0, tiled=True),
    )
    query_piece = lax.all_gather(query_low, "fsdp", axis=0, tiled=True)
    grad_piece = lax.all_gather(grad_attn, "fsdp", axis=0, tiled=True)
    span = query_piece.shape[0]

    def add_update(state):
        lse_piece = stats_all[0].T
        delta_piece = stats_all[1].T
        scores = (
            jnp.einsum("qhd,khd->hqk", query_piece, key_low, preferred_element_type=jnp.float32)
            * score_scale
        )
        query_pos = jnp.arange(span, dtype=jnp.int32)
        allowed = (positions[None, :] <= query_pos[:, None])[None]
        prob_vals = jnp.where(allowed, jnp.exp(scores - lse_piece[..., None]), 0.0)
        grad_probs = jnp.einsum(
            "qhd,khd->hqk", grad_piece, value_low, preferred_element_type=jnp.float32
        )
        grad_scores = (prob_vals * (grad_probs - delta_piece[..., None])).astype(jnp.bfloat16)
        grad_value_acc = jnp.einsum(
            "hqk,qhd->khd",
            prob_vals.astype(jnp.bfloat16),
            grad_piece,
            preferred_element_type=jnp.float32,
        )
        grad_key_acc = jnp.einsum(
            "hqk,qhd->khd", grad_scores, query_piece, preferred_element_type=jnp.float32
        )
        return (grad_key_acc, grad_value_acc)

    grad_key_sum, grad_value_sum = lax.cond(
        jnp.int32(0) + span > first_pos, add_update, lambda state: state, (zero_query, zero_query)
    )
    grad_key_rot = grad_key_sum * score_scale
    grad_value_low = grad_value_sum.reshape(row_count, model_width).astype(jnp.bfloat16)
    query_value, query_pull = jax.vjp(
        lambda raw_vals, scaling: head_prep(raw_vals, scaling, positions), query_raw, gain_q_back
    )
    grad_query_raw, grad_gain_query = query_pull(grad_query_rot)
    key_value, key_pull = jax.vjp(
        lambda raw_vals, scaling: head_prep(raw_vals, scaling, positions), key_raw, gain_k_back
    )
    grad_key_raw, grad_gain_key = key_pull(grad_key_rot)
    grad_query_low = grad_query_raw.astype(jnp.bfloat16)
    grad_key_low = grad_key_raw.astype(jnp.bfloat16)
    grad_wq = jnp.einsum(
        "td,te->de", normed_low, grad_query_low, preferred_element_type=jnp.float32
    )
    grad_wk = jnp.einsum("td,te->de", normed_low, grad_key_low, preferred_element_type=jnp.float32)
    grad_wv = jnp.einsum(
        "td,te->de", normed_low, grad_value_low, preferred_element_type=jnp.float32
    )
    grad_normed = (
        jnp.einsum("te,de->td", grad_query_low, query_back, preferred_element_type=jnp.float32)
        + jnp.einsum("te,de->td", grad_key_low, key_back, preferred_element_type=jnp.float32)
        + jnp.einsum("te,de->td", grad_value_low, value_back, preferred_element_type=jnp.float32)
    )
    in_value, input_pull = jax.vjp(rms_norm, inputs, gain_in_back)
    grad_input_part, grad_gain_in = input_pull(grad_normed)
    grad_tokens = grad_resid + grad_input_part
    dense_grads = (
        lax.psum_scatter(grad_wq, ("dp", "fsdp"), scatter_dimension=0, tiled=True),
        lax.psum_scatter(grad_wk, ("dp", "fsdp"), scatter_dimension=0, tiled=True),
        lax.psum_scatter(grad_wv, ("dp", "fsdp"), scatter_dimension=0, tiled=True),
        lax.psum_scatter(grad_output_w, ("dp", "fsdp"), scatter_dimension=0, tiled=True),
        lax.psum_scatter(grad_router, ("dp", "fsdp"), scatter_dimension=0, tiled=True),
        lax.psum_scatter(grad_gain_in, ("dp", "fsdp"), scatter_dimension=0, tiled=True),
        lax.psum_scatter(grad_gain_query, ("dp", "fsdp"), scatter_dimension=0, tiled=True),
        lax.psum_scatter(grad_gain_key, ("dp", "fsdp"), scatter_dimension=0, tiled=True),
        lax.psum_scatter(grad_gain_mid, ("dp", "fsdp"), scatter_dimension=0, tiled=True),
    )
    return (
        layer_out,
        grad_tokens,
        dense_grads[0],
        dense_grads[1],
        dense_grads[2],
        dense_grads[3],
        dense_grads[4],
        dense_grads[5],
        dense_grads[6],
        dense_grads[7],
        dense_grads[8],
        expert_grads[0],
        expert_grads[1],
        expert_grads[2],
    )


def after(values, ties):
    if callable(ties):
        ties = ties(values)
    if ties is None:
        return values
    return lax.optimization_barrier((values, ties))[0]


class Ring:
    def __init__(self, size, rows):
        self.size = size
        self.half = size // 2
        self.rows = rows
        middle = rows // 2
        self.pieces = [(k, 0, rows) for k in range(self.half)]
        self.pieces += [(self.half, 0, middle), (self.half, middle, middle)]
        self.pieces += [(k, 0, rows) for k in range(self.half + 1, size)]
        self.order = list(range(0, size, 2)) + list(range(size - 1, 0, -2))
        place = [self.order.index(i) for i in range(size)]
        rank = jnp.asarray(place, jnp.int32)[lax.axis_index("fsdp")]
        self.slot_device = jnp.asarray(self.order, jnp.int32)[
            (rank + jnp.arange(size, dtype=jnp.int32)) % size
        ]
        self.device_slot = (jnp.asarray(place, jnp.int32) - rank) % size
        self.up = [(self.order[i], self.order[(i + 1) % size]) for i in range(size)]
        self.down = [(self.order[i], self.order[i - 1]) for i in range(size)]

    def forward(self, values):
        return lax.ppermute(values, "fsdp", self.up)

    def backward(self, values):
        return lax.ppermute(values, "fsdp", self.down)

    def gather(self, block, halves=True):
        return Gather(self, block, halves)

    def reduce(self, pieces):
        return Reduce(self, pieces)


def add_pair_kernel(upper, rising, lower, falling, first, second):
    count, arrived = upper.shape[0], rising.shape[0]
    first[:arrived, :] = upper[:arrived, :] + rising[...]
    second[count - arrived :, :] = lower[count - arrived :, :] + falling[...]
    if arrived < count:
        first[arrived:, :] = upper[arrived:, :]
        second[: count - arrived, :] = lower[: count - arrived, :]


def add_pair(upper, rising, lower, falling):
    shape = jax.ShapeDtypeStruct(upper.shape, upper.dtype)
    return pl.pallas_call(add_pair_kernel, out_shape=[shape, shape], name="add_pair")(
        upper, rising, lower, falling
    )


class Gather:
    def __init__(self, ring, block, halves=True):
        self.ring, self.halves = ring, halves
        self.low, self.high, self.opposite = [block], [block], None

    def step(self, ties=None):
        ring, middle = self.ring, self.ring.rows // 2
        from_low, from_high = after((self.low[-1], self.high[-1]), ties)
        if len(self.low) < ring.half:
            self.low.append(ring.forward(from_low))
            self.high.append(ring.backward(from_high))
            return self.low[-1], self.high[-1]
        if self.halves:
            self.opposite = [ring.forward(from_low[:middle]), ring.backward(from_high[middle:])]
        else:
            self.opposite = [ring.forward(from_low)]
        return tuple(self.opposite)

    def stacked(self):
        return jnp.stack(self.blocks())[self.ring.device_slot]

    def blocks(self):
        return self.high + self.opposite + self.low[:0:-1]


class Reduce:
    def __init__(self, ring, pieces):
        self.ring, self.pieces, self.arrived, self.left = ring, pieces, None, ring.half

    def step(self, ties=None, early=None):
        ring, pieces = self.ring, self.pieces
        if self.arrived is None:
            upper, lower = pieces[ring.half], pieces[ring.half + 1]
        else:
            rising, falling = after(self.arrived, early)
            upper, lower = pieces[self.left], pieces[-self.left]
            upper, lower = add_pair(upper, rising, lower, falling)
        upper, lower = after((upper, lower), ties)
        self.sent = (upper, lower)
        self.arrived = (ring.forward(upper), ring.backward(lower))
        self.left -= 1
        return self.arrived

    def last(self):
        return self.pieces[0], *self.arrived

    def total(self, early=None):
        rising, falling = after(self.arrived, early)
        return (
            self.pieces[0].astype(jnp.float32)
            + rising.astype(jnp.float32)
            + falling.astype(jnp.float32)
        )


def exchange_pairs(size, bit):
    return [(i, i ^ bit) for i in range(size)]


def pair_sum(values, axis, size):
    bit = 1
    while bit < size:
        values = values + lax.ppermute(values, axis, exchange_pairs(size, bit))
        bit *= 2
    return values


def pair_gather(values, axis, size, ties=()):
    ties = dict(ties)
    mine = lax.axis_index(axis)
    values = values[None]
    bit = 1
    while bit < size:
        values = after(values, ties.get(bit))
        other = lax.ppermute(values, axis, exchange_pairs(size, bit))
        upper = (mine & bit) != 0
        values = jnp.where(
            upper,
            jnp.concatenate([other, values], axis=0),
            jnp.concatenate([values, other], axis=0),
        )
        bit *= 2
    return values


def share_relative(block, size, ties=(), second=()):
    block = after(block, ties)
    held = {0: block}
    bit = size // 2
    while bit >= 1:
        for index in list(held):
            sent = held[index] if index == 0 else after(held[index], second)
            held[index ^ bit] = lax.ppermute(sent, dp_axes, exchange_pairs(size, bit))
        bit //= 2
    return [held[index] for index in range(size)]


def combine_relative(far, near, ties=(None, None)):
    far = lax.ppermute(after(far, ties[0]), dp_axes, exchange_pairs(4, 1))
    other = near[1] + far[1].astype(jnp.float32)
    other = after(other.astype(jnp.bfloat16), ties[1])
    other = lax.ppermute(other, dp_axes, exchange_pairs(4, 2))
    return near[0] + far[0].astype(jnp.float32) + other.astype(jnp.float32)


anywhere = pl.BlockSpec(memory_space=pl.ANY)
rows_first = (((0,), (0,)), ((), ()))
columns_last = (((1,), (1,)), ((), ()))


def dot(left, right, dims=(((1,), (0,)), ((), ()))):
    return lax.dot_general(left, right, dims, preferred_element_type=jnp.float32)


def low_terms(values, count):
    terms = []
    for _ in range(count):
        terms.append(values.astype(jnp.bfloat16))
        values = values - terms[-1].astype(jnp.float32)
    return terms


def row_sums(*columns):
    total = None
    for i, values in enumerate(columns):
        place = lax.broadcasted_iota(jnp.int32, (8, values.shape[1]), 0) == i
        place = jnp.where(place, 1.0, 0.0).astype(jnp.bfloat16)
        for term in low_terms(values, 2):
            sums = dot(place, term, columns_last)
            total = sums if total is None else total + sums
    return total


def as_columns(rows):
    return rows_as_columns(rows, 8)


def rows_as_columns(rows, columns):
    shape = (rows.shape[0], columns)
    same = lax.broadcasted_iota(jnp.int32, shape, 0) == lax.broadcasted_iota(jnp.int32, shape, 1)
    same = jnp.where(same, 1.0, 0.0).astype(jnp.bfloat16)
    return sum(dot(term, same, rows_first) for term in low_terms(rows, 3))


def whole_block(shape):
    return pl.BlockSpec(shape, lambda *_: (0,) * len(shape))


def piece_copies(pieces, scalars, blocks, target, sems, first_column=0):
    rows = pieces[0][2]
    columns = pl.ds(first_column, target.shape[1])
    copies = []
    for i, (slot, first, count) in enumerate(pieces):
        begin = pl.multiple_of(scalars[slot] * rows + first, count)
        copies.append(
            pltpu.make_async_copy(
                blocks[i].at[:, columns], target.at[pl.ds(begin, count), :], sems.at[i]
            )
        )
    return copies


def piece_results(pieces, scalars, source, blocks, sems):
    rows = pieces[0][2]
    copies = []
    for i, (slot, first, count) in enumerate(pieces):
        begin = pl.multiple_of(scalars[slot] * rows + first, count)
        copies.append(
            pltpu.make_async_copy(source.at[pl.ds(begin, count), :], blocks[i], sems.at[i])
        )
    return copies


def row_copies(scalars, which, blocks, target, sems):
    own = scalars[which]
    count = blocks[0].shape[0]
    return [
        pltpu.make_async_copy(
            block, target.at[pl.ds(pl.multiple_of((own ^ i) * count, count), count), :], sems.at[i]
        )
        for i, block in enumerate(blocks)
    ]


def run_copies(copies):
    for copy in copies:
        copy.start()
    for copy in copies:
        copy.wait()


def piece_shapes(pieces, width):
    return [jax.ShapeDtypeStruct((count, width), jnp.bfloat16) for _, _, count in pieces]


def project_kernel(pieces, parts, chunk, scalars, *refs):
    n = len(pieces)
    blocks, weights, gain = refs[:n], refs[n : n + parts], refs[n + parts]
    normed, raw, factor, squares, kept, tokens, weight, sems, w_sems, k_sem = refs[n + parts + 1 :]
    step = pl.program_id(0)

    @pl.when(step == 0)
    def _():
        run_copies(
            piece_copies(pieces, scalars, blocks, tokens, sems)
            + row_copies(scalars, len(scalars) - 1, weights, weight, w_sems)
        )
        pltpu.make_async_copy(tokens, kept, k_sem).start()

    rows = pl.ds(pl.multiple_of(step * chunk, chunk), chunk)
    values = tokens[rows, :].astype(jnp.float32)
    scale = lax.rsqrt(jnp.mean(values * values, axis=-1, keepdims=True) + epsilon)
    low = (values * scale * gain[...]).astype(jnp.bfloat16)
    normed[...] = low
    factor[...] = scale
    product = dot(low, weight[...])
    raw[...] = product
    part = product.shape[1] // 3
    squares[...] = row_sums(product[:, :part] ** 2, product[:, part : 2 * part] ** 2)

    @pl.when(step == pl.num_programs(0) - 1)
    def _():
        pltpu.make_async_copy(tokens, kept, k_sem).wait()


def project(ring, scalars, blocks, weights, gain):
    width = blocks[0].shape[1]
    span = ring.rows * ring.size
    columns = weights[0].shape[1]
    chunk = min(256, span)
    n = len(ring.pieces)
    by_rows = lambda i, s: (i, 0)
    return pl.pallas_call(
        functools.partial(project_kernel, ring.pieces, len(weights), chunk),
        grid_spec=pltpu.PrefetchScalarGridSpec(
            num_scalar_prefetch=1,
            grid=(span // chunk,),
            in_specs=[anywhere] * (n + len(weights)) + [whole_block((1, width))],
            out_specs=[
                pl.BlockSpec((chunk, width), by_rows),
                pl.BlockSpec((chunk, columns), by_rows),
                pl.BlockSpec((chunk, 1), by_rows),
                pl.BlockSpec((8, chunk), lambda i, s: (0, i)),
                anywhere,
            ],
            scratch_shapes=[
                pltpu.VMEM((span, width), jnp.bfloat16),
                pltpu.VMEM((width, columns), jnp.bfloat16),
                pltpu.SemaphoreType.DMA((n,)),
                pltpu.SemaphoreType.DMA((len(weights),)),
                pltpu.SemaphoreType.DMA,
            ],
        ),
        out_shape=[
            jax.ShapeDtypeStruct((span, width), jnp.bfloat16),
            jax.ShapeDtypeStruct((span, columns), jnp.float32),
            jax.ShapeDtypeStruct((span, 1), jnp.float32),
            jax.ShapeDtypeStruct((8, span), jnp.float32),
            jax.ShapeDtypeStruct((span, width), jnp.bfloat16),
        ],
        name="project",
    )(scalars, *blocks, *weights, gain)


def turned(values, cosine, sine):
    return values * cosine + pltpu.roll(values, values.shape[-1] // 2, 1) * sine


def attend_kernel(pieces, parts, chunk, scale, scalars, *refs):
    q_raw, k_raw, v_raw, factors, gain_q, gain_k, cosine, sine = refs[:8]
    weights = refs[8 : 8 + parts]
    query, key, value, mixed, lse = refs[8 + parts : 13 + parts]
    n = len(pieces)
    results = refs[13 + parts : 13 + parts + n]
    weight, total, summed, w_sems, sems = refs[13 + parts + n :]
    head = pl.program_id(0)
    last = pl.num_programs(0) - 1
    tokens, head_dim = query.shape

    @pl.when(head == 0)
    def _():
        run_copies(row_copies(scalars, len(scalars) - 1, weights, weight, w_sems))

    columns = as_columns(factors[...])
    query[...] = turned(
        q_raw[...] * columns[:, 0:1] * gain_q[...], cosine[...], sine[...]
    ).astype(jnp.bfloat16)
    key[...] = turned(
        k_raw[...] * columns[:, 1:2] * gain_k[...], cosine[...], sine[...]
    ).astype(jnp.bfloat16)
    value[...] = v_raw[...].astype(jnp.bfloat16)
    own_rows = weight[pl.ds(pl.multiple_of(head * head_dim, head_dim), head_dim), :]
    for begin in range(0, tokens, chunk):
        rows, seen = pl.ds(begin, chunk), pl.ds(0, begin + chunk)
        scores = dot(query[rows, :], key[seen, :], columns_last) * scale
        shape = scores.shape
        allowed = lax.broadcasted_iota(jnp.int32, shape, 1) <= begin + lax.broadcasted_iota(
            jnp.int32, shape, 0
        )
        scores = jnp.where(allowed, scores, far_low)
        top = jnp.max(scores, axis=-1, keepdims=True)
        weights_now = jnp.exp(scores - top)
        sums = jnp.sum(weights_now, axis=-1, keepdims=True)
        out = dot(weights_now.astype(jnp.bfloat16), value[seen, :]) / sums
        mixed[rows, :] = out
        lse[rows, :] = top + jnp.log(sums)
        product = dot(out.astype(jnp.bfloat16), own_rows)

        @pl.when(head == 0)
        def _():
            total[rows, :] = product

        @pl.when(jnp.logical_and(head > 0, head < last))
        def _():
            total[rows, :] += product

        @pl.when(jnp.logical_and(head > 0, head == last))
        def _():
            summed[rows, :] = (total[rows, :] + product).astype(jnp.bfloat16)

        @pl.when(jnp.logical_and(head == 0, head == last))
        def _():
            summed[rows, :] = product.astype(jnp.bfloat16)

    @pl.when(head == last)
    def _():
        run_copies(piece_results(pieces, scalars, summed, results, sems))


def attend(ring, scalars, raw, factors, gain_q, gain_k, cosine, sine, weights, head_dim):
    tokens = raw.shape[0]
    part = raw.shape[1] // 3
    heads = part // head_dim
    width = weights[0].shape[1]
    n = len(ring.pieces)
    column = lambda first: pl.BlockSpec((tokens, head_dim), lambda h, s: (0, first + h))
    gain = pl.BlockSpec((1, head_dim), lambda h, s: (0, h))
    table = whole_block((tokens, head_dim))
    low = jax.ShapeDtypeStruct((tokens, part), jnp.bfloat16)
    out = pl.pallas_call(
        functools.partial(
            attend_kernel, ring.pieces, len(weights), min(512, tokens), head_dim ** (-0.5)
        ),
        grid_spec=pltpu.PrefetchScalarGridSpec(
            num_scalar_prefetch=1,
            grid=(heads,),
            in_specs=[column(0), column(heads), column(2 * heads), whole_block((8, tokens))]
            + [gain, gain, table, table]
            + [anywhere] * len(weights),
            out_specs=[column(0)] * 4
            + [pl.BlockSpec((None, tokens, 1), lambda h, s: (h, 0, 0))]
            + [anywhere] * n,
            scratch_shapes=[
                pltpu.VMEM((part, width), jnp.bfloat16),
                pltpu.VMEM((tokens, width), jnp.float32),
                pltpu.VMEM((tokens, width), jnp.bfloat16),
                pltpu.SemaphoreType.DMA((len(weights),)),
                pltpu.SemaphoreType.DMA((n,)),
            ],
        ),
        out_shape=[low, low, low, jax.ShapeDtypeStruct((tokens, part), jnp.float32)]
        + [jax.ShapeDtypeStruct((heads, tokens, 1), jnp.float32)]
        + piece_shapes(ring.pieces, width),
        name="attend",
    )(scalars, raw, raw, raw, factors, gain_q, gain_k, cosine, sine, *weights)
    return out[:5], out[5:]


def attend_back_kernel(pieces, parts, chunk, scale, head, scalars, *refs):
    query, key, value, mixed, lse, q_raw, k_raw, factors, gain_q, gain_k, cosine, sine = refs[:12]
    n = len(pieces)
    weights = refs[12 : 12 + parts]
    blocks = refs[12 + parts : 12 + parts + n]
    outs = refs[12 + parts + n :]
    turn_q, turn_k, d_value, dots, sum_q, sum_k = outs[:6]
    kept = outs[6] if head == 0 else None
    weight, grads, d_key, d_val, d_query, w_sems, sems, k_sem = outs[-8:]
    tokens, head_dim = query.shape
    run_copies(
        row_copies(scalars, len(scalars) - 1, weights, weight, w_sems)
        + piece_copies(pieces, scalars, blocks, grads, sems)
    )
    if kept is not None:
        pltpu.make_async_copy(grads, kept, k_sem).start()
    own_rows = weight[pl.ds(head * head_dim, head_dim), :]
    for begin in range(0, tokens, chunk):
        rows, seen = pl.ds(begin, chunk), pl.ds(0, begin + chunk)
        grad = dot(grads[rows, :], own_rows, columns_last).astype(jnp.bfloat16)
        queries = query[rows, :]
        scores = dot(queries, key[seen, :], columns_last) * scale
        shape = scores.shape
        allowed = lax.broadcasted_iota(jnp.int32, shape, 1) <= begin + lax.broadcasted_iota(
            jnp.int32, shape, 0
        )
        probs = jnp.where(allowed, jnp.exp(scores - lse[rows, :]), 0.0)
        delta = jnp.sum(grad.astype(jnp.float32) * mixed[rows, :], axis=-1, keepdims=True)
        grad_probs = dot(grad, value[seen, :], columns_last)
        grad_scores = (probs * (grad_probs - delta)).astype(jnp.bfloat16)
        d_query[rows, :] = dot(grad_scores, key[seen, :]) * scale
        part_key = dot(grad_scores, queries, rows_first) * scale
        part_value = dot(probs.astype(jnp.bfloat16), grad, rows_first)
        if begin > 0:
            before = pl.ds(0, begin)
            d_key[before, :] += part_key[:begin]
            d_val[before, :] += part_value[:begin]
        d_key[rows, :] = part_key[begin:]
        d_val[rows, :] = part_value[begin:]
    d_value[...] = d_val[...].astype(jnp.bfloat16)
    back_q = turned(d_query[...], cosine[...], -sine[...])
    back_k = turned(d_key[...], cosine[...], -sine[...])
    turn_q[...] = back_q
    turn_k[...] = back_k
    with_q, with_k = back_q * q_raw[...], back_k * k_raw[...]
    columns = as_columns(factors[...])
    sum_q[...] = jnp.sum(with_q * columns[:, 0:1], axis=0, keepdims=True)
    sum_k[...] = jnp.sum(with_k * columns[:, 1:2], axis=0, keepdims=True)
    dots[...] = row_sums(with_q * gain_q[...], with_k * gain_k[...])
    if kept is not None:
        pltpu.make_async_copy(grads, kept, k_sem).wait()


def attend_back(
    ring, scalars, saved, raw, factors, gain_q, gain_k, cosine, sine, weights, blocks, head_dim,
    head,
):
    query, key, value, mixed, lse = saved
    tokens, part = query.shape
    heads = part // head_dim
    width = weights[0].shape[1]
    n = len(ring.pieces)
    column = lambda first: pl.BlockSpec((tokens, head_dim), lambda i, s: (0, first + head))
    gain = pl.BlockSpec((1, head_dim), lambda i, s: (0, head))
    table = whole_block((tokens, head_dim))
    result = jax.ShapeDtypeStruct((tokens, head_dim), jnp.float32)
    sums = jax.ShapeDtypeStruct((1, head_dim), jnp.float32)
    kept = [anywhere] if head == 0 else []
    accumulate = pltpu.VMEM((tokens, head_dim), jnp.float32)
    return pl.pallas_call(
        functools.partial(
            attend_back_kernel, ring.pieces, len(weights), min(256, tokens), head_dim ** (-0.5),
            head,
        ),
        grid_spec=pltpu.PrefetchScalarGridSpec(
            num_scalar_prefetch=1,
            grid=(1,),
            in_specs=[column(0)] * 4
            + [pl.BlockSpec((None, tokens, 1), lambda i, s: (head, 0, 0))]
            + [column(0), column(heads), whole_block((8, tokens)), gain, gain, table, table]
            + [anywhere] * (len(weights) + n),
            out_specs=[table] * 3
            + [whole_block((8, tokens))]
            + [whole_block((1, head_dim))] * 2
            + kept,
            scratch_shapes=[
                pltpu.VMEM((part, width), jnp.bfloat16),
                pltpu.VMEM((tokens, width), jnp.bfloat16),
                accumulate,
                accumulate,
                accumulate,
                pltpu.SemaphoreType.DMA((len(weights),)),
                pltpu.SemaphoreType.DMA((n,)),
                pltpu.SemaphoreType.DMA,
            ],
        ),
        out_shape=[
            result,
            result,
            jax.ShapeDtypeStruct((tokens, head_dim), jnp.bfloat16),
            jax.ShapeDtypeStruct((8, tokens), jnp.float32),
            sums,
            sums,
        ]
        + [jax.ShapeDtypeStruct((tokens, width), jnp.bfloat16)] * len(kept),
        name="attend_back",
    )(
        scalars, query, key, value, mixed, lse, raw, raw, factors, gain_q, gain_k, cosine, sine,
        *weights, *blocks,
    )


def project_back_kernel(pieces, parts, chunk, heads, scalars, *refs):
    turns, refs = refs[: 3 * heads], refs[3 * heads :]
    raw, factors, dots, gain_q, gain_k, tokens, in_factor = refs[:7]
    n = len(pieces)
    weights = refs[7 : 7 + parts]
    grad_raw, sum_in = refs[7 + parts : 9 + parts]
    results = refs[9 + parts : 9 + parts + n]
    weight, summed, w_sems, sems = refs[9 + parts + n :]
    step = pl.program_id(0)
    head_dim = turns[0].shape[1]
    part = heads * head_dim

    @pl.when(step == 0)
    def _():
        run_copies(row_copies(scalars, len(scalars) - 1, weights, weight, w_sems))
        sum_in[...] = jnp.zeros_like(sum_in)

    factor_columns, dot_columns = as_columns(factors[...]), as_columns(dots[...])
    for i, gain in enumerate((gain_q, gain_k)):
        factor = factor_columns[:, i : i + 1]
        cubed = factor * factor * factor * dot_columns[:, i : i + 1]
        for head in range(heads):
            columns = pl.ds(i * part + head * head_dim, head_dim)
            turn = turns[3 * head + i][...] * gain[:, head * head_dim : (head + 1) * head_dim]
            grad_raw[:, columns] = (factor * turn - raw[:, columns] * cubed).astype(jnp.bfloat16)
    for head in range(heads):
        grad_raw[:, pl.ds(2 * part + head * head_dim, head_dim)] = turns[3 * head + 2][...]
    normed = dot(grad_raw[...], weight[...], columns_last)
    sum_in[...] += jnp.sum(
        normed * (tokens[...].astype(jnp.float32) * in_factor[...]), axis=0, keepdims=True
    )
    summed[pl.ds(pl.multiple_of(step * chunk, chunk), chunk), :] = normed.astype(jnp.bfloat16)

    @pl.when(step == pl.num_programs(0) - 1)
    def _():
        run_copies(piece_results(pieces, scalars, summed, results, sems))


def project_back(
    ring, scalars, turns, raw, factors, dots, gain_q, gain_k, tokens, in_factor, weights
):
    span, width = tokens.shape
    heads, head_dim = len(turns) // 3, turns[0].shape[1]
    part = heads * head_dim
    columns = weights[0].shape[1]
    chunk = min(256, span)
    n = len(ring.pieces)
    by_rows = lambda wide: pl.BlockSpec((chunk, wide), lambda i, s: (i, 0))
    out = pl.pallas_call(
        functools.partial(project_back_kernel, ring.pieces, len(weights), chunk, heads),
        grid_spec=pltpu.PrefetchScalarGridSpec(
            num_scalar_prefetch=1,
            grid=(span // chunk,),
            in_specs=[by_rows(head_dim)] * (3 * heads)
            + [by_rows(columns)]
            + [pl.BlockSpec((8, chunk), lambda i, s: (0, i))] * 2
            + [whole_block((1, part))] * 2
            + [by_rows(width), by_rows(1)]
            + [anywhere] * len(weights),
            out_specs=[by_rows(columns), whole_block((1, width))] + [anywhere] * n,
            scratch_shapes=[
                pltpu.VMEM((width, columns), jnp.bfloat16),
                pltpu.VMEM((span, width), jnp.bfloat16),
                pltpu.SemaphoreType.DMA((len(weights),)),
                pltpu.SemaphoreType.DMA((n,)),
            ],
        ),
        out_shape=[
            jax.ShapeDtypeStruct((span, columns), jnp.bfloat16),
            jax.ShapeDtypeStruct((1, width), jnp.float32),
        ]
        + piece_shapes(ring.pieces, width),
        name="project_back",
    )(
        scalars, *turns, raw, factors, dots, gain_q, gain_k, tokens, in_factor, *weights
    )
    return out[0], out[1], out[2:]


def expert_column(scalars, part, parts, wide):
    half = parts // 2
    relative = 2 * (part % half) + jnp.where(part < half, 1, 0)
    return pl.multiple_of((scalars[len(scalars) - 1] ^ relative) * wide, wide)


def weight_copies(groups, scalars, buffers, sems, step, parts):
    expert, part, place = step // parts, step % parts, step % 2
    wide = buffers.shape[2] // len(groups)
    columns = pl.ds(expert_column(scalars, part, parts, wide), wide)
    return [
        pltpu.make_async_copy(
            group.at[expert, :, columns],
            buffers.at[place, :, pl.ds(g * wide, wide)],
            sems.at[place, g],
        )
        for g, group in enumerate(groups)
    ]


def stream(groups, scalars, buffers, sems, parts):
    step = pl.program_id(0)

    @pl.when(step == 0)
    def _():
        for copy in weight_copies(groups, scalars, buffers, sems, step, parts):
            copy.start()

    @pl.when(step + 1 < pl.num_programs(0))
    def _():
        for copy in weight_copies(groups, scalars, buffers, sems, step + 1, parts):
            copy.start()

    for copy in weight_copies(groups, scalars, buffers, sems, step, parts):
        copy.wait()
    return buffers.at[step % 2]


def middle_kernel(experts, tokens, first, rising, falling, gain, router, routes, *refs):
    resid, factor, block, gates, probs, mask, total = refs
    width = tokens.shape[1]
    values = tokens[...].astype(jnp.float32) + (
        first[...].astype(jnp.float32)
        + rising[...].astype(jnp.float32)
        + falling[...].astype(jnp.float32)
    )
    resid[...] = values
    scale = lax.rsqrt(jnp.mean(values * values, axis=-1, keepdims=True) + epsilon)
    factor[...] = scale
    low = (values * scale * gain[...]).astype(jnp.bfloat16)
    block[:, :width] = low
    logits = dot(low, router[...], columns_last)
    column = lax.broadcasted_iota(jnp.int32, logits.shape, 1)
    real = column < experts
    top = jnp.max(jnp.where(real, logits, far_low), axis=-1, keepdims=True)
    weights = jnp.where(real, jnp.exp(logits - top), 0.0)
    prob_vals = weights / jnp.sum(weights, axis=-1, keepdims=True)
    chosen_mask = jnp.zeros(logits.shape, jnp.float32)
    for j in range(routes.shape[1]):
        chosen_mask = jnp.where(column == routes[:, j : j + 1], 1.0, chosen_mask)
    chosen = chosen_mask * prob_vals
    chosen_sum = jnp.sum(chosen, axis=-1, keepdims=True)
    gate_vals = chosen / chosen_sum
    gates[...], probs[...], mask[...], total[...] = gate_vals, prob_vals, chosen_mask, chosen_sum
    high = gate_vals.astype(jnp.bfloat16).astype(jnp.float32)
    rest = pltpu.roll(gate_vals - high, gate_columns, 1)
    block[:, width:] = (high + rest).astype(jnp.bfloat16)


def middle(tokens, sums, gain, router, routes, experts):
    rows, width = tokens.shape
    lanes = 2 * gate_columns
    table = jax.ShapeDtypeStruct((rows, lanes), jnp.float32)
    column = jax.ShapeDtypeStruct((rows, 1), jnp.float32)
    return pl.pallas_call(
        functools.partial(middle_kernel, experts),
        out_shape=[
            jax.ShapeDtypeStruct((rows, width), jnp.float32),
            column,
            jax.ShapeDtypeStruct((rows, width + lanes), jnp.bfloat16),
            table,
            table,
            table,
            column,
        ],
        name="middle",
    )(tokens, *sums, gain, router, routes)


def middle_back_kernel(first, rising, falling, cotangent, resid, factor, block, *refs):
    gates, probs, mask, total, gain, router = refs[:6]
    grad_resid, grad_low, sum_gain, grad_router = refs[6:]
    width = resid.shape[1]
    summed = (
        first[...].astype(jnp.float32)
        + rising[...].astype(jnp.float32)
        + falling[...].astype(jnp.float32)
    )
    lanes = 2 * gate_columns
    gates_back = summed[:, width : width + lanes]
    gates_back = gates_back + summed[:, width + rest_column : width + rest_column + lanes]
    inner = jnp.sum(gates_back * gates[...], axis=-1, keepdims=True)
    grad_probs = mask[...] * ((gates_back - inner) / total[...])
    grad_logits = probs[...] * (
        grad_probs - jnp.sum(probs[...] * grad_probs, axis=-1, keepdims=True)
    )
    logits_low = grad_logits.astype(jnp.bfloat16)
    grad_router[...] = dot(logits_low, block[:, :width], rows_first)
    grad_mid = summed[:, :width] + dot(logits_low, router[...])
    scale, values = factor[...], resid[...]
    scaled = grad_mid * gain[...]
    sum_gain[...] = jnp.sum(grad_mid * values * scale, axis=0, keepdims=True)
    mean = jnp.mean(scaled * values, axis=-1, keepdims=True)
    result = (
        cotangent[...].astype(jnp.float32)
        + scale * scaled
        - values * (scale * scale * scale * mean)
    )
    grad_resid[...] = result
    grad_low[...] = result.astype(jnp.bfloat16)


def middle_back(sums, cotangent, resid, factor, block, gates, probs, mask, total, gain, router):
    rows, width = resid.shape
    return pl.pallas_call(
        middle_back_kernel,
        out_shape=[
            jax.ShapeDtypeStruct((rows, width), jnp.float32),
            jax.ShapeDtypeStruct((rows, width), jnp.bfloat16),
            jax.ShapeDtypeStruct((1, width), jnp.float32),
            jax.ShapeDtypeStruct((2 * gate_columns, width), jnp.float32),
        ],
        name="middle_back",
    )(*sums, cotangent, resid, factor, block, gates, probs, mask, total, gain, router)


def turn_columns(rows_all, result):
    wide = result.shape[0]
    columns = pl.ds(pl.multiple_of(pl.program_id(0) * wide, wide), wide)
    result[...] = rows_all[:, columns].T


def expert_first_kernel(pieces, parts, chunk, scalars, *refs):
    n = len(pieces)
    blocks, down = refs[:n], refs[n]
    product, turned_rows, rows_all, buffers, sems, w_sems = refs[n + 1 :]
    step = pl.program_id(0)

    @pl.when(step == 0)
    def _():
        copies = piece_copies(pieces, scalars, blocks, rows_all, sems)
        for copy in copies:
            copy.start()

    weight = stream([down], scalars, buffers, w_sems, parts)

    @pl.when(step == 0)
    def _():
        for copy in piece_copies(pieces, scalars, blocks, rows_all, sems):
            copy.wait()

    for begin in range(0, rows_all.shape[0], chunk):
        rows = pl.ds(begin, chunk)
        product[rows, :] = dot(rows_all[rows, :], weight[...])
    turn_columns(rows_all, turned_rows)


def expert_first(ring, scalars, blocks, down):
    experts, width, hidden = down.shape
    parts = hidden_parts
    step_hidden = hidden // parts
    span = ring.rows * ring.size
    n = len(ring.pieces)
    return pl.pallas_call(
        functools.partial(expert_first_kernel, ring.pieces, parts, min(256, span)),
        grid_spec=pltpu.PrefetchScalarGridSpec(
            num_scalar_prefetch=1,
            grid=(experts * parts,),
            in_specs=[anywhere] * (n + 1),
            out_specs=[
                pl.BlockSpec((None, span, step_hidden), lambda i, s: (i // parts, 0, i % parts)),
                pl.BlockSpec((width // (experts * parts), span), lambda i, s: (i, 0)),
            ],
            scratch_shapes=[
                pltpu.VMEM((span, width), jnp.bfloat16),
                pltpu.VMEM((2, width, step_hidden), jnp.bfloat16),
                pltpu.SemaphoreType.DMA((n,)),
                pltpu.SemaphoreType.DMA((2, 1)),
            ],
        ),
        out_shape=[
            jax.ShapeDtypeStruct((experts, span, parts * step_hidden), jnp.float32),
            jax.ShapeDtypeStruct((width, span), jnp.bfloat16),
        ],
        name="expert_first",
    )(scalars, *blocks, down)


def expert_hidden_kernel(pieces, parts, chunk, scalars, *refs):
    n = len(pieces)
    blocks, gate, up = refs[:n], refs[n], refs[n + 1]
    product = refs[n + 2]
    act, gated, d_gate, d_up, grad_gates, gates, turned_rows = refs[n + 3 : n + 10]
    rows_all, gates_all, buffers, sems, g_sems, w_sems = refs[n + 10 :]
    step = pl.program_id(0)
    experts = gates.shape[0]
    g_copies = piece_copies(pieces, scalars, blocks, gates_all, g_sems, rows_all.shape[1])

    @pl.when(step == 0)
    def _():
        for copy in piece_copies(pieces, scalars, blocks, rows_all, sems) + g_copies:
            copy.start()

    weight = stream([gate, up], scalars, buffers, w_sems, parts)

    @pl.when(step == 0)
    def _():
        for copy in piece_copies(pieces, scalars, blocks, rows_all, sems) + g_copies:
            copy.wait()
        values = gates_all[...].astype(jnp.float32)
        column = lax.broadcasted_iota(jnp.int32, values.shape, 1) % gate_columns
        for expert in range(experts):
            own = scalars[0] * experts + expert
            gates[expert] = jnp.sum(
                jnp.where(column == own, values, 0.0), axis=-1, keepdims=True
            )

    @pl.when(step % parts == 0)
    def _():
        grad_gates[...] = jnp.zeros_like(grad_gates)

    for begin in range(0, rows_all.shape[0], chunk):
        rows = pl.ds(begin, chunk)
        both = dot(rows_all[rows, :], weight[...])
        gate_hid, up_hid = both[:, : act.shape[1]], both[:, act.shape[1] :]
        own_gate = gates[step // parts, rows, :]
        back = product[rows, :]
        sig = 0.5 + 0.5 * jnp.tanh(0.5 * gate_hid)
        silu = gate_hid * sig
        act_low = (silu * up_hid).astype(jnp.bfloat16)
        act_now = act_low.astype(jnp.float32)
        act[rows, :] = act_low
        gated[rows, :] = (own_gate * act_now).astype(jnp.bfloat16)
        grad_gates[rows, :] += jnp.sum(act_now * back, axis=-1, keepdims=True)
        grad_act = own_gate * back
        d_gate[rows, :] = (grad_act * up_hid * (sig * (1.0 + gate_hid * (1.0 - sig)))).astype(
            jnp.bfloat16
        )
        d_up[rows, :] = (grad_act * silu).astype(jnp.bfloat16)

    turn_columns(rows_all, turned_rows)


def hidden_place(parts, experts):
    half = parts // 2
    return lambda i: ((i % parts) // half * experts + i // parts) * half + (i % parts) % half


def expert_hidden(ring, scalars, blocks, gate, up, product):
    experts, width, hidden_units = gate.shape
    parts = hidden_parts
    step_hidden = hidden_units // parts
    span = ring.rows * ring.size
    n = len(ring.pieces)
    place = hidden_place(parts, experts)
    relative = pl.BlockSpec((None, span, step_hidden), lambda i, s: (i // parts, 0, i % parts))
    placed = pl.BlockSpec((span, step_hidden), lambda i, s: (0, place(i)))
    column = pl.BlockSpec((None, span, 1), lambda i, s: (i // parts, 0, 0))
    hidden = jax.ShapeDtypeStruct((span, experts * parts * step_hidden), jnp.bfloat16)
    return pl.pallas_call(
        functools.partial(expert_hidden_kernel, ring.pieces, parts, min(256, span)),
        grid_spec=pltpu.PrefetchScalarGridSpec(
            num_scalar_prefetch=1,
            grid=(experts * parts,),
            in_specs=[anywhere] * (n + 2) + [relative],
            out_specs=[placed] * 4
            + [column, whole_block((experts, span, 1))]
            + [pl.BlockSpec((width // (experts * parts), span), lambda i, s: (i, 0))],
            scratch_shapes=[
                pltpu.VMEM((span, width), jnp.bfloat16),
                pltpu.VMEM((span, 2 * gate_columns), jnp.bfloat16),
                pltpu.VMEM((2, width, 2 * step_hidden), jnp.bfloat16),
                pltpu.SemaphoreType.DMA((n,)),
                pltpu.SemaphoreType.DMA((n,)),
                pltpu.SemaphoreType.DMA((2, 2)),
            ],
        ),
        out_shape=[
            hidden,
            hidden,
            hidden,
            hidden,
            jax.ShapeDtypeStruct((experts, span, 1), jnp.float32),
            jax.ShapeDtypeStruct((experts, span, 1), jnp.float32),
            jax.ShapeDtypeStruct((width, span), jnp.bfloat16),
        ],
        name="expert_hidden",
    )(scalars, *blocks, gate, up, product)


def pack_weights(scalars, weights, packed, parts):
    experts, _, hidden = weights.shape
    wide = hidden // parts
    place = hidden_place(parts, experts)
    for expert in range(experts):
        for part in range(parts):
            column = place(expert * parts + part) * wide
            relative = 2 * (part % (parts // 2)) + (1 if part < parts // 2 else 0)
            source = pl.multiple_of((scalars[len(scalars) - 1] ^ relative) * wide, wide)
            packed[:, column : column + wide] = weights[expert, :, pl.ds(source, wide)]


def store_pieces(pieces, scalars, source, results):
    rows = pieces[0][2]
    for (slot, first, count), result in zip(pieces, results):
        begin = pl.multiple_of(scalars[slot] * rows + first, count)
        result[...] = source[pl.ds(begin, count), :]


def expert_inputs_kernel(pieces, parts, scalars, *refs):
    d_gate, d_up, gate, up, grad_gates = refs[:5]
    n = len(pieces)
    results = refs[5 : 5 + n]
    packed, summed = refs[5 + n :]
    step = pl.program_id(0)
    last = pl.num_programs(0) - 1

    @pl.when(step < last)
    def _():
        pack_weights(scalars, gate, packed.at[0], parts)
        pack_weights(scalars, up, packed.at[1], parts)
        total = dot(d_gate[...], packed[0], columns_last) + dot(d_up[...], packed[1], columns_last)
        summed[...] = total.astype(jnp.bfloat16)

    @pl.when(step == last)
    def _():
        experts = grad_gates.shape[0]
        column = lax.broadcasted_iota(jnp.int32, summed.shape, 1)
        placed = jnp.zeros(summed.shape, jnp.float32)
        for expert in range(experts):
            value = grad_gates[expert]
            high = value.astype(jnp.bfloat16).astype(jnp.float32)
            own = scalars[0] * experts + expert
            placed = jnp.where(column == own, high, placed)
            placed = jnp.where(column == own + rest_column, value - high, placed)
        summed[...] = placed.astype(jnp.bfloat16)

    store_pieces(pieces, scalars, summed, results)


def expert_inputs(ring, scalars, d_gate, d_up, gate, up, grad_gates):
    experts, width, hidden_units = gate.shape
    parts = hidden_parts
    span, hidden = d_gate.shape
    wide = min(256, width)
    steps = width // wide
    whole = pl.BlockSpec((span, hidden), lambda i, s: (0, 0), pipeline_mode=pl.Buffered(1))
    weight = pl.BlockSpec(
        (experts, wide, hidden_units), lambda i, s: (0, jnp.minimum(i, steps - 1), 0)
    )
    return pl.pallas_call(
        functools.partial(expert_inputs_kernel, ring.pieces, parts),
        grid_spec=pltpu.PrefetchScalarGridSpec(
            num_scalar_prefetch=1,
            grid=(steps + 1,),
            in_specs=[whole] * 2 + [weight] * 2 + [whole_block((experts, span, 1))],
            out_specs=[
                pl.BlockSpec((count, wide), lambda i, s: (0, i)) for _, _, count in ring.pieces
            ],
            scratch_shapes=[
                pltpu.VMEM((2, wide, hidden), jnp.bfloat16),
                pltpu.VMEM((span, wide), jnp.bfloat16),
            ],
        ),
        out_shape=piece_shapes(ring.pieces, width + wide),
        name="expert_inputs",
    )(scalars, d_gate, d_up, gate, up, grad_gates)


def expert_outputs_kernel(pieces, parts, scalars, *refs):
    act, gates = refs[:2]
    down = refs[2]
    n = len(pieces)
    results = refs[3 : 3 + n]
    packed, summed = refs[3 + n :]
    experts, _, hidden_units = down.shape
    pack_weights(scalars, down, packed, parts)
    half = hidden_units // 2
    total = None
    for expert in range(experts):
        first = pl.ds(expert * half, half)
        second = pl.ds((experts + expert) * half, half)
        out = dot(act[:, first], packed[:, first], columns_last)
        out = out + dot(act[:, second], packed[:, second], columns_last)
        out = gates[expert] * out.astype(jnp.bfloat16).astype(jnp.float32)
        total = out if total is None else total + out
    summed[...] = total.astype(jnp.bfloat16)
    store_pieces(pieces, scalars, summed, results)


def expert_outputs(ring, scalars, act, gates, down):
    experts, width, hidden_units = down.shape
    parts = hidden_parts
    span, hidden = act.shape
    wide = min(256, width)
    whole = pl.BlockSpec((span, hidden), lambda i, s: (0, 0), pipeline_mode=pl.Buffered(1))
    return pl.pallas_call(
        functools.partial(expert_outputs_kernel, ring.pieces, parts),
        grid_spec=pltpu.PrefetchScalarGridSpec(
            num_scalar_prefetch=1,
            grid=(width // wide,),
            in_specs=[whole, whole_block((experts, span, 1))]
            + [pl.BlockSpec((experts, wide, hidden_units), lambda i, s: (0, i, 0))],
            out_specs=[
                pl.BlockSpec((count, wide), lambda i, s: (0, i)) for _, _, count in ring.pieces
            ],
            scratch_shapes=[
                pltpu.VMEM((wide, hidden), jnp.bfloat16),
                pltpu.VMEM((span, wide), jnp.bfloat16),
            ],
        ),
        out_shape=piece_shapes(ring.pieces, width),
        name="expert_outputs",
    )(scalars, act, gates, down)


def weight_far_kernel(left, right, result):
    result[...] = dot(left[...], right[...]).astype(jnp.bfloat16)


def weight_far(left, right):
    width, span = left.shape
    split = right.shape[1] // 2
    wide = min(512, width)
    return pl.pallas_call(
        weight_far_kernel,
        grid=(width // wide,),
        in_specs=[
            pl.BlockSpec((wide, span), lambda i: (i, 0)),
            pl.BlockSpec((span, split), lambda i: (0, 0), pipeline_mode=pl.Buffered(1)),
        ],
        out_specs=pl.BlockSpec((wide, split), lambda i: (i, 0)),
        out_shape=jax.ShapeDtypeStruct((width, split), jnp.bfloat16),
        name="weight_far",
    )(left, right)


def weight_near_kernel(scalars, left, right, arrived, result):
    total = dot(left[...], right[...]) + arrived[...].astype(jnp.float32)
    experts, step_hidden = result.shape[0] // 2, result.shape[2]
    own = scalars[len(scalars) - 1] // 2
    for expert in range(experts):
        for other in range(2):
            column = (2 * expert + other) * step_hidden
            result[(own ^ other) * experts + expert] = total[
                :, column : column + step_hidden
            ].astype(jnp.bfloat16)


def weight_near(scalars, left, right, arrived, experts):
    width, span = left.shape
    split = right.shape[1] // 2
    step_hidden = split // (2 * experts)
    wide = min(512, width)
    return pl.pallas_call(
        weight_near_kernel,
        grid_spec=pltpu.PrefetchScalarGridSpec(
            num_scalar_prefetch=1,
            grid=(width // wide,),
            in_specs=[
                pl.BlockSpec((wide, span), lambda i, s: (i, 0)),
                pl.BlockSpec((span, split), lambda i, s: (0, 1), pipeline_mode=pl.Buffered(1)),
                pl.BlockSpec((wide, split), lambda i, s: (i, 0)),
            ],
            out_specs=pl.BlockSpec((2 * experts, wide, step_hidden), lambda i, s: (0, i, 0)),
        ),
        out_shape=jax.ShapeDtypeStruct((2 * experts, width, step_hidden), jnp.bfloat16),
        name="weight_near",
    )(scalars, left, right, arrived)


def weight_rows_kernel(scalars, left, right, sums, far, near):
    columns = right.shape[1]
    value = dot(left[...], right[...], rows_first)
    beside = rows_as_columns(sums[...], far.shape[1] - columns)
    half = pl.num_programs(0) // 2

    @pl.when(pl.program_id(0) < half)
    def _():
        far[:, :columns] = value.astype(jnp.bfloat16)
        far[:, columns:] = beside.astype(jnp.bfloat16)

    @pl.when(pl.program_id(0) >= half)
    def _():
        near[:, :columns] = value
        near[:, columns:] = beside


def weight_rows(scalars, left, right, sums, parts):
    span, width = left.shape
    columns = right.shape[1]
    count = width // parts
    half = parts // 2
    own = scalars.shape[0] - 1
    relative = lambda i: 2 * (i % half) + jnp.where(i < half, 1, 0)
    wide = columns + sum_columns
    return pl.pallas_call(
        weight_rows_kernel,
        grid_spec=pltpu.PrefetchScalarGridSpec(
            num_scalar_prefetch=1,
            grid=(parts,),
            in_specs=[
                pl.BlockSpec((span, count), lambda i, s: (0, s[own] ^ relative(i))),
                whole_block((span, columns)),
                pl.BlockSpec((sums.shape[0], count), lambda i, s: (0, s[own] ^ relative(i))),
            ],
            out_specs=[
                pl.BlockSpec((None, count, wide), lambda i, s: (jnp.minimum(i, half - 1), 0, 0)),
                pl.BlockSpec((None, count, wide), lambda i, s: (jnp.maximum(i - half, 0), 0, 0)),
            ],
        ),
        out_shape=[
            jax.ShapeDtypeStruct((half, count, wide), jnp.bfloat16),
            jax.ShapeDtypeStruct((half, count, wide), jnp.float32),
        ],
        name="weight_rows",
    )(scalars, left, right, sums)


def per_device(
    tokens,
    cotangent,
    routes,
    w_query,
    w_key,
    w_value,
    w_output,
    w_router,
    gain_attn,
    gain_query,
    gain_key,
    gain_ffn,
    expert_gate,
    expert_up,
    expert_down,
):
    rows, width = tokens.shape
    size = lax.axis_size("fsdp")
    dp_size = lax.axis_size("x") * lax.axis_size("core")
    head_dim = width // HEADS
    own_heads = HEADS // size
    part = own_heads * head_dim
    own_rows = w_query.shape[0]
    local_experts = expert_gate.shape[0]
    num_experts = local_experts * size
    group = part // own_rows
    span = rows * size
    f_index = lax.axis_index("fsdp")
    d_index = lax.axis_index(dp_axes)
    low, f32 = jnp.bfloat16, jnp.float32
    ring = Ring(size, rows)
    half = ring.half
    scalars = jnp.concatenate([ring.slot_device, d_index[None].astype(jnp.int32)])
    dp_flat = (*dp_axes, "fsdp")
    to_rows = []
    for flat in range(dp_size * size):
        to_rows.append((flat, (flat % group) * size + flat // group))
    from_rows = [(b, a) for a, b in to_rows]

    packed = jnp.concatenate(
        [w.reshape(own_rows, size, part) for w in (w_query, w_key, w_value)], axis=2
    ).transpose(1, 0, 2)
    packed = lax.all_to_all(packed, "fsdp", split_axis=0, concat_axis=0, tiled=True)
    packed = packed.reshape(size * own_rows, 3 * part)

    small = jnp.concatenate(
        [w_router.T, gain_attn[None], gain_query[None], gain_key[None], gain_ffn[None]], axis=0
    )
    small = pair_gather(small, dp_axes, dp_size)

    token_ring, small_ring = ring.gather(tokens), ring.gather(small, False)
    token_steps = [token_ring.step()]
    for k in range(half):
        small_ring.step(token_steps[0] if k > 1 else None)
    small = small_ring.stacked().transpose(2, 1, 0, 3).reshape(-1, width)
    router = jnp.pad(small[:num_experts], ((0, 2 * gate_columns - num_experts), (0, 0)))
    gains = small[num_experts:].astype(f32)
    gain_in, gain_q, gain_k, gain_mid = (gains[i][None, :] for i in range(4))
    gain_q = lax.dynamic_slice_in_dim(gain_q, f_index * part, part, 1)
    gain_k = lax.dynamic_slice_in_dim(gain_k, f_index * part, part, 1)
    half_dim = head_dim // 2
    inv_freq = rope_base ** (-(jnp.arange(half_dim, dtype=f32) * 2.0) / head_dim)
    angles = jnp.arange(span, dtype=jnp.int32).astype(f32)[:, None] * inv_freq[None, :]
    cosine, sine = jnp.cos(angles), jnp.sin(angles)
    cosine = jnp.concatenate([cosine, cosine], axis=1)
    sine = jnp.concatenate([-sine, sine], axis=1)
    out_rows = lax.ppermute(after(w_output, token_steps[0]), dp_flat, to_rows)
    token_steps.append(token_ring.step(packed))
    token_steps.append(token_ring.step())
    token_steps.append(
        token_ring.step((out_rows, router, gain_in, gain_q, gain_k, gain_mid, cosine, sine))
    )
    token_blocks = token_ring.blocks()
    w_in = share_relative(packed, dp_size, None, token_steps[2])
    w_out = share_relative(out_rows, dp_size, token_steps[2], token_steps[3])

    down_w = lax.all_gather(expert_down, dp_axes, axis=2, tiled=True)
    gate_w = lax.all_gather(expert_gate, dp_axes, axis=2, tiled=True)
    up_w = lax.all_gather(expert_up, dp_axes, axis=2, tiled=True)

    cot_ring = ring.gather(cotangent)
    cot_step = cot_ring.step(token_steps[3])
    normed, raw, in_factor, squares, x_all = project(
        ring, scalars, token_blocks, w_in, gain_in
    )
    squares = pair_sum(after(squares, (cot_step, w_out)), "fsdp", size)
    cot_step = cot_ring.step(squares)
    factors = lax.rsqrt(squares / width + epsilon)
    saved, attn_pieces = attend(
        ring, scalars, raw, factors, gain_q, gain_k, cosine, sine, w_out, head_dim
    )
    attn_ring = ring.reduce(after(attn_pieces, cot_step))
    attn_step = attn_ring.step()
    cot_step = cot_ring.step(attn_step)
    attn_ring.step()
    last_cot = cot_ring.step()
    attn_ring.step(cot_step)
    attn_ring.step(last_cot)
    resid_mid, mid_factor, mid_block, *routing = middle(
        tokens, attn_ring.last(), gain_mid, router, routes, num_experts
    )

    mid_ring = ring.gather(mid_block)
    mid_steps = [mid_ring.step()]
    mid_steps.append(mid_ring.step())
    back_act, cot_all = expert_first(
        ring, after(scalars, mid_steps[0]), cot_ring.blocks(), down_w
    )
    mid_ring.step(back_act)
    mid_ring.step()
    act, act_gated, d_gate, d_up, grad_gates, own_gates, mid_all = expert_hidden(
        ring, scalars, mid_ring.blocks(), gate_w, up_w, back_act
    )
    grad_in = expert_inputs(ring, scalars, d_gate, d_up, gate_w, up_w, grad_gates)

    def far_part(left, right, ties):
        return weight_far(after(left, ties), right)

    def cross(far, ties):
        return lax.ppermute(after(far, ties), dp_axes, exchange_pairs(dp_size, 1))

    def near_part(left, right, far, ties):
        return weight_near(scalars, after(left, ties), right, far, local_experts)

    def finish(near, ties):
        near = after(near, ties)
        return lax.psum_scatter(near, "x", scatter_dimension=0, tiled=True).astype(f32)

    grad_ring = ring.reduce(grad_in)
    grad_steps = [grad_ring.step()]
    gate_far = far_part(mid_all, d_gate, grad_in)
    grad_steps.append(grad_ring.step(gate_far))
    gate_cross = cross(gate_far, grad_steps[0])
    up_far = far_part(mid_all, d_up, grad_steps[0])
    grad_steps.append(grad_ring.step((up_far, gate_cross)))
    up_cross = cross(up_far, grad_steps[1])
    gate_near = near_part(mid_all, d_gate, gate_cross, grad_steps[1])
    grad_steps.append(grad_ring.step((gate_near, up_cross)))
    up_near = near_part(mid_all, d_up, up_cross, grad_steps[2])
    grad_resid, grad_low, grad_gain_mid, grad_router = middle_back(
        after(grad_ring.last(), up_near), cotangent, resid_mid, mid_factor,
        mid_block, *routing, gain_mid, router,
    )

    back_ring = ring.gather(grad_low)
    back_steps = [back_ring.step()]
    down_far = far_part(cot_all, act_gated, grad_low)
    back_steps.append(back_ring.step(down_far))
    down_cross = cross(down_far, back_steps[0])
    moe_pieces = expert_outputs(ring, after(scalars, back_steps[0]), act, own_gates, down_w)
    back_steps.append(back_ring.step((moe_pieces[0], down_cross)))
    down_near = near_part(cot_all, act_gated, down_cross, back_steps[1])
    back_steps.append(back_ring.step(down_near))
    grad_blocks = back_ring.blocks()

    def head_back(head, ties):
        return attend_back(
            ring, after(scalars, ties), saved, raw, factors, gain_q, gain_k, cosine, sine, w_out,
            grad_blocks, head_dim, head,
        )

    moe_ring = ring.reduce(moe_pieces)
    moe_step = moe_ring.step(back_steps[3])
    backs = [head_back(0, (back_steps[3], moe_step))]
    moe_step = moe_ring.step()
    for head in range(1, own_heads):
        backs.append(head_back(head, moe_step))
        if moe_ring.left > 1:
            moe_step = moe_ring.step(early=backs[head - 1][0])
    grad_attn_out = backs[0][6]
    dots = after(sum(back[3] for back in backs), moe_step)
    grad_gain_q = jnp.concatenate([back[4] for back in backs], axis=1)
    grad_gain_k = jnp.concatenate([back[5] for back in backs], axis=1)
    grad_w_out = dot(saved[3].astype(low), after(grad_attn_out, dots), rows_first)
    dots = pair_sum(dots, "fsdp", size) / width
    out_blocks = [
        lax.dynamic_slice_in_dim(grad_w_out, (d_index ^ k) * own_rows, own_rows, 0)
        for k in range(dp_size)
    ]
    out_far = jnp.stack([out_blocks[1], out_blocks[3]]).astype(low)
    while moe_ring.left > 0:
        moe_step = moe_ring.step(dots, backs[-1][0])
    layer_out = (resid_mid + moe_ring.total()).astype(low)
    grad_raw, grad_gain_in, normed_pieces = project_back(
        ring, scalars, [value for back in backs for value in back[:3]], raw, factors,
        after(dots, out_far), gain_q, gain_k, x_all, in_factor, w_in,
    )
    grad_w_out = combine_relative(out_far, [out_blocks[0], out_blocks[2]]).astype(low)
    normed_pieces = after(normed_pieces, (moe_step, grad_w_out))

    in_ring = ring.reduce(normed_pieces)
    in_steps = [in_ring.step()]
    grad_gains = lax.dynamic_update_slice(
        jnp.zeros((2, width), f32),
        jnp.concatenate([grad_gain_q, grad_gain_k], axis=0),
        (0, f_index * part),
    )
    sums = [grad_router[:num_experts], grad_gain_mid, grad_gain_in, grad_gains]
    sums.append(jnp.zeros((-(num_experts + 4) % 8, width), f32))
    grad_w_in = weight_rows(
        scalars, after(normed, normed_pieces), grad_raw, jnp.concatenate(sums, axis=0), dp_size
    )
    grad_gate_w = finish(gate_near, grad_ring.sent)
    grad_up_w = finish(up_near, grad_low)
    grad_down_w = finish(down_near, back_steps[3])
    in_steps.append(in_ring.step(early=grad_w_in))
    grad_w_in = combine_relative(*grad_w_in, (in_steps[0], in_steps[0])).astype(low)
    in_steps.append(in_ring.step(early=(grad_gate_w, grad_up_w)))
    in_steps.append(in_ring.step(early=grad_w_in))
    grad_normed = in_ring.total(grad_down_w)
    grad_w_in = after(grad_w_in, in_steps[2]).reshape(size, own_rows, -1)
    grad_w_in = lax.all_to_all(grad_w_in, "fsdp", split_axis=0, concat_axis=0, tiled=True)
    sums = jnp.sum(grad_w_in[:, :, 3 * part :].astype(f32), axis=0)
    grad_w_in = [
        grad_w_in[:, :, i * part : (i + 1) * part].transpose(1, 0, 2).reshape(own_rows, width)
        for i in range(3)
    ]
    grad_w_in = [values.astype(f32) for values in grad_w_in]
    grad_w_out = lax.ppermute(after(grad_w_out, in_steps[2]), dp_flat, from_rows).astype(f32)
    own_x = tokens.astype(f32)
    own_factor = lax.rsqrt(jnp.mean(own_x * own_x, axis=-1, keepdims=True) + epsilon)
    scaled_in = grad_normed * gain_in
    grad_tokens = (
        grad_resid
        + own_factor * scaled_in
        - own_x * own_factor**3 * jnp.mean(scaled_in * own_x, axis=-1, keepdims=True)
    )
    return (
        layer_out,
        grad_tokens,
        grad_w_in[0],
        grad_w_in[1],
        grad_w_in[2],
        grad_w_out,
        sums[:, :num_experts],
        sums[:, num_experts + 1],
        sums[:, num_experts + 2],
        sums[:, num_experts + 3],
        sums[:, num_experts],
        grad_gate_w,
        grad_up_w,
        grad_down_w,
    )


def splits_evenly(mesh):
    size, dp_size = mesh.shape["fsdp"], mesh.shape["dp"]
    powers = size & (size - 1) == 0 and dp_size & (dp_size - 1) == 0
    return powers and dp_size == 4 and size == 8 and HEADS % size == 0


def solution(mesh):
    split = splits_evenly(mesh)
    dp = "dp"
    if split:
        devices = mesh.devices.reshape(2, 2, mesh.shape["fsdp"])
        mesh, dp = jax.sharding.Mesh(devices, (*dp_axes, "fsdp")), dp_axes
    flat = (*dp_axes, "fsdp") if split else ("dp", "fsdp")
    in_specs = (
        P(flat, None),
        P(flat, None),
        P(flat, None),
        P(flat, None),
        P(flat, None),
        P(flat, None),
        P(flat, None),
        P(flat, None),
        P(flat),
        P(flat),
        P(flat),
        P(flat),
        P("fsdp", None, dp),
        P("fsdp", None, dp),
        P("fsdp", None, dp),
    )
    out_specs = (
        P(flat, None),
        P(flat, None),
        P(flat, None),
        P(flat, None),
        P(flat, None),
        P(flat, None),
        P(flat, None),
        P(flat),
        P(flat),
        P(flat),
        P(flat),
        P("fsdp", None, dp),
        P("fsdp", None, dp),
        P("fsdp", None, dp),
    )
    return jax.shard_map(
        per_device if split else per_device_gathered,
        mesh=mesh,
        in_specs=in_specs,
        out_specs=out_specs,
        check_vma=False,
    )
```

```python
import functools

import jax
import jax.numpy as jnp
from jax import lax
from jax.experimental import pallas as pl
from jax.experimental.pallas import tpu as pltpu
from jax.sharding import PartitionSpec as P

HEADS = 16
TOPK = 8


epsilon = 1e-05
rope_base = 10000.0
hidden_parts = 4
rest_column = 128
gate_columns = 64
sum_columns = 128
dp_axes = ("x", "core")
far_low = -1e30


def rms_norm(values, scaling):
    factor = lax.rsqrt(jnp.mean(values * values, axis=-1, keepdims=True) + epsilon)
    return values * factor * scaling


def rotary(values, positions):
    half_dim = values.shape[-1] // 2
    inv_freq = rope_base ** (-(jnp.arange(half_dim, dtype=jnp.float32) * 2.0) / values.shape[-1])
    angles = positions.astype(jnp.float32)[:, None] * inv_freq[None, :]
    cosine = jnp.cos(angles)[:, None, :]
    sine_vals = jnp.sin(angles)[:, None, :]
    first_half = values[..., :half_dim]
    second = values[..., half_dim:]
    return jnp.concatenate(
        [first_half * cosine - second * sine_vals, second * cosine + first_half * sine_vals],
        axis=-1,
    )


def head_prep(values, scaling, positions):
    normed = rms_norm(values, scaling)
    return rotary(normed.reshape(values.shape[0], HEADS, -1), positions)


def swiglu(gate_hid, up_hid):
    return jax.nn.silu(gate_hid) * up_hid


def gating(logits, routes, num_experts):
    prob_vals = jax.nn.softmax(logits, axis=-1)
    pick_table = (
        routes[:, :, None] == jnp.arange(num_experts, dtype=jnp.int32)[None, None, :]
    ).astype(jnp.float32)
    chosen = jnp.sum(pick_table * prob_vals[:, None, :], axis=-1)
    return chosen / jnp.sum(chosen, axis=-1, keepdims=True)


def per_device_gathered(
    tokens,
    cotangent,
    routes,
    w_query,
    w_key,
    w_value,
    w_output,
    w_router,
    gain_attn,
    gain_query,
    gain_key,
    gain_ffn,
    expert_gate,
    expert_up,
    expert_down,
):
    row_count = tokens.shape[0]
    model_width = tokens.shape[1]
    head_dim = model_width // HEADS
    score_scale = head_dim ** (-0.5)
    fsdp_size = lax.axis_size("fsdp")
    local_experts = expert_gate.shape[0]
    num_experts = local_experts * fsdp_size
    capacity = max(2, (row_count * TOPK * 5 + 4 * num_experts - 1) // (4 * num_experts))
    positions = lax.axis_index("fsdp") * row_count + jnp.arange(row_count, dtype=jnp.int32)
    first_pos = positions[0]
    last_pos = positions[row_count - 1]
    inputs = tokens.astype(jnp.float32)
    dense_full = (
        lax.all_gather(w_query, ("dp", "fsdp"), axis=0, tiled=True),
        lax.all_gather(w_key, ("dp", "fsdp"), axis=0, tiled=True),
        lax.all_gather(w_value, ("dp", "fsdp"), axis=0, tiled=True),
        lax.all_gather(w_output, ("dp", "fsdp"), axis=0, tiled=True),
        lax.all_gather(w_router, ("dp", "fsdp"), axis=0, tiled=True),
        lax.all_gather(gain_attn, ("dp", "fsdp"), axis=0, tiled=True),
        lax.all_gather(gain_query, ("dp", "fsdp"), axis=0, tiled=True),
        lax.all_gather(gain_key, ("dp", "fsdp"), axis=0, tiled=True),
        lax.all_gather(gain_ffn, ("dp", "fsdp"), axis=0, tiled=True),
    )
    expert_full = (
        lax.all_gather(expert_gate, "dp", axis=2, tiled=True),
        lax.all_gather(expert_up, "dp", axis=2, tiled=True),
        lax.all_gather(expert_down, "dp", axis=2, tiled=True),
    )
    query_full, key_full, value_full, output_full, router_full = dense_full[:5]
    gain_in_full = dense_full[5].astype(jnp.float32)
    gain_q_full = dense_full[6].astype(jnp.float32)
    gain_k_full = dense_full[7].astype(jnp.float32)
    gain_mid_full = dense_full[8].astype(jnp.float32)
    normed_low = rms_norm(inputs, gain_in_full).astype(jnp.bfloat16)
    query_raw = jnp.dot(normed_low, query_full, preferred_element_type=jnp.float32)
    key_raw = jnp.dot(normed_low, key_full, preferred_element_type=jnp.float32)
    value_raw = jnp.dot(normed_low, value_full, preferred_element_type=jnp.float32)
    query_low = head_prep(query_raw, gain_q_full, positions).astype(jnp.bfloat16)
    key_low = head_prep(key_raw, gain_k_full, positions).astype(jnp.bfloat16)
    value_low = value_raw.astype(jnp.bfloat16).reshape(row_count, HEADS, head_dim)
    start_state = (
        jnp.full((HEADS, row_count), far_low, jnp.float32),
        jnp.zeros((HEADS, row_count), jnp.float32),
        jnp.zeros((row_count, HEADS, head_dim), jnp.float32),
    )
    shard_piece = (
        lax.all_gather(key_low, "fsdp", axis=0, tiled=True),
        lax.all_gather(value_low, "fsdp", axis=0, tiled=True),
    )

    def attend_update(state):
        run_max, run_sum, run_acc = state
        key_piece, value_piece = shard_piece
        scores = (
            jnp.einsum("qhd,khd->hqk", query_low, key_piece, preferred_element_type=jnp.float32)
            * score_scale
        )
        key_pos = jnp.arange(key_piece.shape[0], dtype=jnp.int32)
        allowed = (key_pos[None, :] <= positions[:, None])[None]
        new_max = jnp.maximum(run_max, jnp.max(jnp.where(allowed, scores, far_low), axis=-1))
        exp_vals = jnp.where(allowed, jnp.exp(scores - new_max[..., None]), 0.0)
        factor = jnp.exp(run_max - new_max)
        run_sum = jnp.sum(exp_vals, axis=-1)
        run_acc = run_acc * factor.T[:, :, None] + jnp.einsum(
            "hqk,khd->qhd",
            exp_vals.astype(jnp.bfloat16),
            value_piece,
            preferred_element_type=jnp.float32,
        )
        return (new_max, run_sum, run_acc)

    run_max, run_sum, run_acc = lax.cond(
        jnp.int32(0) <= last_pos, attend_update, lambda state: state, start_state
    )
    attn_f32 = run_acc / run_sum.T[:, :, None]
    log_sum = run_max + jnp.log(run_sum)
    attn_low = attn_f32.reshape(row_count, model_width).astype(jnp.bfloat16)
    resid_mid = inputs + jnp.dot(attn_low, output_full, preferred_element_type=jnp.float32)
    mid_low = rms_norm(resid_mid, gain_mid_full).astype(jnp.bfloat16)
    logits = jnp.dot(mid_low, router_full, preferred_element_type=jnp.float32)
    gate_vals, gate_pull = jax.vjp(
        lambda logit_vals: gating(logit_vals, routes, num_experts), logits
    )
    route_flat = routes.reshape(-1)
    pick_table = (route_flat[:, None] == jnp.arange(num_experts, dtype=jnp.int32)[None, :]).astype(
        jnp.int32
    )
    slot_index = jnp.sum(pick_table * (jnp.cumsum(pick_table, axis=0) - 1), axis=1)
    target = route_flat * capacity + slot_index
    spread = jnp.repeat(mid_low, TOPK, axis=0)
    send_rows = (
        jnp.zeros((num_experts * capacity, model_width), jnp.bfloat16).at[target].set(spread)
    )
    send_rows = send_rows.reshape(fsdp_size, local_experts, capacity, model_width)
    arrived = lax.all_to_all(send_rows, "fsdp", split_axis=0, concat_axis=0, tiled=True)
    gate_w, up_w, down_w = expert_full
    gate_hid = jnp.einsum("secd,edh->sech", arrived, gate_w, preferred_element_type=jnp.float32)
    up_hid = jnp.einsum("secd,edh->sech", arrived, up_w, preferred_element_type=jnp.float32)
    act_low = swiglu(gate_hid, up_hid).astype(jnp.bfloat16)
    expert_out = jnp.einsum(
        "sech,edh->secd", act_low, down_w, preferred_element_type=jnp.float32
    ).astype(jnp.bfloat16)
    returned = lax.all_to_all(expert_out, "fsdp", split_axis=0, concat_axis=0, tiled=True).reshape(
        num_experts * capacity, model_width
    )
    picked = returned[target].reshape(row_count, TOPK, model_width).astype(jnp.float32)
    resid_out = resid_mid + jnp.sum(gate_vals[:, :, None] * picked, axis=1)
    layer_out = resid_out.astype(jnp.bfloat16)
    back_dense = (
        lax.all_gather(w_query, ("dp", "fsdp"), axis=0, tiled=True),
        lax.all_gather(w_key, ("dp", "fsdp"), axis=0, tiled=True),
        lax.all_gather(w_value, ("dp", "fsdp"), axis=0, tiled=True),
        lax.all_gather(w_output, ("dp", "fsdp"), axis=0, tiled=True),
        lax.all_gather(w_router, ("dp", "fsdp"), axis=0, tiled=True),
        lax.all_gather(gain_attn, ("dp", "fsdp"), axis=0, tiled=True),
        lax.all_gather(gain_query, ("dp", "fsdp"), axis=0, tiled=True),
        lax.all_gather(gain_key, ("dp", "fsdp"), axis=0, tiled=True),
        lax.all_gather(gain_ffn, ("dp", "fsdp"), axis=0, tiled=True),
    )
    back_experts = (
        lax.all_gather(expert_gate, "dp", axis=2, tiled=True),
        lax.all_gather(expert_up, "dp", axis=2, tiled=True),
        lax.all_gather(expert_down, "dp", axis=2, tiled=True),
    )
    query_back, key_back, value_back, output_back, router_back = back_dense[:5]
    gain_in_back = back_dense[5].astype(jnp.float32)
    gain_q_back = back_dense[6].astype(jnp.float32)
    gain_k_back = back_dense[7].astype(jnp.float32)
    gain_mid_back = back_dense[8].astype(jnp.float32)
    gate_back, up_back, down_back = back_experts
    grad_out = cotangent.astype(jnp.float32)
    grad_gates = jnp.sum(grad_out[:, None, :] * picked, axis=-1)
    grad_routed = (
        (gate_vals[:, :, None] * grad_out[:, None, :]).astype(jnp.bfloat16).reshape(-1, model_width)
    )
    send_grads = (
        jnp.zeros((num_experts * capacity, model_width), jnp.bfloat16).at[target].set(grad_routed)
    )
    send_grads = send_grads.reshape(fsdp_size, local_experts, capacity, model_width)
    grad_arrived = lax.all_to_all(send_grads, "fsdp", split_axis=0, concat_axis=0, tiled=True)
    gate_again = jnp.einsum(
        "secd,edh->sech", arrived, gate_back, preferred_element_type=jnp.float32
    )
    up_again = jnp.einsum("secd,edh->sech", arrived, up_back, preferred_element_type=jnp.float32)
    act_vals, act_pull = jax.vjp(swiglu, gate_again, up_again)
    act_again = act_vals.astype(jnp.bfloat16)
    grad_act = jnp.einsum(
        "secd,edh->sech", grad_arrived, down_back, preferred_element_type=jnp.float32
    )
    grad_down = jnp.einsum(
        "secd,sech->edh", grad_arrived, act_again, preferred_element_type=jnp.float32
    )
    grad_gate_hid, grad_up_hid = act_pull(grad_act)
    grad_gate_low = grad_gate_hid.astype(jnp.bfloat16)
    grad_up_low = grad_up_hid.astype(jnp.bfloat16)
    grad_gate_w = jnp.einsum(
        "secd,sech->edh", arrived, grad_gate_low, preferred_element_type=jnp.float32
    )
    grad_up_w = jnp.einsum(
        "secd,sech->edh", arrived, grad_up_low, preferred_element_type=jnp.float32
    )
    grad_inputs = jnp.einsum(
        "sech,edh->secd", grad_gate_low, gate_back, preferred_element_type=jnp.float32
    ) + jnp.einsum("sech,edh->secd", grad_up_low, up_back, preferred_element_type=jnp.float32)
    grad_returned = lax.all_to_all(
        grad_inputs.astype(jnp.bfloat16), "fsdp", split_axis=0, concat_axis=0, tiled=True
    )
    grad_returned = grad_returned.reshape(num_experts * capacity, model_width)
    grad_mid = jnp.sum(
        grad_returned[target].reshape(row_count, TOPK, model_width).astype(jnp.float32), axis=1
    )
    expert_grads = (
        lax.psum_scatter(
            grad_gate_w.astype(jnp.bfloat16), "dp", scatter_dimension=2, tiled=True
        ).astype(jnp.float32),
        lax.psum_scatter(
            grad_up_w.astype(jnp.bfloat16), "dp", scatter_dimension=2, tiled=True
        ).astype(jnp.float32),
        lax.psum_scatter(
            grad_down.astype(jnp.bfloat16), "dp", scatter_dimension=2, tiled=True
        ).astype(jnp.float32),
    )
    (grad_logits,) = gate_pull(grad_gates)
    grad_logits_low = grad_logits.astype(jnp.bfloat16)
    grad_router = jnp.einsum(
        "td,te->de", mid_low, grad_logits_low, preferred_element_type=jnp.float32
    )
    grad_mid = grad_mid + jnp.einsum(
        "te,de->td", grad_logits_low, router_back, preferred_element_type=jnp.float32
    )
    mid_value, mid_pull = jax.vjp(rms_norm, resid_mid, gain_mid_back)
    grad_resid_part, grad_gain_mid = mid_pull(grad_mid)
    grad_resid = grad_out + grad_resid_part
    grad_attn_out = grad_resid.astype(jnp.bfloat16)
    grad_output_w = jnp.einsum(
        "td,te->de", attn_low, grad_attn_out, preferred_element_type=jnp.float32
    )
    grad_attn = jnp.einsum(
        "te,de->td", grad_attn_out, output_back, preferred_element_type=jnp.float32
    )
    grad_attn = grad_attn.astype(jnp.bfloat16).reshape(row_count, HEADS, head_dim)
    delta_rows = jnp.sum(grad_attn.astype(jnp.float32) * attn_f32, axis=-1).T
    key_all, value_all = (
        lax.all_gather(key_low, "fsdp", axis=0, tiled=True),
        lax.all_gather(value_low, "fsdp", axis=0, tiled=True),
    )

    def probs_block(key_block, value_block, begin_at):
        scores = (
            jnp.einsum("qhd,khd->hqk", query_low, key_block, preferred_element_type=jnp.float32)
            * score_scale
        )
        key_pos = begin_at + jnp.arange(key_block.shape[0], dtype=jnp.int32)
        allowed = (key_pos[None, :] <= positions[:, None])[None]
        prob_vals = jnp.where(allowed, jnp.exp(scores - log_sum[..., None]), 0.0)
        grad_probs = jnp.einsum(
            "qhd,khd->hqk", grad_attn, value_block, preferred_element_type=jnp.float32
        )
        grad_scores = (prob_vals * (grad_probs - delta_rows[..., None])).astype(jnp.bfloat16)
        return (prob_vals, grad_scores)

    block_rows = 8 * row_count
    block_needed = last_pos // block_rows + 1
    zero_query = jnp.zeros((row_count, HEADS, head_dim), jnp.float32)

    def query_step(block_index, accum):
        begin_at = block_index * block_rows
        key_block = lax.dynamic_slice_in_dim(key_all, begin_at, block_rows, 0)
        value_block = lax.dynamic_slice_in_dim(value_all, begin_at, block_rows, 0)
        prob_vals, grad_scores = probs_block(key_block, value_block, begin_at)
        return accum + jnp.einsum(
            "hqk,khd->qhd", grad_scores, key_block, preferred_element_type=jnp.float32
        )

    grad_query_rot = lax.fori_loop(0, block_needed, query_step, zero_query) * score_scale
    stats_all = (
        lax.all_gather(log_sum.T, "fsdp", axis=0, tiled=True),
        lax.all_gather(delta_rows.T, "fsdp", axis=0, tiled=True),
    )
    query_piece = lax.all_gather(query_low, "fsdp", axis=0, tiled=True)
    grad_piece = lax.all_gather(grad_attn, "fsdp", axis=0, tiled=True)
    span = query_piece.shape[0]

    def add_update(state):
        lse_piece = stats_all[0].T
        delta_piece = stats_all[1].T
        scores = (
            jnp.einsum("qhd,khd->hqk", query_piece, key_low, preferred_element_type=jnp.float32)
            * score_scale
        )
        query_pos = jnp.arange(span, dtype=jnp.int32)
        allowed = (positions[None, :] <= query_pos[:, None])[None]
        prob_vals = jnp.where(allowed, jnp.exp(scores - lse_piece[..., None]), 0.0)
        grad_probs = jnp.einsum(
            "qhd,khd->hqk", grad_piece, value_low, preferred_element_type=jnp.float32
        )
        grad_scores = (prob_vals * (grad_probs - delta_piece[..., None])).astype(jnp.bfloat16)
        grad_value_acc = jnp.einsum(
            "hqk,qhd->khd",
            prob_vals.astype(jnp.bfloat16),
            grad_piece,
            preferred_element_type=jnp.float32,
        )
        grad_key_acc = jnp.einsum(
            "hqk,qhd->khd", grad_scores, query_piece, preferred_element_type=jnp.float32
        )
        return (grad_key_acc, grad_value_acc)

    grad_key_sum, grad_value_sum = lax.cond(
        jnp.int32(0) + span > first_pos, add_update, lambda state: state, (zero_query, zero_query)
    )
    grad_key_rot = grad_key_sum * score_scale
    grad_value_low = grad_value_sum.reshape(row_count, model_width).astype(jnp.bfloat16)
    query_value, query_pull = jax.vjp(
        lambda raw_vals, scaling: head_prep(raw_vals, scaling, positions), query_raw, gain_q_back
    )
    grad_query_raw, grad_gain_query = query_pull(grad_query_rot)
    key_value, key_pull = jax.vjp(
        lambda raw_vals, scaling: head_prep(raw_vals, scaling, positions), key_raw, gain_k_back
    )
    grad_key_raw, grad_gain_key = key_pull(grad_key_rot)
    grad_query_low = grad_query_raw.astype(jnp.bfloat16)
    grad_key_low = grad_key_raw.astype(jnp.bfloat16)
    grad_wq = jnp.einsum(
        "td,te->de", normed_low, grad_query_low, preferred_element_type=jnp.float32
    )
    grad_wk = jnp.einsum("td,te->de", normed_low, grad_key_low, preferred_element_type=jnp.float32)
    grad_wv = jnp.einsum(
        "td,te->de", normed_low, grad_value_low, preferred_element_type=jnp.float32
    )
    grad_normed = (
        jnp.einsum("te,de->td", grad_query_low, query_back, preferred_element_type=jnp.float32)
        + jnp.einsum("te,de->td", grad_key_low, key_back, preferred_element_type=jnp.float32)
        + jnp.einsum("te,de->td", grad_value_low, value_back, preferred_element_type=jnp.float32)
    )
    in_value, input_pull = jax.vjp(rms_norm, inputs, gain_in_back)
    grad_input_part, grad_gain_in = input_pull(grad_normed)
    grad_tokens = grad_resid + grad_input_part
    dense_grads = (
        lax.psum_scatter(grad_wq, ("dp", "fsdp"), scatter_dimension=0, tiled=True),
        lax.psum_scatter(grad_wk, ("dp", "fsdp"), scatter_dimension=0, tiled=True),
        lax.psum_scatter(grad_wv, ("dp", "fsdp"), scatter_dimension=0, tiled=True),
        lax.psum_scatter(grad_output_w, ("dp", "fsdp"), scatter_dimension=0, tiled=True),
        lax.psum_scatter(grad_router, ("dp", "fsdp"), scatter_dimension=0, tiled=True),
        lax.psum_scatter(grad_gain_in, ("dp", "fsdp"), scatter_dimension=0, tiled=True),
        lax.psum_scatter(grad_gain_query, ("dp", "fsdp"), scatter_dimension=0, tiled=True),
        lax.psum_scatter(grad_gain_key, ("dp", "fsdp"), scatter_dimension=0, tiled=True),
        lax.psum_scatter(grad_gain_mid, ("dp", "fsdp"), scatter_dimension=0, tiled=True),
    )
    return (
        layer_out,
        grad_tokens,
        dense_grads[0],
        dense_grads[1],
        dense_grads[2],
        dense_grads[3],
        dense_grads[4],
        dense_grads[5],
        dense_grads[6],
        dense_grads[7],
        dense_grads[8],
        expert_grads[0],
        expert_grads[1],
        expert_grads[2],
    )


def after(values, ties):
    if callable(ties):
        ties = ties(values)
    if ties is None:
        return values
    return lax.optimization_barrier((values, ties))[0]


class Ring:
    def __init__(self, size, rows):
        self.size = size
        self.half = size // 2
        self.rows = rows
        middle = rows // 2
        self.pieces = [(k, 0, rows) for k in range(self.half)]
        self.pieces += [(self.half, 0, middle), (self.half, middle, middle)]
        self.pieces += [(k, 0, rows) for k in range(self.half + 1, size)]
        self.order = list(range(0, size, 2)) + list(range(size - 1, 0, -2))
        place = [self.order.index(i) for i in range(size)]
        rank = jnp.asarray(place, jnp.int32)[lax.axis_index("fsdp")]
        self.slot_device = jnp.asarray(self.order, jnp.int32)[
            (rank + jnp.arange(size, dtype=jnp.int32)) % size
        ]
        self.device_slot = (jnp.asarray(place, jnp.int32) - rank) % size
        self.up = [(self.order[i], self.order[(i + 1) % size]) for i in range(size)]
        self.down = [(self.order[i], self.order[i - 1]) for i in range(size)]

    def forward(self, values):
        return lax.ppermute(values, "fsdp", self.up)

    def backward(self, values):
        return lax.ppermute(values, "fsdp", self.down)

    def gather(self, block, halves=True):
        return Gather(self, block, halves)

    def reduce(self, pieces):
        return Reduce(self, pieces)


def add_pair_kernel(upper, rising, lower, falling, first, second):
    count, arrived = upper.shape[0], rising.shape[0]
    first[:arrived, :] = upper[:arrived, :] + rising[...]
    second[count - arrived :, :] = lower[count - arrived :, :] + falling[...]
    if arrived < count:
        first[arrived:, :] = upper[arrived:, :]
        second[: count - arrived, :] = lower[: count - arrived, :]


def add_pair(upper, rising, lower, falling):
    shape = jax.ShapeDtypeStruct(upper.shape, upper.dtype)
    return pl.pallas_call(add_pair_kernel, out_shape=[shape, shape], name="add_pair")(
        upper, rising, lower, falling
    )


class Gather:
    def __init__(self, ring, block, halves=True):
        self.ring, self.halves = ring, halves
        self.low, self.high, self.opposite = [block], [block], None

    def step(self, ties=None):
        ring, middle = self.ring, self.ring.rows // 2
        from_low, from_high = after((self.low[-1], self.high[-1]), ties)
        if len(self.low) < ring.half:
            self.low.append(ring.forward(from_low))
            self.high.append(ring.backward(from_high))
            return self.low[-1], self.high[-1]
        if self.halves:
            self.opposite = [ring.forward(from_low[:middle]), ring.backward(from_high[middle:])]
        else:
            self.opposite = [ring.forward(from_low)]
        return tuple(self.opposite)

    def stacked(self):
        return jnp.stack(self.blocks())[self.ring.device_slot]

    def blocks(self):
        return self.high + self.opposite + self.low[:0:-1]


class Reduce:
    def __init__(self, ring, pieces):
        self.ring, self.pieces, self.arrived, self.left = ring, pieces, None, ring.half

    def step(self, ties=None, early=None):
        ring, pieces = self.ring, self.pieces
        if self.arrived is None:
            upper, lower = pieces[ring.half], pieces[ring.half + 1]
        else:
            rising, falling = after(self.arrived, early)
            upper, lower = pieces[self.left], pieces[-self.left]
            upper, lower = add_pair(upper, rising, lower, falling)
        upper, lower = after((upper, lower), ties)
        self.sent = (upper, lower)
        self.arrived = (ring.forward(upper), ring.backward(lower))
        self.left -= 1
        return self.arrived

    def last(self):
        return self.pieces[0], *self.arrived

    def total(self, early=None):
        rising, falling = after(self.arrived, early)
        return (
            self.pieces[0].astype(jnp.float32)
            + rising.astype(jnp.float32)
            + falling.astype(jnp.float32)
        )


def exchange_pairs(size, bit):
    return [(i, i ^ bit) for i in range(size)]


def pair_sum(values, axis, size):
    bit = 1
    while bit < size:
        values = values + lax.ppermute(values, axis, exchange_pairs(size, bit))
        bit *= 2
    return values


def pair_gather(values, axis, size, ties=()):
    ties = dict(ties)
    mine = lax.axis_index(axis)
    values = values[None]
    bit = 1
    while bit < size:
        values = after(values, ties.get(bit))
        other = lax.ppermute(values, axis, exchange_pairs(size, bit))
        upper = (mine & bit) != 0
        values = jnp.where(
            upper,
            jnp.concatenate([other, values], axis=0),
            jnp.concatenate([values, other], axis=0),
        )
        bit *= 2
    return values


def share_relative(block, size, ties=(), second=()):
    block = after(block, ties)
    held = {0: block}
    bit = size // 2
    while bit >= 1:
        for index in list(held):
            sent = held[index] if index == 0 else after(held[index], second)
            held[index ^ bit] = lax.ppermute(sent, dp_axes, exchange_pairs(size, bit))
        bit //= 2
    return [held[index] for index in range(size)]


def combine_relative(far, near, ties=(None, None)):
    far = lax.ppermute(after(far, ties[0]), dp_axes, exchange_pairs(4, 1))
    other = near[1] + far[1].astype(jnp.float32)
    other = after(other.astype(jnp.bfloat16), ties[1])
    other = lax.ppermute(other, dp_axes, exchange_pairs(4, 2))
    return near[0] + far[0].astype(jnp.float32) + other.astype(jnp.float32)


anywhere = pl.BlockSpec(memory_space=pl.ANY)
rows_first = (((0,), (0,)), ((), ()))
columns_last = (((1,), (1,)), ((), ()))


def dot(left, right, dims=(((1,), (0,)), ((), ()))):
    return lax.dot_general(left, right, dims, preferred_element_type=jnp.float32)


def low_terms(values, count):
    terms = []
    for _ in range(count):
        terms.append(values.astype(jnp.bfloat16))
        values = values - terms[-1].astype(jnp.float32)
    return terms


def row_sums(*columns):
    total = None
    for i, values in enumerate(columns):
        place = lax.broadcasted_iota(jnp.int32, (8, values.shape[1]), 0) == i
        place = jnp.where(place, 1.0, 0.0).astype(jnp.bfloat16)
        for term in low_terms(values, 2):
            sums = dot(place, term, columns_last)
            total = sums if total is None else total + sums
    return total


def as_columns(rows):
    return rows_as_columns(rows, 8)


def rows_as_columns(rows, columns):
    shape = (rows.shape[0], columns)
    same = lax.broadcasted_iota(jnp.int32, shape, 0) == lax.broadcasted_iota(jnp.int32, shape, 1)
    same = jnp.where(same, 1.0, 0.0).astype(jnp.bfloat16)
    return sum(dot(term, same, rows_first) for term in low_terms(rows, 3))


def whole_block(shape):
    return pl.BlockSpec(shape, lambda *_: (0,) * len(shape))


def piece_copies(pieces, scalars, blocks, target, sems, first_column=0):
    rows = pieces[0][2]
    columns = pl.ds(first_column, target.shape[1])
    copies = []
    for i, (slot, first, count) in enumerate(pieces):
        begin = pl.multiple_of(scalars[slot] * rows + first, count)
        copies.append(
            pltpu.make_async_copy(
                blocks[i].at[:, columns], target.at[pl.ds(begin, count), :], sems.at[i]
            )
        )
    return copies


def piece_results(pieces, scalars, source, blocks, sems):
    rows = pieces[0][2]
    copies = []
    for i, (slot, first, count) in enumerate(pieces):
        begin = pl.multiple_of(scalars[slot] * rows + first, count)
        copies.append(
            pltpu.make_async_copy(source.at[pl.ds(begin, count), :], blocks[i], sems.at[i])
        )
    return copies


def row_copies(scalars, which, blocks, target, sems):
    own = scalars[which]
    count = blocks[0].shape[0]
    return [
        pltpu.make_async_copy(
            block, target.at[pl.ds(pl.multiple_of((own ^ i) * count, count), count), :], sems.at[i]
        )
        for i, block in enumerate(blocks)
    ]


def run_copies(copies):
    for copy in copies:
        copy.start()
    for copy in copies:
        copy.wait()


def piece_shapes(pieces, width):
    return [jax.ShapeDtypeStruct((count, width), jnp.bfloat16) for _, _, count in pieces]


def project_kernel(pieces, parts, chunk, scalars, *refs):
    n = len(pieces)
    blocks, weights, gain = refs[:n], refs[n : n + parts], refs[n + parts]
    normed, raw, factor, squares, kept, tokens, weight, sems, w_sems, k_sem = refs[n + parts + 1 :]
    step = pl.program_id(0)

    @pl.when(step == 0)
    def _():
        run_copies(
            piece_copies(pieces, scalars, blocks, tokens, sems)
            + row_copies(scalars, len(scalars) - 1, weights, weight, w_sems)
        )
        pltpu.make_async_copy(tokens, kept, k_sem).start()

    rows = pl.ds(pl.multiple_of(step * chunk, chunk), chunk)
    values = tokens[rows, :].astype(jnp.float32)
    scale = lax.rsqrt(jnp.mean(values * values, axis=-1, keepdims=True) + epsilon)
    low = (values * scale * gain[...]).astype(jnp.bfloat16)
    normed[...] = low
    factor[...] = scale
    product = dot(low, weight[...])
    raw[...] = product
    part = product.shape[1] // 3
    squares[...] = row_sums(product[:, :part] ** 2, product[:, part : 2 * part] ** 2)

    @pl.when(step == pl.num_programs(0) - 1)
    def _():
        pltpu.make_async_copy(tokens, kept, k_sem).wait()


def project(ring, scalars, blocks, weights, gain):
    width = blocks[0].shape[1]
    span = ring.rows * ring.size
    columns = weights[0].shape[1]
    chunk = min(256, span)
    n = len(ring.pieces)
    by_rows = lambda i, s: (i, 0)
    return pl.pallas_call(
        functools.partial(project_kernel, ring.pieces, len(weights), chunk),
        grid_spec=pltpu.PrefetchScalarGridSpec(
            num_scalar_prefetch=1,
            grid=(span // chunk,),
            in_specs=[anywhere] * (n + len(weights)) + [whole_block((1, width))],
            out_specs=[
                pl.BlockSpec((chunk, width), by_rows),
                pl.BlockSpec((chunk, columns), by_rows),
                pl.BlockSpec((chunk, 1), by_rows),
                pl.BlockSpec((8, chunk), lambda i, s: (0, i)),
                anywhere,
            ],
            scratch_shapes=[
                pltpu.VMEM((span, width), jnp.bfloat16),
                pltpu.VMEM((width, columns), jnp.bfloat16),
                pltpu.SemaphoreType.DMA((n,)),
                pltpu.SemaphoreType.DMA((len(weights),)),
                pltpu.SemaphoreType.DMA,
            ],
        ),
        out_shape=[
            jax.ShapeDtypeStruct((span, width), jnp.bfloat16),
            jax.ShapeDtypeStruct((span, columns), jnp.float32),
            jax.ShapeDtypeStruct((span, 1), jnp.float32),
            jax.ShapeDtypeStruct((8, span), jnp.float32),
            jax.ShapeDtypeStruct((span, width), jnp.bfloat16),
        ],
        name="project",
    )(scalars, *blocks, *weights, gain)


def turned(values, cosine, sine):
    return values * cosine + pltpu.roll(values, values.shape[-1] // 2, 1) * sine


def attend_kernel(pieces, parts, chunk, scale, scalars, *refs):
    q_raw, k_raw, v_raw, factors, gain_q, gain_k, cosine, sine = refs[:8]
    weights = refs[8 : 8 + parts]
    query, key, value, mixed, lse = refs[8 + parts : 13 + parts]
    n = len(pieces)
    results = refs[13 + parts : 13 + parts + n]
    weight, total, summed, w_sems, sems = refs[13 + parts + n :]
    head = pl.program_id(0)
    last = pl.num_programs(0) - 1
    tokens, head_dim = query.shape

    @pl.when(head == 0)
    def _():
        run_copies(row_copies(scalars, len(scalars) - 1, weights, weight, w_sems))

    columns = as_columns(factors[...])
    query[...] = turned(
        q_raw[...] * columns[:, 0:1] * gain_q[...], cosine[...], sine[...]
    ).astype(jnp.bfloat16)
    key[...] = turned(
        k_raw[...] * columns[:, 1:2] * gain_k[...], cosine[...], sine[...]
    ).astype(jnp.bfloat16)
    value[...] = v_raw[...].astype(jnp.bfloat16)
    own_rows = weight[pl.ds(pl.multiple_of(head * head_dim, head_dim), head_dim), :]
    for begin in range(0, tokens, chunk):
        rows, seen = pl.ds(begin, chunk), pl.ds(0, begin + chunk)
        scores = dot(query[rows, :], key[seen, :], columns_last) * scale
        shape = scores.shape
        allowed = lax.broadcasted_iota(jnp.int32, shape, 1) <= begin + lax.broadcasted_iota(
            jnp.int32, shape, 0
        )
        scores = jnp.where(allowed, scores, far_low)
        top = jnp.max(scores, axis=-1, keepdims=True)
        weights_now = jnp.exp(scores - top)
        sums = jnp.sum(weights_now, axis=-1, keepdims=True)
        out = dot(weights_now.astype(jnp.bfloat16), value[seen, :]) / sums
        mixed[rows, :] = out
        lse[rows, :] = top + jnp.log(sums)
        product = dot(out.astype(jnp.bfloat16), own_rows)

        @pl.when(head == 0)
        def _():
            total[rows, :] = product

        @pl.when(jnp.logical_and(head > 0, head < last))
        def _():
            total[rows, :] += product

        @pl.when(jnp.logical_and(head > 0, head == last))
        def _():
            summed[rows, :] = (total[rows, :] + product).astype(jnp.bfloat16)

        @pl.when(jnp.logical_and(head == 0, head == last))
        def _():
            summed[rows, :] = product.astype(jnp.bfloat16)

    @pl.when(head == last)
    def _():
        run_copies(piece_results(pieces, scalars, summed, results, sems))


def attend(ring, scalars, raw, factors, gain_q, gain_k, cosine, sine, weights, head_dim):
    tokens = raw.shape[0]
    part = raw.shape[1] // 3
    heads = part // head_dim
    width = weights[0].shape[1]
    n = len(ring.pieces)
    column = lambda first: pl.BlockSpec((tokens, head_dim), lambda h, s: (0, first + h))
    gain = pl.BlockSpec((1, head_dim), lambda h, s: (0, h))
    table = whole_block((tokens, head_dim))
    low = jax.ShapeDtypeStruct((tokens, part), jnp.bfloat16)
    out = pl.pallas_call(
        functools.partial(
            attend_kernel, ring.pieces, len(weights), min(512, tokens), head_dim ** (-0.5)
        ),
        grid_spec=pltpu.PrefetchScalarGridSpec(
            num_scalar_prefetch=1,
            grid=(heads,),
            in_specs=[column(0), column(heads), column(2 * heads), whole_block((8, tokens))]
            + [gain, gain, table, table]
            + [anywhere] * len(weights),
            out_specs=[column(0)] * 4
            + [pl.BlockSpec((None, tokens, 1), lambda h, s: (h, 0, 0))]
            + [anywhere] * n,
            scratch_shapes=[
                pltpu.VMEM((part, width), jnp.bfloat16),
                pltpu.VMEM((tokens, width), jnp.float32),
                pltpu.VMEM((tokens, width), jnp.bfloat16),
                pltpu.SemaphoreType.DMA((len(weights),)),
                pltpu.SemaphoreType.DMA((n,)),
            ],
        ),
        out_shape=[low, low, low, jax.ShapeDtypeStruct((tokens, part), jnp.float32)]
        + [jax.ShapeDtypeStruct((heads, tokens, 1), jnp.float32)]
        + piece_shapes(ring.pieces, width),
        name="attend",
    )(scalars, raw, raw, raw, factors, gain_q, gain_k, cosine, sine, *weights)
    return out[:5], out[5:]


def attend_back_kernel(pieces, parts, chunk, scale, head, scalars, *refs):
    query, key, value, mixed, lse, q_raw, k_raw, factors, gain_q, gain_k, cosine, sine = refs[:12]
    n = len(pieces)
    weights = refs[12 : 12 + parts]
    blocks = refs[12 + parts : 12 + parts + n]
    outs = refs[12 + parts + n :]
    turn_q, turn_k, d_value, dots, sum_q, sum_k = outs[:6]
    kept = outs[6] if head == 0 else None
    weight, grads, d_key, d_val, d_query, w_sems, sems, k_sem = outs[-8:]
    tokens, head_dim = query.shape
    run_copies(
        row_copies(scalars, len(scalars) - 1, weights, weight, w_sems)
        + piece_copies(pieces, scalars, blocks, grads, sems)
    )
    if kept is not None:
        pltpu.make_async_copy(grads, kept, k_sem).start()
    own_rows = weight[pl.ds(head * head_dim, head_dim), :]
    for begin in range(0, tokens, chunk):
        rows, seen = pl.ds(begin, chunk), pl.ds(0, begin + chunk)
        grad = dot(grads[rows, :], own_rows, columns_last).astype(jnp.bfloat16)
        queries = query[rows, :]
        scores = dot(queries, key[seen, :], columns_last) * scale
        shape = scores.shape
        allowed = lax.broadcasted_iota(jnp.int32, shape, 1) <= begin + lax.broadcasted_iota(
            jnp.int32, shape, 0
        )
        probs = jnp.where(allowed, jnp.exp(scores - lse[rows, :]), 0.0)
        delta = jnp.sum(grad.astype(jnp.float32) * mixed[rows, :], axis=-1, keepdims=True)
        grad_probs = dot(grad, value[seen, :], columns_last)
        grad_scores = (probs * (grad_probs - delta)).astype(jnp.bfloat16)
        d_query[rows, :] = dot(grad_scores, key[seen, :]) * scale
        part_key = dot(grad_scores, queries, rows_first) * scale
        part_value = dot(probs.astype(jnp.bfloat16), grad, rows_first)
        if begin > 0:
            before = pl.ds(0, begin)
            d_key[before, :] += part_key[:begin]
            d_val[before, :] += part_value[:begin]
        d_key[rows, :] = part_key[begin:]
        d_val[rows, :] = part_value[begin:]
    d_value[...] = d_val[...].astype(jnp.bfloat16)
    back_q = turned(d_query[...], cosine[...], -sine[...])
    back_k = turned(d_key[...], cosine[...], -sine[...])
    turn_q[...] = back_q
    turn_k[...] = back_k
    with_q, with_k = back_q * q_raw[...], back_k * k_raw[...]
    columns = as_columns(factors[...])
    sum_q[...] = jnp.sum(with_q * columns[:, 0:1], axis=0, keepdims=True)
    sum_k[...] = jnp.sum(with_k * columns[:, 1:2], axis=0, keepdims=True)
    dots[...] = row_sums(with_q * gain_q[...], with_k * gain_k[...])
    if kept is not None:
        pltpu.make_async_copy(grads, kept, k_sem).wait()


def attend_back(
    ring, scalars, saved, raw, factors, gain_q, gain_k, cosine, sine, weights, blocks, head_dim,
    head,
):
    query, key, value, mixed, lse = saved
    tokens, part = query.shape
    heads = part // head_dim
    width = weights[0].shape[1]
    n = len(ring.pieces)
    column = lambda first: pl.BlockSpec((tokens, head_dim), lambda i, s: (0, first + head))
    gain = pl.BlockSpec((1, head_dim), lambda i, s: (0, head))
    table = whole_block((tokens, head_dim))
    result = jax.ShapeDtypeStruct((tokens, head_dim), jnp.float32)
    sums = jax.ShapeDtypeStruct((1, head_dim), jnp.float32)
    kept = [anywhere] if head == 0 else []
    accumulate = pltpu.VMEM((tokens, head_dim), jnp.float32)
    return pl.pallas_call(
        functools.partial(
            attend_back_kernel, ring.pieces, len(weights), min(256, tokens), head_dim ** (-0.5),
            head,
        ),
        grid_spec=pltpu.PrefetchScalarGridSpec(
            num_scalar_prefetch=1,
            grid=(1,),
            in_specs=[column(0)] * 4
            + [pl.BlockSpec((None, tokens, 1), lambda i, s: (head, 0, 0))]
            + [column(0), column(heads), whole_block((8, tokens)), gain, gain, table, table]
            + [anywhere] * (len(weights) + n),
            out_specs=[table] * 3
            + [whole_block((8, tokens))]
            + [whole_block((1, head_dim))] * 2
            + kept,
            scratch_shapes=[
                pltpu.VMEM((part, width), jnp.bfloat16),
                pltpu.VMEM((tokens, width), jnp.bfloat16),
                accumulate,
                accumulate,
                accumulate,
                pltpu.SemaphoreType.DMA((len(weights),)),
                pltpu.SemaphoreType.DMA((n,)),
                pltpu.SemaphoreType.DMA,
            ],
        ),
        out_shape=[
            result,
            result,
            jax.ShapeDtypeStruct((tokens, head_dim), jnp.bfloat16),
            jax.ShapeDtypeStruct((8, tokens), jnp.float32),
            sums,
            sums,
        ]
        + [jax.ShapeDtypeStruct((tokens, width), jnp.bfloat16)] * len(kept),
        name="attend_back",
    )(
        scalars, query, key, value, mixed, lse, raw, raw, factors, gain_q, gain_k, cosine, sine,
        *weights, *blocks,
    )


def project_back_kernel(pieces, parts, chunk, heads, scalars, *refs):
    turns, refs = refs[: 3 * heads], refs[3 * heads :]
    raw, factors, dots, gain_q, gain_k, tokens, in_factor = refs[:7]
    n = len(pieces)
    weights = refs[7 : 7 + parts]
    grad_raw, sum_in = refs[7 + parts : 9 + parts]
    results = refs[9 + parts : 9 + parts + n]
    weight, summed, w_sems, sems = refs[9 + parts + n :]
    step = pl.program_id(0)
    head_dim = turns[0].shape[1]
    part = heads * head_dim

    @pl.when(step == 0)
    def _():
        run_copies(row_copies(scalars, len(scalars) - 1, weights, weight, w_sems))
        sum_in[...] = jnp.zeros_like(sum_in)

    factor_columns, dot_columns = as_columns(factors[...]), as_columns(dots[...])
    for i, gain in enumerate((gain_q, gain_k)):
        factor = factor_columns[:, i : i + 1]
        cubed = factor * factor * factor * dot_columns[:, i : i + 1]
        for head in range(heads):
            columns = pl.ds(i * part + head * head_dim, head_dim)
            turn = turns[3 * head + i][...] * gain[:, head * head_dim : (head + 1) * head_dim]
            grad_raw[:, columns] = (factor * turn - raw[:, columns] * cubed).astype(jnp.bfloat16)
    for head in range(heads):
        grad_raw[:, pl.ds(2 * part + head * head_dim, head_dim)] = turns[3 * head + 2][...]
    normed = dot(grad_raw[...], weight[...], columns_last)
    sum_in[...] += jnp.sum(
        normed * (tokens[...].astype(jnp.float32) * in_factor[...]), axis=0, keepdims=True
    )
    summed[pl.ds(pl.multiple_of(step * chunk, chunk), chunk), :] = normed.astype(jnp.bfloat16)

    @pl.when(step == pl.num_programs(0) - 1)
    def _():
        run_copies(piece_results(pieces, scalars, summed, results, sems))


def project_back(
    ring, scalars, turns, raw, factors, dots, gain_q, gain_k, tokens, in_factor, weights
):
    span, width = tokens.shape
    heads, head_dim = len(turns) // 3, turns[0].shape[1]
    part = heads * head_dim
    columns = weights[0].shape[1]
    chunk = min(256, span)
    n = len(ring.pieces)
    by_rows = lambda wide: pl.BlockSpec((chunk, wide), lambda i, s: (i, 0))
    out = pl.pallas_call(
        functools.partial(project_back_kernel, ring.pieces, len(weights), chunk, heads),
        grid_spec=pltpu.PrefetchScalarGridSpec(
            num_scalar_prefetch=1,
            grid=(span // chunk,),
            in_specs=[by_rows(head_dim)] * (3 * heads)
            + [by_rows(columns)]
            + [pl.BlockSpec((8, chunk), lambda i, s: (0, i))] * 2
            + [whole_block((1, part))] * 2
            + [by_rows(width), by_rows(1)]
            + [anywhere] * len(weights),
            out_specs=[by_rows(columns), whole_block((1, width))] + [anywhere] * n,
            scratch_shapes=[
                pltpu.VMEM((width, columns), jnp.bfloat16),
                pltpu.VMEM((span, width), jnp.bfloat16),
                pltpu.SemaphoreType.DMA((len(weights),)),
                pltpu.SemaphoreType.DMA((n,)),
            ],
        ),
        out_shape=[
            jax.ShapeDtypeStruct((span, columns), jnp.bfloat16),
            jax.ShapeDtypeStruct((1, width), jnp.float32),
        ]
        + piece_shapes(ring.pieces, width),
        name="project_back",
    )(
        scalars, *turns, raw, factors, dots, gain_q, gain_k, tokens, in_factor, *weights
    )
    return out[0], out[1], out[2:]


def expert_column(scalars, part, parts, wide):
    half = parts // 2
    relative = 2 * (part % half) + jnp.where(part < half, 1, 0)
    return pl.multiple_of((scalars[len(scalars) - 1] ^ relative) * wide, wide)


def weight_copies(groups, scalars, buffers, sems, step, parts):
    expert, part, place = step // parts, step % parts, step % 2
    wide = buffers.shape[2] // len(groups)
    columns = pl.ds(expert_column(scalars, part, parts, wide), wide)
    return [
        pltpu.make_async_copy(
            group.at[expert, :, columns],
            buffers.at[place, :, pl.ds(g * wide, wide)],
            sems.at[place, g],
        )
        for g, group in enumerate(groups)
    ]


def stream(groups, scalars, buffers, sems, parts):
    step = pl.program_id(0)

    @pl.when(step == 0)
    def _():
        for copy in weight_copies(groups, scalars, buffers, sems, step, parts):
            copy.start()

    @pl.when(step + 1 < pl.num_programs(0))
    def _():
        for copy in weight_copies(groups, scalars, buffers, sems, step + 1, parts):
            copy.start()

    for copy in weight_copies(groups, scalars, buffers, sems, step, parts):
        copy.wait()
    return buffers.at[step % 2]


def middle_kernel(experts, tokens, first, rising, falling, gain, router, routes, *refs):
    resid, factor, block, gates, probs, mask, total = refs
    width = tokens.shape[1]
    values = tokens[...].astype(jnp.float32) + (
        first[...].astype(jnp.float32)
        + rising[...].astype(jnp.float32)
        + falling[...].astype(jnp.float32)
    )
    resid[...] = values
    scale = lax.rsqrt(jnp.mean(values * values, axis=-1, keepdims=True) + epsilon)
    factor[...] = scale
    low = (values * scale * gain[...]).astype(jnp.bfloat16)
    block[:, :width] = low
    logits = dot(low, router[...], columns_last)
    column = lax.broadcasted_iota(jnp.int32, logits.shape, 1)
    real = column < experts
    top = jnp.max(jnp.where(real, logits, far_low), axis=-1, keepdims=True)
    weights = jnp.where(real, jnp.exp(logits - top), 0.0)
    prob_vals = weights / jnp.sum(weights, axis=-1, keepdims=True)
    chosen_mask = jnp.zeros(logits.shape, jnp.float32)
    for j in range(routes.shape[1]):
        chosen_mask = jnp.where(column == routes[:, j : j + 1], 1.0, chosen_mask)
    chosen = chosen_mask * prob_vals
    chosen_sum = jnp.sum(chosen, axis=-1, keepdims=True)
    gate_vals = chosen / chosen_sum
    gates[...], probs[...], mask[...], total[...] = gate_vals, prob_vals, chosen_mask, chosen_sum
    high = gate_vals.astype(jnp.bfloat16).astype(jnp.float32)
    rest = pltpu.roll(gate_vals - high, gate_columns, 1)
    block[:, width:] = (high + rest).astype(jnp.bfloat16)


def middle(tokens, sums, gain, router, routes, experts):
    rows, width = tokens.shape
    lanes = 2 * gate_columns
    table = jax.ShapeDtypeStruct((rows, lanes), jnp.float32)
    column = jax.ShapeDtypeStruct((rows, 1), jnp.float32)
    return pl.pallas_call(
        functools.partial(middle_kernel, experts),
        out_shape=[
            jax.ShapeDtypeStruct((rows, width), jnp.float32),
            column,
            jax.ShapeDtypeStruct((rows, width + lanes), jnp.bfloat16),
            table,
            table,
            table,
            column,
        ],
        name="middle",
    )(tokens, *sums, gain, router, routes)


def middle_back_kernel(first, rising, falling, cotangent, resid, factor, block, *refs):
    gates, probs, mask, total, gain, router = refs[:6]
    grad_resid, grad_low, sum_gain, grad_router = refs[6:]
    width = resid.shape[1]
    summed = (
        first[...].astype(jnp.float32)
        + rising[...].astype(jnp.float32)
        + falling[...].astype(jnp.float32)
    )
    lanes = 2 * gate_columns
    gates_back = summed[:, width : width + lanes]
    gates_back = gates_back + summed[:, width + rest_column : width + rest_column + lanes]
    inner = jnp.sum(gates_back * gates[...], axis=-1, keepdims=True)
    grad_probs = mask[...] * ((gates_back - inner) / total[...])
    grad_logits = probs[...] * (
        grad_probs - jnp.sum(probs[...] * grad_probs, axis=-1, keepdims=True)
    )
    logits_low = grad_logits.astype(jnp.bfloat16)
    grad_router[...] = dot(logits_low, block[:, :width], rows_first)
    grad_mid = summed[:, :width] + dot(logits_low, router[...])
    scale, values = factor[...], resid[...]
    scaled = grad_mid * gain[...]
    sum_gain[...] = jnp.sum(grad_mid * values * scale, axis=0, keepdims=True)
    mean = jnp.mean(scaled * values, axis=-1, keepdims=True)
    result = (
        cotangent[...].astype(jnp.float32)
        + scale * scaled
        - values * (scale * scale * scale * mean)
    )
    grad_resid[...] = result
    grad_low[...] = result.astype(jnp.bfloat16)


def middle_back(sums, cotangent, resid, factor, block, gates, probs, mask, total, gain, router):
    rows, width = resid.shape
    return pl.pallas_call(
        middle_back_kernel,
        out_shape=[
            jax.ShapeDtypeStruct((rows, width), jnp.float32),
            jax.ShapeDtypeStruct((rows, width), jnp.bfloat16),
            jax.ShapeDtypeStruct((1, width), jnp.float32),
            jax.ShapeDtypeStruct((2 * gate_columns, width), jnp.float32),
        ],
        name="middle_back",
    )(*sums, cotangent, resid, factor, block, gates, probs, mask, total, gain, router)


def turn_columns(rows_all, result):
    wide = result.shape[0]
    columns = pl.ds(pl.multiple_of(pl.program_id(0) * wide, wide), wide)
    result[...] = rows_all[:, columns].T


def expert_first_kernel(pieces, parts, chunk, scalars, *refs):
    n = len(pieces)
    blocks, down = refs[:n], refs[n]
    product, turned_rows, rows_all, buffers, sems, w_sems = refs[n + 1 :]
    step = pl.program_id(0)

    @pl.when(step == 0)
    def _():
        copies = piece_copies(pieces, scalars, blocks, rows_all, sems)
        for copy in copies:
            copy.start()

    weight = stream([down], scalars, buffers, w_sems, parts)

    @pl.when(step == 0)
    def _():
        for copy in piece_copies(pieces, scalars, blocks, rows_all, sems):
            copy.wait()

    for begin in range(0, rows_all.shape[0], chunk):
        rows = pl.ds(begin, chunk)
        product[rows, :] = dot(rows_all[rows, :], weight[...])
    turn_columns(rows_all, turned_rows)


def expert_first(ring, scalars, blocks, down):
    experts, width, hidden = down.shape
    parts = hidden_parts
    step_hidden = hidden // parts
    span = ring.rows * ring.size
    n = len(ring.pieces)
    return pl.pallas_call(
        functools.partial(expert_first_kernel, ring.pieces, parts, min(256, span)),
        grid_spec=pltpu.PrefetchScalarGridSpec(
            num_scalar_prefetch=1,
            grid=(experts * parts,),
            in_specs=[anywhere] * (n + 1),
            out_specs=[
                pl.BlockSpec((None, span, step_hidden), lambda i, s: (i // parts, 0, i % parts)),
                pl.BlockSpec((width // (experts * parts), span), lambda i, s: (i, 0)),
            ],
            scratch_shapes=[
                pltpu.VMEM((span, width), jnp.bfloat16),
                pltpu.VMEM((2, width, step_hidden), jnp.bfloat16),
                pltpu.SemaphoreType.DMA((n,)),
                pltpu.SemaphoreType.DMA((2, 1)),
            ],
        ),
        out_shape=[
            jax.ShapeDtypeStruct((experts, span, parts * step_hidden), jnp.float32),
            jax.ShapeDtypeStruct((width, span), jnp.bfloat16),
        ],
        name="expert_first",
    )(scalars, *blocks, down)


def expert_hidden_kernel(pieces, parts, chunk, scalars, *refs):
    n = len(pieces)
    blocks, gate, up = refs[:n], refs[n], refs[n + 1]
    product = refs[n + 2]
    act, gated, d_gate, d_up, grad_gates, gates, turned_rows = refs[n + 3 : n + 10]
    rows_all, gates_all, buffers, sems, g_sems, w_sems = refs[n + 10 :]
    step = pl.program_id(0)
    experts = gates.shape[0]
    g_copies = piece_copies(pieces, scalars, blocks, gates_all, g_sems, rows_all.shape[1])

    @pl.when(step == 0)
    def _():
        for copy in piece_copies(pieces, scalars, blocks, rows_all, sems) + g_copies:
            copy.start()

    weight = stream([gate, up], scalars, buffers, w_sems, parts)

    @pl.when(step == 0)
    def _():
        for copy in piece_copies(pieces, scalars, blocks, rows_all, sems) + g_copies:
            copy.wait()
        values = gates_all[...].astype(jnp.float32)
        column = lax.broadcasted_iota(jnp.int32, values.shape, 1) % gate_columns
        for expert in range(experts):
            own = scalars[0] * experts + expert
            gates[expert] = jnp.sum(
                jnp.where(column == own, values, 0.0), axis=-1, keepdims=True
            )

    @pl.when(step % parts == 0)
    def _():
        grad_gates[...] = jnp.zeros_like(grad_gates)

    for begin in range(0, rows_all.shape[0], chunk):
        rows = pl.ds(begin, chunk)
        both = dot(rows_all[rows, :], weight[...])
        gate_hid, up_hid = both[:, : act.shape[1]], both[:, act.shape[1] :]
        own_gate = gates[step // parts, rows, :]
        back = product[rows, :]
        sig = 0.5 + 0.5 * jnp.tanh(0.5 * gate_hid)
        silu = gate_hid * sig
        act_low = (silu * up_hid).astype(jnp.bfloat16)
        act_now = act_low.astype(jnp.float32)
        act[rows, :] = act_low
        gated[rows, :] = (own_gate * act_now).astype(jnp.bfloat16)
        grad_gates[rows, :] += jnp.sum(act_now * back, axis=-1, keepdims=True)
        grad_act = own_gate * back
        d_gate[rows, :] = (grad_act * up_hid * (sig * (1.0 + gate_hid * (1.0 - sig)))).astype(
            jnp.bfloat16
        )
        d_up[rows, :] = (grad_act * silu).astype(jnp.bfloat16)

    turn_columns(rows_all, turned_rows)


def hidden_place(parts, experts):
    half = parts // 2
    return lambda i: ((i % parts) // half * experts + i // parts) * half + (i % parts) % half


def expert_hidden(ring, scalars, blocks, gate, up, product):
    experts, width, hidden_units = gate.shape
    parts = hidden_parts
    step_hidden = hidden_units // parts
    span = ring.rows * ring.size
    n = len(ring.pieces)
    place = hidden_place(parts, experts)
    relative = pl.BlockSpec((None, span, step_hidden), lambda i, s: (i // parts, 0, i % parts))
    placed = pl.BlockSpec((span, step_hidden), lambda i, s: (0, place(i)))
    column = pl.BlockSpec((None, span, 1), lambda i, s: (i // parts, 0, 0))
    hidden = jax.ShapeDtypeStruct((span, experts * parts * step_hidden), jnp.bfloat16)
    return pl.pallas_call(
        functools.partial(expert_hidden_kernel, ring.pieces, parts, min(512, span)),
        grid_spec=pltpu.PrefetchScalarGridSpec(
            num_scalar_prefetch=1,
            grid=(experts * parts,),
            in_specs=[anywhere] * (n + 2) + [relative],
            out_specs=[placed] * 4
            + [column, whole_block((experts, span, 1))]
            + [pl.BlockSpec((width // (experts * parts), span), lambda i, s: (i, 0))],
            scratch_shapes=[
                pltpu.VMEM((span, width), jnp.bfloat16),
                pltpu.VMEM((span, 2 * gate_columns), jnp.bfloat16),
                pltpu.VMEM((2, width, 2 * step_hidden), jnp.bfloat16),
                pltpu.SemaphoreType.DMA((n,)),
                pltpu.SemaphoreType.DMA((n,)),
                pltpu.SemaphoreType.DMA((2, 2)),
            ],
        ),
        out_shape=[
            hidden,
            hidden,
            hidden,
            hidden,
            jax.ShapeDtypeStruct((experts, span, 1), jnp.float32),
            jax.ShapeDtypeStruct((experts, span, 1), jnp.float32),
            jax.ShapeDtypeStruct((width, span), jnp.bfloat16),
        ],
        name="expert_hidden",
    )(scalars, *blocks, gate, up, product)


def pack_weights(scalars, weights, packed, parts):
    experts, _, hidden = weights.shape
    wide = hidden // parts
    place = hidden_place(parts, experts)
    for expert in range(experts):
        for part in range(parts):
            column = place(expert * parts + part) * wide
            relative = 2 * (part % (parts // 2)) + (1 if part < parts // 2 else 0)
            source = pl.multiple_of((scalars[len(scalars) - 1] ^ relative) * wide, wide)
            packed[:, column : column + wide] = weights[expert, :, pl.ds(source, wide)]


def store_pieces(pieces, scalars, source, results):
    rows = pieces[0][2]
    for (slot, first, count), result in zip(pieces, results):
        begin = pl.multiple_of(scalars[slot] * rows + first, count)
        result[...] = source[pl.ds(begin, count), :]


def expert_inputs_kernel(pieces, parts, scalars, *refs):
    d_gate, d_up, gate, up, grad_gates = refs[:5]
    n = len(pieces)
    results = refs[5 : 5 + n]
    packed, summed = refs[5 + n :]
    step = pl.program_id(0)
    last = pl.num_programs(0) - 1

    @pl.when(step < last)
    def _():
        pack_weights(scalars, gate, packed.at[0], parts)
        pack_weights(scalars, up, packed.at[1], parts)
        total = dot(d_gate[...], packed[0], columns_last) + dot(d_up[...], packed[1], columns_last)
        summed[...] = total.astype(jnp.bfloat16)

    @pl.when(step == last)
    def _():
        experts = grad_gates.shape[0]
        column = lax.broadcasted_iota(jnp.int32, summed.shape, 1)
        placed = jnp.zeros(summed.shape, jnp.float32)
        for expert in range(experts):
            value = grad_gates[expert]
            high = value.astype(jnp.bfloat16).astype(jnp.float32)
            own = scalars[0] * experts + expert
            placed = jnp.where(column == own, high, placed)
            placed = jnp.where(column == own + rest_column, value - high, placed)
        summed[...] = placed.astype(jnp.bfloat16)

    store_pieces(pieces, scalars, summed, results)


def expert_inputs(ring, scalars, d_gate, d_up, gate, up, grad_gates):
    experts, width, hidden_units = gate.shape
    parts = hidden_parts
    span, hidden = d_gate.shape
    wide = min(256, width)
    steps = width // wide
    whole = pl.BlockSpec((span, hidden), lambda i, s: (0, 0), pipeline_mode=pl.Buffered(1))
    weight = pl.BlockSpec(
        (experts, wide, hidden_units), lambda i, s: (0, jnp.minimum(i, steps - 1), 0)
    )
    return pl.pallas_call(
        functools.partial(expert_inputs_kernel, ring.pieces, parts),
        grid_spec=pltpu.PrefetchScalarGridSpec(
            num_scalar_prefetch=1,
            grid=(steps + 1,),
            in_specs=[whole] * 2 + [weight] * 2 + [whole_block((experts, span, 1))],
            out_specs=[
                pl.BlockSpec((count, wide), lambda i, s: (0, i)) for _, _, count in ring.pieces
            ],
            scratch_shapes=[
                pltpu.VMEM((2, wide, hidden), jnp.bfloat16),
                pltpu.VMEM((span, wide), jnp.bfloat16),
            ],
        ),
        out_shape=piece_shapes(ring.pieces, width + wide),
        name="expert_inputs",
    )(scalars, d_gate, d_up, gate, up, grad_gates)


def expert_outputs_kernel(pieces, parts, scalars, *refs):
    act, gates = refs[:2]
    down = refs[2]
    n = len(pieces)
    results = refs[3 : 3 + n]
    packed, summed = refs[3 + n :]
    experts, _, hidden_units = down.shape
    pack_weights(scalars, down, packed, parts)
    half = hidden_units // 2
    total = None
    for expert in range(experts):
        first = pl.ds(expert * half, half)
        second = pl.ds((experts + expert) * half, half)
        out = dot(act[:, first], packed[:, first], columns_last)
        out = out + dot(act[:, second], packed[:, second], columns_last)
        out = gates[expert] * out.astype(jnp.bfloat16).astype(jnp.float32)
        total = out if total is None else total + out
    summed[...] = total.astype(jnp.bfloat16)
    store_pieces(pieces, scalars, summed, results)


def expert_outputs(ring, scalars, act, gates, down):
    experts, width, hidden_units = down.shape
    parts = hidden_parts
    span, hidden = act.shape
    wide = min(256, width)
    whole = pl.BlockSpec((span, hidden), lambda i, s: (0, 0), pipeline_mode=pl.Buffered(1))
    return pl.pallas_call(
        functools.partial(expert_outputs_kernel, ring.pieces, parts),
        grid_spec=pltpu.PrefetchScalarGridSpec(
            num_scalar_prefetch=1,
            grid=(width // wide,),
            in_specs=[whole, whole_block((experts, span, 1))]
            + [pl.BlockSpec((experts, wide, hidden_units), lambda i, s: (0, i, 0))],
            out_specs=[
                pl.BlockSpec((count, wide), lambda i, s: (0, i)) for _, _, count in ring.pieces
            ],
            scratch_shapes=[
                pltpu.VMEM((wide, hidden), jnp.bfloat16),
                pltpu.VMEM((span, wide), jnp.bfloat16),
            ],
        ),
        out_shape=piece_shapes(ring.pieces, width),
        name="expert_outputs",
    )(scalars, act, gates, down)


def weight_far_kernel(left, right, result):
    result[...] = dot(left[...], right[...]).astype(jnp.bfloat16)


def weight_far(left, right):
    width, span = left.shape
    split = right.shape[1] // 2
    wide = min(512, width)
    return pl.pallas_call(
        weight_far_kernel,
        grid=(width // wide,),
        in_specs=[
            pl.BlockSpec((wide, span), lambda i: (i, 0)),
            pl.BlockSpec((span, split), lambda i: (0, 0), pipeline_mode=pl.Buffered(1)),
        ],
        out_specs=pl.BlockSpec((wide, split), lambda i: (i, 0)),
        out_shape=jax.ShapeDtypeStruct((width, split), jnp.bfloat16),
        name="weight_far",
    )(left, right)


def weight_near_kernel(scalars, left, right, arrived, result):
    total = dot(left[...], right[...]) + arrived[...].astype(jnp.float32)
    experts, step_hidden = result.shape[0] // 2, result.shape[2]
    own = scalars[len(scalars) - 1] // 2
    for expert in range(experts):
        for other in range(2):
            column = (2 * expert + other) * step_hidden
            result[(own ^ other) * experts + expert] = total[
                :, column : column + step_hidden
            ].astype(jnp.bfloat16)


def weight_near(scalars, left, right, arrived, experts):
    width, span = left.shape
    split = right.shape[1] // 2
    step_hidden = split // (2 * experts)
    wide = min(512, width)
    return pl.pallas_call(
        weight_near_kernel,
        grid_spec=pltpu.PrefetchScalarGridSpec(
            num_scalar_prefetch=1,
            grid=(width // wide,),
            in_specs=[
                pl.BlockSpec((wide, span), lambda i, s: (i, 0)),
                pl.BlockSpec((span, split), lambda i, s: (0, 1), pipeline_mode=pl.Buffered(1)),
                pl.BlockSpec((wide, split), lambda i, s: (i, 0)),
            ],
            out_specs=pl.BlockSpec((2 * experts, wide, step_hidden), lambda i, s: (0, i, 0)),
        ),
        out_shape=jax.ShapeDtypeStruct((2 * experts, width, step_hidden), jnp.bfloat16),
        name="weight_near",
    )(scalars, left, right, arrived)


def weight_rows_kernel(scalars, left, right, sums, far, near):
    columns = right.shape[1]
    value = dot(left[...], right[...], rows_first)
    beside = rows_as_columns(sums[...], far.shape[1] - columns)
    half = pl.num_programs(0) // 2

    @pl.when(pl.program_id(0) < half)
    def _():
        far[:, :columns] = value.astype(jnp.bfloat16)
        far[:, columns:] = beside.astype(jnp.bfloat16)

    @pl.when(pl.program_id(0) >= half)
    def _():
        near[:, :columns] = value
        near[:, columns:] = beside


def weight_rows(scalars, left, right, sums, parts):
    span, width = left.shape
    columns = right.shape[1]
    count = width // parts
    half = parts // 2
    own = scalars.shape[0] - 1
    relative = lambda i: 2 * (i % half) + jnp.where(i < half, 1, 0)
    wide = columns + sum_columns
    return pl.pallas_call(
        weight_rows_kernel,
        grid_spec=pltpu.PrefetchScalarGridSpec(
            num_scalar_prefetch=1,
            grid=(parts,),
            in_specs=[
                pl.BlockSpec((span, count), lambda i, s: (0, s[own] ^ relative(i))),
                whole_block((span, columns)),
                pl.BlockSpec((sums.shape[0], count), lambda i, s: (0, s[own] ^ relative(i))),
            ],
            out_specs=[
                pl.BlockSpec((None, count, wide), lambda i, s: (jnp.minimum(i, half - 1), 0, 0)),
                pl.BlockSpec((None, count, wide), lambda i, s: (jnp.maximum(i - half, 0), 0, 0)),
            ],
        ),
        out_shape=[
            jax.ShapeDtypeStruct((half, count, wide), jnp.bfloat16),
            jax.ShapeDtypeStruct((half, count, wide), jnp.float32),
        ],
        name="weight_rows",
    )(scalars, left, right, sums)


def per_device(
    tokens,
    cotangent,
    routes,
    w_query,
    w_key,
    w_value,
    w_output,
    w_router,
    gain_attn,
    gain_query,
    gain_key,
    gain_ffn,
    expert_gate,
    expert_up,
    expert_down,
):
    rows, width = tokens.shape
    size = lax.axis_size("fsdp")
    dp_size = lax.axis_size("x") * lax.axis_size("core")
    head_dim = width // HEADS
    own_heads = HEADS // size
    part = own_heads * head_dim
    own_rows = w_query.shape[0]
    local_experts = expert_gate.shape[0]
    num_experts = local_experts * size
    group = part // own_rows
    span = rows * size
    f_index = lax.axis_index("fsdp")
    d_index = lax.axis_index(dp_axes)
    low, f32 = jnp.bfloat16, jnp.float32
    ring = Ring(size, rows)
    half = ring.half
    scalars = jnp.concatenate([ring.slot_device, d_index[None].astype(jnp.int32)])
    dp_flat = (*dp_axes, "fsdp")
    to_rows = []
    for flat in range(dp_size * size):
        to_rows.append((flat, (flat % group) * size + flat // group))
    from_rows = [(b, a) for a, b in to_rows]

    packed = jnp.concatenate(
        [w.reshape(own_rows, size, part) for w in (w_query, w_key, w_value)], axis=2
    ).transpose(1, 0, 2)
    packed = lax.all_to_all(packed, "fsdp", split_axis=0, concat_axis=0, tiled=True)
    packed = packed.reshape(size * own_rows, 3 * part)

    small = jnp.concatenate(
        [w_router.T, gain_attn[None], gain_query[None], gain_key[None], gain_ffn[None]], axis=0
    )
    small = pair_gather(small, dp_axes, dp_size)

    token_ring, small_ring = ring.gather(tokens), ring.gather(small, False)
    token_steps = [token_ring.step()]
    for k in range(half):
        small_ring.step(token_steps[0] if k > 1 else None)
    small = small_ring.stacked().transpose(2, 1, 0, 3).reshape(-1, width)
    router = jnp.pad(small[:num_experts], ((0, 2 * gate_columns - num_experts), (0, 0)))
    gains = small[num_experts:].astype(f32)
    gain_in, gain_q, gain_k, gain_mid = (gains[i][None, :] for i in range(4))
    gain_q = lax.dynamic_slice_in_dim(gain_q, f_index * part, part, 1)
    gain_k = lax.dynamic_slice_in_dim(gain_k, f_index * part, part, 1)
    half_dim = head_dim // 2
    inv_freq = rope_base ** (-(jnp.arange(half_dim, dtype=f32) * 2.0) / head_dim)
    angles = jnp.arange(span, dtype=jnp.int32).astype(f32)[:, None] * inv_freq[None, :]
    cosine, sine = jnp.cos(angles), jnp.sin(angles)
    cosine = jnp.concatenate([cosine, cosine], axis=1)
    sine = jnp.concatenate([-sine, sine], axis=1)
    out_rows = lax.ppermute(after(w_output, token_steps[0]), dp_flat, to_rows)
    token_steps.append(token_ring.step(packed))
    token_steps.append(token_ring.step())
    token_steps.append(
        token_ring.step((out_rows, router, gain_in, gain_q, gain_k, gain_mid, cosine, sine))
    )
    token_blocks = token_ring.blocks()
    w_in = share_relative(packed, dp_size, None, token_steps[2])
    w_out = share_relative(out_rows, dp_size, token_steps[2], token_steps[3])

    down_w = lax.all_gather(expert_down, dp_axes, axis=2, tiled=True)
    gate_w = lax.all_gather(expert_gate, dp_axes, axis=2, tiled=True)
    up_w = lax.all_gather(expert_up, dp_axes, axis=2, tiled=True)

    cot_ring = ring.gather(cotangent)
    cot_step = cot_ring.step(token_steps[3])
    normed, raw, in_factor, squares, x_all = project(
        ring, scalars, token_blocks, w_in, gain_in
    )
    squares = pair_sum(after(squares, (cot_step, w_out)), "fsdp", size)
    cot_step = cot_ring.step(squares)
    factors = lax.rsqrt(squares / width + epsilon)
    saved, attn_pieces = attend(
        ring, scalars, raw, factors, gain_q, gain_k, cosine, sine, w_out, head_dim
    )
    attn_ring = ring.reduce(after(attn_pieces, cot_step))
    attn_step = attn_ring.step()
    cot_step = cot_ring.step(attn_step)
    attn_ring.step()
    last_cot = cot_ring.step()
    attn_ring.step(cot_step)
    attn_ring.step(last_cot)
    resid_mid, mid_factor, mid_block, *routing = middle(
        tokens, attn_ring.last(), gain_mid, router, routes, num_experts
    )

    mid_ring = ring.gather(mid_block)
    mid_steps = [mid_ring.step()]
    mid_steps.append(mid_ring.step())
    back_act, cot_all = expert_first(
        ring, after(scalars, mid_steps[0]), cot_ring.blocks(), down_w
    )
    mid_ring.step(back_act)
    mid_ring.step()
    act, act_gated, d_gate, d_up, grad_gates, own_gates, mid_all = expert_hidden(
        ring, scalars, mid_ring.blocks(), gate_w, up_w, back_act
    )
    grad_in = expert_inputs(ring, scalars, d_gate, d_up, gate_w, up_w, grad_gates)

    def far_part(left, right, ties):
        return weight_far(after(left, ties), right)

    def cross(far, ties):
        return lax.ppermute(after(far, ties), dp_axes, exchange_pairs(dp_size, 1))

    def near_part(left, right, far, ties):
        return weight_near(scalars, after(left, ties), right, far, local_experts)

    def finish(near, ties):
        near = after(near, ties)
        return lax.psum_scatter(near, "x", scatter_dimension=0, tiled=True).astype(f32)

    grad_ring = ring.reduce(grad_in)
    grad_steps = [grad_ring.step()]
    gate_far = far_part(mid_all, d_gate, grad_in)
    grad_steps.append(grad_ring.step(gate_far))
    gate_cross = cross(gate_far, grad_steps[0])
    up_far = far_part(mid_all, d_up, grad_steps[0])
    grad_steps.append(grad_ring.step((up_far, gate_cross)))
    up_cross = cross(up_far, grad_steps[1])
    gate_near = near_part(mid_all, d_gate, gate_cross, grad_steps[1])
    grad_steps.append(grad_ring.step((gate_near, up_cross)))
    up_near = near_part(mid_all, d_up, up_cross, grad_steps[2])
    grad_resid, grad_low, grad_gain_mid, grad_router = middle_back(
        after(grad_ring.last(), up_near), cotangent, resid_mid, mid_factor,
        mid_block, *routing, gain_mid, router,
    )

    back_ring = ring.gather(grad_low)
    back_steps = [back_ring.step()]
    down_far = far_part(cot_all, act_gated, grad_low)
    back_steps.append(back_ring.step(down_far))
    down_cross = cross(down_far, back_steps[0])
    moe_pieces = expert_outputs(ring, after(scalars, back_steps[0]), act, own_gates, down_w)
    back_steps.append(back_ring.step((moe_pieces[0], down_cross)))
    down_near = near_part(cot_all, act_gated, down_cross, back_steps[1])
    back_steps.append(back_ring.step(down_near))
    grad_blocks = back_ring.blocks()

    def head_back(head, ties):
        return attend_back(
            ring, after(scalars, ties), saved, raw, factors, gain_q, gain_k, cosine, sine, w_out,
            grad_blocks, head_dim, head,
        )

    moe_ring = ring.reduce(moe_pieces)
    moe_step = moe_ring.step(back_steps[3])
    backs = [head_back(0, (back_steps[3], moe_step))]
    moe_step = moe_ring.step()
    for head in range(1, own_heads):
        backs.append(head_back(head, moe_step))
        if moe_ring.left > 1:
            moe_step = moe_ring.step(early=backs[head - 1][0])
    grad_attn_out = backs[0][6]
    dots = after(sum(back[3] for back in backs), moe_step)
    grad_gain_q = jnp.concatenate([back[4] for back in backs], axis=1)
    grad_gain_k = jnp.concatenate([back[5] for back in backs], axis=1)
    grad_w_out = dot(saved[3].astype(low), after(grad_attn_out, dots), rows_first)
    dots = pair_sum(dots, "fsdp", size) / width
    out_blocks = [
        lax.dynamic_slice_in_dim(grad_w_out, (d_index ^ k) * own_rows, own_rows, 0)
        for k in range(dp_size)
    ]
    out_far = jnp.stack([out_blocks[1], out_blocks[3]]).astype(low)
    while moe_ring.left > 0:
        moe_step = moe_ring.step(dots, backs[-1][0])
    layer_out = (resid_mid + moe_ring.total()).astype(low)
    grad_raw, grad_gain_in, normed_pieces = project_back(
        ring, scalars, [value for back in backs for value in back[:3]], raw, factors,
        after(dots, out_far), gain_q, gain_k, x_all, in_factor, w_in,
    )
    grad_w_out = combine_relative(out_far, [out_blocks[0], out_blocks[2]]).astype(low)
    normed_pieces = after(normed_pieces, (moe_step, grad_w_out))

    in_ring = ring.reduce(normed_pieces)
    in_steps = [in_ring.step()]
    grad_gains = lax.dynamic_update_slice(
        jnp.zeros((2, width), f32),
        jnp.concatenate([grad_gain_q, grad_gain_k], axis=0),
        (0, f_index * part),
    )
    sums = [grad_router[:num_experts], grad_gain_mid, grad_gain_in, grad_gains]
    sums.append(jnp.zeros((-(num_experts + 4) % 8, width), f32))
    grad_w_in = weight_rows(
        scalars, after(normed, normed_pieces), grad_raw, jnp.concatenate(sums, axis=0), dp_size
    )
    grad_gate_w = finish(gate_near, grad_ring.sent)
    grad_up_w = finish(up_near, grad_low)
    grad_down_w = finish(down_near, back_steps[3])
    in_steps.append(in_ring.step(early=grad_w_in))
    grad_w_in = combine_relative(*grad_w_in, (in_steps[0], in_steps[0])).astype(low)
    in_steps.append(in_ring.step(early=(grad_gate_w, grad_up_w)))
    in_steps.append(in_ring.step(early=grad_w_in))
    grad_normed = in_ring.total(grad_down_w)
    grad_w_in = after(grad_w_in, in_steps[2]).reshape(size, own_rows, -1)
    grad_w_in = lax.all_to_all(grad_w_in, "fsdp", split_axis=0, concat_axis=0, tiled=True)
    sums = jnp.sum(grad_w_in[:, :, 3 * part :].astype(f32), axis=0)
    grad_w_in = [
        grad_w_in[:, :, i * part : (i + 1) * part].transpose(1, 0, 2).reshape(own_rows, width)
        for i in range(3)
    ]
    grad_w_in = [values.astype(f32) for values in grad_w_in]
    grad_w_out = lax.ppermute(after(grad_w_out, in_steps[2]), dp_flat, from_rows).astype(f32)
    own_x = tokens.astype(f32)
    own_factor = lax.rsqrt(jnp.mean(own_x * own_x, axis=-1, keepdims=True) + epsilon)
    scaled_in = grad_normed * gain_in
    grad_tokens = (
        grad_resid
        + own_factor * scaled_in
        - own_x * own_factor**3 * jnp.mean(scaled_in * own_x, axis=-1, keepdims=True)
    )
    return (
        layer_out,
        grad_tokens,
        grad_w_in[0],
        grad_w_in[1],
        grad_w_in[2],
        grad_w_out,
        sums[:, :num_experts],
        sums[:, num_experts + 1],
        sums[:, num_experts + 2],
        sums[:, num_experts + 3],
        sums[:, num_experts],
        grad_gate_w,
        grad_up_w,
        grad_down_w,
    )


def splits_evenly(mesh):
    size, dp_size = mesh.shape["fsdp"], mesh.shape["dp"]
    powers = size & (size - 1) == 0 and dp_size & (dp_size - 1) == 0
    return powers and dp_size == 4 and size == 8 and HEADS % size == 0


def solution(mesh):
    split = splits_evenly(mesh)
    dp = "dp"
    if split:
        devices = mesh.devices.reshape(2, 2, mesh.shape["fsdp"])
        mesh, dp = jax.sharding.Mesh(devices, (*dp_axes, "fsdp")), dp_axes
    flat = (*dp_axes, "fsdp") if split else ("dp", "fsdp")
    in_specs = (
        P(flat, None),
        P(flat, None),
        P(flat, None),
        P(flat, None),
        P(flat, None),
        P(flat, None),
        P(flat, None),
        P(flat, None),
        P(flat),
        P(flat),
        P(flat),
        P(flat),
        P("fsdp", None, dp),
        P("fsdp", None, dp),
        P("fsdp", None, dp),
    )
    out_specs = (
        P(flat, None),
        P(flat, None),
        P(flat, None),
        P(flat, None),
        P(flat, None),
        P(flat, None),
        P(flat, None),
        P(flat),
        P(flat),
        P(flat),
        P(flat),
        P("fsdp", None, dp),
        P("fsdp", None, dp),
        P("fsdp", None, dp),
    )
    return jax.shard_map(
        per_device if split else per_device_gathered,
        mesh=mesh,
        in_specs=in_specs,
        out_specs=out_specs,
        check_vma=False,
    )
```
